32 devices in a mesh: seq: 4 (over y, x), ctx: 8 (over z, core).
Axes of the slice: x: 2, y: 2, z: 4, core: 2. Of those that a mesh axis runs over, the one named last changes fastest.
Arguments:
- hidden_in: bfloat16 [4, 2048, 2048], P('seq', 'ctx'), may hold values from -6 to 6
- attn_gain: bfloat16 [2048], P(('seq', 'ctx')), may hold values from 0.5 to 1.5
- w_query: bfloat16 [2048, 2048], P(('seq', 'ctx')), may hold values from -0.125 to 0.125
- w_key: bfloat16 [2048, 256], P(('seq', 'ctx')), may hold values from -0.125 to 0.125
- w_value: bfloat16 [2048, 256], P(('seq', 'ctx')), may hold values from -0.125 to 0.125
- w_out: bfloat16 [2048, 2048], P(('seq', 'ctx')), may hold values from -1 to 1
- ffn_gain: bfloat16 [2048], P(('seq', 'ctx')), may hold values from 0.5 to 1.5
- w_gate: bfloat16 [2048, 5632], P(('seq', 'ctx')), may hold values from -0.125 to 0.125
- w_up: bfloat16 [2048, 5632], P(('seq', 'ctx')), may hold values from -0.125 to 0.125
- w_down: bfloat16 [5632, 2048], P(('seq', 'ctx')), may hold values from -0.078125 to 0.078125
- cotangent: bfloat16 [4, 2048, 2048], P('seq', 'ctx'), may hold values from -6 to 6
- doc_lengths: int32 [4, 8], P('seq'), may hold values from 1 to 1024, 2048 in all within a row
- selected: int32 [4, 2048], P('seq', 'ctx'), may hold values 0 or 1
- block_order: int32 [16], replicated, may hold values from 0 to 15, each once
Outputs:
- output: bfloat16 [4, 2048, 2048], P('seq', 'ctx')
- grad_input: float32 [4, 2048, 2048], P('seq', 'ctx')
- grad_attn_gain: float32 [2048], P(('seq', 'ctx'))
- grad_w_query: float32 [2048, 2048], P(('seq', 'ctx'))
- grad_w_key: float32 [2048, 256], P(('seq', 'ctx'))
- grad_w_value: float32 [2048, 256], P(('seq', 'ctx'))
- grad_w_out: float32 [2048, 2048], P(('seq', 'ctx'))
- grad_ffn_gain: float32 [2048], P(('seq', 'ctx'))
- grad_w_gate: float32 [2048, 5632], P(('seq', 'ctx'))
- grad_w_up: float32 [2048, 5632], P(('seq', 'ctx'))
- grad_w_down: float32 [5632, 2048], P(('seq', 'ctx'))
The draws below stay inside these ranges and needn't reach their ends.
Inputs may be any that keep to these rules, and one draw needn't show every extreme that they name: `doc_lengths`: each row holds 8 lengths that sum to 2048; the largest is exactly 1024. `block_order`: each number appears once.
All inputs are finite; a program needn't handle non-finite values. No bound on the sum of `selected` on one device may be relied on, other than what follows from the above.
Results may differ from the reference program's by a relative error of at most 0.014.
Values may be sent and summed in bfloat16 or wider, within the bound.
A program may use at most 384 MiB of HBM per device.

```python
import math
import jax
import jax.numpy as jnp
import numpy as np
from jax import lax

D = 2048
HEADS = 32
KV_HEADS = 4
HEAD_DIM = 64
FF = 5632
LEN = 2048
DOCS = 8
SEQUENCES = 4
SPANS = 16
SPAN = 128
DOC_MOST = 1024


def plant(array, key, least, largest):
    dims = array.shape
    index_at = [jax.random.randint(jax.random.fold_in(key, axis), (), 0, dims[axis]) for axis in range(len(dims))]
    array = array.at[tuple(index_at)].set(least)
    longest = dims.index(max(dims))
    index_at[longest] = (index_at[longest] + 1) % dims[longest]
    return array.at[tuple(index_at)].set(largest)


def steps_of(key, shape, pieces, smallest, largest):
    gain, own = 1.0, jax.random.fold_in(key, 6)
    for position, shards_of in pieces:
        heights = jnp.exp(jax.random.uniform(jax.random.fold_in(own, position), (shards_of,), jnp.float32, smallest / len(pieces), largest / len(pieces)))
        gain = gain * jnp.repeat(heights, shape[position] // shards_of).reshape([-1 if axis == position else 1 for axis in range(len(shape))])
    return gain


def length_profile(number_of, total, limit, slope):
    portions = [(1 << 20) // math.isqrt(grade ** slope) + 1 for grade in range(2, number_of + 1)]
    surplus, holding = total - limit - (number_of - 1), [1] * (number_of - 1)
    while surplus > 0:
        movable = [i for i in range(number_of - 1) if holding[i] < limit]
        pool, remaining = sum([portions[i] for i in movable]), surplus
        for i in movable:
            extra = min(limit - holding[i], max(1, remaining * portions[i] // pool), surplus)
            holding[i] = holding[i] + extra
            surplus = surplus - extra
    return np.array([limit] + holding)


def ragged(rng, number_of, total, bound, skew):
    if number_of == 2:
        one = jax.random.randint(rng, (), max(1, total - bound), min(bound, total - 1) + 1)
        return jnp.stack([one, total - one])
    tallies = jnp.asarray(length_profile(number_of, total, bound, skew), jnp.int32)
    twos = (number_of - 1) // 2
    giver, sink = tallies[1:1 + 2 * twos:2], tallies[2:2 + 2 * twos:2]
    room = jnp.minimum(giver - 1, bound - sink)
    moved = jax.random.randint(jax.random.fold_in(rng, 1), (twos,), 0, 1 << 20) % (room + 1)
    tallies = tallies.at[1:1 + 2 * twos:2].set(giver - moved).at[2:2 + 2 * twos:2].set(sink + moved)
    return tallies[jax.random.permutation(jax.random.fold_in(rng, 2), number_of)]


def noise(rng, extent, width, bound, split=(), kind=jnp.bfloat16):
    drawn = width * jax.random.normal(rng, extent, jnp.float32)
    if split:
        drawn = drawn * steps_of(rng, extent, split, -0.22, 0.18)
    return jnp.clip(drawn, -bound, bound).astype(kind)


def setup_inputs(seed: int = 0) -> dict:
    splits = jax.random.split(jax.random.key(seed), 15)
    return {
        "hidden_in": noise(splits[0], (SEQUENCES, LEN, D), 1.0, 6.0, ((0, 4), (1, 8))),
        "attn_gain": jnp.clip(1.0 + 0.1 * jax.random.normal(splits[1], (D,), jnp.float32), 0.5, 1.5).astype(jnp.bfloat16),
        "w_query": noise(splits[2], (D, HEADS * HEAD_DIM), D ** -0.5, 0.125, ((0, 32),)),
        "w_key": noise(splits[3], (D, KV_HEADS * HEAD_DIM), D ** -0.5, 0.125, ((0, 32),)),
        "w_value": noise(splits[4], (D, KV_HEADS * HEAD_DIM), D ** -0.5, 0.125, ((0, 32),)),
        "w_out": noise(splits[5], (HEADS * HEAD_DIM, D), (HEADS * HEAD_DIM // 64) ** -0.5, 1.0, ((0, 32),)),
        "ffn_gain": jnp.clip(1.0 + 0.1 * jax.random.normal(splits[6], (D,), jnp.float32), 0.5, 1.5).astype(jnp.bfloat16),
        "w_gate": noise(splits[7], (D, FF), D ** -0.5, 0.125, ((0, 32),)),
        "w_up": noise(splits[8], (D, FF), D ** -0.5, 0.125, ((0, 32),)),
        "w_down": noise(splits[9], (FF, D), FF ** -0.5, 0.078125, ((0, 32),)),
        "cotangent": noise(splits[10], (SEQUENCES, LEN, D), 1.0, 6.0, ((0, 4), (1, 8))),
        "doc_lengths": jax.vmap(lambda own: ragged(own, DOCS, LEN, DOC_MOST, 2))(jax.random.split(splits[11], SEQUENCES)).reshape((SEQUENCES, DOCS)).astype(jnp.int32),
        "selected": plant((jax.random.randint(splits[12], (SEQUENCES, LEN), 0, 5) < 3).astype(jnp.int32), jax.random.fold_in(splits[12], 1), 0, 1),
        "block_order": jax.random.permutation(splits[13], SPANS).astype(jnp.int32),
    }


@jax.custom_vjp
def low(v):
    return lax.optimization_barrier(v.astype(jnp.bfloat16)).astype(jnp.float32)

@jax.custom_vjp
def low_back(v):
    return v

def low_keep(v):
    return (low(v), None)

def low_pass(kept, grad):
    return (grad,)

def back_keep(v):
    return (v, None)

def back_low(kept, grad):
    return (low(grad),)
low.defvjp(low_keep, low_pass)
low_back.defvjp(back_keep, back_low)
EPS = 1e-05
ROPE_BASE = 10000.0
NEG = -1e+30
PRECISE = lax.Precision.HIGHEST

def matmul(left, right):
    return jnp.dot(left, right, precision=PRECISE, preferred_element_type=jnp.float32)

def rotate(values):
    half = values.shape[-1] // 2
    return jnp.concatenate([-values[..., half:], values[..., :half]], axis=-1)

def rope_tables(positions, head_size):
    half = head_size // 2
    inverse = ROPE_BASE ** (-(jnp.arange(half, dtype=jnp.float32) * 2.0 / head_size))
    angle = positions.astype(jnp.float32)[:, None] * inverse[None, :]
    cosine = jnp.concatenate([jnp.cos(angle), jnp.cos(angle)], axis=1)
    sine = jnp.concatenate([jnp.sin(angle), jnp.sin(angle)], axis=1)
    return (cosine, sine)

def layer_one(hidden, documents, params, positions, cosine, sine):
    gain_a, w_query, w_key, w_value, w_out, gain_f, w_gate, w_up, w_down = params
    length = hidden.shape[0]
    group = HEADS // KV_HEADS
    scale = 1.0 / math.sqrt(HEAD_DIM)
    rms_a = lax.rsqrt(lax.optimization_barrier(jnp.mean(hidden * hidden, axis=1, keepdims=True)) + EPS)
    x_norm = low(hidden * rms_a * gain_a)
    queries = low_back(matmul(x_norm, w_query)).reshape(length, KV_HEADS, group, HEAD_DIM)
    queries = low(queries * cosine[:, None, None, :] + rotate(queries) * sine[:, None, None, :])
    keys = low_back(matmul(x_norm, w_key)).reshape(length, KV_HEADS, HEAD_DIM)
    keys = low(keys * cosine[:, None, :] + rotate(keys) * sine[:, None, :])
    values = low(low_back(matmul(x_norm, w_value))).reshape(length, KV_HEADS, HEAD_DIM)
    query_block = min(512, length)
    query_count = length // query_block

    def attend(items):
        part_q, part_pos, part_doc = items
        raw = jnp.einsum('rkgd,skd->kgrs', part_q, keys, precision=PRECISE)
        scores = low_back(raw * scale)
        allowed = (positions[None, :] <= part_pos[:, None]) & (documents[None, :] == part_doc[:, None])
        scores = jnp.where(allowed[None, None], scores, NEG)
        top_score = lax.optimization_barrier(jnp.max(scores, axis=-1, keepdims=True))
        expo = jnp.exp(scores - top_score)
        probs = expo / lax.optimization_barrier(jnp.sum(expo, axis=-1, keepdims=True))
        return jnp.einsum('kgrs,skd->rkgd', low(probs), values, precision=PRECISE)
    mixed = lax.map(jax.checkpoint(attend), (queries.reshape(query_count, query_block, KV_HEADS, group, HEAD_DIM), positions.reshape(query_count, query_block), documents.reshape(query_count, query_block)))
    attn_mix = low(low_back(mixed.reshape(length, HEADS * HEAD_DIM)))
    middle = hidden + low_back(matmul(attn_mix, w_out))
    rms_f = lax.rsqrt(lax.optimization_barrier(jnp.mean(middle * middle, axis=1, keepdims=True)) + EPS)
    f_norm = low(middle * rms_f * gain_f)
    gate = low_back(matmul(f_norm, w_gate))
    up_val = low_back(matmul(f_norm, w_up))
    hidden_act = low(gate * jax.nn.sigmoid(gate) * up_val)
    return middle + low_back(matmul(hidden_act, w_down))

def reference(hidden_in, attn_gain, w_query, w_key, w_value, w_out, ffn_gain, w_gate, w_up, w_down, cotangent, doc_lengths, selected, block_order):
    positions = (block_order[:, None] * SPAN + jnp.arange(SPAN, dtype=jnp.int32)[None, :]).reshape(LEN).astype(jnp.int32)
    ends = jnp.cumsum(doc_lengths, axis=1).astype(jnp.int32)
    documents = lax.optimization_barrier(jnp.sum((positions[None, :, None] >= ends[:, None, :]).astype(jnp.int32), axis=2))
    cosine, sine = rope_tables(positions, HEAD_DIM)
    params = (attn_gain.astype(jnp.float32), w_query.astype(jnp.float32), w_key.astype(jnp.float32), w_value.astype(jnp.float32), w_out.astype(jnp.float32), ffn_gain.astype(jnp.float32), w_gate.astype(jnp.float32), w_up.astype(jnp.float32), w_down.astype(jnp.float32))

    def forward(hidden_all, weights):

        def one_sequence(items):
            return layer_one(items[0], items[1], weights, positions, cosine, sine)
        return lax.map(jax.checkpoint(one_sequence), (hidden_all, documents))
    result, pullback = jax.vjp(forward, hidden_in.astype(jnp.float32), params)
    weighting = cotangent.astype(jnp.float32) * selected.astype(jnp.float32)[:, :, None]
    grad_input, grads = pullback(weighting)
    return (result.astype(jnp.bfloat16), grad_input, grads[0], grads[1], grads[2], grads[3], grads[4], grads[5], grads[6], grads[7], grads[8])
```

```python
import functools
import math

import jax
import jax.numpy as jnp
from jax import lax
from jax.experimental import pallas as pl
from jax.experimental.pallas import tpu as pltpu
from jax.sharding import PartitionSpec as P

HEADS = 32
KV_HEADS = 4
HEAD_DIM = 64
GROUP = HEADS // KV_HEADS
SCALE = 1.0 / math.sqrt(HEAD_DIM)
LOG2E = math.log2(math.e)


EPS = 1e-05
ROPE_BASE = 10000.0
NEG = -1e30

F32 = jnp.float32
BF16 = jnp.bfloat16
VMEM_MOST = 56 * 1024 * 1024


def dot32(left, right, dims):
    return lax.dot_general(left, right, (dims, ((), ())), preferred_element_type=F32)


def span_bounds(order_ref, lens_ref, span_len, spans, own_first, own):
    docs = lens_ref.shape[1]
    base = order_ref[own_first + own] * span_len
    pos = lax.broadcasted_iota(jnp.int32, (1, span_len), 1) + base
    start = jnp.zeros((1, span_len), jnp.int32)
    first_start = jnp.int32(0)
    end = jnp.int32(0)
    for number in range(docs):
        end = end + lens_ref[0, number]
        start = jnp.where(pos >= end, end, start)
        first_start = jnp.where(base >= end, end, first_start)
    return base, pos, start, first_start


def allowed_tile(key_base, span_len, pos, start):
    key_pos = lax.broadcasted_iota(jnp.int32, (span_len, span_len), 0) + key_base
    tile = (key_pos <= pos) & (key_pos >= start)
    return jnp.concatenate([tile.astype(F32)] * GROUP, axis=1) > 0.5


def stack_heads(ref, head, own, span_len):
    pieces = []
    for member in range(GROUP):
        row = (head * GROUP + member) * HEAD_DIM
        pieces.append(ref[row : row + HEAD_DIM, own * span_len : (own + 1) * span_len])
    return jnp.concatenate(pieces, axis=1)


def unstack_heads(ref, value, head, own, span_len):
    for member in range(GROUP):
        row = (head * GROUP + member) * HEAD_DIM
        ref[row : row + HEAD_DIM, own * span_len : (own + 1) * span_len] = value[
            :, member * span_len : (member + 1) * span_len
        ].astype(ref.dtype)


def attend_forward_kernel(
    span_len, spans, place_ref, order_ref, lens_ref, q_ref, kv_ref, o_ref, lse_ref, top_ref, sum_ref, acc_ref
):
    own_count = q_ref.shape[1] // span_len
    own_first = place_ref[0] * own_count
    width = KV_HEADS * HEAD_DIM
    for own in range(own_count):
        base, pos, start, first_start = span_bounds(
            order_ref, lens_ref, span_len, spans, own_first, own
        )
        top_ref[...] = jnp.full(top_ref.shape, NEG, F32)
        sum_ref[...] = jnp.zeros(sum_ref.shape, F32)
        acc_ref[...] = jnp.zeros(acc_ref.shape, F32)
        stacked = [stack_heads(q_ref, head, own, span_len) for head in range(KV_HEADS)]

        @pl.loop(0, spans)
        def _(number):
            key_base = order_ref[number] * span_len

            @pl.when((key_base <= base) & (key_base + span_len > first_start))
            def _():
                allowed = allowed_tile(key_base, span_len, pos, start)
                rows = pl.ds(pl.multiple_of(number * span_len, span_len), span_len)
                for head in range(KV_HEADS):
                    lower = head * HEAD_DIM
                    key = kv_ref[rows, lower : lower + HEAD_DIM]
                    value = kv_ref[rows, width + lower : width + lower + HEAD_DIM]
                    scores = dot32(key, stacked[head], ((1,), (0,))) * (SCALE * LOG2E)
                    scores = jnp.where(allowed, scores, NEG)
                    old = top_ref[head : head + 1, :]
                    new = jnp.maximum(old, jnp.max(scores, axis=0, keepdims=True))
                    decay = jnp.exp2(old - new)
                    expo = jnp.exp2(scores - new)
                    top_ref[head : head + 1, :] = new
                    sum_ref[head : head + 1, :] = sum_ref[head : head + 1, :] * decay + jnp.sum(
                        expo, axis=0, keepdims=True
                    )
                    part = dot32(value, expo.astype(BF16), ((0,), (0,)))
                    acc_ref[head] = acc_ref[head] * decay + part

        for head in range(KV_HEADS):
            total = sum_ref[head : head + 1, :]
            mixed = acc_ref[head] / total
            unstack_heads(o_ref, mixed, head, own, span_len)
            lse_ref[own, head : head + 1, :] = top_ref[head : head + 1, :] + jnp.log2(total)


def attend_backward_kernel(
    span_len,
    spans,
    place_ref,
    order_ref,
    lens_ref,
    q_ref,
    kv_ref,
    o_ref,
    lse_ref,
    do_ref,
    dq_ref,
    dkv_ref,
    dkv_acc,
    dq_acc,
    delta_ref,
):
    own_count = q_ref.shape[1] // span_len
    own_first = place_ref[0] * own_count
    width = KV_HEADS * HEAD_DIM
    dkv_acc[...] = jnp.zeros(dkv_acc.shape, F32)
    for own in range(own_count):
        base, pos, start, first_start = span_bounds(
            order_ref, lens_ref, span_len, spans, own_first, own
        )
        dq_acc[...] = jnp.zeros(dq_acc.shape, F32)
        queries = [stack_heads(q_ref, head, own, span_len) for head in range(KV_HEADS)]
        grads = [stack_heads(do_ref, head, own, span_len) for head in range(KV_HEADS)]
        for head in range(KV_HEADS):
            mixed = stack_heads(o_ref, head, own, span_len)
            delta_ref[head : head + 1, :] = jnp.sum(
                mixed.astype(F32) * grads[head].astype(F32), axis=0, keepdims=True
            )

        @pl.loop(0, spans)
        def _(number):
            key_base = order_ref[number] * span_len

            @pl.when((key_base <= base) & (key_base + span_len > first_start))
            def _():
                allowed = allowed_tile(key_base, span_len, pos, start)
                rows = pl.ds(pl.multiple_of(number * span_len, span_len), span_len)
                for head in range(KV_HEADS):
                    lower = head * HEAD_DIM
                    key = kv_ref[rows, lower : lower + HEAD_DIM]
                    value = kv_ref[rows, width + lower : width + lower + HEAD_DIM]
                    scores = dot32(key, queries[head], ((1,), (0,))) * (SCALE * LOG2E)
                    probs = jnp.where(
                        allowed, jnp.exp2(scores - lse_ref[own, head : head + 1, :]), 0.0
                    )
                    grad_probs = dot32(value, grads[head], ((1,), (0,)))
                    grad_scores = (probs * (grad_probs - delta_ref[head : head + 1, :])).astype(BF16)
                    probs = probs.astype(BF16)
                    dq_acc[head] = dq_acc[head] + dot32(key, grad_scores, ((0,), (0,)))
                    dkv_acc[rows, lower : lower + HEAD_DIM] = (
                        dkv_acc[rows, lower : lower + HEAD_DIM]
                        + dot32(grad_scores, queries[head], ((1,), (1,))) * SCALE
                    )
                    dkv_acc[rows, width + lower : width + lower + HEAD_DIM] = dkv_acc[
                        rows, width + lower : width + lower + HEAD_DIM
                    ] + dot32(probs, grads[head], ((1,), (1,)))

        for head in range(KV_HEADS):
            unstack_heads(dq_ref, dq_acc[head] * SCALE, head, own, span_len)
    dkv_ref[...] = dkv_acc[...].astype(dkv_ref.dtype)


def smem():
    return pl.BlockSpec(memory_space=pltpu.SMEM)


def vmem():
    return pl.BlockSpec(memory_space=pltpu.VMEM)


def attend_forward(place, block_order, doc_lengths, q_t, kv):
    spans = block_order.shape[0]
    span_len = kv.shape[0] // spans
    own_count = q_t.shape[1] // span_len
    lanes = GROUP * span_len
    return pl.pallas_call(
        functools.partial(attend_forward_kernel, span_len, spans),
        out_shape=(
            jax.ShapeDtypeStruct(q_t.shape, BF16),
            jax.ShapeDtypeStruct((own_count, KV_HEADS, lanes), F32),
        ),
        in_specs=[smem(), smem(), smem(), vmem(), vmem()],
        out_specs=(vmem(), vmem()),
        scratch_shapes=[
            pltpu.VMEM((KV_HEADS, lanes), F32),
            pltpu.VMEM((KV_HEADS, lanes), F32),
            pltpu.VMEM((KV_HEADS, HEAD_DIM, lanes), F32),
        ],
        compiler_params=pltpu.CompilerParams(vmem_limit_bytes=VMEM_MOST),
        cost_estimate=pl.CostEstimate(
            flops=2 * HEADS * HEAD_DIM * kv.shape[0] * q_t.shape[1],
            transcendentals=HEADS * kv.shape[0] * q_t.shape[1] // 2,
            bytes_accessed=4 * q_t.size + 2 * kv.size,
        ),
        name="attend_forward",
    )(place, block_order, doc_lengths, q_t, kv)


def attend_backward(place, block_order, doc_lengths, q_t, kv, o_t, lse, do_t):
    spans = block_order.shape[0]
    span_len = kv.shape[0] // spans
    lanes = GROUP * span_len
    return pl.pallas_call(
        functools.partial(attend_backward_kernel, span_len, spans),
        out_shape=(
            jax.ShapeDtypeStruct(q_t.shape, F32),
            jax.ShapeDtypeStruct(kv.shape, BF16),
        ),
        in_specs=[smem(), smem(), smem(), vmem(), vmem(), vmem(), vmem(), vmem()],
        out_specs=(vmem(), vmem()),
        scratch_shapes=[
            pltpu.VMEM(kv.shape, F32),
            pltpu.VMEM((KV_HEADS, HEAD_DIM, lanes), F32),
            pltpu.VMEM((KV_HEADS, lanes), F32),
        ],
        compiler_params=pltpu.CompilerParams(vmem_limit_bytes=VMEM_MOST),
        cost_estimate=pl.CostEstimate(
            flops=5 * HEADS * HEAD_DIM * kv.shape[0] * q_t.shape[1],
            transcendentals=HEADS * kv.shape[0] * q_t.shape[1] // 2,
            bytes_accessed=10 * q_t.size + 4 * kv.size,
        ),
        name="attend_backward",
    )(place, block_order, doc_lengths, q_t, kv, o_t, lse, do_t)


EVERY = ("seq", "ctx")


def gather(value, axes, dim=0):
    return lax.all_gather(value, axes, axis=dim, tiled=True)


def scatter_sum(value, axes, dim=0):
    return lax.psum_scatter(value, axes, scatter_dimension=dim, tiled=True)


def rotate_t(value):
    half = HEAD_DIM // 2
    heads = value.reshape(-1, HEAD_DIM, value.shape[1])
    return jnp.concatenate([-heads[:, half:], heads[:, :half]], axis=1)


def rope_t(value, cosine, sine):
    heads = value.reshape(-1, HEAD_DIM, value.shape[1])
    return (heads * cosine[None] + rotate_t(value) * sine[None]).reshape(value.shape)


def rope_back_t(value, cosine, sine):
    heads = value.reshape(-1, HEAD_DIM, value.shape[1])
    turned = rotate_t((heads * sine[None]).reshape(value.shape))
    return (heads * cosine[None] - turned).reshape(value.shape)


def norm_back(grad_normed, source, rms_val, gain_val, normed):
    grad_gain = jnp.sum(grad_normed * normed, axis=0)
    scaled = grad_normed * gain_val
    grad_source = rms_val * scaled - source * (rms_val * rms_val * rms_val) * jnp.mean(
        scaled * source, axis=1, keepdims=True
    )
    return (grad_gain, grad_source)


def local(
    hidden_in,
    attn_gain,
    w_query,
    w_key,
    w_value,
    w_out,
    ffn_gain,
    w_gate,
    w_up,
    w_down,
    cotangent,
    doc_lengths,
    selected,
    block_order,
):
    one, rows, model = hidden_in.shape
    seq_count = lax.axis_size("seq")
    ctx_count = lax.axis_size("ctx")
    place = lax.axis_index("ctx").astype(jnp.int32).reshape(1)
    length = rows * ctx_count
    span_len = length // block_order.shape[0]
    q_width = HEADS * HEAD_DIM
    kv_width = KV_HEADS * HEAD_DIM
    own_rows = w_gate.shape[0]
    ff_part = w_gate.shape[1] // seq_count

    def ffn_columns(weight):
        split = weight.reshape(own_rows, seq_count, ff_part).transpose(1, 0, 2)
        mine = lax.all_to_all(split, "seq", 0, 0, tiled=True)
        return gather(mine, "ctx", 1).reshape(model, ff_part)

    own_spans = lax.dynamic_slice_in_dim(block_order, place[0] * (rows // span_len), rows // span_len)
    local_pos = (
        own_spans[:, None] * span_len + jnp.arange(span_len, dtype=jnp.int32)[None, :]
    ).reshape(rows)
    half = HEAD_DIM // 2
    inverse = ROPE_BASE ** (-(jnp.arange(half, dtype=F32) * 2.0 / HEAD_DIM))
    angle = inverse[:, None] * local_pos.astype(F32)[None, :]
    cosine = jnp.concatenate([jnp.cos(angle)] * 2, axis=0)
    sine = jnp.concatenate([jnp.sin(angle)] * 2, axis=0)

    gains = gather(jnp.stack([attn_gain, ffn_gain])[None], EVERY)
    gain_a = gains[:, 0].reshape(model).astype(F32)
    gain_f = gains[:, 1].reshape(model).astype(F32)
    w_qkv = gather(jnp.concatenate([w_query, w_key, w_value], axis=1), EVERY)
    full_out = gather(w_out, EVERY)
    full_gate = ffn_columns(w_gate)
    full_up = ffn_columns(w_up)
    full_down = gather(w_down, "ctx")

    tokens = hidden_in.reshape(rows, model).astype(F32)
    rms_a = lax.rsqrt(jnp.mean(tokens * tokens, axis=1, keepdims=True) + EPS)
    normed_a = tokens * rms_a
    x_norm = (normed_a * gain_a).astype(BF16)
    qkv_t = jnp.einsum("td,dh->ht", x_norm, w_qkv, preferred_element_type=F32)
    q_t = rope_t(qkv_t[:q_width], cosine, sine).astype(BF16)
    k_t = rope_t(qkv_t[q_width : q_width + kv_width], cosine, sine).astype(BF16)
    v_t = qkv_t[q_width + kv_width :].astype(BF16)
    kv = gather(jnp.concatenate([k_t, v_t], axis=0).T, "ctx")
    o_t, lse = attend_forward(place, block_order, doc_lengths, q_t, kv)

    middle = tokens + jnp.einsum("ht,hd->td", o_t, full_out, preferred_element_type=F32)
    rms_f = lax.rsqrt(jnp.mean(middle * middle, axis=1, keepdims=True) + EPS)
    normed_f = middle * rms_f
    f_norm = (normed_f * gain_f).astype(BF16)

    grad_y = (
        cotangent.reshape(rows, model).astype(F32) * selected.reshape(rows).astype(F32)[:, None]
    )
    g_all = gather(grad_y.astype(BF16), "seq")
    f_all = gather(f_norm, "seq")
    gate = jnp.dot(f_all, full_gate, preferred_element_type=F32)
    up_val = jnp.dot(f_all, full_up, preferred_element_type=F32)
    sigma = jax.nn.sigmoid(gate)
    activated = gate * sigma
    hidden_act = (activated * up_val).astype(BF16)
    ffn_out = scatter_sum(
        jnp.dot(hidden_act, full_down, preferred_element_type=F32).astype(BF16), "seq"
    )
    output = (middle + ffn_out.astype(F32)).astype(BF16).reshape(one, rows, model)

    grad_hidden = jnp.einsum("td,fd->tf", g_all, full_down, preferred_element_type=F32)
    grad_gate = (grad_hidden * up_val * (sigma + activated * (1.0 - sigma))).astype(BF16)
    grad_up = (grad_hidden * activated).astype(BF16)
    grad_f_part = jnp.einsum(
        "tf,df->td", grad_gate, full_gate, preferred_element_type=F32
    ) + jnp.einsum("tf,df->td", grad_up, full_up, preferred_element_type=F32)
    grad_f_norm = scatter_sum(grad_f_part.astype(BF16), "seq").astype(F32)
    part_down = jnp.einsum("tf,td->fd", hidden_act, g_all, preferred_element_type=F32).astype(BF16)
    part_gate = jnp.einsum("td,tf->df", f_all, grad_gate, preferred_element_type=F32).astype(BF16)
    part_up = jnp.einsum("td,tf->df", f_all, grad_up, preferred_element_type=F32).astype(BF16)

    def ffn_rows(part):
        mine = scatter_sum(part.reshape(seq_count, model // seq_count, ff_part), "ctx", 1)
        return (
            lax.all_to_all(mine, "seq", 0, 0, tiled=True)
            .transpose(1, 0, 2)
            .reshape(own_rows, seq_count * ff_part)
            .astype(F32)
        )

    grad_w_down = scatter_sum(part_down, "ctx").astype(F32)
    grad_w_gate = ffn_rows(part_gate)
    grad_w_up = ffn_rows(part_up)

    grad_ffn_gain, grad_from_f = norm_back(grad_f_norm, middle, rms_f, gain_f, normed_f)
    grad_middle = grad_y + grad_from_f
    g_attn = grad_middle.astype(BF16)
    do_t = jnp.einsum("td,hd->ht", g_attn, full_out, preferred_element_type=F32).astype(BF16)
    part_out = jnp.einsum("ht,td->hd", o_t, g_attn, preferred_element_type=F32).astype(BF16)
    dq_t, dkv = attend_backward(place, block_order, doc_lengths, q_t, kv, o_t, lse, do_t)
    dkv_t = scatter_sum(dkv, "ctx").astype(F32).T
    grad_qkv_t = jnp.concatenate(
        [
            rope_back_t(dq_t, cosine, sine).astype(BF16),
            rope_back_t(dkv_t[:kv_width], cosine, sine).astype(BF16),
            dkv_t[kv_width:].astype(BF16),
        ],
        axis=0,
    )
    part_qkv = jnp.einsum("td,ht->dh", x_norm, grad_qkv_t, preferred_element_type=F32).astype(BF16)
    grad_x_norm = jnp.einsum("ht,dh->td", grad_qkv_t, w_qkv, preferred_element_type=F32)
    grad_attn_gain, grad_from_a = norm_back(grad_x_norm, tokens, rms_a, gain_a, normed_a)
    grad_input = (grad_middle + grad_from_a).reshape(one, rows, model)
    grad_w_out = scatter_sum(part_out, EVERY).astype(F32)
    grad_w_qkv = scatter_sum(part_qkv, EVERY).astype(F32)
    grad_gains = scatter_sum(jnp.stack([grad_attn_gain, grad_ffn_gain], axis=1), EVERY)
    return (
        output,
        grad_input,
        grad_gains[:, 0],
        grad_w_qkv[:, :q_width],
        grad_w_qkv[:, q_width : q_width + kv_width],
        grad_w_qkv[:, q_width + kv_width :],
        grad_w_out,
        grad_gains[:, 1],
        grad_w_gate,
        grad_w_up,
        grad_w_down,
    )


def solution(mesh):
    return jax.shard_map(
        local,
        mesh=mesh,
        in_specs=(
            P("seq", "ctx", None),
            P(("seq", "ctx")),
            P(("seq", "ctx"), None),
            P(("seq", "ctx"), None),
            P(("seq", "ctx"), None),
            P(("seq", "ctx"), None),
            P(("seq", "ctx")),
            P(("seq", "ctx"), None),
            P(("seq", "ctx"), None),
            P(("seq", "ctx"), None),
            P("seq", "ctx", None),
            P("seq", None),
            P("seq", "ctx"),
            P(),
        ),
        out_specs=(
            P("seq", "ctx", None),
            P("seq", "ctx", None),
            P(("seq", "ctx")),
            P(("seq", "ctx"), None),
            P(("seq", "ctx"), None),
            P(("seq", "ctx"), None),
            P(("seq", "ctx"), None),
            P(("seq", "ctx")),
            P(("seq", "ctx"), None),
            P(("seq", "ctx"), None),
            P(("seq", "ctx"), None),
        ),
        check_vma=False,
    )
```

```python
import functools
import math

import jax
import jax.numpy as jnp
from jax import lax
from jax.experimental import pallas as pl
from jax.experimental.pallas import tpu as pltpu
from jax.sharding import PartitionSpec as P

HEADS = 32
KV_HEADS = 4
HEAD_DIM = 64
GROUP = HEADS // KV_HEADS
SCALE = 1.0 / math.sqrt(HEAD_DIM)
LOG2E = math.log2(math.e)


EPS = 1e-05
ROPE_BASE = 10000.0
NEG = -1e30

F32 = jnp.float32
BF16 = jnp.bfloat16
VMEM_MOST = 56 * 1024 * 1024


def dot32(left, right, dims):
    return lax.dot_general(left, right, (dims, ((), ())), preferred_element_type=F32)


def span_bounds(order_ref, lens_ref, span_len, spans, own_first, own):
    docs = lens_ref.shape[1]
    base = order_ref[own_first + own] * span_len
    pos = lax.broadcasted_iota(jnp.int32, (1, span_len), 1) + base
    start = jnp.zeros((1, span_len), jnp.int32)
    first_start = jnp.int32(0)
    end = jnp.int32(0)
    for number in range(docs):
        end = end + lens_ref[0, number]
        start = jnp.where(pos >= end, end, start)
        first_start = jnp.where(base >= end, end, first_start)
    return base, pos, start, first_start


def allowed_tile(key_base, span_len, pos, start):
    key_pos = lax.broadcasted_iota(jnp.int32, (span_len, span_len), 0) + key_base
    tile = (key_pos <= pos) & (key_pos >= start)
    return jnp.concatenate([tile.astype(F32)] * GROUP, axis=1) > 0.5


def stack_heads(ref, head, own, span_len):
    pieces = []
    for member in range(GROUP):
        row = (head * GROUP + member) * HEAD_DIM
        pieces.append(ref[row : row + HEAD_DIM, own * span_len : (own + 1) * span_len])
    return jnp.concatenate(pieces, axis=1)


def unstack_heads(ref, value, head, own, span_len):
    for member in range(GROUP):
        row = (head * GROUP + member) * HEAD_DIM
        ref[row : row + HEAD_DIM, own * span_len : (own + 1) * span_len] = value[
            :, member * span_len : (member + 1) * span_len
        ].astype(ref.dtype)


def attend_forward_kernel(
    span_len, spans, place_ref, order_ref, lens_ref, q_ref, kv_ref, o_ref, lse_ref, top_ref, sum_ref, acc_ref
):
    own_count = q_ref.shape[1] // span_len
    own_first = place_ref[0] * own_count
    width = KV_HEADS * HEAD_DIM
    for own in range(own_count):
        base, pos, start, first_start = span_bounds(
            order_ref, lens_ref, span_len, spans, own_first, own
        )
        top_ref[...] = jnp.full(top_ref.shape, NEG, F32)
        sum_ref[...] = jnp.zeros(sum_ref.shape, F32)
        acc_ref[...] = jnp.zeros(acc_ref.shape, F32)
        stacked = [stack_heads(q_ref, head, own, span_len) for head in range(KV_HEADS)]

        @pl.loop(0, spans)
        def _(number):
            key_base = order_ref[number] * span_len

            @pl.when((key_base <= base) & (key_base + span_len > first_start))
            def _():
                allowed = allowed_tile(key_base, span_len, pos, start)
                rows = pl.ds(pl.multiple_of(number * span_len, span_len), span_len)
                for head in range(KV_HEADS):
                    lower = head * HEAD_DIM
                    key = kv_ref[rows, lower : lower + HEAD_DIM]
                    value = kv_ref[rows, width + lower : width + lower + HEAD_DIM]
                    scores = dot32(key, stacked[head], ((1,), (0,))) * (SCALE * LOG2E)
                    scores = jnp.where(allowed, scores, NEG)
                    old = top_ref[head : head + 1, :]
                    new = jnp.maximum(old, jnp.max(scores, axis=0, keepdims=True))
                    decay = jnp.exp2(old - new)
                    expo = jnp.exp2(scores - new)
                    top_ref[head : head + 1, :] = new
                    sum_ref[head : head + 1, :] = sum_ref[head : head + 1, :] * decay + jnp.sum(
                        expo, axis=0, keepdims=True
                    )
                    part = dot32(value, expo.astype(BF16), ((0,), (0,)))
                    acc_ref[head] = acc_ref[head] * decay + part

        for head in range(KV_HEADS):
            total = sum_ref[head : head + 1, :]
            mixed = acc_ref[head] / total
            unstack_heads(o_ref, mixed, head, own, span_len)
            lse_ref[own, head : head + 1, :] = top_ref[head : head + 1, :] + jnp.log2(total)


def attend_backward_kernel(
    span_len,
    spans,
    place_ref,
    order_ref,
    lens_ref,
    q_ref,
    kv_ref,
    o_ref,
    lse_ref,
    do_ref,
    dq_ref,
    dkv_ref,
    dkv_acc,
    dq_acc,
    delta_ref,
):
    own_count = q_ref.shape[1] // span_len
    own_first = place_ref[0] * own_count
    width = KV_HEADS * HEAD_DIM
    dkv_acc[...] = jnp.zeros(dkv_acc.shape, F32)
    for own in range(own_count):
        base, pos, start, first_start = span_bounds(
            order_ref, lens_ref, span_len, spans, own_first, own
        )
        dq_acc[...] = jnp.zeros(dq_acc.shape, F32)
        queries = [stack_heads(q_ref, head, own, span_len) for head in range(KV_HEADS)]
        grads = [stack_heads(do_ref, head, own, span_len) for head in range(KV_HEADS)]
        for head in range(KV_HEADS):
            mixed = stack_heads(o_ref, head, own, span_len)
            delta_ref[head : head + 1, :] = jnp.sum(
                mixed.astype(F32) * grads[head].astype(F32), axis=0, keepdims=True
            )

        @pl.loop(0, spans)
        def _(number):
            key_base = order_ref[number] * span_len

            @pl.when((key_base <= base) & (key_base + span_len > first_start))
            def _():
                allowed = allowed_tile(key_base, span_len, pos, start)
                rows = pl.ds(pl.multiple_of(number * span_len, span_len), span_len)
                for head in range(KV_HEADS):
                    lower = head * HEAD_DIM
                    key = kv_ref[rows, lower : lower + HEAD_DIM]
                    value = kv_ref[rows, width + lower : width + lower + HEAD_DIM]
                    scores = dot32(key, queries[head], ((1,), (0,))) * (SCALE * LOG2E)
                    probs = jnp.where(
                        allowed, jnp.exp2(scores - lse_ref[own, head : head + 1, :]), 0.0
                    )
                    grad_probs = dot32(value, grads[head], ((1,), (0,)))
                    grad_scores = (probs * (grad_probs - delta_ref[head : head + 1, :])).astype(BF16)
                    probs = probs.astype(BF16)
                    dq_acc[head] = dq_acc[head] + dot32(key, grad_scores, ((0,), (0,)))
                    dkv_acc[rows, lower : lower + HEAD_DIM] = (
                        dkv_acc[rows, lower : lower + HEAD_DIM]
                        + dot32(grad_scores, queries[head], ((1,), (1,))) * SCALE
                    )
                    dkv_acc[rows, width + lower : width + lower + HEAD_DIM] = dkv_acc[
                        rows, width + lower : width + lower + HEAD_DIM
                    ] + dot32(probs, grads[head], ((1,), (1,)))

        for head in range(KV_HEADS):
            unstack_heads(dq_ref, dq_acc[head] * SCALE, head, own, span_len)
    dkv_ref[...] = dkv_acc[...].astype(dkv_ref.dtype)


def smem():
    return pl.BlockSpec(memory_space=pltpu.SMEM)


def vmem():
    return pl.BlockSpec(memory_space=pltpu.VMEM)


def attend_forward(place, block_order, doc_lengths, q_t, kv):
    spans = block_order.shape[0]
    span_len = kv.shape[0] // spans
    own_count = q_t.shape[1] // span_len
    lanes = GROUP * span_len
    return pl.pallas_call(
        functools.partial(attend_forward_kernel, span_len, spans),
        out_shape=(
            jax.ShapeDtypeStruct(q_t.shape, BF16),
            jax.ShapeDtypeStruct((own_count, KV_HEADS, lanes), F32),
        ),
        in_specs=[smem(), smem(), smem(), vmem(), vmem()],
        out_specs=(vmem(), vmem()),
        scratch_shapes=[
            pltpu.VMEM((KV_HEADS, lanes), F32),
            pltpu.VMEM((KV_HEADS, lanes), F32),
            pltpu.VMEM((KV_HEADS, HEAD_DIM, lanes), F32),
        ],
        compiler_params=pltpu.CompilerParams(vmem_limit_bytes=VMEM_MOST),
        cost_estimate=pl.CostEstimate(
            flops=2 * HEADS * HEAD_DIM * kv.shape[0] * q_t.shape[1],
            transcendentals=HEADS * kv.shape[0] * q_t.shape[1] // 2,
            bytes_accessed=4 * q_t.size + 2 * kv.size,
        ),
        name="attend_forward",
    )(place, block_order, doc_lengths, q_t, kv)


def attend_backward(place, block_order, doc_lengths, q_t, kv, o_t, lse, do_t):
    spans = block_order.shape[0]
    span_len = kv.shape[0] // spans
    lanes = GROUP * span_len
    return pl.pallas_call(
        functools.partial(attend_backward_kernel, span_len, spans),
        out_shape=(
            jax.ShapeDtypeStruct(q_t.shape, F32),
            jax.ShapeDtypeStruct(kv.shape, BF16),
        ),
        in_specs=[smem(), smem(), smem(), vmem(), vmem(), vmem(), vmem(), vmem()],
        out_specs=(vmem(), vmem()),
        scratch_shapes=[
            pltpu.VMEM(kv.shape, F32),
            pltpu.VMEM((KV_HEADS, HEAD_DIM, lanes), F32),
            pltpu.VMEM((KV_HEADS, lanes), F32),
        ],
        compiler_params=pltpu.CompilerParams(vmem_limit_bytes=VMEM_MOST),
        cost_estimate=pl.CostEstimate(
            flops=5 * HEADS * HEAD_DIM * kv.shape[0] * q_t.shape[1],
            transcendentals=HEADS * kv.shape[0] * q_t.shape[1] // 2,
            bytes_accessed=10 * q_t.size + 4 * kv.size,
        ),
        name="attend_backward",
    )(place, block_order, doc_lengths, q_t, kv, o_t, lse, do_t)


MESH = pl.DeviceIdType.MESH


def coords():
    ctx = lax.axis_index("ctx")
    return lax.axis_index("seq"), ctx // 2, lax.rem(ctx, 2)


def other(place, step, count):
    return lax.rem(place + step, count)


def meet(devices):
    barrier = pltpu.get_barrier_semaphore()
    for device in devices:
        pl.semaphore_signal(barrier, inc=1, device_id=device, device_id_type=MESH)
    pl.semaphore_wait(barrier, len(devices))


def remote(source, target, send_sem, recv_sem, device):
    return pltpu.make_async_remote_copy(
        src_ref=source,
        dst_ref=target,
        send_sem=send_sem,
        recv_sem=recv_sem,
        device_id=device,
        device_id_type=MESH,
    )


def spread_kernel(scopes, seq_count, chip_count, *refs):
    count = len(scopes)
    sources, results = refs[:count], refs[count : 2 * count]
    sends, recvs, local_sem = refs[2 * count : 3 * count], refs[3 * count : 4 * count], refs[4 * count]
    seq, chip, core = coords()
    ctx = lax.axis_index("ctx")
    planes = [other(seq, step, seq_count) for step in range(1, seq_count)]
    chips = [other(chip, step, chip_count) for step in range(1, chip_count)]
    use_plane = any(scope != "ctx" for scope in scopes)
    use_ctx = any(scope in ("ctx", "all") for scope in scopes)
    sibling = {"ctx": chip * 2 + 1 - core}
    peers = []
    if use_plane:
        peers += [{"seq": place} for place in planes]
    if use_ctx:
        peers += [{"ctx": place * 2 + core} for place in chips] + [sibling]
    meet(peers)

    ctx_count = 2 * chip_count
    started = []
    numbers = [0] * count

    def block(item, at_seq, at_ctx):
        scope = scopes[item]
        if scope == "all":
            return results[item].at[at_seq, at_ctx], at_seq * ctx_count + at_ctx
        if scope == "ctx":
            return results[item].at[at_ctx], at_ctx
        return results[item].at[at_seq], at_seq

    def send(item, at_seq, at_ctx, device, source=None):
        target, number = block(item, at_seq, at_ctx)
        copy = remote(
            target if source is None else source,
            target,
            sends[item].at[numbers[item]],
            recvs[item].at[number],
            device,
        )
        numbers[item] += 1
        copy.start()
        started.append(copy)

    def arrive(item, at_seq, at_ctx):
        target, number = block(item, at_seq, at_ctx)
        remote(target, target, sends[item].at[0], recvs[item].at[number], sibling).wait_recv()

    locals_ = []
    for item, scope in enumerate(scopes):
        target, _ = block(item, seq, ctx)
        own = sources[item].at[seq] if scope == "swap" else sources[item]
        copy = pltpu.make_async_copy(own, target, local_sem.at[item])
        copy.start()
        locals_.append(copy)
    for item, scope in enumerate(scopes):
        if scope in ("seq", "swap"):
            for place in planes:
                source = sources[item].at[place] if scope == "swap" else sources[item]
                send(item, seq, ctx, {"seq": place}, source)
    for item, scope in enumerate(scopes):
        if scope in ("ctx", "all"):
            for place in chips:
                send(item, seq, ctx, {"ctx": place * 2 + core}, sources[item])
            if scope == "all":
                for place in planes:
                    send(item, seq, ctx, {"seq": place}, sources[item])
            send(item, seq, ctx, sibling, sources[item])
    for item, scope in enumerate(scopes):
        if scope in ("ctx", "all"):
            for place in chips:
                arrive(item, seq, place * 2 + core)
                if scope == "all":
                    for at_seq in planes:
                        send(item, seq, place * 2 + core, {"seq": at_seq})
                send(item, seq, place * 2 + core, sibling)
    for item, scope in enumerate(scopes):
        if scope == "all":
            for place in [chip] + chips:
                for at_seq in planes:
                    arrive(item, at_seq, place * 2 + core)
                    send(item, at_seq, place * 2 + core, sibling)
        elif scope in ("seq", "swap"):
            for at_seq in planes:
                arrive(item, at_seq, ctx)
    for item, scope in enumerate(scopes):
        if scope in ("ctx", "all"):
            for at_seq in [seq] + (planes if scope == "all" else []):
                for place in [chip] + chips:
                    arrive(item, at_seq, place * 2 + 1 - core)
    for copy in locals_:
        copy.wait()
    for copy in started:
        copy.wait_send()


def spread(name, collective_id, arrays, scopes, micros):
    seq_count, ctx_count = lax.axis_size("seq"), lax.axis_size("ctx")
    chip_count = ctx_count // 2
    shapes, send_sems, recv_sems = [], [], []
    for array, scope in zip(arrays, scopes):
        if scope == "all":
            lead, sends = (seq_count, ctx_count), seq_count * ctx_count - 1
        elif scope == "ctx":
            lead, sends = (ctx_count,), chip_count - 1 + chip_count
        elif scope == "seq":
            lead, sends = (seq_count,), seq_count - 1
        else:
            lead, sends = (), seq_count - 1
        shapes.append(jax.ShapeDtypeStruct(lead + array.shape, array.dtype))
        send_sems.append(pltpu.SemaphoreType.DMA((sends,)))
        recv_sems.append(pltpu.SemaphoreType.DMA((max(1, math.prod(lead)) if scope != "swap" else seq_count,)))
    anywhere = pl.BlockSpec(memory_space=pl.ANY)
    return pl.pallas_call(
        functools.partial(spread_kernel, scopes, seq_count, chip_count),
        out_shape=tuple(shapes),
        in_specs=[anywhere] * len(arrays),
        out_specs=(anywhere,) * len(arrays),
        scratch_shapes=send_sems + recv_sems + [pltpu.SemaphoreType.DMA((len(arrays),))],
        compiler_params=pltpu.CompilerParams(collective_id=collective_id, has_side_effects=True),
        cost_estimate=pl.CostEstimate(
            flops=0, transcendentals=0, bytes_accessed=int(micros * 3_000_000)
        ),
        name=name,
    )(*arrays)


def fold_kernel(plans, seq_count, chip_count, *refs):
    count = len(plans)
    sources, results = refs[:count], refs[count : 2 * count]
    rest = refs[2 * count :]
    per = 8
    seq, chip, core = coords()
    planes = [other(seq, step, seq_count) for step in range(1, seq_count)]
    chips = [other(chip, step, chip_count) for step in range(1, chip_count)]
    sibling = {"ctx": chip * 2 + 1 - core}
    peers = [{"ctx": place * 2 + core} for place in chips] + [sibling]
    if any(parts > 1 for parts, _ in plans):
        peers += [{"seq": place} for place in planes]
    meet(peers)

    waits = []
    firsts = []
    for item, (parts, chunks) in enumerate(plans):
        got1, _, _, _, _, _, sem_s, sem_r = rest[item * per : (item + 1) * per]
        width = sources[item].shape[-1] // chunks
        row = []
        for chunk in range(chunks):
            cols = slice(chunk * width, (chunk + 1) * width)
            copy = remote(
                sources[item].at[:, :, 1 - core, :, cols],
                got1.at[:, :, :, cols],
                sem_s.at[0, chunk, 0],
                sem_r.at[0, chunk, 0],
                sibling,
            )
            copy.start()
            row.append(copy)
        firsts.append(row)
        waits += row

    seconds = []
    for item, (parts, chunks) in enumerate(plans):
        got1, pass2, got2, keep, pass3, got3, sem_s, sem_r = rest[item * per : (item + 1) * per]
        width = sources[item].shape[-1] // chunks
        rows_of = []
        for chunk in range(chunks):
            cols = slice(chunk * width, (chunk + 1) * width)
            firsts[item][chunk].wait_recv()
            mine = []
            if parts > 1:
                for step, place in enumerate(planes):
                    pass2[step, :, :, cols] = (
                        sources[item][place, :, core, :, cols].astype(F32)
                        + got1[place, :, :, cols].astype(F32)
                    ).astype(BF16)
                    copy = remote(
                        pass2.at[step, :, :, cols],
                        got2.at[step, :, :, cols],
                        sem_s.at[1, chunk, step],
                        sem_r.at[1, chunk, step],
                        {"seq": place},
                    )
                    copy.start()
                    mine.append(copy)
                own = seq
            else:
                own = 0
            keep[:, :, cols] = sources[item][own, :, core, :, cols].astype(F32) + got1[
                own, :, :, cols
            ].astype(F32)
            rows_of.append(mine)
            waits += mine
        seconds.append(rows_of)

    thirds = []
    for item, (parts, chunks) in enumerate(plans):
        got1, pass2, got2, keep, pass3, got3, sem_s, sem_r = rest[item * per : (item + 1) * per]
        width = sources[item].shape[-1] // chunks
        rows_of = []
        for chunk in range(chunks):
            cols = slice(chunk * width, (chunk + 1) * width)
            if parts > 1:
                for copy in seconds[item][chunk]:
                    copy.wait_recv()

            def total(place):
                value = keep[place, :, cols]
                if parts > 1:
                    for step in range(seq_count - 1):
                        value = value + got2[step, place, :, cols].astype(F32)
                return value

            mine = []
            for step, place in enumerate(chips):
                pass3[step, :, cols] = total(place).astype(BF16)
                copy = remote(
                    pass3.at[step, :, cols],
                    got3.at[step, :, cols],
                    sem_s.at[2, chunk, step],
                    sem_r.at[2, chunk, step],
                    {"ctx": place * 2 + core},
                )
                copy.start()
                mine.append(copy)
            results[item][:, cols] = total(chip)
            rows_of.append(mine)
            waits += mine
        thirds.append(rows_of)

    for item, (parts, chunks) in enumerate(plans):
        got3 = rest[item * per + 5]
        width = sources[item].shape[-1] // chunks
        for chunk in range(chunks):
            cols = slice(chunk * width, (chunk + 1) * width)
            for copy in thirds[item][chunk]:
                copy.wait_recv()
            value = results[item][:, cols]
            for step in range(chip_count - 1):
                value = value + got3[step, :, cols].astype(F32)
            results[item][:, cols] = value
    for copy in waits:
        copy.wait_send()


def fold(name, collective_id, arrays, over_all, chunk_counts, micros):
    seq_count, ctx_count = lax.axis_size("seq"), lax.axis_size("ctx")
    chip_count = ctx_count // 2
    plans, inputs, shapes, scratch = [], [], [], []
    for array, every, chunks in zip(arrays, over_all, chunk_counts):
        parts = seq_count if every else 1
        rows = array.shape[0] // (parts * ctx_count)
        cols = array.shape[1]
        plans.append((parts, chunks))
        inputs.append(array.reshape(parts, chip_count, 2, rows, cols))
        shapes.append(jax.ShapeDtypeStruct((rows, cols), F32))
        many = max(parts - 1, 1)
        most = max(many, chip_count - 1)
        lines = chip_count if every else 1
        scratch += [
            pltpu.VMEM((parts, chip_count, rows, cols), BF16),
            pltpu.VMEM((many, lines, rows, cols), BF16),
            pltpu.VMEM((many, lines, rows, cols), BF16),
            pltpu.VMEM((chip_count, rows, cols), F32),
            pltpu.VMEM((chip_count - 1, rows, cols), BF16),
            pltpu.VMEM((chip_count - 1, rows, cols), BF16),
            pltpu.SemaphoreType.DMA((3, chunks, most)),
            pltpu.SemaphoreType.DMA((3, chunks, most)),
        ]
    return pl.pallas_call(
        functools.partial(fold_kernel, tuple(plans), seq_count, chip_count),
        out_shape=tuple(shapes),
        in_specs=[vmem()] * len(arrays),
        out_specs=(vmem(),) * len(arrays),
        scratch_shapes=scratch,
        compiler_params=pltpu.CompilerParams(
            collective_id=collective_id, has_side_effects=True, vmem_limit_bytes=VMEM_MOST
        ),
        cost_estimate=pl.CostEstimate(
            flops=0, transcendentals=0, bytes_accessed=int(micros * 3_000_000)
        ),
        name=name,
    )(*inputs)


EVERY = ("seq", "ctx")


def gather(value, axes, dim=0):
    return lax.all_gather(value, axes, axis=dim, tiled=True)


def scatter_sum(value, axes, dim=0):
    return lax.psum_scatter(value, axes, scatter_dimension=dim, tiled=True)


def rotate_t(value):
    half = HEAD_DIM // 2
    heads = value.reshape(-1, HEAD_DIM, value.shape[1])
    return jnp.concatenate([-heads[:, half:], heads[:, :half]], axis=1)


def rope_t(value, cosine, sine):
    heads = value.reshape(-1, HEAD_DIM, value.shape[1])
    return (heads * cosine[None] + rotate_t(value) * sine[None]).reshape(value.shape)


def rope_back_t(value, cosine, sine):
    heads = value.reshape(-1, HEAD_DIM, value.shape[1])
    turned = rotate_t((heads * sine[None]).reshape(value.shape))
    return (heads * cosine[None] - turned).reshape(value.shape)


def norm_back(grad_normed, source, rms_val, gain_val, normed):
    grad_gain = jnp.sum(grad_normed * normed, axis=0)
    scaled = grad_normed * gain_val
    grad_source = rms_val * scaled - source * (rms_val * rms_val * rms_val) * jnp.mean(
        scaled * source, axis=1, keepdims=True
    )
    return (grad_gain, grad_source)


def local(
    hidden_in,
    attn_gain,
    w_query,
    w_key,
    w_value,
    w_out,
    ffn_gain,
    w_gate,
    w_up,
    w_down,
    cotangent,
    doc_lengths,
    selected,
    block_order,
):
    one, rows, model = hidden_in.shape
    seq_count = lax.axis_size("seq")
    ctx_count = lax.axis_size("ctx")
    place = lax.axis_index("ctx").astype(jnp.int32).reshape(1)
    length = rows * ctx_count
    span_len = length // block_order.shape[0]
    q_width = HEADS * HEAD_DIM
    kv_width = KV_HEADS * HEAD_DIM
    own_rows = w_gate.shape[0]
    ff_part = w_gate.shape[1] // seq_count

    def split_columns(weight):
        return weight.reshape(own_rows, seq_count, ff_part).transpose(1, 0, 2)

    own_spans = lax.dynamic_slice_in_dim(block_order, place[0] * (rows // span_len), rows // span_len)
    local_pos = (
        own_spans[:, None] * span_len + jnp.arange(span_len, dtype=jnp.int32)[None, :]
    ).reshape(rows)
    half = HEAD_DIM // 2
    inverse = ROPE_BASE ** (-(jnp.arange(half, dtype=F32) * 2.0 / HEAD_DIM))
    angle = inverse[:, None] * local_pos.astype(F32)[None, :]
    cosine = jnp.concatenate([jnp.cos(angle)] * 2, axis=0)
    sine = jnp.concatenate([jnp.sin(angle)] * 2, axis=0)

    full_down = gather(w_down, "ctx")
    gain_row = jnp.pad(jnp.concatenate([attn_gain, ffn_gain])[None], ((0, 15), (0, 128 - 2 * own_rows)))
    gains, w_qkv, gate_mine, up_mine = spread(
        "gather_qkv",
        0,
        [
            gain_row,
            jnp.concatenate([w_query, w_key, w_value], axis=1),
            split_columns(w_gate),
            split_columns(w_up),
        ],
        ("all", "all", "swap", "swap"),
        85,
    )
    gain_a = gains[:, :, 0, :own_rows].reshape(model).astype(F32)
    gain_f = gains[:, :, 0, own_rows : 2 * own_rows].reshape(model).astype(F32)
    w_qkv = w_qkv.reshape(model, q_width + 2 * kv_width)
    full_gate = gather(gate_mine, "ctx", 1).reshape(model, ff_part)
    full_up = gather(up_mine, "ctx", 1).reshape(model, ff_part)

    tokens = hidden_in.reshape(rows, model).astype(F32)
    rms_a = lax.rsqrt(jnp.mean(tokens * tokens, axis=1, keepdims=True) + EPS)
    normed_a = tokens * rms_a
    x_norm = (normed_a * gain_a).astype(BF16)
    qkv_t = jnp.einsum("td,dh->ht", x_norm, w_qkv, preferred_element_type=F32)
    q_t = rope_t(qkv_t[:q_width], cosine, sine).astype(BF16)
    k_t = rope_t(qkv_t[q_width : q_width + kv_width], cosine, sine).astype(BF16)
    v_t = qkv_t[q_width + kv_width :].astype(BF16)
    kv, full_out = spread(
        "gather_kv_out", 1, [jnp.concatenate([k_t, v_t], axis=0).T, w_out], ("ctx", "all"), 85
    )
    kv = kv.reshape(length, 2 * kv_width)
    full_out = full_out.reshape(q_width, model)
    o_t, lse = attend_forward(place, block_order, doc_lengths, q_t, kv)

    middle = tokens + jnp.einsum("ht,hd->td", o_t, full_out, preferred_element_type=F32)
    rms_f = lax.rsqrt(jnp.mean(middle * middle, axis=1, keepdims=True) + EPS)
    normed_f = middle * rms_f
    f_norm = (normed_f * gain_f).astype(BF16)

    grad_y = (
        cotangent.reshape(rows, model).astype(F32) * selected.reshape(rows).astype(F32)[:, None]
    )
    g_all = gather(grad_y.astype(BF16), "seq")
    (f_all,) = spread("gather_f", 2, [f_norm], ("seq",), 45)
    f_all = f_all.reshape(seq_count * rows, model)
    gate = jnp.dot(f_all, full_gate, preferred_element_type=F32)
    up_val = jnp.dot(f_all, full_up, preferred_element_type=F32)
    sigma = jax.nn.sigmoid(gate)
    activated = gate * sigma
    hidden_act = (activated * up_val).astype(BF16)
    ffn_out = scatter_sum(
        jnp.dot(hidden_act, full_down, preferred_element_type=F32).astype(BF16), "seq"
    )
    output = (middle + ffn_out.astype(F32)).astype(BF16).reshape(one, rows, model)

    grad_hidden = jnp.einsum("td,fd->tf", g_all, full_down, preferred_element_type=F32)
    grad_gate = (grad_hidden * up_val * (sigma + activated * (1.0 - sigma))).astype(BF16)
    grad_up = (grad_hidden * activated).astype(BF16)
    grad_f_part = jnp.einsum(
        "tf,df->td", grad_gate, full_gate, preferred_element_type=F32
    ) + jnp.einsum("tf,df->td", grad_up, full_up, preferred_element_type=F32)
    (grad_f_parts,) = spread(
        "swap_grad_f", 3, [grad_f_part.astype(BF16).reshape(seq_count, rows, model)], ("swap",), 45
    )
    grad_f_norm = jnp.sum(grad_f_parts.astype(F32), axis=0)
    part_down = jnp.einsum("tf,td->fd", hidden_act, g_all, preferred_element_type=F32).astype(BF16)
    part_gate = jnp.einsum("td,tf->df", f_all, grad_gate, preferred_element_type=F32).astype(BF16)
    part_up = jnp.einsum("td,tf->df", f_all, grad_up, preferred_element_type=F32).astype(BF16)

    def ffn_rows(part):
        mine = scatter_sum(part.reshape(seq_count, model // seq_count, ff_part), "ctx", 1)
        return (
            lax.all_to_all(mine, "seq", 0, 0, tiled=True)
            .transpose(1, 0, 2)
            .reshape(own_rows, seq_count * ff_part)
            .astype(F32)
        )

    grad_w_down = scatter_sum(part_down, "ctx").astype(F32)
    grad_w_gate = ffn_rows(part_gate)
    grad_w_up = ffn_rows(part_up)

    grad_ffn_gain, grad_from_f = norm_back(grad_f_norm, middle, rms_f, gain_f, normed_f)
    grad_middle = grad_y + grad_from_f
    g_attn = grad_middle.astype(BF16)
    do_t = jnp.einsum("td,hd->ht", g_attn, full_out, preferred_element_type=F32).astype(BF16)
    part_out = jnp.einsum("ht,td->hd", o_t, g_attn, preferred_element_type=F32).astype(BF16)
    dq_t, dkv = attend_backward(place, block_order, doc_lengths, q_t, kv, o_t, lse, do_t)
    dkv_own, grad_w_out = fold("fold_kv_out", 4, [dkv, part_out], (False, True), (1, 4), 75)
    dkv_t = dkv_own.T
    grad_qkv_t = jnp.concatenate(
        [
            rope_back_t(dq_t, cosine, sine).astype(BF16),
            rope_back_t(dkv_t[:kv_width], cosine, sine).astype(BF16),
            dkv_t[kv_width:].astype(BF16),
        ],
        axis=0,
    )
    part_qkv = jnp.einsum("td,ht->dh", x_norm, grad_qkv_t, preferred_element_type=F32).astype(BF16)
    grad_x_norm = jnp.einsum("ht,dh->td", grad_qkv_t, w_qkv, preferred_element_type=F32)
    grad_attn_gain, grad_from_a = norm_back(grad_x_norm, tokens, rms_a, gain_a, normed_a)
    grad_input = (grad_middle + grad_from_a).reshape(one, rows, model)
    part_gains = jnp.concatenate(
        [grad_attn_gain.reshape(-1, own_rows), grad_ffn_gain.reshape(-1, own_rows)], axis=1
    )
    part_gains = jnp.pad(part_gains[:, None], ((0, 0), (0, 15), (0, 128 - 2 * own_rows)))
    grad_w_qkv, grad_gains = fold(
        "fold_qkv", 5, [part_qkv, part_gains.reshape(-1, 128).astype(BF16)], (True, True), (5, 1), 80
    )
    return (
        output,
        grad_input,
        grad_gains[0, :own_rows],
        grad_w_qkv[:, :q_width],
        grad_w_qkv[:, q_width : q_width + kv_width],
        grad_w_qkv[:, q_width + kv_width :],
        grad_w_out,
        grad_gains[0, own_rows : 2 * own_rows],
        grad_w_gate,
        grad_w_up,
        grad_w_down,
    )


def solution(mesh):
    return jax.shard_map(
        local,
        mesh=mesh,
        in_specs=(
            P("seq", "ctx", None),
            P(("seq", "ctx")),
            P(("seq", "ctx"), None),
            P(("seq", "ctx"), None),
            P(("seq", "ctx"), None),
            P(("seq", "ctx"), None),
            P(("seq", "ctx")),
            P(("seq", "ctx"), None),
            P(("seq", "ctx"), None),
            P(("seq", "ctx"), None),
            P("seq", "ctx", None),
            P("seq", None),
            P("seq", "ctx"),
            P(),
        ),
        out_specs=(
            P("seq", "ctx", None),
            P("seq", "ctx", None),
            P(("seq", "ctx")),
            P(("seq", "ctx"), None),
            P(("seq", "ctx"), None),
            P(("seq", "ctx"), None),
            P(("seq", "ctx"), None),
            P(("seq", "ctx")),
            P(("seq", "ctx"), None),
            P(("seq", "ctx"), None),
            P(("seq", "ctx"), None),
        ),
        check_vma=False,
    )
```

```python
import functools
import math

import jax
import jax.numpy as jnp
from jax import lax
from jax.experimental import pallas as pl
from jax.experimental.pallas import tpu as pltpu
from jax.sharding import PartitionSpec as P

HEADS = 32
KV_HEADS = 4
HEAD_DIM = 64
GROUP = HEADS // KV_HEADS
SCALE = 1.0 / math.sqrt(HEAD_DIM)
LOG2E = math.log2(math.e)


EPS = 1e-05
ROPE_BASE = 10000.0
NEG = -1e30

F32 = jnp.float32
BF16 = jnp.bfloat16
VMEM_MOST = 56 * 1024 * 1024


def dot32(left, right, dims):
    return lax.dot_general(left, right, (dims, ((), ())), preferred_element_type=F32)


def span_bounds(order_ref, lens_ref, span_len, spans, own_first, own):
    docs = lens_ref.shape[1]
    base = order_ref[own_first + own] * span_len
    pos = lax.broadcasted_iota(jnp.int32, (1, span_len), 1) + base
    start = jnp.zeros((1, span_len), jnp.int32)
    first_start = jnp.int32(0)
    end = jnp.int32(0)
    for number in range(docs):
        end = end + lens_ref[0, number]
        start = jnp.where(pos >= end, end, start)
        first_start = jnp.where(base >= end, end, first_start)
    return base, pos, start, first_start


def allowed_tile(key_base, span_len, pos, start):
    key_pos = lax.broadcasted_iota(jnp.int32, (span_len, span_len), 0) + key_base
    tile = (key_pos <= pos) & (key_pos >= start)
    return jnp.concatenate([tile.astype(F32)] * GROUP, axis=1) > 0.5


def stack_heads(ref, head, own, span_len):
    pieces = []
    for member in range(GROUP):
        row = (head * GROUP + member) * HEAD_DIM
        pieces.append(ref[row : row + HEAD_DIM, own * span_len : (own + 1) * span_len])
    return jnp.concatenate(pieces, axis=1)


def unstack_heads(ref, value, head, own, span_len):
    for member in range(GROUP):
        row = (head * GROUP + member) * HEAD_DIM
        ref[row : row + HEAD_DIM, own * span_len : (own + 1) * span_len] = value[
            :, member * span_len : (member + 1) * span_len
        ].astype(ref.dtype)


def attend_forward_kernel(
    span_len, spans, place_ref, order_ref, lens_ref, q_ref, kv_ref, o_ref, lse_ref, top_ref, sum_ref, acc_ref
):
    own_count = q_ref.shape[1] // span_len
    own_first = place_ref[0] * own_count
    width = KV_HEADS * HEAD_DIM
    for own in range(own_count):
        base, pos, start, first_start = span_bounds(
            order_ref, lens_ref, span_len, spans, own_first, own
        )
        top_ref[...] = jnp.full(top_ref.shape, NEG, F32)
        sum_ref[...] = jnp.zeros(sum_ref.shape, F32)
        acc_ref[...] = jnp.zeros(acc_ref.shape, F32)
        stacked = [stack_heads(q_ref, head, own, span_len) for head in range(KV_HEADS)]

        @pl.loop(0, spans)
        def _(number):
            key_base = order_ref[number] * span_len

            @pl.when((key_base <= base) & (key_base + span_len > first_start))
            def _():
                allowed = allowed_tile(key_base, span_len, pos, start)
                rows = pl.ds(pl.multiple_of(number * span_len, span_len), span_len)
                for head in range(KV_HEADS):
                    lower = head * HEAD_DIM
                    key = kv_ref[rows, lower : lower + HEAD_DIM]
                    value = kv_ref[rows, width + lower : width + lower + HEAD_DIM]
                    scores = dot32(key, stacked[head], ((1,), (0,))) * (SCALE * LOG2E)
                    scores = jnp.where(allowed, scores, NEG)
                    old = top_ref[head : head + 1, :]
                    new = jnp.maximum(old, jnp.max(scores, axis=0, keepdims=True))
                    decay = jnp.exp2(old - new)
                    expo = jnp.exp2(scores - new)
                    top_ref[head : head + 1, :] = new
                    sum_ref[head : head + 1, :] = sum_ref[head : head + 1, :] * decay + jnp.sum(
                        expo, axis=0, keepdims=True
                    )
                    part = dot32(value, expo.astype(BF16), ((0,), (0,)))
                    acc_ref[head] = acc_ref[head] * decay + part

        for head in range(KV_HEADS):
            total = sum_ref[head : head + 1, :]
            mixed = acc_ref[head] / total
            unstack_heads(o_ref, mixed, head, own, span_len)
            lse_ref[own, head : head + 1, :] = top_ref[head : head + 1, :] + jnp.log2(total)


def attend_backward_kernel(
    span_len,
    spans,
    place_ref,
    order_ref,
    lens_ref,
    q_ref,
    kv_ref,
    o_ref,
    lse_ref,
    do_ref,
    dq_ref,
    dkv_ref,
    dkv_acc,
    dq_acc,
    delta_ref,
):
    own_count = q_ref.shape[1] // span_len
    own_first = place_ref[0] * own_count
    width = KV_HEADS * HEAD_DIM
    dkv_acc[...] = jnp.zeros(dkv_acc.shape, F32)
    for own in range(own_count):
        base, pos, start, first_start = span_bounds(
            order_ref, lens_ref, span_len, spans, own_first, own
        )
        dq_acc[...] = jnp.zeros(dq_acc.shape, F32)
        queries = [stack_heads(q_ref, head, own, span_len) for head in range(KV_HEADS)]
        grads = [stack_heads(do_ref, head, own, span_len) for head in range(KV_HEADS)]
        for head in range(KV_HEADS):
            mixed = stack_heads(o_ref, head, own, span_len)
            delta_ref[head : head + 1, :] = jnp.sum(
                mixed.astype(F32) * grads[head].astype(F32), axis=0, keepdims=True
            )

        @pl.loop(0, spans)
        def _(number):
            key_base = order_ref[number] * span_len

            @pl.when((key_base <= base) & (key_base + span_len > first_start))
            def _():
                allowed = allowed_tile(key_base, span_len, pos, start)
                rows = pl.ds(pl.multiple_of(number * span_len, span_len), span_len)
                for head in range(KV_HEADS):
                    lower = head * HEAD_DIM
                    key = kv_ref[rows, lower : lower + HEAD_DIM]
                    value = kv_ref[rows, width + lower : width + lower + HEAD_DIM]
                    scores = dot32(key, queries[head], ((1,), (0,))) * (SCALE * LOG2E)
                    probs = jnp.where(
                        allowed, jnp.exp2(scores - lse_ref[own, head : head + 1, :]), 0.0
                    )
                    grad_probs = dot32(value, grads[head], ((1,), (0,)))
                    grad_scores = (probs * (grad_probs - delta_ref[head : head + 1, :])).astype(BF16)
                    probs = probs.astype(BF16)
                    dq_acc[head] = dq_acc[head] + dot32(key, grad_scores, ((0,), (0,)))
                    dkv_acc[rows, lower : lower + HEAD_DIM] = (
                        dkv_acc[rows, lower : lower + HEAD_DIM]
                        + dot32(grad_scores, queries[head], ((1,), (1,))) * SCALE
                    )
                    dkv_acc[rows, width + lower : width + lower + HEAD_DIM] = dkv_acc[
                        rows, width + lower : width + lower + HEAD_DIM
                    ] + dot32(probs, grads[head], ((1,), (1,)))

        for head in range(KV_HEADS):
            unstack_heads(dq_ref, dq_acc[head] * SCALE, head, own, span_len)
    dkv_ref[...] = dkv_acc[...].astype(dkv_ref.dtype)


def smem():
    return pl.BlockSpec(memory_space=pltpu.SMEM)


def vmem():
    return pl.BlockSpec(memory_space=pltpu.VMEM)


def attend_forward(place, block_order, doc_lengths, q_t, kv):
    spans = block_order.shape[0]
    span_len = kv.shape[0] // spans
    own_count = q_t.shape[1] // span_len
    lanes = GROUP * span_len
    return pl.pallas_call(
        functools.partial(attend_forward_kernel, span_len, spans),
        out_shape=(
            jax.ShapeDtypeStruct(q_t.shape, BF16),
            jax.ShapeDtypeStruct((own_count, KV_HEADS, lanes), F32),
        ),
        in_specs=[smem(), smem(), smem(), vmem(), vmem()],
        out_specs=(vmem(), vmem()),
        scratch_shapes=[
            pltpu.VMEM((KV_HEADS, lanes), F32),
            pltpu.VMEM((KV_HEADS, lanes), F32),
            pltpu.VMEM((KV_HEADS, HEAD_DIM, lanes), F32),
        ],
        compiler_params=pltpu.CompilerParams(vmem_limit_bytes=VMEM_MOST),
        cost_estimate=pl.CostEstimate(
            flops=2 * HEADS * HEAD_DIM * kv.shape[0] * q_t.shape[1],
            transcendentals=HEADS * kv.shape[0] * q_t.shape[1] // 2,
            bytes_accessed=4 * q_t.size + 2 * kv.size,
        ),
        name="attend_forward",
    )(place, block_order, doc_lengths, q_t, kv)


def attend_backward(place, block_order, doc_lengths, q_t, kv, o_t, lse, do_t):
    spans = block_order.shape[0]
    span_len = kv.shape[0] // spans
    lanes = GROUP * span_len
    return pl.pallas_call(
        functools.partial(attend_backward_kernel, span_len, spans),
        out_shape=(
            jax.ShapeDtypeStruct(q_t.shape, F32),
            jax.ShapeDtypeStruct(kv.shape, BF16),
        ),
        in_specs=[smem(), smem(), smem(), vmem(), vmem(), vmem(), vmem(), vmem()],
        out_specs=(vmem(), vmem()),
        scratch_shapes=[
            pltpu.VMEM(kv.shape, F32),
            pltpu.VMEM((KV_HEADS, HEAD_DIM, lanes), F32),
            pltpu.VMEM((KV_HEADS, lanes), F32),
        ],
        compiler_params=pltpu.CompilerParams(vmem_limit_bytes=VMEM_MOST),
        cost_estimate=pl.CostEstimate(
            flops=5 * HEADS * HEAD_DIM * kv.shape[0] * q_t.shape[1],
            transcendentals=HEADS * kv.shape[0] * q_t.shape[1] // 2,
            bytes_accessed=10 * q_t.size + 4 * kv.size,
        ),
        name="attend_backward",
    )(place, block_order, doc_lengths, q_t, kv, o_t, lse, do_t)


MESH = pl.DeviceIdType.MESH


def coords():
    ctx = lax.axis_index("ctx")
    return lax.axis_index("seq"), ctx // 2, lax.rem(ctx, 2)


def other(place, step, count):
    return lax.rem(place + step, count)


def meet(devices):
    barrier = pltpu.get_barrier_semaphore()
    for device in devices:
        pl.semaphore_signal(barrier, inc=1, device_id=device, device_id_type=MESH)
    pl.semaphore_wait(barrier, len(devices))


def remote(source, target, send_sem, recv_sem, device):
    return pltpu.make_async_remote_copy(
        src_ref=source,
        dst_ref=target,
        send_sem=send_sem,
        recv_sem=recv_sem,
        device_id=device,
        device_id_type=MESH,
    )


def spread_kernel(scopes, halves, seq_count, chip_count, *refs):
    count = len(scopes)
    sources, results = refs[:count], refs[count : 2 * count]
    sends, recvs, local_sem = refs[2 * count : 3 * count], refs[3 * count : 4 * count], refs[4 * count]
    seq, chip, core = coords()
    ctx = lax.axis_index("ctx")
    ctx_count = 2 * chip_count
    planes = [other(seq, step, seq_count) for step in range(1, seq_count)]
    chips = [other(chip, step, chip_count) for step in range(1, chip_count)]
    beside, above = seq + 1 - 2 * lax.rem(seq, 2), other(seq, 2, 4)
    sibling = {"ctx": chip * 2 + 1 - core}
    peers = []
    if any(scope != "ctx" for scope in scopes):
        peers += [{"seq": place} for place in planes]
    if any(scope in ("ctx", "all") for scope in scopes):
        peers += [{"ctx": place * 2 + core} for place in chips] + [sibling]
    meet(peers)

    started = []
    numbers = [0] * count

    def block(item, at_seq, at_ctx, half):
        scope = scopes[item]
        if scope == "all":
            ref, number = results[item].at[at_seq, at_ctx], at_seq * ctx_count + at_ctx
        elif scope == "ctx":
            ref, number = results[item].at[at_ctx], at_ctx
        else:
            ref, number = results[item].at[at_seq], at_seq
        return part(ref, item, half), 2 * number + (half or 0)

    def part(ref, item, half):
        if half is None:
            return ref
        rows = results[item].shape[-2] // 2
        return ref.at[pl.ds(half * rows, rows)]

    def send(item, at_seq, at_ctx, half, device, source=None):
        target, number = block(item, at_seq, at_ctx, half)
        copy = remote(
            target if source is None else part(source, item, half),
            target,
            sends[item].at[numbers[item]],
            recvs[item].at[number],
            device,
        )
        numbers[item] += 1
        copy.start()
        started.append(copy)

    def arrive(item, at_seq, at_ctx, half):
        target, number = block(item, at_seq, at_ctx, half)
        remote(target, target, sends[item].at[0], recvs[item].at[number], sibling).wait_recv()

    def cut(item):
        return (0, 1) if halves[item] else (None,)

    def plane_send(item, at_ctx, half, source=None):
        places = planes
        if halves[item]:
            places = (beside, above) if half == 0 else (above, beside)
        for place in places:
            send(item, seq, at_ctx, half, {"seq": place}, source)

    def plane_relay(item, at_ctx):
        if halves[item]:
            arrive(item, beside, at_ctx, 0)
            send(item, beside, at_ctx, 0, {"seq": above})
            arrive(item, above, at_ctx, 1)
            send(item, above, at_ctx, 1, {"seq": beside})

    def plane_end(item, at_ctx):
        if halves[item]:
            arrive(item, beside, at_ctx, 1)
            arrive(item, above, at_ctx, 0)
            arrive(item, 3 - seq, at_ctx, 0)
            arrive(item, 3 - seq, at_ctx, 1)
        else:
            for place in planes:
                arrive(item, place, at_ctx, None)
        if scopes[item] == "all":
            for place in planes:
                send(item, place, at_ctx, None, sibling)

    items = range(count)
    lines = [item for item in items if scopes[item] in ("ctx", "all")]
    flats = [item for item in items if scopes[item] in ("seq", "all")]
    everywhere = [item for item in items if scopes[item] == "all"]
    swaps = [item for item in items if scopes[item] == "swap"]
    locals_ = []
    for item in items:
        target, _ = block(item, seq, ctx, None)
        own = sources[item].at[seq] if scopes[item] == "swap" else sources[item]
        copy = pltpu.make_async_copy(own, target, local_sem.at[item])
        copy.start()
        locals_.append(copy)
    for item in lines:
        for half in cut(item):
            for place in chips:
                send(item, seq, ctx, half, {"ctx": place * 2 + core}, sources[item])
    for item in swaps:
        for place in planes:
            send(item, seq, ctx, None, {"seq": place}, sources[item].at[place])
    for item in flats:
        for half in cut(item):
            plane_send(item, ctx, half, sources[item])
    for item in lines:
        send(item, seq, ctx, None, sibling, sources[item])
    for item in flats:
        plane_relay(item, ctx)
    for index, place in enumerate(chips):
        at_ctx = place * 2 + core
        for item in lines:
            for half in cut(item):
                arrive(item, seq, at_ctx, half)
                if scopes[item] == "all":
                    plane_send(item, at_ctx, half)
            send(item, seq, at_ctx, None, sibling)
        for item in everywhere:
            if index:
                plane_relay(item, chips[index - 1] * 2 + core)
        if index == 0:
            for item in flats:
                plane_end(item, ctx)
        elif index > 1:
            for item in everywhere:
                plane_end(item, chips[index - 2] * 2 + core)
    for item in everywhere:
        plane_relay(item, chips[-1] * 2 + core)
        for place in chips[-2:]:
            plane_end(item, place * 2 + core)
    for item in swaps:
        for place in planes:
            arrive(item, place, ctx, None)
    for item in lines:
        for at_seq in [seq] + (planes if scopes[item] == "all" else []):
            for place in [chip] + chips:
                arrive(item, at_seq, place * 2 + 1 - core, None)
    for copy in locals_:
        copy.wait()
    for copy in started:
        copy.wait_send()


def spread(name, collective_id, arrays, scopes, micros):
    seq_count, ctx_count = lax.axis_size("seq"), lax.axis_size("ctx")
    chip_count = ctx_count // 2
    shapes, send_sems, recv_sems, halves = [], [], [], []
    for array, scope in zip(arrays, scopes):
        halved = seq_count == 4 and scope in ("all", "seq") and array.shape[0] % 32 == 0
        across = 6 if halved else seq_count - 1
        if scope == "all":
            lead = (seq_count, ctx_count)
            sends = (2 if halved else 1) * (chip_count - 1) + across * chip_count + seq_count * chip_count
        elif scope == "ctx":
            lead, sends = (ctx_count,), 2 * chip_count - 1
        else:
            lead, sends = (seq_count,), across
        halves.append(halved)
        shape = array.shape if scope == "swap" else lead + array.shape
        shapes.append(jax.ShapeDtypeStruct(shape, array.dtype))
        send_sems.append(pltpu.SemaphoreType.DMA((sends,)))
        recv_sems.append(pltpu.SemaphoreType.DMA((2 * math.prod(lead),)))
    anywhere = pl.BlockSpec(memory_space=pl.ANY)
    return pl.pallas_call(
        functools.partial(spread_kernel, scopes, tuple(halves), seq_count, chip_count),
        out_shape=tuple(shapes),
        in_specs=[anywhere] * len(arrays),
        out_specs=(anywhere,) * len(arrays),
        scratch_shapes=send_sems + recv_sems + [pltpu.SemaphoreType.DMA((len(arrays),))],
        compiler_params=pltpu.CompilerParams(collective_id=collective_id, has_side_effects=True),
        cost_estimate=pl.CostEstimate(
            flops=0, transcendentals=0, bytes_accessed=int(micros * 3_000_000)
        ),
        name=name,
    )(*arrays)


def fold_kernel(plans, swap_count, sum_count, seq_count, chip_count, *refs):
    count = len(plans)
    every = count + swap_count + sum_count
    sources, swap_sources = refs[:count], refs[count : count + swap_count]
    sum_sources = refs[count + swap_count : every]
    all_results = refs[every : 2 * every]
    results, swap_results = all_results[:count], all_results[count : count + swap_count]
    sum_results = all_results[count + swap_count :]
    rest = refs[2 * every :]
    per = 8
    swap_rest = rest[count * per :]
    sum_rest = swap_rest[4 * swap_count :]
    seq, chip, core = coords()
    planes = [other(seq, step, seq_count) for step in range(1, seq_count)]
    chips = [other(chip, step, chip_count) for step in range(1, chip_count)]
    sibling = {"ctx": chip * 2 + 1 - core}
    peers = [{"ctx": place * 2 + core} for place in chips] + [sibling]
    if swap_count or sum_count or any(parts > 1 for parts, _ in plans):
        peers += [{"seq": place} for place in planes]
    meet(peers)

    waits = []
    swapped = []
    for item in range(swap_count):
        got, sem_s, sem_r, sem_own = swap_rest[4 * item : 4 * item + 4]
        own = pltpu.make_async_copy(swap_sources[item].at[seq], got.at[seq], sem_own)
        own.start()
        swapped.append(own)
        for step, place in enumerate(planes):
            copy = remote(
                swap_sources[item].at[place], got.at[seq], sem_s.at[step], sem_r.at[seq], {"seq": place}
            )
            copy.start()
            waits.append(copy)
    firsts = []
    for item, (parts, chunks) in enumerate(plans):
        got1, _, _, _, _, _, sem_s, sem_r = rest[item * per : (item + 1) * per]
        width = sources[item].shape[-1] // chunks
        row = []
        for chunk in range(chunks):
            cols = slice(chunk * width, (chunk + 1) * width)
            copy = remote(
                sources[item].at[:, :, 1 - core, :, cols],
                got1.at[:, :, :, cols],
                sem_s.at[0, chunk, 0],
                sem_r.at[0, chunk, 0],
                sibling,
            )
            copy.start()
            row.append(copy)
        firsts.append(row)
        waits += row

    seconds = []
    for item, (parts, chunks) in enumerate(plans):
        got1, pass2, got2, keep, pass3, got3, sem_s, sem_r = rest[item * per : (item + 1) * per]
        width = sources[item].shape[-1] // chunks
        rows_of = []
        for chunk in range(chunks):
            cols = slice(chunk * width, (chunk + 1) * width)
            firsts[item][chunk].wait_recv()
            mine = []
            if parts > 1:
                for step, place in enumerate(planes):
                    pass2[step, :, :, cols] = (
                        sources[item][place, :, core, :, cols].astype(F32)
                        + got1[place, :, :, cols].astype(F32)
                    ).astype(BF16)
                    copy = remote(
                        pass2.at[step, :, :, cols],
                        got2.at[step, :, :, cols],
                        sem_s.at[1, chunk, step],
                        sem_r.at[1, chunk, step],
                        {"seq": place},
                    )
                    copy.start()
                    mine.append(copy)
                own = seq
            else:
                own = 0
            keep[:, :, cols] = sources[item][own, :, core, :, cols].astype(F32) + got1[
                own, :, :, cols
            ].astype(F32)
            rows_of.append(mine)
            waits += mine
        seconds.append(rows_of)

    slots, there = plane_slots(seq_count)
    summed = []
    for item in range(sum_count):
        got, sem_s, sem_r = sum_rest[3 * item : 3 * item + 3]
        row = []
        for slot in range(1, seq_count):
            copy = remote(
                sum_sources[item].at[slot],
                got.at[there[slot] - 1],
                sem_s.at[slot],
                sem_r.at[there[slot]],
                {"seq": slots[slot]},
            )
            copy.start()
            row.append(copy)
        summed.append(row)
        waits += row
    thirds = []
    for item, (parts, chunks) in enumerate(plans):
        got1, pass2, got2, keep, pass3, got3, sem_s, sem_r = rest[item * per : (item + 1) * per]
        width = sources[item].shape[-1] // chunks
        rows_of = []
        for chunk in range(chunks):
            cols = slice(chunk * width, (chunk + 1) * width)
            if parts > 1:
                for copy in seconds[item][chunk]:
                    copy.wait_recv()

            def total(place):
                value = keep[place, :, cols]
                if parts > 1:
                    for step in range(seq_count - 1):
                        value = value + got2[step, place, :, cols].astype(F32)
                return value

            mine = []
            for step, place in enumerate(chips):
                pass3[step, :, cols] = total(place).astype(BF16)
                copy = remote(
                    pass3.at[step, :, cols],
                    got3.at[step, :, cols],
                    sem_s.at[2, chunk, step],
                    sem_r.at[2, chunk, step],
                    {"ctx": place * 2 + core},
                )
                copy.start()
                mine.append(copy)
            results[item][:, cols] = total(chip)
            rows_of.append(mine)
            waits += mine
        thirds.append(rows_of)

    for item, (parts, chunks) in enumerate(plans):
        got3 = rest[item * per + 5]
        width = sources[item].shape[-1] // chunks
        for chunk in range(chunks):
            cols = slice(chunk * width, (chunk + 1) * width)
            for copy in thirds[item][chunk]:
                copy.wait_recv()
            value = results[item][:, cols]
            for step in range(chip_count - 1):
                value = value + got3[step, :, cols].astype(F32)
            results[item][:, cols] = value
    for item in range(sum_count):
        got = sum_rest[3 * item]
        for copy in summed[item]:
            copy.wait_recv()
        value = sum_sources[item][0].astype(F32)
        for step in range(seq_count - 1):
            value = value + got[step].astype(F32)
        sum_results[item][...] = value
    for item in range(swap_count):
        got, sem_s, sem_r, _ = swap_rest[4 * item : 4 * item + 4]
        swapped[item].wait()
        for place in planes:
            remote(got.at[place], got.at[place], sem_s.at[0], sem_r.at[place], sibling).wait_recv()
        width = got.shape[-1]
        for place in range(seq_count):
            swap_results[item][:, place * width : (place + 1) * width] = got[place].astype(F32)
    for copy in waits:
        copy.wait_send()


def fold(name, collective_id, arrays, over_all, chunk_counts, micros, swaps=(), sums=()):
    seq_count, ctx_count = lax.axis_size("seq"), lax.axis_size("ctx")
    chip_count = ctx_count // 2
    plans, inputs, shapes, scratch = [], [], [], []
    for array, every, chunks in zip(arrays, over_all, chunk_counts):
        parts = seq_count if every else 1
        rows = array.shape[0] // (parts * ctx_count)
        cols = array.shape[1]
        plans.append((parts, chunks))
        inputs.append(array.reshape(parts, chip_count, 2, rows, cols))
        shapes.append(jax.ShapeDtypeStruct((rows, cols), F32))
        many = max(parts - 1, 1)
        most = max(many, chip_count - 1)
        lines = chip_count if every else 1
        scratch += [
            pltpu.VMEM((parts, chip_count, rows, cols), BF16),
            pltpu.VMEM((many, lines, rows, cols), BF16),
            pltpu.VMEM((many, lines, rows, cols), BF16),
            pltpu.VMEM((chip_count, rows, cols), F32),
            pltpu.VMEM((chip_count - 1, rows, cols), BF16),
            pltpu.VMEM((chip_count - 1, rows, cols), BF16),
            pltpu.SemaphoreType.DMA((3, chunks, most)),
            pltpu.SemaphoreType.DMA((3, chunks, most)),
        ]
    for array in swaps:
        inputs.append(array)
        shapes.append(jax.ShapeDtypeStruct((array.shape[1], seq_count * array.shape[2]), F32))
        scratch += [
            pltpu.VMEM(array.shape, BF16),
            pltpu.SemaphoreType.DMA((seq_count - 1,)),
            pltpu.SemaphoreType.DMA((seq_count,)),
            pltpu.SemaphoreType.DMA,
        ]
    for array in sums:
        inputs.append(array)
        shapes.append(jax.ShapeDtypeStruct(array.shape[1:], F32))
        scratch += [
            pltpu.VMEM((seq_count - 1, *array.shape[1:]), BF16),
            pltpu.SemaphoreType.DMA((seq_count,)),
            pltpu.SemaphoreType.DMA((seq_count,)),
        ]
    return pl.pallas_call(
        functools.partial(
            fold_kernel, tuple(plans), len(swaps), len(sums), seq_count, chip_count
        ),
        out_shape=tuple(shapes),
        in_specs=[vmem()] * len(inputs),
        out_specs=(vmem(),) * len(inputs),
        scratch_shapes=scratch,
        compiler_params=pltpu.CompilerParams(
            collective_id=collective_id, has_side_effects=True, vmem_limit_bytes=VMEM_MOST
        ),
        cost_estimate=pl.CostEstimate(
            flops=0, transcendentals=0, bytes_accessed=int(micros * 3_000_000)
        ),
        name=name,
    )(*inputs)


def tiles(extent, width, visit):
    whole = extent // width

    @pl.loop(0, whole)
    def _(number):
        visit(pl.ds(pl.multiple_of(number * width, width), width))

    if extent % width:
        visit(pl.ds(whole * width, extent % width))


def stream_rows(extent, width, produce, stage, sem, target):
    whole = extent // width

    def leave(slot, rows, size):
        return pltpu.make_async_copy(
            stage.at[slot, pl.ds(0, size)], target.at[rows], sem.at[slot]
        )

    @pl.loop(0, whole)
    def _(number):
        slot = lax.rem(number, 2)
        rows = pl.ds(pl.multiple_of(number * width, width), width)

        @pl.when(number >= 2)
        def _():
            leave(slot, rows, width).wait()

        stage[slot] = produce(rows).astype(stage.dtype)
        leave(slot, rows, width).start()

    for number in range(max(0, whole - 2), whole):
        leave(number % 2, pl.ds(number * width, width), width).wait()
    if extent % width:
        size = extent % width
        rows = pl.ds(whole * width, size)
        stage[0, :size] = produce(rows).astype(stage.dtype)
        leave(0, rows, size).start()
        leave(0, rows, size).wait()


def plane_slots(seq_count):
    seq = lax.axis_index("seq")
    if seq_count == 4:
        beside, above = seq + 1 - 2 * lax.rem(seq, 2), other(seq, 2, 4)
        return [seq, beside, above, 3 - seq], [0, 1, 2, 3]
    return [seq] + [other(seq, step, seq_count) for step in range(1, seq_count)], [0] + [
        seq_count - step for step in range(1, seq_count)
    ]


def ffn_kernel(
    seq_count,
    f_ref,
    g_ref,
    wg_ref,
    wu_ref,
    wd_ref,
    gf_ref,
    out_ref,
    pg_ref,
    pu_ref,
    pd_ref,
    f_s,
    g_s,
    wg,
    wu,
    wd,
    gh,
    hid,
    gg,
    gu,
    parts,
    got,
    stage_f,
    stage_d,
    stage_o,
    in_sem,
    f_send,
    f_recv,
    x_send,
    x_recv,
    leave_sem,
):
    rows = f_ref.shape[0]
    model, width = wg.shape
    places, there = plane_slots(seq_count)
    meet([{"seq": place} for place in places[1:]])

    started = []

    def f_block(slot, half):
        if half is None:
            return f_s.at[pl.ds(slot * rows, rows)]
        return f_s.at[pl.ds(slot * rows + half * (rows // 2), rows // 2)]

    def f_copy(source, to, slot, half):
        copy = remote(
            source,
            f_block(slot, half),
            f_send.at[len(started)],
            f_recv.at[slot, half or 0],
            {"seq": places[to]},
        )
        copy.start()
        started.append(copy)

    def f_arrive(slot, half):
        block = f_block(slot, half)
        remote(
            block, block, f_send.at[0], f_recv.at[slot, half or 0], {"seq": places[1]}
        ).wait_recv()

    if seq_count == 4:
        for half in (0, 1):
            source = f_ref.at[pl.ds(half * (rows // 2), rows // 2)]
            for to in (1, 2) if half == 0 else (2, 1):
                f_copy(source, to, to, half)
    else:
        for to in range(1, seq_count):
            f_copy(f_ref, to, there[to], None)
    loads = []
    for slot in range(seq_count):
        loads.append(
            pltpu.make_async_copy(
                g_ref.at[places[slot]], g_s.at[pl.ds(slot * rows, rows)], in_sem.at[slot]
            )
        )
    load_wd = pltpu.make_async_copy(wd_ref, wd, in_sem.at[seq_count])
    load_f = pltpu.make_async_copy(f_ref, f_block(0, None), in_sem.at[seq_count + 1])
    load_wg = pltpu.make_async_copy(wg_ref, wg, in_sem.at[seq_count + 2])
    load_wu = pltpu.make_async_copy(wu_ref, wu, in_sem.at[seq_count + 3])
    for load in [*loads, load_wd, load_f, load_wg, load_wu]:
        load.start()
    for load in [*loads, load_wd]:
        load.wait()

    def grad_hidden(cols):
        gh[:, cols] = dot32(g_s[...], wd[cols, :], ((1,), (1,)))

    tiles(width, 256, grad_hidden)
    for load in (load_f, load_wg, load_wu):
        load.wait()

    def act(first, count, tile):
        own = slice(first, first + count)

        def visit(cols):
            gate = dot32(f_s[own, :], wg[:, cols], ((1,), (0,)))
            up_val = dot32(f_s[own, :], wu[:, cols], ((1,), (0,)))
            grad = gh[own, cols]
            sigma = jax.nn.sigmoid(gate)
            activated = gate * sigma
            hid[own, cols] = (activated * up_val).astype(BF16)
            gg[own, cols] = (grad * up_val * (sigma + activated * (1.0 - sigma))).astype(BF16)
            gu[own, cols] = (grad * activated).astype(BF16)

        tiles(width, tile, visit)

    act(0, rows, 256)
    if seq_count == 4:
        f_arrive(1, 0)
        f_copy(f_block(1, 0), 2, 3, 0)
        f_arrive(2, 1)
        f_copy(f_block(2, 1), 1, 3, 1)
        f_arrive(1, 1)
        f_arrive(2, 0)
        act(rows, 2 * rows, 256)
        f_arrive(3, 0)
        f_arrive(3, 1)
        act(3 * rows, rows, 256)
    else:
        for slot in range(1, seq_count):
            f_arrive(slot, None)
        act(rows, (seq_count - 1) * rows, 256)

    def part_copy(slot, cols):
        return remote(
            parts.at[pl.ds((slot - 1) * rows, rows), cols],
            got.at[there[slot] - 1, :, cols],
            x_send.at[slot],
            x_recv.at[there[slot]],
            {"seq": places[slot]},
        )

    def grad_f(cols):
        part = dot32(gg[...], wg[cols, :], ((1,), (1,))) + dot32(gu[...], wu[cols, :], ((1,), (1,)))
        gf_ref[:, cols] = part[:rows]
        parts[:, cols] = part[rows:].astype(BF16)
        for slot in range(1, seq_count):
            part_copy(slot, cols).start()

    tiles(model, 256, grad_f)
    stream_rows(
        width,
        256,
        lambda own: dot32(hid[:, own], g_s[...], ((0,), (0,))),
        stage_d,
        leave_sem.at[0],
        pd_ref,
    )
    stream_rows(
        model,
        256,
        lambda own: dot32(f_s[:, own], gg[...], ((0,), (0,))),
        stage_f,
        leave_sem.at[1],
        pg_ref,
    )
    stream_rows(
        model,
        256,
        lambda own: dot32(f_s[:, own], gu[...], ((0,), (0,))),
        stage_f,
        leave_sem.at[1],
        pu_ref,
    )

    def out_copy(cols):
        return pltpu.make_async_copy(stage_o.at[:, cols], out_ref.at[:, cols], leave_sem.at[2, 0])

    def out_part(cols):
        stage_o[:, cols] = dot32(hid[...], wd[:, cols], ((1,), (0,))).astype(BF16)
        out_copy(cols).start()

    tiles(model, 256, out_part)
    everything = pl.ds(0, model)
    out_copy(everything).wait()
    for slot in range(1, seq_count):
        part_copy(slot, everything).wait_recv()
    total = gf_ref[...]
    for slot in range(seq_count - 1):
        total = total + got[slot].astype(F32)
    gf_ref[...] = total
    for slot in range(1, seq_count):
        part_copy(slot, everything).wait_send()
    for copy in started:
        copy.wait_send()


def feed_forward(collective_id, f_norm, g_all, w_gate, w_up, w_down):
    seq_count = lax.axis_size("seq")
    rows, model = f_norm.shape
    width = w_gate.shape[1]
    count = seq_count * rows
    anywhere = pl.BlockSpec(memory_space=pl.ANY)
    dma = pltpu.SemaphoreType.DMA
    return pl.pallas_call(
        functools.partial(ffn_kernel, seq_count),
        out_shape=(
            jax.ShapeDtypeStruct((rows, model), F32),
            jax.ShapeDtypeStruct((count, model), BF16),
            jax.ShapeDtypeStruct((model, width), BF16),
            jax.ShapeDtypeStruct((model, width), BF16),
            jax.ShapeDtypeStruct((width, model), BF16),
        ),
        in_specs=[anywhere] * 5,
        out_specs=(vmem(), anywhere, anywhere, anywhere, anywhere),
        scratch_shapes=[
            pltpu.VMEM((count, model), BF16),
            pltpu.VMEM((count, model), BF16),
            pltpu.VMEM((model, width), BF16),
            pltpu.VMEM((model, width), BF16),
            pltpu.VMEM((width, model), BF16),
            pltpu.VMEM((count, width), F32),
            pltpu.VMEM((count, width), BF16),
            pltpu.VMEM((count, width), BF16),
            pltpu.VMEM((count, width), BF16),
            pltpu.VMEM((count - rows, model), BF16),
            pltpu.VMEM((seq_count - 1, rows, model), BF16),
            pltpu.VMEM((2, 256, width), BF16),
            pltpu.VMEM((2, 256, model), BF16),
            pltpu.VMEM((count, model), BF16),
            dma((seq_count + 4,)),
            dma((max(6, seq_count),)),
            dma((seq_count, 2)),
            dma((seq_count,)),
            dma((seq_count,)),
            dma((3, 2)),
        ],
        compiler_params=pltpu.CompilerParams(
            collective_id=collective_id, has_side_effects=True, vmem_limit_bytes=60 * 1024 * 1024
        ),
        cost_estimate=pl.CostEstimate(
            flops=18 * count * model * width,
            transcendentals=count * width,
            bytes_accessed=4 * (3 * width * model + 3 * count * model),
        ),
        name="feed_forward",
    )(f_norm, g_all.reshape(seq_count, rows, model), w_gate, w_up, w_down)


EVERY = ("seq", "ctx")


def gather(value, axes, dim=0):
    return lax.all_gather(value, axes, axis=dim, tiled=True)


def scatter_sum(value, axes, dim=0):
    return lax.psum_scatter(value, axes, scatter_dimension=dim, tiled=True)


def rotate_t(value):
    half = HEAD_DIM // 2
    heads = value.reshape(-1, HEAD_DIM, value.shape[1])
    return jnp.concatenate([-heads[:, half:], heads[:, :half]], axis=1)


def rope_t(value, cosine, sine):
    heads = value.reshape(-1, HEAD_DIM, value.shape[1])
    return (heads * cosine[None] + rotate_t(value) * sine[None]).reshape(value.shape)


def rope_back_t(value, cosine, sine):
    heads = value.reshape(-1, HEAD_DIM, value.shape[1])
    turned = rotate_t((heads * sine[None]).reshape(value.shape))
    return (heads * cosine[None] - turned).reshape(value.shape)


def norm_back(grad_normed, source, rms_val, gain_val, normed):
    grad_gain = jnp.sum(grad_normed * normed, axis=0)
    scaled = grad_normed * gain_val
    grad_source = rms_val * scaled - source * (rms_val * rms_val * rms_val) * jnp.mean(
        scaled * source, axis=1, keepdims=True
    )
    return (grad_gain, grad_source)


def local(
    hidden_in,
    attn_gain,
    w_query,
    w_key,
    w_value,
    w_out,
    ffn_gain,
    w_gate,
    w_up,
    w_down,
    cotangent,
    doc_lengths,
    selected,
    block_order,
):
    one, rows, model = hidden_in.shape
    seq_count = lax.axis_size("seq")
    ctx_count = lax.axis_size("ctx")
    place = lax.axis_index("ctx").astype(jnp.int32).reshape(1)
    length = rows * ctx_count
    span_len = length // block_order.shape[0]
    q_width = HEADS * HEAD_DIM
    kv_width = KV_HEADS * HEAD_DIM
    own_rows = w_gate.shape[0]
    ff_part = w_gate.shape[1] // seq_count

    def split_columns(weight):
        return weight.reshape(own_rows, seq_count, ff_part).transpose(1, 0, 2)

    own_spans = lax.dynamic_slice_in_dim(block_order, place[0] * (rows // span_len), rows // span_len)
    local_pos = (
        own_spans[:, None] * span_len + jnp.arange(span_len, dtype=jnp.int32)[None, :]
    ).reshape(rows)
    half = HEAD_DIM // 2
    inverse = ROPE_BASE ** (-(jnp.arange(half, dtype=F32) * 2.0 / HEAD_DIM))
    angle = inverse[:, None] * local_pos.astype(F32)[None, :]
    cosine = jnp.concatenate([jnp.cos(angle)] * 2, axis=0)
    sine = jnp.concatenate([jnp.sin(angle)] * 2, axis=0)

    full_down = gather(w_down, "ctx")
    gain_row = jnp.pad(jnp.concatenate([attn_gain, ffn_gain])[None], ((0, 15), (0, 128 - 2 * own_rows)))
    gains, w_qkv, gate_mine, up_mine = spread(
        "gather_qkv",
        0,
        [
            gain_row,
            jnp.concatenate([w_query, w_key, w_value], axis=1),
            split_columns(w_gate),
            split_columns(w_up),
        ],
        ("all", "all", "swap", "swap"),
        85,
    )
    gain_a = gains[:, :, 0, :own_rows].reshape(model).astype(F32)
    gain_f = gains[:, :, 0, own_rows : 2 * own_rows].reshape(model).astype(F32)
    w_qkv = w_qkv.reshape(model, q_width + 2 * kv_width)
    full_down, gate_mine, up_mine = lax.optimization_barrier((full_down, gate_mine, up_mine))
    full_gate = gather(gate_mine, "ctx", 1).reshape(model, ff_part)
    full_up = gather(up_mine, "ctx", 1).reshape(model, ff_part)

    grad_y = (
        cotangent.reshape(rows, model).astype(F32) * selected.reshape(rows).astype(F32)[:, None]
    )
    tokens = hidden_in.reshape(rows, model).astype(F32)
    rms_a = lax.rsqrt(jnp.mean(tokens * tokens, axis=1, keepdims=True) + EPS)
    normed_a = tokens * rms_a
    x_norm = (normed_a * gain_a).astype(BF16)
    qkv_t = jnp.einsum("td,dh->ht", x_norm, w_qkv, preferred_element_type=F32)
    q_t = rope_t(qkv_t[:q_width], cosine, sine).astype(BF16)
    k_t = rope_t(qkv_t[q_width : q_width + kv_width], cosine, sine).astype(BF16)
    v_t = qkv_t[q_width + kv_width :].astype(BF16)
    kv, full_out, g_all = spread(
        "gather_kv_out",
        1,
        [jnp.concatenate([k_t, v_t], axis=0).T, w_out, grad_y.astype(BF16)],
        ("ctx", "all", "seq"),
        85,
    )
    g_all = g_all.reshape(seq_count * rows, model)
    kv = kv.reshape(length, 2 * kv_width)
    full_out = full_out.reshape(q_width, model)
    o_t, lse = attend_forward(place, block_order, doc_lengths, q_t, kv)

    middle = tokens + jnp.einsum("ht,hd->td", o_t, full_out, preferred_element_type=F32)
    rms_f = lax.rsqrt(jnp.mean(middle * middle, axis=1, keepdims=True) + EPS)
    normed_f = middle * rms_f
    f_norm = (normed_f * gain_f).astype(BF16)

    grad_f_norm, ffn_part, part_gate, part_up, part_down = feed_forward(
        2, f_norm, g_all, full_gate, full_up, full_down
    )

    def ffn_rows(part):
        return scatter_sum(part.reshape(seq_count, model // seq_count, ff_part), "ctx", 1)

    grad_w_down = scatter_sum(part_down, "ctx").astype(F32)
    rows_gate = ffn_rows(part_gate)
    rows_up = ffn_rows(part_up)
    grad_ffn_gain, grad_from_f = norm_back(grad_f_norm, middle, rms_f, gain_f, normed_f)
    grad_middle = grad_y + grad_from_f
    g_attn = grad_middle.astype(BF16)
    do_t = jnp.einsum("td,hd->ht", g_attn, full_out, preferred_element_type=F32).astype(BF16)
    part_out = jnp.einsum("ht,td->hd", o_t, g_attn, preferred_element_type=F32).astype(BF16)
    dq_t, dkv = attend_backward(place, block_order, doc_lengths, q_t, kv, o_t, lse, do_t)
    dkv_own, grad_w_out, ffn_out = fold(
        "fold_kv_out",
        4,
        [dkv, part_out],
        (False, True),
        (1, 4),
        100,
        sums=[ffn_part.reshape(seq_count, rows, model)],
    )
    output = (middle + ffn_out).astype(BF16).reshape(one, rows, model)
    dkv_t = dkv_own.T
    grad_qkv_t = jnp.concatenate(
        [
            rope_back_t(dq_t, cosine, sine).astype(BF16),
            rope_back_t(dkv_t[:kv_width], cosine, sine).astype(BF16),
            dkv_t[kv_width:].astype(BF16),
        ],
        axis=0,
    )
    part_qkv = jnp.einsum("td,ht->dh", x_norm, grad_qkv_t, preferred_element_type=F32).astype(BF16)
    grad_x_norm = jnp.einsum("ht,dh->td", grad_qkv_t, w_qkv, preferred_element_type=F32)
    grad_attn_gain, grad_from_a = norm_back(grad_x_norm, tokens, rms_a, gain_a, normed_a)
    grad_input = (grad_middle + grad_from_a).reshape(one, rows, model)
    part_gains = jnp.concatenate(
        [grad_attn_gain.reshape(-1, own_rows), grad_ffn_gain.reshape(-1, own_rows)], axis=1
    )
    part_gains = jnp.pad(part_gains[:, None], ((0, 0), (0, 15), (0, 128 - 2 * own_rows)))
    grad_w_qkv, grad_gains, grad_w_gate, grad_w_up = fold(
        "fold_qkv",
        5,
        [part_qkv, part_gains.reshape(-1, 128).astype(BF16)],
        (True, True),
        (5, 1),
        80,
        [rows_gate, rows_up],
    )
    return (
        output,
        grad_input,
        grad_gains[0, :own_rows],
        grad_w_qkv[:, :q_width],
        grad_w_qkv[:, q_width : q_width + kv_width],
        grad_w_qkv[:, q_width + kv_width :],
        grad_w_out,
        grad_gains[0, own_rows : 2 * own_rows],
        grad_w_gate,
        grad_w_up,
        grad_w_down,
    )


def solution(mesh):
    return jax.shard_map(
        local,
        mesh=mesh,
        in_specs=(
            P("seq", "ctx", None),
            P(("seq", "ctx")),
            P(("seq", "ctx"), None),
            P(("seq", "ctx"), None),
            P(("seq", "ctx"), None),
            P(("seq", "ctx"), None),
            P(("seq", "ctx")),
            P(("seq", "ctx"), None),
            P(("seq", "ctx"), None),
            P(("seq", "ctx"), None),
            P("seq", "ctx", None),
            P("seq", None),
            P("seq", "ctx"),
            P(),
        ),
        out_specs=(
            P("seq", "ctx", None),
            P("seq", "ctx", None),
            P(("seq", "ctx")),
            P(("seq", "ctx"), None),
            P(("seq", "ctx"), None),
            P(("seq", "ctx"), None),
            P(("seq", "ctx"), None),
            P(("seq", "ctx")),
            P(("seq", "ctx"), None),
            P(("seq", "ctx"), None),
            P(("seq", "ctx"), None),
        ),
        check_vma=False,
    )
```

```python
import functools
import math

import jax
import jax.numpy as jnp
from jax import lax
from jax.experimental import pallas as pl
from jax.experimental.pallas import tpu as pltpu
from jax.sharding import PartitionSpec as P

HEADS = 32
KV_HEADS = 4
HEAD_DIM = 64
GROUP = HEADS // KV_HEADS
SCALE = 1.0 / math.sqrt(HEAD_DIM)
LOG2E = math.log2(math.e)


EPS = 1e-05
ROPE_BASE = 10000.0
NEG = -1e30

F32 = jnp.float32
BF16 = jnp.bfloat16
VMEM_MOST = 56 * 1024 * 1024


def dot32(left, right, dims):
    return lax.dot_general(left, right, (dims, ((), ())), preferred_element_type=F32)


def span_bounds(order_ref, lens_ref, span_len, spans, own_first, own):
    docs = lens_ref.shape[1]
    base = order_ref[own_first + own] * span_len
    pos = lax.broadcasted_iota(jnp.int32, (1, span_len), 1) + base
    start = jnp.zeros((1, span_len), jnp.int32)
    first_start = jnp.int32(0)
    end = jnp.int32(0)
    for number in range(docs):
        end = end + lens_ref[0, number]
        start = jnp.where(pos >= end, end, start)
        first_start = jnp.where(base >= end, end, first_start)
    return base, pos, start, first_start


def allowed_tile(key_base, span_len, pos, start):
    key_pos = lax.broadcasted_iota(jnp.int32, (span_len, span_len), 0) + key_base
    tile = (key_pos <= pos) & (key_pos >= start)
    return jnp.concatenate([tile.astype(F32)] * GROUP, axis=1) > 0.5


def stack_heads(ref, head, own, span_len):
    pieces = []
    for member in range(GROUP):
        row = (head * GROUP + member) * HEAD_DIM
        pieces.append(ref[row : row + HEAD_DIM, own * span_len : (own + 1) * span_len])
    return jnp.concatenate(pieces, axis=1)


def unstack_heads(ref, value, head, own, span_len):
    for member in range(GROUP):
        row = (head * GROUP + member) * HEAD_DIM
        ref[row : row + HEAD_DIM, own * span_len : (own + 1) * span_len] = value[
            :, member * span_len : (member + 1) * span_len
        ].astype(ref.dtype)


def attend_forward_kernel(
    span_len, spans, place_ref, order_ref, lens_ref, q_ref, kv_ref, o_ref, lse_ref, top_ref, sum_ref, acc_ref
):
    own_count = q_ref.shape[1] // span_len
    own_first = place_ref[0] * own_count
    width = KV_HEADS * HEAD_DIM
    for own in range(own_count):
        base, pos, start, first_start = span_bounds(
            order_ref, lens_ref, span_len, spans, own_first, own
        )
        top_ref[...] = jnp.full(top_ref.shape, NEG, F32)
        sum_ref[...] = jnp.zeros(sum_ref.shape, F32)
        acc_ref[...] = jnp.zeros(acc_ref.shape, F32)
        stacked = [stack_heads(q_ref, head, own, span_len) for head in range(KV_HEADS)]

        @pl.loop(0, spans)
        def _(number):
            key_base = order_ref[number] * span_len

            @pl.when((key_base <= base) & (key_base + span_len > first_start))
            def _():
                allowed = allowed_tile(key_base, span_len, pos, start)
                rows = pl.ds(pl.multiple_of(number * span_len, span_len), span_len)
                for head in range(KV_HEADS):
                    lower = head * HEAD_DIM
                    key = kv_ref[rows, lower : lower + HEAD_DIM]
                    value = kv_ref[rows, width + lower : width + lower + HEAD_DIM]
                    scores = dot32(key, stacked[head], ((1,), (0,))) * (SCALE * LOG2E)
                    scores = jnp.where(allowed, scores, NEG)
                    old = top_ref[head : head + 1, :]
                    new = jnp.maximum(old, jnp.max(scores, axis=0, keepdims=True))
                    decay = jnp.exp2(old - new)
                    expo = jnp.exp2(scores - new)
                    top_ref[head : head + 1, :] = new
                    sum_ref[head : head + 1, :] = sum_ref[head : head + 1, :] * decay + jnp.sum(
                        expo, axis=0, keepdims=True
                    )
                    part = dot32(value, expo.astype(BF16), ((0,), (0,)))
                    acc_ref[head] = acc_ref[head] * decay + part

        for head in range(KV_HEADS):
            total = sum_ref[head : head + 1, :]
            mixed = acc_ref[head] / total
            unstack_heads(o_ref, mixed, head, own, span_len)
            lse_ref[own, head : head + 1, :] = top_ref[head : head + 1, :] + jnp.log2(total)


def attend_backward_kernel(
    span_len,
    spans,
    place_ref,
    order_ref,
    lens_ref,
    q_ref,
    kv_ref,
    o_ref,
    lse_ref,
    do_ref,
    dq_ref,
    dkv_ref,
    dkv_acc,
    dq_acc,
    delta_ref,
):
    own_count = q_ref.shape[1] // span_len
    own_first = place_ref[0] * own_count
    width = KV_HEADS * HEAD_DIM
    dkv_acc[...] = jnp.zeros(dkv_acc.shape, F32)
    for own in range(own_count):
        base, pos, start, first_start = span_bounds(
            order_ref, lens_ref, span_len, spans, own_first, own
        )
        dq_acc[...] = jnp.zeros(dq_acc.shape, F32)
        queries = [stack_heads(q_ref, head, own, span_len) for head in range(KV_HEADS)]
        grads = [stack_heads(do_ref, head, own, span_len) for head in range(KV_HEADS)]
        for head in range(KV_HEADS):
            mixed = stack_heads(o_ref, head, own, span_len)
            delta_ref[head : head + 1, :] = jnp.sum(
                mixed.astype(F32) * grads[head].astype(F32), axis=0, keepdims=True
            )

        @pl.loop(0, spans)
        def _(number):
            key_base = order_ref[number] * span_len

            @pl.when((key_base <= base) & (key_base + span_len > first_start))
            def _():
                allowed = allowed_tile(key_base, span_len, pos, start)
                rows = pl.ds(pl.multiple_of(number * span_len, span_len), span_len)
                for head in range(KV_HEADS):
                    lower = head * HEAD_DIM
                    key = kv_ref[rows, lower : lower + HEAD_DIM]
                    value = kv_ref[rows, width + lower : width + lower + HEAD_DIM]
                    scores = dot32(key, queries[head], ((1,), (0,))) * (SCALE * LOG2E)
                    probs = jnp.where(
                        allowed, jnp.exp2(scores - lse_ref[own, head : head + 1, :]), 0.0
                    )
                    grad_probs = dot32(value, grads[head], ((1,), (0,)))
                    grad_scores = (probs * (grad_probs - delta_ref[head : head + 1, :])).astype(BF16)
                    probs = probs.astype(BF16)
                    dq_acc[head] = dq_acc[head] + dot32(key, grad_scores, ((0,), (0,)))
                    dkv_acc[rows, lower : lower + HEAD_DIM] = (
                        dkv_acc[rows, lower : lower + HEAD_DIM]
                        + dot32(grad_scores, queries[head], ((1,), (1,))) * SCALE
                    )
                    dkv_acc[rows, width + lower : width + lower + HEAD_DIM] = dkv_acc[
                        rows, width + lower : width + lower + HEAD_DIM
                    ] + dot32(probs, grads[head], ((1,), (1,)))

        for head in range(KV_HEADS):
            unstack_heads(dq_ref, dq_acc[head] * SCALE, head, own, span_len)
    dkv_ref[...] = dkv_acc[...].astype(dkv_ref.dtype)


def smem():
    return pl.BlockSpec(memory_space=pltpu.SMEM)


def vmem():
    return pl.BlockSpec(memory_space=pltpu.VMEM)


def attend_forward(place, block_order, doc_lengths, q_t, kv):
    spans = block_order.shape[0]
    span_len = kv.shape[0] // spans
    own_count = q_t.shape[1] // span_len
    lanes = GROUP * span_len
    return pl.pallas_call(
        functools.partial(attend_forward_kernel, span_len, spans),
        out_shape=(
            jax.ShapeDtypeStruct(q_t.shape, BF16),
            jax.ShapeDtypeStruct((own_count, KV_HEADS, lanes), F32),
        ),
        in_specs=[smem(), smem(), smem(), vmem(), vmem()],
        out_specs=(vmem(), vmem()),
        scratch_shapes=[
            pltpu.VMEM((KV_HEADS, lanes), F32),
            pltpu.VMEM((KV_HEADS, lanes), F32),
            pltpu.VMEM((KV_HEADS, HEAD_DIM, lanes), F32),
        ],
        compiler_params=pltpu.CompilerParams(vmem_limit_bytes=VMEM_MOST),
        cost_estimate=pl.CostEstimate(
            flops=2 * HEADS * HEAD_DIM * kv.shape[0] * q_t.shape[1],
            transcendentals=HEADS * kv.shape[0] * q_t.shape[1] // 2,
            bytes_accessed=4 * q_t.size + 2 * kv.size,
        ),
        name="attend_forward",
    )(place, block_order, doc_lengths, q_t, kv)


def attend_backward(place, block_order, doc_lengths, q_t, kv, o_t, lse, do_t):
    spans = block_order.shape[0]
    span_len = kv.shape[0] // spans
    lanes = GROUP * span_len
    return pl.pallas_call(
        functools.partial(attend_backward_kernel, span_len, spans),
        out_shape=(
            jax.ShapeDtypeStruct(q_t.shape, F32),
            jax.ShapeDtypeStruct(kv.shape, BF16),
        ),
        in_specs=[smem(), smem(), smem(), vmem(), vmem(), vmem(), vmem(), vmem()],
        out_specs=(vmem(), vmem()),
        scratch_shapes=[
            pltpu.VMEM(kv.shape, F32),
            pltpu.VMEM((KV_HEADS, HEAD_DIM, lanes), F32),
            pltpu.VMEM((KV_HEADS, lanes), F32),
        ],
        compiler_params=pltpu.CompilerParams(vmem_limit_bytes=VMEM_MOST),
        cost_estimate=pl.CostEstimate(
            flops=5 * HEADS * HEAD_DIM * kv.shape[0] * q_t.shape[1],
            transcendentals=HEADS * kv.shape[0] * q_t.shape[1] // 2,
            bytes_accessed=10 * q_t.size + 4 * kv.size,
        ),
        name="attend_backward",
    )(place, block_order, doc_lengths, q_t, kv, o_t, lse, do_t)


MESH = pl.DeviceIdType.MESH


def coords():
    ctx = lax.axis_index("ctx")
    return lax.axis_index("seq"), ctx // 2, lax.rem(ctx, 2)


def other(place, step, count):
    return lax.rem(place + step, count)


def meet(devices):
    barrier = pltpu.get_barrier_semaphore()
    for device in devices:
        pl.semaphore_signal(barrier, inc=1, device_id=device, device_id_type=MESH)
    pl.semaphore_wait(barrier, len(devices))


def remote(source, target, send_sem, recv_sem, device):
    return pltpu.make_async_remote_copy(
        src_ref=source,
        dst_ref=target,
        send_sem=send_sem,
        recv_sem=recv_sem,
        device_id=device,
        device_id_type=MESH,
    )


def plane_slots(seq_count):
    seq = lax.axis_index("seq")
    if seq_count == 4:
        beside, above = seq + 1 - 2 * lax.rem(seq, 2), other(seq, 2, 4)
        return [seq, beside, above, 3 - seq], [0, 1, 2, 3]
    return [seq] + [other(seq, step, seq_count) for step in range(1, seq_count)], [0] + [
        seq_count - step for step in range(1, seq_count)
    ]


def spread_kernel(scopes, halves, seq_count, chip_count, *refs):
    count = len(scopes)
    sources, results = refs[:count], refs[count : 2 * count]
    sends, recvs, local_sem = refs[2 * count : 3 * count], refs[3 * count : 4 * count], refs[4 * count]
    _, chip, core = coords()
    ctx = lax.axis_index("ctx")
    ctx_count = 2 * chip_count
    slots, _ = plane_slots(seq_count)
    seq, planes = slots[0], slots[1:]
    sibling = {"ctx": chip * 2 + 1 - core}
    last = chip_count - 1
    sides = [
        (chip < last, {"ctx": lax.rem(chip + 1, chip_count) * 2 + core}),
        (chip > 0, {"ctx": lax.rem(chip + last, chip_count) * 2 + core}),
    ]
    use_lines = any(scope in ("ctx", "all") for scope in scopes)
    peers = []
    if any(scope != "ctx" for scope in scopes):
        peers += [{"seq": place} for place in planes]
    if use_lines:
        peers += [{"ctx": other(chip, step, chip_count) * 2 + core} for step in range(1, chip_count)]
        peers += [sibling]
    meet(peers)

    started = []

    def part(ref, item, half):
        if half is None:
            return ref
        rows = results[item].shape[-2] // 2
        return ref.at[pl.ds(half * rows, rows)]

    def block(item, at_seq, place, at_core):
        scope = scopes[item]
        at_ctx = place * 2 + at_core
        if scope == "all":
            return results[item].at[at_seq, at_ctx], at_seq * ctx_count + at_ctx
        if scope == "ctx":
            return results[item].at[at_ctx], at_ctx
        return results[item].at[at_seq], at_seq

    def descriptor(item, at_seq, place, half, kind, device, source=None):
        target, number = block(item, at_seq, place, core)
        row = place if scopes[item] in ("ctx", "all") else 0
        return remote(
            part(target if source is None else source, item, half),
            part(target, item, half),
            sends[item].at[row, kind],
            recvs[item].at[2 * number + (half or 0)],
            device,
        )

    def arrival(item, at_seq, place, half, at_core=None):
        target, number = block(item, at_seq, place, core if at_core is None else at_core)
        view = part(target, item, half)
        return remote(
            view, view, sends[item].at[0, 0], recvs[item].at[2 * number + (half or 0)], sibling
        )

    def start(copies, there=None):
        for copy in copies:
            copy.start()
            started.append((there, copy))

    def cut(item):
        return (0, 1) if halves[item] else (None,)

    def plane_copies(item, place, half, source=None):
        if not halves[item]:
            return [
                descriptor(item, seq, place, None, 4 + number, {"seq": to}, source)
                for number, to in enumerate(planes)
            ]
        order = (1, 2) if half == 0 else (2, 1)
        return [
            descriptor(item, seq, place, half, 2 + 2 * half + to + 1, {"seq": slots[to]}, source)
            for to in order
        ]

    kinds_relay = 4 + max(4, seq_count - 1)

    def plane_relay(item, place, there=None):
        if not halves[item]:
            return
        steps = [
            (
                arrival(item, slots[give], place, half),
                descriptor(
                    item, slots[give], place, half, kinds_relay + half, {"seq": slots[3 - give]}
                ),
            )
            for give, half in ((1, 0), (2, 1))
        ]

        def run():
            for got, copy in steps:
                got.wait_recv()
                start([copy], there)

        run() if there is None else pl.when(there)(run)

    def plane_end(item, place, there=None):
        if halves[item]:
            ends = [
                (arrival(item, slots[slot], place, half))
                for slot, half in ((1, 1), (2, 0), (3, 0), (3, 1))
            ]
        else:
            ends = [arrival(item, at_seq, place, None) for at_seq in planes]
        copies = []
        if scopes[item] == "all":
            copies = [
                descriptor(item, at_seq, place, None, kinds_relay + 3 + number, sibling)
                for number, at_seq in enumerate(planes)
            ]

        def run():
            for got in ends:
                got.wait_recv()
            start(copies, there)

        run() if there is None else pl.when(there)(run)

    items = range(count)
    lines = [item for item in items if scopes[item] in ("ctx", "all")]
    flats = [item for item in items if scopes[item] in ("seq", "all")]
    everywhere = [item for item in items if scopes[item] == "all"]
    swaps = [item for item in items if scopes[item] == "swap"]
    locals_ = []
    for item in items:
        target, _ = block(item, seq, chip, core)
        own = sources[item].at[seq] if scopes[item] == "swap" else sources[item]
        copy = pltpu.make_async_copy(own, target, local_sem.at[item])
        copy.start()
        locals_.append(copy)
    for item in lines:
        for half in cut(item):
            for side, (there, device) in enumerate(sides):
                copy = descriptor(
                    item, seq, chip, half, 2 * side + (half or 0), device, sources[item]
                )
                pl.when(there)(functools.partial(start, [copy], there))
    for item in swaps:
        start(
            [
                descriptor(item, seq, chip, None, number, {"seq": place}, sources[item].at[place])
                for number, place in enumerate(planes)
            ]
        )
    for item in flats:
        for half in cut(item):
            start(plane_copies(item, chip, half, sources[item]))
    for item in lines:
        start([descriptor(item, seq, chip, None, kinds_relay + 2, sibling, sources[item])])
    for item in flats:
        plane_relay(item, chip)

    def pass_on(item, place, there, onward, device):
        steps = []
        for half in cut(item):
            steps.append(
                (
                    arrival(item, seq, place, half),
                    descriptor(item, seq, place, half, half or 0, device),
                    plane_copies(item, place, half) if scopes[item] == "all" else [],
                )
            )
        final = descriptor(item, seq, place, None, kinds_relay + 2, sibling)

        def run():
            for got, copy, copies in steps:
                got.wait_recv()
                pl.when(onward)(copy.start)
                start(copies, there)
            start([final], there)

        pl.when(there)(run)
        for _, copy, _ in steps:
            started.append((there & onward, copy))

    waves = []
    for step in range(1, chip_count):
        wave = [
            (lax.rem(chip + chip_count - step, chip_count), chip >= step, *sides[0]),
            (lax.rem(chip + step, chip_count), chip <= last - step, *sides[1]),
        ]
        for place, there, onward, device in wave:
            for item in lines:
                pass_on(item, place, there, onward, device)
        for item in everywhere:
            for place, there, _, _ in waves[-1] if waves else []:
                plane_relay(item, place, there)
        if step == 1:
            for item in flats:
                plane_end(item, chip)
        elif step > 2:
            for item in everywhere:
                for place, there, _, _ in waves[-2]:
                    plane_end(item, place, there)
        waves.append(wave)
    for item in everywhere:
        for place, there, _, _ in waves[-1]:
            plane_relay(item, place, there)
        for wave in waves[-2:]:
            for place, there, _, _ in wave:
                plane_end(item, place, there)
    for item in swaps:
        for place in planes:
            arrival(item, place, chip, None).wait_recv()
    for item in lines:
        for at_seq in [seq] + (planes if scopes[item] == "all" else []):
            for step in range(chip_count):
                arrival(item, at_seq, other(chip, step, chip_count), None, 1 - core).wait_recv()
    for copy in locals_:
        copy.wait()
    for there, copy in started:
        if there is None:
            copy.wait_send()
        else:
            pl.when(there)(copy.wait_send)


def spread(name, collective_id, arrays, scopes, micros):
    seq_count, ctx_count = lax.axis_size("seq"), lax.axis_size("ctx")
    chip_count = ctx_count // 2
    shapes, send_sems, recv_sems, halves = [], [], [], []
    kinds = 4 + max(4, seq_count - 1) + 3 + seq_count - 1
    for array, scope in zip(arrays, scopes):
        lead = {"all": (seq_count, ctx_count), "ctx": (ctx_count,)}.get(scope, (seq_count,))
        halves.append(seq_count == 4 and scope in ("all", "seq") and array.shape[0] % 32 == 0)
        shape = array.shape if scope == "swap" else lead + array.shape
        shapes.append(jax.ShapeDtypeStruct(shape, array.dtype))
        rows = chip_count if scope in ("all", "ctx") else 1
        send_sems.append(pltpu.SemaphoreType.DMA((rows, kinds)))
        recv_sems.append(pltpu.SemaphoreType.DMA((2 * math.prod(lead),)))
    anywhere = pl.BlockSpec(memory_space=pl.ANY)
    return pl.pallas_call(
        functools.partial(spread_kernel, scopes, tuple(halves), seq_count, chip_count),
        out_shape=tuple(shapes),
        in_specs=[anywhere] * len(arrays),
        out_specs=(anywhere,) * len(arrays),
        scratch_shapes=send_sems + recv_sems + [pltpu.SemaphoreType.DMA((len(arrays),))],
        compiler_params=pltpu.CompilerParams(collective_id=collective_id, has_side_effects=True),
        cost_estimate=pl.CostEstimate(
            flops=0, transcendentals=0, bytes_accessed=int(micros * 3_000_000)
        ),
        name=name,
    )(*arrays)


FOLD_SCRATCH = 9
WINDOW = 4


def fold_kernel(kinds, chunk_counts, swap_count, work, seq_count, chip_count, *refs):
    count = len(kinds)
    every = count + swap_count
    sources, swap_sources = refs[:count], refs[count:every]
    extra_in, extra_out = (work[0], work[1]) if work else (0, 0)
    first_out = every + extra_in
    results = refs[first_out : first_out + count]
    swap_results = refs[first_out + count : first_out + every]
    first_rest = first_out + every + extra_out
    rest = refs[first_rest:]
    swap_rest = rest[count * FOLD_SCRATCH : count * FOLD_SCRATCH + 4 * swap_count]
    extra = (
        refs[every:first_out],
        refs[first_out + every : first_rest],
        rest[count * FOLD_SCRATCH + 4 * swap_count :],
    )
    seq, chip, core = coords()
    slots, there = plane_slots(seq_count)
    planes = slots[1:]
    chips = [other(chip, step, chip_count) for step in range(1, chip_count)]
    sibling = {"ctx": chip * 2 + 1 - core}
    peers = []
    if any(kind != "seq" for kind in kinds):
        peers += [{"ctx": place * 2 + core} for place in chips] + [sibling]
    if swap_count or any(kind != "ctx" for kind in kinds):
        peers += [{"seq": place} for place in planes]

    def scratch(item):
        return rest[item * FOLD_SCRATCH : (item + 1) * FOLD_SCRATCH]

    def columns(item, chunk):
        width = sources[item].shape[-1] // chunk_counts[item]
        return slice(chunk * width, (chunk + 1) * width)

    order = []
    for chunk in range(max(chunk_counts, default=0)):
        order += [(item, chunk) for item in range(count) if chunk < chunk_counts[item]]

    loads = []
    for item in range(count):
        mine, sem_s = scratch(item)[0], scratch(item)[7]
        if kinds[item] != "seq":
            load = pltpu.make_async_copy(
                sources[item].at[:, :, core], mine, sem_s.at[4, 0, 0]
            )
            load.start()
            loads.append(load)
    meet(peers)

    waits = []

    def go(source, target, send_sem, recv_sem, device):
        copy = remote(source, target, send_sem, recv_sem, device)
        copy.start()
        waits.append(copy)
        return copy

    firsts = {}
    for item, chunk in order:
        if kinds[item] != "seq":
            _, got1, _, _, _, _, _, sem_s, sem_r = scratch(item)
            cols = columns(item, chunk)
            firsts[item, chunk] = go(
                sources[item].at[:, :, 1 - core, :, cols],
                got1.at[:, :, :, cols],
                sem_s.at[0, chunk, 0],
                sem_r.at[0, chunk, 0],
                sibling,
            )
    swapped = []
    for item in range(swap_count):
        got, sem_s, sem_r, sem_own = swap_rest[4 * item : 4 * item + 4]
        own = pltpu.make_async_copy(swap_sources[item].at[seq], got.at[seq], sem_own)
        own.start()
        swapped.append(own)
        for step, place in enumerate(planes):
            go(swap_sources[item].at[place], got.at[seq], sem_s.at[step], sem_r.at[seq], {"seq": place})
    for load in loads:
        load.wait()

    def block(item, slot, cols):
        if kinds[item] == "seq":
            return sources[item][slot, :, cols].astype(F32)[None]
        mine, got1 = scratch(item)[:2]
        place = slots[slot] if kinds[item] == "all" else 0
        return mine[place, :, :, cols].astype(F32) + got1[place, :, :, cols].astype(F32)

    def turn(chunk):
        return (1, 2) if chunk % 2 == 0 else (2, 1)

    seconds = {}

    def plane_first(item, chunk):
        _, got1, _, got2, keep, _, _, sem_s, sem_r = scratch(item)
        cols = columns(item, chunk)
        if kinds[item] == "all":
            firsts[item, chunk].wait_recv()
        first, _ = turn(chunk)
        targets = [(slot, slot) for slot in range(1, seq_count)]
        if seq_count == 4:
            targets = [(3, first), (first, first)]
        row = []
        for number, (slot, to) in enumerate(targets):
            if kinds[item] == "all":
                held = got1.at[slots[slot], :, :, cols]
                held[...] = block(item, slot, cols).astype(BF16)
            else:
                held = sources[item].at[pl.ds(slot, 1), :, cols]
            index = number if seq_count == 4 else there[slot] - 1
            row.append(
                go(
                    held,
                    got2.at[index, :, :, cols],
                    sem_s.at[1, chunk, number],
                    sem_r.at[1, chunk, index],
                    {"seq": slots[to]},
                )
            )
        seconds[item, chunk] = row
        keep[:, :, cols] = block(item, 0, cols)

    def plane_second(item, chunk):
        if seq_count != 4:
            return
        _, got1, spare, got2, keep, _, _, sem_s, sem_r = scratch(item)
        cols = columns(item, chunk)
        _, second = turn(chunk)
        across, mine = seconds[item, chunk]
        across.wait_recv()
        if kinds[item] == "all":
            held = got1.at[slots[second], :, :, cols]
        else:
            held = spare.at[:, :, cols]
        held[...] = (block(item, second, cols) + got2[0, :, :, cols].astype(F32)).astype(BF16)
        last = go(
            held,
            got2.at[2, :, :, cols],
            sem_s.at[2, chunk, 0],
            sem_r.at[2, chunk, 0],
            {"seq": slots[second]},
        )
        mine.wait_recv()
        keep[:, :, cols] = keep[:, :, cols] + got2[1, :, :, cols].astype(F32)
        seconds[item, chunk] = [last]

    thirds = {}

    def line(item, chunk):
        _, _, _, got2, keep, pass3, got3, sem_s, sem_r = scratch(item)
        cols = columns(item, chunk)
        if kinds[item] == "ctx":
            firsts[item, chunk].wait_recv()
            keep[:, :, cols] = block(item, 0, cols)
        else:
            for copy in seconds[item, chunk]:
                copy.wait_recv()

        def total(place):
            value = keep[place, :, cols]
            if kinds[item] != "ctx":
                for index in (2,) if seq_count == 4 else range(seq_count - 1):
                    value = value + got2[index, place, :, cols].astype(F32)
            return value

        if kinds[item] == "seq":
            results[item][:, cols] = total(0)
            return
        row = []
        for step, place in enumerate(chips):
            pass3[step, :, cols] = total(place).astype(BF16)
            row.append(
                go(
                    pass3.at[step, :, cols],
                    got3.at[step, :, cols],
                    sem_s.at[3, chunk, step],
                    sem_r.at[3, chunk, step],
                    {"ctx": place * 2 + core},
                )
            )
        results[item][:, cols] = total(chip)
        thirds[item, chunk] = row

    lines = [step for step in order if kinds[step[0]] == "ctx"]
    everywhere = [step for step in order if kinds[step[0]] == "all"]
    flats = [step for step in order if kinds[step[0]] == "seq"]
    for step in lines:
        line(*step)
    for step in everywhere[:WINDOW]:
        plane_first(*step)
    for number, step in enumerate(everywhere):
        plane_second(*step)
        for later in everywhere[number + WINDOW : number + WINDOW + 1]:
            plane_first(*later)
        if number:
            line(*everywhere[number - 1])
    for step in flats:
        plane_first(*step)
    if work:
        work[2](*extra)
    for step in everywhere[-1:]:
        line(*step)
    for step in flats:
        plane_second(*step)
    for step in flats:
        line(*step)
    for item, chunk in lines + everywhere:
        got3 = scratch(item)[6]
        cols = columns(item, chunk)
        for copy in thirds[item, chunk]:
            copy.wait_recv()
        value = results[item][:, cols]
        for step in range(chip_count - 1):
            value = value + got3[step, :, cols].astype(F32)
        results[item][:, cols] = value
    if work:
        work[3](results[0], *extra)
    for item in range(swap_count):
        got, sem_s, sem_r, _ = swap_rest[4 * item : 4 * item + 4]
        swapped[item].wait()
        for place in planes:
            remote(got.at[place], got.at[place], sem_s.at[0], sem_r.at[place], sibling).wait_recv()
        width = got.shape[-1]
        for place in range(seq_count):
            swap_results[item][:, place * width : (place + 1) * width] = got[place].astype(F32)
    for copy in waits:
        copy.wait_send()


def fold(name, collective_id, arrays, kinds, chunk_counts, micros, swaps=(), work=None):
    seq_count, ctx_count = lax.axis_size("seq"), lax.axis_size("ctx")
    chip_count = ctx_count // 2
    inputs, shapes, scratch, in_specs = [], [], [], []
    small = (1, 1, 8, 128)
    dma = pltpu.SemaphoreType.DMA
    for array, kind, chunks in zip(arrays, kinds, chunk_counts):
        parts = 1 if kind == "ctx" else seq_count
        blocks = seq_count if kind == "seq" else parts * ctx_count
        rows, cols = array.shape[0] // blocks, array.shape[1]
        lines = 1 if kind == "seq" else chip_count
        if kind == "seq":
            inputs.append(array.reshape(seq_count, rows, cols))
            in_specs.append(vmem())
            got1, spare = small, (1, rows, cols)
        else:
            inputs.append(array.reshape(parts, chip_count, 2, rows, cols))
            in_specs.append(pl.BlockSpec(memory_space=pl.ANY))
            got1, spare = (parts, chip_count, rows, cols), small[1:]
        shapes.append(jax.ShapeDtypeStruct((rows, cols), F32))
        got2 = small if kind == "ctx" else (seq_count - 1, lines, rows, cols)
        got3 = small[1:] if kind == "seq" else (chip_count - 1, rows, cols)
        most = max(seq_count, chip_count)
        scratch += [
            pltpu.VMEM(got1, BF16),
            pltpu.VMEM(got1, BF16),
            pltpu.VMEM(spare, BF16),
            pltpu.VMEM(got2, BF16),
            pltpu.VMEM((lines, rows, cols), F32),
            pltpu.VMEM(got3, BF16),
            pltpu.VMEM(got3, BF16),
            dma((5, chunks, most)),
            dma((4, chunks, most)),
        ]
    for array in swaps:
        inputs.append(array)
        in_specs.append(pl.BlockSpec(memory_space=pl.ANY))
        shapes.append(jax.ShapeDtypeStruct((array.shape[1], seq_count * array.shape[2]), F32))
        scratch += [
            pltpu.VMEM(array.shape, BF16),
            dma((seq_count - 1,)),
            dma((seq_count,)),
            dma,
        ]
    out_specs = [vmem()] * len(inputs)
    does = None
    if work:
        does = (len(work["inputs"]), len(work["shapes"]), work["during"], work["after"])
        inputs += work["inputs"]
        in_specs += work["in_specs"]
        shapes += work["shapes"]
        out_specs += work["out_specs"]
        scratch += work["scratch"]
    return pl.pallas_call(
        functools.partial(
            fold_kernel, tuple(kinds), tuple(chunk_counts), len(swaps), does, seq_count, chip_count
        ),
        out_shape=tuple(shapes),
        in_specs=in_specs,
        out_specs=tuple(out_specs),
        scratch_shapes=scratch,
        compiler_params=pltpu.CompilerParams(
            collective_id=collective_id, has_side_effects=True, vmem_limit_bytes=VMEM_MOST
        ),
        cost_estimate=pl.CostEstimate(
            flops=0, transcendentals=0, bytes_accessed=int(micros * 3_000_000)
        ),
        name=name,
    )(*inputs)


def tiles(extent, width, visit):
    whole = extent // width

    @pl.loop(0, whole)
    def _(number):
        visit(pl.ds(pl.multiple_of(number * width, width), width))

    if extent % width:
        visit(pl.ds(whole * width, extent % width))


def stream_rows(extent, width, produce, stage, sem, target):
    whole = extent // width

    def leave(slot, rows, size):
        return pltpu.make_async_copy(
            stage.at[slot, pl.ds(0, size)], target.at[rows], sem.at[slot]
        )

    @pl.loop(0, whole)
    def _(number):
        slot = lax.rem(number, 2)
        rows = pl.ds(pl.multiple_of(number * width, width), width)

        @pl.when(number >= 2)
        def _():
            leave(slot, rows, width).wait()

        stage[slot] = produce(rows).astype(stage.dtype)
        leave(slot, rows, width).start()

    for number in range(max(0, whole - 2), whole):
        leave(number % 2, pl.ds(number * width, width), width).wait()
    if extent % width:
        size = extent % width
        rows = pl.ds(whole * width, size)
        stage[0, :size] = produce(rows).astype(stage.dtype)
        leave(0, rows, size).start()
        leave(0, rows, size).wait()


def ffn_first_kernel(
    seq_count, f_ref, g_ref, wg_ref, wd_ref, f_out, g_out, gate_ref, gh_ref, f_s, g_s, wg, wd, in_sem, f_send, f_recv, out_sem
):
    rows = f_ref.shape[0]
    width = wg.shape[1]
    places, there = plane_slots(seq_count)
    load_f = pltpu.make_async_copy(f_ref, f_s.at[pl.ds(0, rows)], in_sem.at[seq_count])
    load_wd = pltpu.make_async_copy(wd_ref, wd, in_sem.at[seq_count + 1])
    load_wg = pltpu.make_async_copy(wg_ref, wg, in_sem.at[seq_count + 2])
    loads = [load_wd]
    for slot in range(seq_count):
        loads.append(
            pltpu.make_async_copy(
                g_ref.at[places[slot]], g_s.at[pl.ds(slot * rows, rows)], in_sem.at[slot]
            )
        )
    for load in [*loads, load_f, load_wg]:
        load.start()
    meet([{"seq": place} for place in places[1:]])

    started = []

    def f_block(slot, half):
        if half is None:
            return f_s.at[pl.ds(slot * rows, rows)]
        return f_s.at[pl.ds(slot * rows + half * (rows // 2), rows // 2)]

    def f_copy(source, to, slot, half):
        copy = remote(
            source,
            f_block(slot, half),
            f_send.at[len(started)],
            f_recv.at[slot, half or 0],
            {"seq": places[to]},
        )
        copy.start()
        started.append(copy)

    def f_arrive(slot, half):
        block = f_block(slot, half)
        remote(
            block, block, f_send.at[0], f_recv.at[slot, half or 0], {"seq": places[1]}
        ).wait_recv()

    if seq_count == 4:
        for half in (0, 1):
            source = f_ref.at[pl.ds(half * (rows // 2), rows // 2)]
            for to in (1, 2) if half == 0 else (2, 1):
                f_copy(source, to, to, half)
    else:
        for to in range(1, seq_count):
            f_copy(f_ref, to, there[to], None)

    def gate_rows(first, count):
        own = slice(first, first + count)

        def visit(cols):
            gate_ref[own, cols] = dot32(f_s[own, :], wg[:, cols], ((1,), (0,)))

        tiles(width, 256, visit)

    for load in loads:
        load.wait()
    leave_g = pltpu.make_async_copy(g_s, g_out, out_sem.at[1])
    leave_g.start()

    def grad_hidden(cols):
        gh_ref[:, cols] = dot32(g_s[...], wd[cols, :], ((1,), (1,))).astype(gh_ref.dtype)

    tiles(width, 256, grad_hidden)
    for load in (load_f, load_wg):
        load.wait()
    gate_rows(0, rows)
    if seq_count == 4:
        f_arrive(1, 0)
        f_copy(f_block(1, 0), 2, 3, 0)
        f_arrive(2, 1)
        f_copy(f_block(2, 1), 1, 3, 1)
        f_arrive(1, 1)
        f_arrive(2, 0)
        gate_rows(rows, 2 * rows)
        f_arrive(3, 0)
        f_arrive(3, 1)
        leave = pltpu.make_async_copy(f_s, f_out, out_sem.at[0])
        leave.start()
        gate_rows(3 * rows, rows)
    else:
        for slot in range(1, seq_count):
            f_arrive(slot, None)
        leave = pltpu.make_async_copy(f_s, f_out, out_sem.at[0])
        leave.start()
        gate_rows(rows, (seq_count - 1) * rows)
    leave.wait()
    leave_g.wait()
    for copy in started:
        copy.wait_send()


def ffn_act_kernel(
    f_ref, gate_ref, gh_ref, wu_ref, hid, gg, gu, pg_ref, f_s, gate_s, gh_s, wu, stage_f, in_sem, leave_sem
):
    model, width = wu.shape
    loads = [
        pltpu.make_async_copy(source, target, in_sem.at[number])
        for number, (source, target) in enumerate(
            [(f_ref, f_s), (wu_ref, wu), (gate_ref, gate_s), (gh_ref, gh_s)]
        )
    ]
    for load in loads:
        load.start()
    for load in loads:
        load.wait()

    def act(cols):
        up_val = dot32(f_s[...], wu[:, cols], ((1,), (0,)))
        gate = gate_s[:, cols]
        grad = gh_s[:, cols].astype(F32)
        sigma = jax.nn.sigmoid(gate)
        activated = gate * sigma
        hid[:, cols] = (activated * up_val).astype(BF16)
        gg[:, cols] = (grad * up_val * (sigma + activated * (1.0 - sigma))).astype(BF16)
        gu[:, cols] = (grad * activated).astype(BF16)

    tiles(width, 256, act)
    stream_rows(
        model,
        256,
        lambda own: dot32(f_s[:, own], gg[...], ((0,), (0,))),
        stage_f,
        leave_sem,
        pg_ref,
    )


def ffn_grad_kernel(
    seq_count,
    f_ref,
    hid_ref,
    gg_ref,
    gu_ref,
    g_ref,
    wg_ref,
    wu_ref,
    wd_ref,
    gf_ref,
    out_ref,
    pu_ref,
    pd_ref,
    f_s,
    g_s,
    hid,
    gg,
    gu,
    wg,
    wu,
    wd,
    parts,
    got,
    stage_f,
    stage_d,
    in_sem,
    x_send,
    x_recv,
    leave_sem,
):
    rows = gf_ref.shape[0]
    model, width = wg.shape
    places, there = plane_slots(seq_count)
    loads = [
        pltpu.make_async_copy(source, target, in_sem.at[number])
        for number, (source, target) in enumerate(
            [
                (gg_ref, gg),
                (gu_ref, gu),
                (wg_ref, wg),
                (wu_ref, wu),
                (f_ref, f_s),
                (hid_ref, hid),
                (g_ref, g_s),
                (wd_ref, wd),
            ]
        )
    ]
    for load in loads:
        load.start()
    meet([{"seq": place} for place in places[1:]])
    for load in loads[:4]:
        load.wait()

    def part_copy(slot, cols):
        return remote(
            parts.at[pl.ds((slot - 1) * rows, rows), cols],
            got.at[there[slot] - 1, :, cols],
            x_send.at[slot],
            x_recv.at[there[slot]],
            {"seq": places[slot]},
        )

    def grad_f(cols):
        part = dot32(gg[...], wg[cols, :], ((1,), (1,))) + dot32(gu[...], wu[cols, :], ((1,), (1,)))
        gf_ref[:, cols] = part[:rows]
        parts[:, cols] = part[rows:].astype(BF16)
        for slot in range(1, seq_count):
            part_copy(slot, cols).start()

    tiles(model, 256, grad_f)
    for load in loads[4:]:
        load.wait()
    stream_rows(
        model,
        256,
        lambda own: dot32(f_s[:, own], gu[...], ((0,), (0,))),
        stage_f,
        leave_sem.at[0],
        pu_ref,
    )
    stream_rows(
        width,
        256,
        lambda own: dot32(hid[:, own], g_s[...], ((0,), (0,))),
        stage_d,
        leave_sem.at[2],
        pd_ref,
    )

    def out_copy(cols):
        return pltpu.make_async_copy(f_s.at[:, cols], out_ref.at[:, cols], leave_sem.at[1, 0])

    def out_part(cols):
        f_s[:, cols] = dot32(hid[...], wd[:, cols], ((1,), (0,))).astype(BF16)
        out_copy(cols).start()

    tiles(model, 256, out_part)
    everything = pl.ds(0, model)
    out_copy(everything).wait()
    for slot in range(1, seq_count):
        part_copy(slot, everything).wait_recv()
    total = gf_ref[...]
    for slot in range(seq_count - 1):
        total = total + got[slot].astype(F32)
    gf_ref[...] = total
    for slot in range(1, seq_count):
        part_copy(slot, everything).wait_send()


def ffn_first(collective_id, f_norm, g_all, w_gate, w_down):
    seq_count = lax.axis_size("seq")
    rows, model = f_norm.shape
    width = w_gate.shape[1]
    count = seq_count * rows
    anywhere = pl.BlockSpec(memory_space=pl.ANY)
    dma = pltpu.SemaphoreType.DMA
    return pl.pallas_call(
        functools.partial(ffn_first_kernel, seq_count),
        out_shape=(
            jax.ShapeDtypeStruct((count, model), BF16),
            jax.ShapeDtypeStruct((count, model), BF16),
            jax.ShapeDtypeStruct((count, width), F32),
            jax.ShapeDtypeStruct((count, width), BF16),
        ),
        in_specs=[anywhere] * 4,
        out_specs=(anywhere, anywhere, vmem(), vmem()),
        scratch_shapes=[
            pltpu.VMEM((count, model), BF16),
            pltpu.VMEM((count, model), BF16),
            pltpu.VMEM((model, width), BF16),
            pltpu.VMEM((width, model), BF16),
            dma((seq_count + 3,)),
            dma((max(6, seq_count),)),
            dma((seq_count, 2)),
            dma((2,)),
        ],
        compiler_params=pltpu.CompilerParams(
            collective_id=collective_id, has_side_effects=True, vmem_limit_bytes=VMEM_MOST
        ),
        cost_estimate=pl.CostEstimate(
            flops=8 * count * model * width,
            transcendentals=0,
            bytes_accessed=4 * (2 * width * model + 3 * count * model),
        ),
        name="ffn_first",
    )(f_norm, g_all.reshape(seq_count, rows, model), w_gate, w_down)


def ffn_act(f_all, gate, grad_hidden, w_up):
    count, model = f_all.shape
    width = w_up.shape[1]
    anywhere = pl.BlockSpec(memory_space=pl.ANY)
    dma = pltpu.SemaphoreType.DMA
    return pl.pallas_call(
        ffn_act_kernel,
        out_shape=(
            jax.ShapeDtypeStruct((count, width), BF16),
            jax.ShapeDtypeStruct((count, width), BF16),
            jax.ShapeDtypeStruct((count, width), BF16),
            jax.ShapeDtypeStruct((model, width), BF16),
        ),
        in_specs=[anywhere] * 4,
        out_specs=(vmem(), vmem(), vmem(), anywhere),
        scratch_shapes=[
            pltpu.VMEM((count, model), BF16),
            pltpu.VMEM((count, width), F32),
            pltpu.VMEM((count, width), BF16),
            pltpu.VMEM((model, width), BF16),
            pltpu.VMEM((2, 256, width), BF16),
            dma((4,)),
            dma((2,)),
        ],
        compiler_params=pltpu.CompilerParams(vmem_limit_bytes=VMEM_MOST),
        cost_estimate=pl.CostEstimate(
            flops=4 * count * model * width,
            transcendentals=count * width,
            bytes_accessed=4 * (width * model + 2 * count * model + 3 * count * width),
        ),
        name="ffn_act",
    )(f_all, gate, grad_hidden, w_up)


def ffn_grad(collective_id, rows, f_all, hidden_act, grad_gate, grad_up, g_all, w_gate, w_up, w_down):
    seq_count = lax.axis_size("seq")
    count, model = f_all.shape
    width = w_gate.shape[1]
    anywhere = pl.BlockSpec(memory_space=pl.ANY)
    dma = pltpu.SemaphoreType.DMA
    return pl.pallas_call(
        functools.partial(ffn_grad_kernel, seq_count),
        out_shape=(
            jax.ShapeDtypeStruct((rows, model), F32),
            jax.ShapeDtypeStruct((count, model), BF16),
            jax.ShapeDtypeStruct((model, width), BF16),
            jax.ShapeDtypeStruct((width, model), BF16),
        ),
        in_specs=[anywhere] * 8,
        out_specs=(vmem(), anywhere, anywhere, anywhere),
        scratch_shapes=[
            pltpu.VMEM((count, model), BF16),
            pltpu.VMEM((count, model), BF16),
            pltpu.VMEM((count, width), BF16),
            pltpu.VMEM((count, width), BF16),
            pltpu.VMEM((count, width), BF16),
            pltpu.VMEM((model, width), BF16),
            pltpu.VMEM((model, width), BF16),
            pltpu.VMEM((width, model), BF16),
            pltpu.VMEM((count - rows, model), BF16),
            pltpu.VMEM((seq_count - 1, rows, model), BF16),
            pltpu.VMEM((2, 256, width), BF16),
            pltpu.VMEM((2, 256, model), BF16),
            dma((8,)),
            dma((seq_count,)),
            dma((seq_count,)),
            dma((3, 2)),
        ],
        compiler_params=pltpu.CompilerParams(
            collective_id=collective_id, has_side_effects=True, vmem_limit_bytes=VMEM_MOST
        ),
        cost_estimate=pl.CostEstimate(
            flops=14 * count * model * width,
            transcendentals=0,
            bytes_accessed=4 * (3 * width * model + 3 * count * model),
        ),
        name="ffn_grad",
    )(f_all, hidden_act, grad_gate, grad_up, g_all, w_gate, w_up, w_down)


def half_turn(value):
    half = HEAD_DIM // 2
    return jnp.concatenate([-value[half:], value[:half]], axis=0)


def project_kernel(
    x_ref, gain_ref, cos_ref, sin_ref, w_ref, normed_ref, rms_ref, q_ref, kv_ref, w_s, sem
):
    tile = KV_HEADS * HEAD_DIM
    count = w_ref.shape[1] // tile

    def load(number):
        cols = pl.ds(pl.multiple_of(number * tile, tile), tile)
        return pltpu.make_async_copy(w_ref.at[:, cols], w_s.at[:, cols], sem.at[number])

    for number in range(count):
        load(number).start()
    x = x_ref[...].astype(F32)
    rms = lax.rsqrt(jnp.mean(x * x, axis=1, keepdims=True) + EPS)
    rms_ref[...] = rms
    normed_ref[...] = (x * rms * gain_ref[...]).astype(BF16)

    def product(number):
        load(number).wait()
        cols = pl.ds(pl.multiple_of(number * tile, tile), tile)
        return dot32(normed_ref[...], w_s[:, cols], ((1,), (0,)))

    def rotated(value):
        turned = value.T
        pieces = []
        for head in range(tile // HEAD_DIM):
            one = turned[head * HEAD_DIM : (head + 1) * HEAD_DIM]
            pieces.append(one * cos_ref[...] + half_turn(one) * sin_ref[...])
        return jnp.concatenate(pieces, axis=0)

    @pl.loop(0, count - 2)
    def _(number):
        own = pl.ds(pl.multiple_of(number * tile, tile), tile)
        q_ref[own, :] = rotated(product(number)).astype(BF16)

    kv_ref[:, :tile] = rotated(product(count - 2)).T.astype(BF16)
    kv_ref[:, tile:] = product(count - 1).astype(BF16)


def project(x, gain, cosine, sine, w_qkv):
    rows, model = x.shape
    width = w_qkv.shape[1]
    tile = KV_HEADS * HEAD_DIM
    return pl.pallas_call(
        project_kernel,
        out_shape=(
            jax.ShapeDtypeStruct((rows, model), BF16),
            jax.ShapeDtypeStruct((rows, 1), F32),
            jax.ShapeDtypeStruct((width - 2 * tile, rows), BF16),
            jax.ShapeDtypeStruct((rows, 2 * tile), BF16),
        ),
        in_specs=[vmem()] * 4 + [pl.BlockSpec(memory_space=pl.ANY)],
        out_specs=(vmem(),) * 4,
        scratch_shapes=[
            pltpu.VMEM(w_qkv.shape, BF16),
            pltpu.SemaphoreType.DMA((width // tile,)),
        ],
        compiler_params=pltpu.CompilerParams(vmem_limit_bytes=VMEM_MOST),
        cost_estimate=pl.CostEstimate(
            flops=2 * rows * model * width, transcendentals=0, bytes_accessed=2 * model * width
        ),
        name="project",
    )(x, gain, cosine, sine, w_qkv)


def rotated_back(value, cos_ref, sin_ref):
    pieces = []
    for head in range(value.shape[0] // HEAD_DIM):
        one = value[head * HEAD_DIM : (head + 1) * HEAD_DIM]
        pieces.append(one * cos_ref[...] - half_turn(one * sin_ref[...]))
    return jnp.concatenate(pieces, axis=0).T.astype(BF16)


def back_during(inputs, outputs, scratch):
    dq_ref, o_ref, cos_ref, sin_ref, normed_ref, x_ref, rms_ref, gain_ref, grad_ref, w_ref = inputs
    part_out, part_query, part_kv, out_ref, gain_out = outputs
    w_s, g_s, gx_s, ga_s, stage, stage_kv, load_sem, leave_sem = scratch
    tile = KV_HEADS * HEAD_DIM
    q_width = dq_ref.shape[0]
    model = x_ref.shape[1]
    pltpu.make_async_copy(w_ref, w_s, load_sem).start()
    ga_s[...] = grad_ref[...].astype(BF16)
    stream_rows(
        q_width,
        256,
        lambda own: dot32(o_ref[own, :], ga_s[...], ((1,), (0,))),
        stage,
        leave_sem,
        part_out,
    )

    @pl.loop(0, q_width // tile)
    def _(number):
        own = pl.ds(pl.multiple_of(number * tile, tile), tile)
        g_s[:, own] = rotated_back(dq_ref[own, :], cos_ref, sin_ref)

    stream_rows(
        model,
        256,
        lambda own: dot32(normed_ref[:, own], g_s[:, :q_width], ((0,), (0,))),
        stage,
        leave_sem,
        part_query,
    )
    pltpu.make_async_copy(w_ref, w_s, load_sem).wait()

    def grad_x(cols):
        gx_s[:, cols] = dot32(g_s[:, :q_width], w_s[cols, :q_width], ((1,), (1,)))

    tiles(model, 256, grad_x)


def back_after(dkv_ref, inputs, outputs, scratch):
    dq_ref, o_ref, cos_ref, sin_ref, normed_ref, x_ref, rms_ref, gain_ref, grad_ref, w_ref = inputs
    part_out, part_query, part_kv, out_ref, gain_out = outputs
    w_s, g_s, gx_s, ga_s, stage, stage_kv, load_sem, leave_sem = scratch
    tile = KV_HEADS * HEAD_DIM
    q_width = dq_ref.shape[0]
    model = x_ref.shape[1]
    g_s[:, q_width : q_width + tile] = rotated_back(dkv_ref[:, :tile].T, cos_ref, sin_ref)
    g_s[:, q_width + tile :] = dkv_ref[:, tile:].astype(BF16)
    stream_rows(
        model,
        256,
        lambda own: dot32(normed_ref[:, own], g_s[:, q_width:], ((0,), (0,))),
        stage_kv,
        leave_sem,
        part_kv,
    )

    def grad_x(cols):
        gx_s[:, cols] = gx_s[:, cols] + dot32(g_s[:, q_width:], w_s[cols, q_width:], ((1,), (1,)))

    tiles(model, 256, grad_x)
    x = x_ref[...].astype(F32)
    rms = rms_ref[...]
    gain_out[...] = jnp.sum(gx_s[...] * (x * rms), axis=0, keepdims=True)
    scaled = gx_s[...] * gain_ref[...]
    mean = jnp.mean(scaled * x, axis=1, keepdims=True)
    out_ref[...] = grad_ref[...] + (rms * scaled - x * (rms * rms * rms * mean))


def back_work(dq_t, o_t, cosine, sine, normed, x, rms, gain, grad, w_qkv):
    rows, model = x.shape
    width = w_qkv.shape[1]
    q_width = dq_t.shape[0]
    anywhere = pl.BlockSpec(memory_space=pl.ANY)
    return {
        "inputs": [dq_t, o_t, cosine, sine, normed, x, rms, gain, grad, w_qkv],
        "in_specs": [vmem()] * 9 + [anywhere],
        "shapes": [
            jax.ShapeDtypeStruct((q_width, model), BF16),
            jax.ShapeDtypeStruct((model, q_width), BF16),
            jax.ShapeDtypeStruct((model, width - q_width), BF16),
            jax.ShapeDtypeStruct((rows, model), F32),
            jax.ShapeDtypeStruct((1, model), F32),
        ],
        "out_specs": [anywhere, anywhere, anywhere, vmem(), vmem()],
        "scratch": [
            pltpu.VMEM(w_qkv.shape, BF16),
            pltpu.VMEM((rows, width), BF16),
            pltpu.VMEM((rows, model), F32),
            pltpu.VMEM((rows, model), BF16),
            pltpu.VMEM((2, 256, max(model, q_width)), BF16),
            pltpu.VMEM((2, 256, width - q_width), BF16),
            pltpu.SemaphoreType.DMA,
            pltpu.SemaphoreType.DMA((2,)),
        ],
        "during": back_during,
        "after": back_after,
    }


def gather(value, axes, dim=0):
    return lax.all_gather(value, axes, axis=dim, tiled=True)


def scatter_sum(value, axes, dim=0):
    return lax.psum_scatter(value, axes, scatter_dimension=dim, tiled=True)


def norm_back(grad_normed, source, rms_val, gain_val, normed):
    grad_gain = jnp.sum(grad_normed * normed, axis=0)
    scaled = grad_normed * gain_val
    grad_source = rms_val * scaled - source * (rms_val * rms_val * rms_val) * jnp.mean(
        scaled * source, axis=1, keepdims=True
    )
    return (grad_gain, grad_source)


def local(
    hidden_in,
    attn_gain,
    w_query,
    w_key,
    w_value,
    w_out,
    ffn_gain,
    w_gate,
    w_up,
    w_down,
    cotangent,
    doc_lengths,
    selected,
    block_order,
):
    one, rows, model = hidden_in.shape
    seq_count = lax.axis_size("seq")
    ctx_count = lax.axis_size("ctx")
    place = lax.axis_index("ctx").astype(jnp.int32).reshape(1)
    length = rows * ctx_count
    span_len = length // block_order.shape[0]
    q_width = HEADS * HEAD_DIM
    kv_width = KV_HEADS * HEAD_DIM
    own_rows = w_gate.shape[0]
    ff_part = w_gate.shape[1] // seq_count

    def split_columns(weight):
        return weight.reshape(own_rows, seq_count, ff_part).transpose(1, 0, 2)

    own_spans = lax.dynamic_slice_in_dim(block_order, place[0] * (rows // span_len), rows // span_len)
    local_pos = (
        own_spans[:, None] * span_len + jnp.arange(span_len, dtype=jnp.int32)[None, :]
    ).reshape(rows)
    half = HEAD_DIM // 2
    inverse = ROPE_BASE ** (-(jnp.arange(half, dtype=F32) * 2.0 / HEAD_DIM))
    angle = inverse[:, None] * local_pos.astype(F32)[None, :]
    cosine = jnp.concatenate([jnp.cos(angle)] * 2, axis=0)
    sine = jnp.concatenate([jnp.sin(angle)] * 2, axis=0)

    full_down = gather(w_down, "ctx")
    gain_row = jnp.pad(jnp.concatenate([attn_gain, ffn_gain])[None], ((0, 15), (0, 128 - 2 * own_rows)))
    gains, w_qkv, gate_mine, up_mine = spread(
        "gather_qkv",
        0,
        [
            gain_row,
            jnp.concatenate([w_query, w_key, w_value], axis=1),
            split_columns(w_gate),
            split_columns(w_up),
        ],
        ("all", "all", "swap", "swap"),
        85,
    )
    gain_a = gains[:, :, 0, :own_rows].reshape(1, model).astype(F32)
    gain_f = gains[:, :, 0, own_rows : 2 * own_rows].reshape(1, model).astype(F32)
    w_qkv = w_qkv.reshape(model, q_width + 2 * kv_width)
    full_down, gate_mine, up_mine = lax.optimization_barrier((full_down, gate_mine, up_mine))
    full_gate = gather(gate_mine, "ctx", 1).reshape(model, ff_part)
    full_up = gather(up_mine, "ctx", 1).reshape(model, ff_part)

    grad_y = (
        cotangent.reshape(rows, model).astype(F32) * selected.reshape(rows).astype(F32)[:, None]
    )
    tokens = hidden_in.reshape(rows, model).astype(F32)
    x_norm, rms_a, q_t, kv_own = project(
        hidden_in.reshape(rows, model), gain_a, cosine, sine, w_qkv
    )
    kv, full_out, g_all = spread(
        "gather_kv_out",
        1,
        [kv_own, w_out, grad_y.astype(BF16)],
        ("ctx", "all", "seq"),
        85,
    )
    g_all = g_all.reshape(seq_count * rows, model)
    kv = kv.reshape(length, 2 * kv_width)
    full_out = full_out.reshape(q_width, model)
    o_t, lse = attend_forward(place, block_order, doc_lengths, q_t, kv)

    middle = tokens + jnp.einsum("ht,hd->td", o_t, full_out, preferred_element_type=F32)
    rms_f = lax.rsqrt(jnp.mean(middle * middle, axis=1, keepdims=True) + EPS)
    normed_f = middle * rms_f
    f_norm = (normed_f * gain_f).astype(BF16)

    f_all, g_slots, gate, grad_hidden = ffn_first(2, f_norm, g_all, full_gate, full_down)
    hidden_act, grad_gate, grad_up, part_gate = ffn_act(f_all, gate, grad_hidden, full_up)
    grad_f_norm, ffn_part, part_up, part_down = ffn_grad(
        3, rows, f_all, hidden_act, grad_gate, grad_up, g_slots, full_gate, full_up, full_down
    )

    def ffn_rows(part):
        return scatter_sum(part.reshape(seq_count, model // seq_count, ff_part), "ctx", 1)

    rows_gate = ffn_rows(part_gate)
    rows_up = ffn_rows(part_up)
    grad_ffn_gain, grad_from_f = norm_back(grad_f_norm, middle, rms_f, gain_f, normed_f)
    grad_middle = grad_y + grad_from_f
    g_attn = grad_middle.astype(BF16)
    do_t = jnp.einsum("td,hd->ht", g_attn, full_out, preferred_element_type=F32).astype(BF16)
    dq_t, dkv = attend_backward(place, block_order, doc_lengths, q_t, kv, o_t, lse, do_t)
    part_down, rows_gate, dkv = lax.optimization_barrier((part_down, rows_gate, dkv))
    grad_w_down = scatter_sum(part_down, "ctx").astype(F32)
    _, ffn_out, part_out, part_query, part_kv, grad_input, grad_attn_gain = fold(
        "fold_kv",
        4,
        [dkv, ffn_part],
        ("ctx", "seq"),
        (1, 2),
        60,
        work=back_work(
            dq_t,
            o_t,
            cosine,
            sine,
            x_norm,
            hidden_in.reshape(rows, model),
            rms_a,
            gain_a,
            grad_middle,
            w_qkv,
        ),
    )
    output = (middle + ffn_out).astype(BF16).reshape(one, rows, model)
    part_gains = jnp.concatenate(
        [grad_attn_gain.reshape(-1, own_rows), grad_ffn_gain.reshape(-1, own_rows)], axis=1
    )
    part_gains = jnp.pad(part_gains[:, None], ((0, 0), (0, 15), (0, 128 - 2 * own_rows)))
    grad_w_out, grad_w_query, grad_w_kv, grad_gains, grad_w_gate, grad_w_up = fold(
        "fold_weights",
        5,
        [part_out, part_query, part_kv, part_gains.reshape(-1, 128).astype(BF16)],
        ("all", "all", "all", "all"),
        (8, 8, 2, 1),
        110,
        [rows_gate, rows_up],
    )
    return (
        output,
        grad_input.reshape(one, rows, model),
        grad_gains[0, :own_rows],
        grad_w_query,
        grad_w_kv[:, :kv_width],
        grad_w_kv[:, kv_width:],
        grad_w_out,
        grad_gains[0, own_rows : 2 * own_rows],
        grad_w_gate,
        grad_w_up,
        grad_w_down,
    )


def solution(mesh):
    return jax.shard_map(
        local,
        mesh=mesh,
        in_specs=(
            P("seq", "ctx", None),
            P(("seq", "ctx")),
            P(("seq", "ctx"), None),
            P(("seq", "ctx"), None),
            P(("seq", "ctx"), None),
            P(("seq", "ctx"), None),
            P(("seq", "ctx")),
            P(("seq", "ctx"), None),
            P(("seq", "ctx"), None),
            P(("seq", "ctx"), None),
            P("seq", "ctx", None),
            P("seq", None),
            P("seq", "ctx"),
            P(),
        ),
        out_specs=(
            P("seq", "ctx", None),
            P("seq", "ctx", None),
            P(("seq", "ctx")),
            P(("seq", "ctx"), None),
            P(("seq", "ctx"), None),
            P(("seq", "ctx"), None),
            P(("seq", "ctx"), None),
            P(("seq", "ctx")),
            P(("seq", "ctx"), None),
            P(("seq", "ctx"), None),
            P(("seq", "ctx"), None),
        ),
        check_vma=False,
    )
```

```python
import functools
import math

import jax
import jax.numpy as jnp
from jax import lax
from jax.experimental import pallas as pl
from jax.experimental.pallas import tpu as pltpu
from jax.sharding import PartitionSpec as P

HEADS = 32
KV_HEADS = 4
HEAD_DIM = 64
GROUP = HEADS // KV_HEADS
SCALE = 1.0 / math.sqrt(HEAD_DIM)
LOG2E = math.log2(math.e)


EPS = 1e-05
ROPE_BASE = 10000.0
NEG = -1e30

F32 = jnp.float32
BF16 = jnp.bfloat16
VMEM_MOST = 56 * 1024 * 1024


def dot32(left, right, dims):
    return lax.dot_general(left, right, (dims, ((), ())), preferred_element_type=F32)


def span_bounds(order_ref, lens_ref, span_len, spans, own_first, own):
    docs = lens_ref.shape[1]
    base = order_ref[own_first + own] * span_len
    pos = lax.broadcasted_iota(jnp.int32, (1, span_len), 1) + base
    start = jnp.zeros((1, span_len), jnp.int32)
    first_start = jnp.int32(0)
    end = jnp.int32(0)
    for number in range(docs):
        end = end + lens_ref[0, number]
        start = jnp.where(pos >= end, end, start)
        first_start = jnp.where(base >= end, end, first_start)
    return base, pos, start, first_start


def allowed_tile(key_base, span_len, pos, start):
    key_pos = lax.broadcasted_iota(jnp.int32, (span_len, span_len), 0) + key_base
    tile = (key_pos <= pos) & (key_pos >= start)
    return jnp.concatenate([tile.astype(F32)] * GROUP, axis=1) > 0.5


def stack_heads(ref, head, own, span_len):
    pieces = []
    for member in range(GROUP):
        row = (head * GROUP + member) * HEAD_DIM
        pieces.append(ref[row : row + HEAD_DIM, own * span_len : (own + 1) * span_len])
    return jnp.concatenate(pieces, axis=1)


def unstack_heads(ref, value, head, own, span_len):
    for member in range(GROUP):
        row = (head * GROUP + member) * HEAD_DIM
        ref[row : row + HEAD_DIM, own * span_len : (own + 1) * span_len] = value[
            :, member * span_len : (member + 1) * span_len
        ].astype(ref.dtype)


def attend_forward_kernel(
    span_len, spans, place_ref, order_ref, lens_ref, q_ref, kv_ref, o_ref, lse_ref, top_ref, sum_ref, acc_ref
):
    own_count = q_ref.shape[1] // span_len
    own_first = place_ref[0] * own_count
    width = KV_HEADS * HEAD_DIM
    for own in range(own_count):
        base, pos, start, first_start = span_bounds(
            order_ref, lens_ref, span_len, spans, own_first, own
        )
        top_ref[...] = jnp.full(top_ref.shape, NEG, F32)
        sum_ref[...] = jnp.zeros(sum_ref.shape, F32)
        acc_ref[...] = jnp.zeros(acc_ref.shape, F32)
        stacked = [stack_heads(q_ref, head, own, span_len) for head in range(KV_HEADS)]

        @pl.loop(0, spans)
        def _(number):
            key_base = order_ref[number] * span_len

            @pl.when((key_base <= base) & (key_base + span_len > first_start))
            def _():
                allowed = allowed_tile(key_base, span_len, pos, start)
                rows = pl.ds(pl.multiple_of(number * span_len, span_len), span_len)
                for head in range(KV_HEADS):
                    lower = head * HEAD_DIM
                    key = kv_ref[rows, lower : lower + HEAD_DIM]
                    value = kv_ref[rows, width + lower : width + lower + HEAD_DIM]
                    scores = dot32(key, stacked[head], ((1,), (0,))) * (SCALE * LOG2E)
                    scores = jnp.where(allowed, scores, NEG)
                    old = top_ref[head : head + 1, :]
                    new = jnp.maximum(old, jnp.max(scores, axis=0, keepdims=True))
                    decay = jnp.exp2(old - new)
                    expo = jnp.exp2(scores - new)
                    top_ref[head : head + 1, :] = new
                    sum_ref[head : head + 1, :] = sum_ref[head : head + 1, :] * decay + jnp.sum(
                        expo, axis=0, keepdims=True
                    )
                    part = dot32(value, expo.astype(BF16), ((0,), (0,)))
                    acc_ref[head] = acc_ref[head] * decay + part

        for head in range(KV_HEADS):
            total = sum_ref[head : head + 1, :]
            mixed = acc_ref[head] / total
            unstack_heads(o_ref, mixed, head, own, span_len)
            lse_ref[own, head : head + 1, :] = top_ref[head : head + 1, :] + jnp.log2(total)


def attend_backward_kernel(
    span_len,
    spans,
    place_ref,
    order_ref,
    lens_ref,
    q_ref,
    kv_ref,
    o_ref,
    lse_ref,
    do_ref,
    dq_ref,
    dkv_ref,
    dkv_acc,
    dq_acc,
    delta_ref,
):
    own_count = q_ref.shape[1] // span_len
    own_first = place_ref[0] * own_count
    width = KV_HEADS * HEAD_DIM
    dkv_acc[...] = jnp.zeros(dkv_acc.shape, F32)
    for own in range(own_count):
        base, pos, start, first_start = span_bounds(
            order_ref, lens_ref, span_len, spans, own_first, own
        )
        dq_acc[...] = jnp.zeros(dq_acc.shape, F32)
        queries = [stack_heads(q_ref, head, own, span_len) for head in range(KV_HEADS)]
        grads = [stack_heads(do_ref, head, own, span_len) for head in range(KV_HEADS)]
        for head in range(KV_HEADS):
            mixed = stack_heads(o_ref, head, own, span_len)
            delta_ref[head : head + 1, :] = jnp.sum(
                mixed.astype(F32) * grads[head].astype(F32), axis=0, keepdims=True
            )

        @pl.loop(0, spans)
        def _(number):
            key_base = order_ref[number] * span_len

            @pl.when((key_base <= base) & (key_base + span_len > first_start))
            def _():
                allowed = allowed_tile(key_base, span_len, pos, start)
                rows = pl.ds(pl.multiple_of(number * span_len, span_len), span_len)
                for head in range(KV_HEADS):
                    lower = head * HEAD_DIM
                    key = kv_ref[rows, lower : lower + HEAD_DIM]
                    value = kv_ref[rows, width + lower : width + lower + HEAD_DIM]
                    scores = dot32(key, queries[head], ((1,), (0,))) * (SCALE * LOG2E)
                    probs = jnp.where(
                        allowed, jnp.exp2(scores - lse_ref[own, head : head + 1, :]), 0.0
                    )
                    grad_probs = dot32(value, grads[head], ((1,), (0,)))
                    grad_scores = (probs * (grad_probs - delta_ref[head : head + 1, :])).astype(BF16)
                    probs = probs.astype(BF16)
                    dq_acc[head] = dq_acc[head] + dot32(key, grad_scores, ((0,), (0,)))
                    dkv_acc[rows, lower : lower + HEAD_DIM] = (
                        dkv_acc[rows, lower : lower + HEAD_DIM]
                        + dot32(grad_scores, queries[head], ((1,), (1,))) * SCALE
                    )
                    dkv_acc[rows, width + lower : width + lower + HEAD_DIM] = dkv_acc[
                        rows, width + lower : width + lower + HEAD_DIM
                    ] + dot32(probs, grads[head], ((1,), (1,)))

        for head in range(KV_HEADS):
            unstack_heads(dq_ref, dq_acc[head] * SCALE, head, own, span_len)
    dkv_ref[...] = dkv_acc[...].astype(dkv_ref.dtype)


def smem():
    return pl.BlockSpec(memory_space=pltpu.SMEM)


def vmem():
    return pl.BlockSpec(memory_space=pltpu.VMEM)


def attend_forward(place, block_order, doc_lengths, q_t, kv):
    spans = block_order.shape[0]
    span_len = kv.shape[0] // spans
    own_count = q_t.shape[1] // span_len
    lanes = GROUP * span_len
    return pl.pallas_call(
        functools.partial(attend_forward_kernel, span_len, spans),
        out_shape=(
            jax.ShapeDtypeStruct(q_t.shape, BF16),
            jax.ShapeDtypeStruct((own_count, KV_HEADS, lanes), F32),
        ),
        in_specs=[smem(), smem(), smem(), vmem(), vmem()],
        out_specs=(vmem(), vmem()),
        scratch_shapes=[
            pltpu.VMEM((KV_HEADS, lanes), F32),
            pltpu.VMEM((KV_HEADS, lanes), F32),
            pltpu.VMEM((KV_HEADS, HEAD_DIM, lanes), F32),
        ],
        compiler_params=pltpu.CompilerParams(vmem_limit_bytes=VMEM_MOST),
        cost_estimate=pl.CostEstimate(
            flops=2 * HEADS * HEAD_DIM * kv.shape[0] * q_t.shape[1],
            transcendentals=HEADS * kv.shape[0] * q_t.shape[1] // 2,
            bytes_accessed=4 * q_t.size + 2 * kv.size,
        ),
        name="attend_forward",
    )(place, block_order, doc_lengths, q_t, kv)


def attend_backward(place, block_order, doc_lengths, q_t, kv, o_t, lse, do_t):
    spans = block_order.shape[0]
    span_len = kv.shape[0] // spans
    lanes = GROUP * span_len
    return pl.pallas_call(
        functools.partial(attend_backward_kernel, span_len, spans),
        out_shape=(
            jax.ShapeDtypeStruct(q_t.shape, F32),
            jax.ShapeDtypeStruct(kv.shape, BF16),
        ),
        in_specs=[smem(), smem(), smem(), vmem(), vmem(), vmem(), vmem(), vmem()],
        out_specs=(vmem(), vmem()),
        scratch_shapes=[
            pltpu.VMEM(kv.shape, F32),
            pltpu.VMEM((KV_HEADS, HEAD_DIM, lanes), F32),
            pltpu.VMEM((KV_HEADS, lanes), F32),
        ],
        compiler_params=pltpu.CompilerParams(vmem_limit_bytes=VMEM_MOST),
        cost_estimate=pl.CostEstimate(
            flops=5 * HEADS * HEAD_DIM * kv.shape[0] * q_t.shape[1],
            transcendentals=HEADS * kv.shape[0] * q_t.shape[1] // 2,
            bytes_accessed=10 * q_t.size + 4 * kv.size,
        ),
        name="attend_backward",
    )(place, block_order, doc_lengths, q_t, kv, o_t, lse, do_t)


MESH = pl.DeviceIdType.MESH


def coords():
    ctx = lax.axis_index("ctx")
    return lax.axis_index("seq"), ctx // 2, lax.rem(ctx, 2)


def other(place, step, count):
    return lax.rem(place + step, count)


def meet(devices):
    barrier = pltpu.get_barrier_semaphore()
    for device in devices:
        pl.semaphore_signal(barrier, inc=1, device_id=device, device_id_type=MESH)
    pl.semaphore_wait(barrier, len(devices))


def remote(source, target, send_sem, recv_sem, device):
    return pltpu.make_async_remote_copy(
        src_ref=source,
        dst_ref=target,
        send_sem=send_sem,
        recv_sem=recv_sem,
        device_id=device,
        device_id_type=MESH,
    )


def plane_slots(seq_count):
    seq = lax.axis_index("seq")
    if seq_count == 4:
        beside, above = seq + 1 - 2 * lax.rem(seq, 2), other(seq, 2, 4)
        return [seq, beside, above, 3 - seq], [0, 1, 2, 3]
    return [seq] + [other(seq, step, seq_count) for step in range(1, seq_count)], [0] + [
        seq_count - step for step in range(1, seq_count)
    ]


def spread_tools(scopes, halves, seq_count, chip_count, sources, results, sends, recvs, local_sem):
    _, chip, core = coords()
    ctx = lax.axis_index("ctx")
    ctx_count = 2 * chip_count
    slots, _ = plane_slots(seq_count)
    seq, planes = slots[0], slots[1:]
    sibling = {"ctx": chip * 2 + 1 - core}
    last = chip_count - 1
    sides = [
        (chip < last, {"ctx": lax.rem(chip + 1, chip_count) * 2 + core}),
        (chip > 0, {"ctx": lax.rem(chip + last, chip_count) * 2 + core}),
    ]
    peers = []
    if any(scope != "ctx" for scope in scopes):
        peers += [{"seq": place} for place in planes]
    if any(scope in ("ctx", "all") for scope in scopes):
        peers += [{"ctx": other(chip, step, chip_count) * 2 + core} for step in range(1, chip_count)]
        peers += [sibling]
    locals_ = {}

    def pick(items, *names):
        return [item for item in items if scopes[item] in names]

    started = []

    def part(ref, item, half):
        if half is None:
            return ref
        rows = results[item].shape[-2] // 2
        return ref.at[pl.ds(half * rows, rows)]

    def block(item, at_seq, place, at_core):
        scope = scopes[item]
        at_ctx = place * 2 + at_core
        if scope == "all":
            return results[item].at[at_seq, at_ctx], at_seq * ctx_count + at_ctx
        if scope == "ctx":
            return results[item].at[at_ctx], at_ctx
        return results[item].at[at_seq], at_seq

    def descriptor(item, at_seq, place, half, kind, device, source=None):
        target, number = block(item, at_seq, place, core)
        row = place if scopes[item] in ("ctx", "all") else 0
        return remote(
            part(target if source is None else source, item, half),
            part(target, item, half),
            sends[item].at[row, kind],
            recvs[item].at[2 * number + (half or 0)],
            device,
        )

    def arrival(item, at_seq, place, half, at_core=None):
        target, number = block(item, at_seq, place, core if at_core is None else at_core)
        view = part(target, item, half)
        return remote(
            view, view, sends[item].at[0, 0], recvs[item].at[2 * number + (half or 0)], sibling
        )

    def start(copies, there=None):
        for copy in copies:
            copy.start()
            started.append((there, copy))

    def cut(item):
        return (0, 1) if halves[item] else (None,)

    def plane_copies(item, place, half, source=None):
        if not halves[item]:
            return [
                descriptor(item, seq, place, None, 4 + number, {"seq": to}, source)
                for number, to in enumerate(planes)
            ]
        order = (1, 2) if half == 0 else (2, 1)
        return [
            descriptor(item, seq, place, half, 2 + 2 * half + to + 1, {"seq": slots[to]}, source)
            for to in order
        ]

    kinds_relay = 4 + max(4, seq_count - 1)

    def plane_relay(item, place, there=None):
        if not halves[item]:
            return
        steps = [
            (
                arrival(item, slots[give], place, half),
                descriptor(
                    item, slots[give], place, half, kinds_relay + half, {"seq": slots[3 - give]}
                ),
            )
            for give, half in ((1, 0), (2, 1))
        ]

        def run():
            for got, copy in steps:
                got.wait_recv()
                start([copy], there)

        run() if there is None else pl.when(there)(run)

    def plane_end(item, place, there=None):
        if halves[item]:
            ends = [
                (arrival(item, slots[slot], place, half))
                for slot, half in ((1, 1), (2, 0), (3, 0), (3, 1))
            ]
        else:
            ends = [arrival(item, at_seq, place, None) for at_seq in planes]
        copies = []
        if scopes[item] == "all":
            copies = [
                descriptor(item, at_seq, place, None, kinds_relay + 3 + number, sibling)
                for number, at_seq in enumerate(planes)
            ]

        def run():
            for got in ends:
                got.wait_recv()
            start(copies, there)

        run() if there is None else pl.when(there)(run)

    def pass_on(item, place, there, onward, device):
        steps = []
        for half in cut(item):
            steps.append(
                (
                    arrival(item, seq, place, half),
                    descriptor(item, seq, place, half, half or 0, device),
                    plane_copies(item, place, half) if scopes[item] == "all" else [],
                )
            )
        final = descriptor(item, seq, place, None, kinds_relay + 2, sibling)

        def run():
            for got, copy, copies in steps:
                got.wait_recv()
                pl.when(onward)(copy.start)
                start(copies, there)
            start([final], there)

        pl.when(there)(run)
        for _, copy, _ in steps:
            started.append((there & onward, copy))

    def begin(items):
        for item in items:
            target, _ = block(item, seq, chip, core)
            own = sources[item].at[seq] if scopes[item] == "swap" else sources[item]
            locals_[item] = pltpu.make_async_copy(own, target, local_sem.at[item])
            locals_[item].start()
        for item in pick(items, "ctx", "all"):
            for half in cut(item):
                for side, (there, device) in enumerate(sides):
                    copy = descriptor(
                        item, seq, chip, half, 2 * side + (half or 0), device, sources[item]
                    )
                    pl.when(there)(functools.partial(start, [copy], there))
        for item in pick(items, "swap"):
            start(
                [
                    descriptor(
                        item, seq, chip, None, number, {"seq": place}, sources[item].at[place]
                    )
                    for number, place in enumerate(planes)
                ]
            )
        for item in pick(items, "seq", "all"):
            for half in cut(item):
                start(plane_copies(item, chip, half, sources[item]))
        for item in pick(items, "ctx", "all"):
            start([descriptor(item, seq, chip, None, kinds_relay + 2, sibling, sources[item])])

    def relays(items):
        for item in pick(items, "seq", "all"):
            plane_relay(item, chip)

    def waves(items):
        lines, everywhere = pick(items, "ctx", "all"), pick(items, "all")
        done = []
        for step in range(1, chip_count):
            wave = [
                (lax.rem(chip + chip_count - step, chip_count), chip >= step, *sides[0]),
                (lax.rem(chip + step, chip_count), chip <= last - step, *sides[1]),
            ]
            for place, there, onward, device in wave:
                for item in lines:
                    pass_on(item, place, there, onward, device)
            for item in everywhere:
                for place, there, _, _ in done[-1] if done else []:
                    plane_relay(item, place, there)
            if step == 1:
                for item in pick(items, "seq", "all"):
                    plane_end(item, chip)
            elif step > 2:
                for item in everywhere:
                    for place, there, _, _ in done[-2]:
                        plane_end(item, place, there)
            done.append(wave)
        for item in everywhere:
            for place, there, _, _ in done[-1]:
                plane_relay(item, place, there)
            for wave in done[-2:]:
                for place, there, _, _ in wave:
                    plane_end(item, place, there)

    def settle(items):
        for item in pick(items, "swap"):
            for place in planes:
                arrival(item, place, chip, None).wait_recv()
        for item in pick(items, "ctx", "all"):
            for at_seq in [seq] + (planes if scopes[item] == "all" else []):
                for step in range(chip_count):
                    arrival(item, at_seq, other(chip, step, chip_count), None, 1 - core).wait_recv()
        for item in items:
            locals_[item].wait()

    def end():
        for there, copy in started:
            if there is None:
                copy.wait_send()
            else:
                pl.when(there)(copy.wait_send)

    return peers, begin, relays, waves, settle, end


def spread_sems(arrays, scopes, seq_count, chip_count):
    kinds = 4 + max(4, seq_count - 1) + 3 + seq_count - 1
    sends, recvs, halves, shapes = [], [], [], []
    for array, scope in zip(arrays, scopes):
        lead = {"all": (seq_count, 2 * chip_count), "ctx": (2 * chip_count,)}.get(scope, (seq_count,))
        halves.append(seq_count == 4 and scope in ("all", "seq") and array.shape[0] % 32 == 0)
        shape = array.shape if scope == "swap" else lead + array.shape
        shapes.append(jax.ShapeDtypeStruct(shape, array.dtype))
        rows = chip_count if scope in ("all", "ctx") else 1
        sends.append(pltpu.SemaphoreType.DMA((rows, kinds)))
        recvs.append(pltpu.SemaphoreType.DMA((2 * math.prod(lead),)))
    return shapes, tuple(halves), sends + recvs + [pltpu.SemaphoreType.DMA((len(arrays),))]


def swap_kernel(scopes, halves, seq_count, chip_count, *refs):
    count = len(scopes)
    peers, begin, _, _, settle, end = spread_tools(
        scopes,
        halves,
        seq_count,
        chip_count,
        refs[:count],
        refs[count : 2 * count],
        refs[2 * count : 3 * count],
        refs[3 * count : 4 * count],
        refs[4 * count],
    )
    meet(peers)
    begin(range(count))
    settle(range(count))
    end()


def swap(collective_id, arrays):
    seq_count, chip_count = lax.axis_size("seq"), lax.axis_size("ctx") // 2
    scopes = ("swap",) * len(arrays)
    shapes, halves, sems = spread_sems(arrays, scopes, seq_count, chip_count)
    anywhere = pl.BlockSpec(memory_space=pl.ANY)
    return pl.pallas_call(
        functools.partial(swap_kernel, scopes, halves, seq_count, chip_count),
        out_shape=tuple(shapes),
        in_specs=[anywhere] * len(arrays),
        out_specs=(anywhere,) * len(arrays),
        scratch_shapes=sems,
        compiler_params=pltpu.CompilerParams(collective_id=collective_id, has_side_effects=True),
        cost_estimate=pl.CostEstimate(
            flops=0, transcendentals=0, bytes_accessed=20 * 3_000_000
        ),
        name="swap",
    )(*arrays)


FOLD_SCRATCH = 9
WINDOW = 4


def fold_kernel(kinds, chunk_counts, swap_count, work, seq_count, chip_count, *refs):
    count = len(kinds)
    every = count + swap_count
    sources, swap_sources = refs[:count], refs[count:every]
    extra_in, extra_out = (work[0], work[1]) if work else (0, 0)
    first_out = every + extra_in
    results = refs[first_out : first_out + count]
    swap_results = refs[first_out + count : first_out + every]
    first_rest = first_out + every + extra_out
    rest = refs[first_rest:]
    swap_rest = rest[count * FOLD_SCRATCH : count * FOLD_SCRATCH + 4 * swap_count]
    extra = (
        refs[every:first_out],
        refs[first_out + every : first_rest],
        rest[count * FOLD_SCRATCH + 4 * swap_count :],
    )
    seq, chip, core = coords()
    slots, there = plane_slots(seq_count)
    planes = slots[1:]
    chips = [other(chip, step, chip_count) for step in range(1, chip_count)]
    sibling = {"ctx": chip * 2 + 1 - core}
    peers = []
    if any(kind != "seq" for kind in kinds):
        peers += [{"ctx": place * 2 + core} for place in chips] + [sibling]
    if swap_count or any(kind != "ctx" for kind in kinds):
        peers += [{"seq": place} for place in planes]

    def scratch(item):
        return rest[item * FOLD_SCRATCH : (item + 1) * FOLD_SCRATCH]

    def columns(item, chunk):
        width = sources[item].shape[-1] // chunk_counts[item]
        return slice(chunk * width, (chunk + 1) * width)

    order = []
    for chunk in range(max(chunk_counts, default=0)):
        order += [(item, chunk) for item in range(count) if chunk < chunk_counts[item]]

    loads = []
    for item in range(count):
        mine, sem_s = scratch(item)[0], scratch(item)[7]
        if kinds[item] != "seq":
            load = pltpu.make_async_copy(
                sources[item].at[:, :, core], mine, sem_s.at[4, 0, 0]
            )
            load.start()
            loads.append(load)
    meet(peers)

    waits = []

    def go(source, target, send_sem, recv_sem, device):
        copy = remote(source, target, send_sem, recv_sem, device)
        copy.start()
        waits.append(copy)
        return copy

    firsts = {}
    for item, chunk in order:
        if kinds[item] != "seq":
            _, got1, _, _, _, _, _, sem_s, sem_r = scratch(item)
            cols = columns(item, chunk)
            firsts[item, chunk] = go(
                sources[item].at[:, :, 1 - core, :, cols],
                got1.at[:, :, :, cols],
                sem_s.at[0, chunk, 0],
                sem_r.at[0, chunk, 0],
                sibling,
            )
    swapped = []
    for item in range(swap_count):
        got, sem_s, sem_r, sem_own = swap_rest[4 * item : 4 * item + 4]
        own = pltpu.make_async_copy(swap_sources[item].at[seq], got.at[seq], sem_own)
        own.start()
        swapped.append(own)
        for step, place in enumerate(planes):
            go(swap_sources[item].at[place], got.at[seq], sem_s.at[step], sem_r.at[seq], {"seq": place})
    for load in loads:
        load.wait()

    def block(item, slot, cols):
        if kinds[item] == "seq":
            return sources[item][slot, :, cols].astype(F32)[None]
        mine, got1 = scratch(item)[:2]
        place = slots[slot] if kinds[item] == "all" else 0
        return mine[place, :, :, cols].astype(F32) + got1[place, :, :, cols].astype(F32)

    def turn(item, chunk):
        return (1, 2) if (item + chunk) % 2 == 0 else (2, 1)

    seconds = {}

    def plane_first(item, chunk):
        _, got1, _, got2, keep, _, _, sem_s, sem_r = scratch(item)
        cols = columns(item, chunk)
        if kinds[item] == "all":
            firsts[item, chunk].wait_recv()
        first, _ = turn(item, chunk)
        targets = [(slot, slot) for slot in range(1, seq_count)]
        if seq_count == 4:
            targets = [(3, first), (first, first)]
        row = []
        for number, (slot, to) in enumerate(targets):
            if kinds[item] == "all":
                held = got1.at[slots[slot], :, :, cols]
                held[...] = block(item, slot, cols).astype(BF16)
            else:
                held = sources[item].at[pl.ds(slot, 1), :, cols]
            index = number if seq_count == 4 else there[slot] - 1
            row.append(
                go(
                    held,
                    got2.at[index, :, :, cols],
                    sem_s.at[1, chunk, number],
                    sem_r.at[1, chunk, index],
                    {"seq": slots[to]},
                )
            )
        seconds[item, chunk] = row
        keep[:, :, cols] = block(item, 0, cols)

    def plane_second(item, chunk):
        if seq_count != 4:
            return
        _, got1, spare, got2, keep, _, _, sem_s, sem_r = scratch(item)
        cols = columns(item, chunk)
        _, second = turn(item, chunk)
        across, mine = seconds[item, chunk]
        across.wait_recv()
        if kinds[item] == "all":
            held = got1.at[slots[second], :, :, cols]
        else:
            held = spare.at[:, :, cols]
        held[...] = (block(item, second, cols) + got2[0, :, :, cols].astype(F32)).astype(BF16)
        last = go(
            held,
            got2.at[2, :, :, cols],
            sem_s.at[2, chunk, 0],
            sem_r.at[2, chunk, 0],
            {"seq": slots[second]},
        )
        mine.wait_recv()
        keep[:, :, cols] = keep[:, :, cols] + got2[1, :, :, cols].astype(F32)
        seconds[item, chunk] = [last]

    thirds = {}

    def line(item, chunk):
        _, _, _, got2, keep, pass3, got3, sem_s, sem_r = scratch(item)
        cols = columns(item, chunk)
        if kinds[item] == "ctx":
            firsts[item, chunk].wait_recv()
            keep[:, :, cols] = block(item, 0, cols)
        else:
            for copy in seconds[item, chunk]:
                copy.wait_recv()

        def total(place):
            value = keep[place, :, cols]
            if kinds[item] != "ctx":
                for index in (2,) if seq_count == 4 else range(seq_count - 1):
                    value = value + got2[index, place, :, cols].astype(F32)
            return value

        if kinds[item] == "seq":
            results[item][:, cols] = total(0)
            return
        row = []
        for step, place in enumerate(chips):
            pass3[step, :, cols] = total(place).astype(BF16)
            row.append(
                go(
                    pass3.at[step, :, cols],
                    got3.at[step, :, cols],
                    sem_s.at[3, chunk, step],
                    sem_r.at[3, chunk, step],
                    {"ctx": place * 2 + core},
                )
            )
        results[item][:, cols] = total(chip)
        thirds[item, chunk] = row

    lines = [step for step in order if kinds[step[0]] == "ctx"]
    everywhere = [step for step in order if kinds[step[0]] == "all"]
    flats = [step for step in order if kinds[step[0]] == "seq"]
    for step in lines:
        line(*step)
    for step in everywhere[:WINDOW]:
        plane_first(*step)
    for number, step in enumerate(everywhere):
        plane_second(*step)
        for later in everywhere[number + WINDOW : number + WINDOW + 1]:
            plane_first(*later)
        if number:
            line(*everywhere[number - 1])
    for step in flats:
        plane_first(*step)
    if work:
        work[2](*extra)
    for step in everywhere[-1:]:
        line(*step)
    for step in flats:
        plane_second(*step)
    for step in flats:
        line(*step)
    for item, chunk in lines + everywhere:
        got3 = scratch(item)[6]
        cols = columns(item, chunk)
        for copy in thirds[item, chunk]:
            copy.wait_recv()
        value = results[item][:, cols]
        for step in range(chip_count - 1):
            value = value + got3[step, :, cols].astype(F32)
        results[item][:, cols] = value
    if work:
        work[3](results[0], *extra)
    for item in range(swap_count):
        got, sem_s, sem_r, _ = swap_rest[4 * item : 4 * item + 4]
        swapped[item].wait()
        for place in planes:
            remote(got.at[place], got.at[place], sem_s.at[0], sem_r.at[place], sibling).wait_recv()
        width = got.shape[-1]
        for place in range(seq_count):
            swap_results[item][:, place * width : (place + 1) * width] = got[place].astype(F32)
    for copy in waits:
        copy.wait_send()


def fold(name, collective_id, arrays, kinds, chunk_counts, micros, swaps=(), work=None):
    seq_count, ctx_count = lax.axis_size("seq"), lax.axis_size("ctx")
    chip_count = ctx_count // 2
    inputs, shapes, scratch, in_specs = [], [], [], []
    small = (1, 1, 8, 128)
    dma = pltpu.SemaphoreType.DMA
    for array, kind, chunks in zip(arrays, kinds, chunk_counts):
        parts = 1 if kind == "ctx" else seq_count
        blocks = seq_count if kind == "seq" else parts * ctx_count
        rows, cols = array.shape[0] // blocks, array.shape[1]
        lines = 1 if kind == "seq" else chip_count
        if kind == "seq":
            inputs.append(array.reshape(seq_count, rows, cols))
            in_specs.append(vmem())
            got1, spare = small, (1, rows, cols)
        else:
            inputs.append(array.reshape(parts, chip_count, 2, rows, cols))
            in_specs.append(pl.BlockSpec(memory_space=pl.ANY))
            got1, spare = (parts, chip_count, rows, cols), small[1:]
        shapes.append(jax.ShapeDtypeStruct((rows, cols), F32))
        got2 = small if kind == "ctx" else (seq_count - 1, lines, rows, cols)
        got3 = small[1:] if kind == "seq" else (chip_count - 1, rows, cols)
        most = max(seq_count, chip_count)
        scratch += [
            pltpu.VMEM(got1, BF16),
            pltpu.VMEM(got1, BF16),
            pltpu.VMEM(spare, BF16),
            pltpu.VMEM(got2, BF16),
            pltpu.VMEM((lines, rows, cols), F32),
            pltpu.VMEM(got3, BF16),
            pltpu.VMEM(got3, BF16),
            dma((5, chunks, most)),
            dma((4, chunks, most)),
        ]
    for array in swaps:
        inputs.append(array)
        in_specs.append(pl.BlockSpec(memory_space=pl.ANY))
        shapes.append(jax.ShapeDtypeStruct((array.shape[1], seq_count * array.shape[2]), F32))
        scratch += [
            pltpu.VMEM(array.shape, BF16),
            dma((seq_count - 1,)),
            dma((seq_count,)),
            dma,
        ]
    out_specs = [vmem()] * len(inputs)
    does = None
    if work:
        does = (len(work["inputs"]), len(work["shapes"]), work["during"], work["after"])
        inputs += work["inputs"]
        in_specs += work["in_specs"]
        shapes += work["shapes"]
        out_specs += work["out_specs"]
        scratch += work["scratch"]
    return pl.pallas_call(
        functools.partial(
            fold_kernel, tuple(kinds), tuple(chunk_counts), len(swaps), does, seq_count, chip_count
        ),
        out_shape=tuple(shapes),
        in_specs=in_specs,
        out_specs=tuple(out_specs),
        scratch_shapes=scratch,
        compiler_params=pltpu.CompilerParams(
            collective_id=collective_id, has_side_effects=True, vmem_limit_bytes=VMEM_MOST
        ),
        cost_estimate=pl.CostEstimate(
            flops=0, transcendentals=0, bytes_accessed=int(micros * 3_000_000)
        ),
        name=name,
    )(*inputs)


def tiles(extent, width, visit, first=0):
    whole = extent // width

    @pl.loop(first, whole)
    def _(number):
        visit(pl.ds(pl.multiple_of(number * width, width), width))

    if extent % width:
        visit(pl.ds(whole * width, extent % width))


def stream_rows(extent, width, produce, stage, sem, target):
    whole = extent // width

    def leave(slot, rows, size):
        return pltpu.make_async_copy(
            stage.at[slot, pl.ds(0, size)], target.at[rows], sem.at[slot]
        )

    @pl.loop(0, whole)
    def _(number):
        slot = lax.rem(number, 2)
        rows = pl.ds(pl.multiple_of(number * width, width), width)

        @pl.when(number >= 2)
        def _():
            leave(slot, rows, width).wait()

        stage[slot] = produce(rows).astype(stage.dtype)
        leave(slot, rows, width).start()

    for number in range(max(0, whole - 2), whole):
        leave(number % 2, pl.ds(number * width, width), width).wait()
    if extent % width:
        size = extent % width
        rows = pl.ds(whole * width, size)
        stage[0, :size] = produce(rows).astype(stage.dtype)
        leave(0, rows, size).start()
        leave(0, rows, size).wait()


def ffn_first_kernel(
    seq_count, f_ref, g_ref, wg_ref, wd_ref, f_out, g_out, gate_ref, gh_ref, f_s, g_s, wg, wd, in_sem, f_send, f_recv, out_sem
):
    rows = f_ref.shape[0]
    width = wg.shape[1]
    places, there = plane_slots(seq_count)
    load_f = pltpu.make_async_copy(f_ref, f_s.at[pl.ds(0, rows)], in_sem.at[seq_count])
    load_wd = pltpu.make_async_copy(wd_ref, wd, in_sem.at[seq_count + 1])
    load_wg = pltpu.make_async_copy(wg_ref, wg, in_sem.at[seq_count + 2])
    loads = [load_wd]
    for slot in range(seq_count):
        loads.append(
            pltpu.make_async_copy(
                g_ref.at[places[slot]], g_s.at[pl.ds(slot * rows, rows)], in_sem.at[slot]
            )
        )
    for load in [*loads, load_f, load_wg]:
        load.start()
    meet([{"seq": place} for place in places[1:]])

    started = []

    def f_block(slot, half):
        if half is None:
            return f_s.at[pl.ds(slot * rows, rows)]
        return f_s.at[pl.ds(slot * rows + half * (rows // 2), rows // 2)]

    def f_copy(source, to, slot, half):
        copy = remote(
            source,
            f_block(slot, half),
            f_send.at[len(started)],
            f_recv.at[slot, half or 0],
            {"seq": places[to]},
        )
        copy.start()
        started.append(copy)

    def f_arrive(slot, half):
        block = f_block(slot, half)
        remote(
            block, block, f_send.at[0], f_recv.at[slot, half or 0], {"seq": places[1]}
        ).wait_recv()

    if seq_count == 4:
        for half in (0, 1):
            source = f_ref.at[pl.ds(half * (rows // 2), rows // 2)]
            for to in (1, 2) if half == 0 else (2, 1):
                f_copy(source, to, to, half)
    else:
        for to in range(1, seq_count):
            f_copy(f_ref, to, there[to], None)

    def gate_rows(first, count):
        own = slice(first, first + count)

        def visit(cols):
            gate_ref[own, cols] = dot32(f_s[own, :], wg[:, cols], ((1,), (0,)))

        tiles(width, 256, visit)

    for load in loads:
        load.wait()
    leave_g = pltpu.make_async_copy(g_s, g_out, out_sem.at[1])
    leave_g.start()

    def grad_hidden(cols):
        gh_ref[:, cols] = dot32(g_s[...], wd[cols, :], ((1,), (1,))).astype(gh_ref.dtype)

    tiles(width, 256, grad_hidden)
    for load in (load_f, load_wg):
        load.wait()
    gate_rows(0, rows)
    if seq_count == 4:
        f_arrive(1, 0)
        f_copy(f_block(1, 0), 2, 3, 0)
        f_arrive(2, 1)
        f_copy(f_block(2, 1), 1, 3, 1)
        f_arrive(1, 1)
        f_arrive(2, 0)
        gate_rows(rows, 2 * rows)
        f_arrive(3, 0)
        f_arrive(3, 1)
        leave = pltpu.make_async_copy(f_s, f_out, out_sem.at[0])
        leave.start()
        gate_rows(3 * rows, rows)
    else:
        for slot in range(1, seq_count):
            f_arrive(slot, None)
        leave = pltpu.make_async_copy(f_s, f_out, out_sem.at[0])
        leave.start()
        gate_rows(rows, (seq_count - 1) * rows)
    leave.wait()
    leave_g.wait()
    for copy in started:
        copy.wait_send()


def ffn_act_kernel(
    f_ref, gate_ref, gh_ref, wu_ref, hid, gg, gu, pg_ref, f_s, gate_s, gh_s, wu, stage_f, in_sem, leave_sem
):
    model, width = wu.shape
    loads = [
        pltpu.make_async_copy(source, target, in_sem.at[number])
        for number, (source, target) in enumerate(
            [(f_ref, f_s), (wu_ref, wu), (gate_ref, gate_s), (gh_ref, gh_s)]
        )
    ]
    for load in loads:
        load.start()
    for load in loads[:2]:
        load.wait()

    def act(cols, ready=None):
        up_val = dot32(f_s[...], wu[:, cols], ((1,), (0,)))
        if ready is not None:
            ready()
        gate = gate_s[:, cols]
        grad = gh_s[:, cols].astype(F32)
        sigma = jax.nn.sigmoid(gate)
        activated = gate * sigma
        hid[:, cols] = (activated * up_val).astype(BF16)
        gg[:, cols] = (grad * up_val * (sigma + activated * (1.0 - sigma))).astype(BF16)
        gu[:, cols] = (grad * activated).astype(BF16)

    def ready():
        for load in loads[2:]:
            load.wait()

    act(pl.ds(0, 256), ready)
    tiles(width, 256, act, 1)
    stream_rows(
        model,
        256,
        lambda own: dot32(f_s[:, own], gg[...], ((0,), (0,))),
        stage_f,
        leave_sem,
        pg_ref,
    )


def ffn_grad_kernel(
    seq_count,
    f_ref,
    hid_ref,
    gg_ref,
    gu_ref,
    g_ref,
    wg_ref,
    wu_ref,
    wd_ref,
    gf_ref,
    out_ref,
    pu_ref,
    pd_ref,
    f_s,
    g_s,
    hid,
    gg,
    gu,
    wg,
    wu,
    wd,
    parts,
    got,
    stage_f,
    stage_d,
    in_sem,
    x_send,
    x_recv,
    leave_sem,
):
    rows = gf_ref.shape[0]
    model, width = wg.shape
    places, there = plane_slots(seq_count)
    loads = [
        pltpu.make_async_copy(source, target, in_sem.at[number])
        for number, (source, target) in enumerate(
            [
                (gg_ref, gg),
                (gu_ref, gu),
                (wg_ref, wg),
                (wu_ref, wu),
                (f_ref, f_s),
                (hid_ref, hid),
                (g_ref, g_s),
                (wd_ref, wd),
            ]
        )
    ]
    for load in loads[:4]:
        load.start()
    meet([{"seq": place} for place in places[1:]])
    for load in loads[:4]:
        load.wait()
    for load in loads[4:]:
        load.start()

    def part_copy(slot, cols):
        return remote(
            parts.at[pl.ds((slot - 1) * rows, rows), cols],
            got.at[there[slot] - 1, :, cols],
            x_send.at[slot],
            x_recv.at[there[slot]],
            {"seq": places[slot]},
        )

    def grad_f(cols):
        part = dot32(gg[...], wg[cols, :], ((1,), (1,))) + dot32(gu[...], wu[cols, :], ((1,), (1,)))
        gf_ref[:, cols] = part[:rows]
        parts[:, cols] = part[rows:].astype(BF16)
        for slot in range(1, seq_count):
            part_copy(slot, cols).start()

    tiles(model, 256, grad_f)
    for load in loads[4:]:
        load.wait()
    stream_rows(
        model,
        256,
        lambda own: dot32(f_s[:, own], gu[...], ((0,), (0,))),
        stage_f,
        leave_sem.at[0],
        pu_ref,
    )
    stream_rows(
        width,
        256,
        lambda own: dot32(hid[:, own], g_s[...], ((0,), (0,))),
        stage_d,
        leave_sem.at[2],
        pd_ref,
    )

    def out_copy(cols):
        return pltpu.make_async_copy(f_s.at[:, cols], out_ref.at[:, cols], leave_sem.at[1, 0])

    def out_part(cols):
        f_s[:, cols] = dot32(hid[...], wd[:, cols], ((1,), (0,))).astype(BF16)
        out_copy(cols).start()

    tiles(model, 256, out_part)
    everything = pl.ds(0, model)
    out_copy(everything).wait()
    for slot in range(1, seq_count):
        part_copy(slot, everything).wait_recv()
    total = gf_ref[...]
    for slot in range(seq_count - 1):
        total = total + got[slot].astype(F32)
    gf_ref[...] = total
    for slot in range(1, seq_count):
        part_copy(slot, everything).wait_send()


def ffn_first(collective_id, f_norm, g_all, w_gate, w_down):
    seq_count = lax.axis_size("seq")
    rows, model = f_norm.shape
    width = w_gate.shape[1]
    count = seq_count * rows
    anywhere = pl.BlockSpec(memory_space=pl.ANY)
    dma = pltpu.SemaphoreType.DMA
    return pl.pallas_call(
        functools.partial(ffn_first_kernel, seq_count),
        out_shape=(
            jax.ShapeDtypeStruct((count, model), BF16),
            jax.ShapeDtypeStruct((count, model), BF16),
            jax.ShapeDtypeStruct((count, width), F32),
            jax.ShapeDtypeStruct((count, width), BF16),
        ),
        in_specs=[anywhere] * 4,
        out_specs=(anywhere, anywhere, vmem(), vmem()),
        scratch_shapes=[
            pltpu.VMEM((count, model), BF16),
            pltpu.VMEM((count, model), BF16),
            pltpu.VMEM((model, width), BF16),
            pltpu.VMEM((width, model), BF16),
            dma((seq_count + 3,)),
            dma((max(6, seq_count),)),
            dma((seq_count, 2)),
            dma((2,)),
        ],
        compiler_params=pltpu.CompilerParams(
            collective_id=collective_id, has_side_effects=True, vmem_limit_bytes=VMEM_MOST
        ),
        cost_estimate=pl.CostEstimate(
            flops=8 * count * model * width,
            transcendentals=0,
            bytes_accessed=4 * (2 * width * model + 3 * count * model),
        ),
        name="ffn_first",
    )(f_norm, g_all.reshape(seq_count, rows, model), w_gate, w_down)


def ffn_act(f_all, gate, grad_hidden, w_up):
    count, model = f_all.shape
    width = w_up.shape[1]
    anywhere = pl.BlockSpec(memory_space=pl.ANY)
    dma = pltpu.SemaphoreType.DMA
    return pl.pallas_call(
        ffn_act_kernel,
        out_shape=(
            jax.ShapeDtypeStruct((count, width), BF16),
            jax.ShapeDtypeStruct((count, width), BF16),
            jax.ShapeDtypeStruct((count, width), BF16),
            jax.ShapeDtypeStruct((model, width), BF16),
        ),
        in_specs=[anywhere] * 4,
        out_specs=(vmem(), vmem(), vmem(), anywhere),
        scratch_shapes=[
            pltpu.VMEM((count, model), BF16),
            pltpu.VMEM((count, width), F32),
            pltpu.VMEM((count, width), BF16),
            pltpu.VMEM((model, width), BF16),
            pltpu.VMEM((2, 256, width), BF16),
            dma((4,)),
            dma((2,)),
        ],
        compiler_params=pltpu.CompilerParams(vmem_limit_bytes=VMEM_MOST),
        cost_estimate=pl.CostEstimate(
            flops=4 * count * model * width,
            transcendentals=count * width,
            bytes_accessed=4 * (width * model + 2 * count * model + 3 * count * width),
        ),
        name="ffn_act",
    )(f_all, gate, grad_hidden, w_up)


def ffn_grad(collective_id, rows, f_all, hidden_act, grad_gate, grad_up, g_all, w_gate, w_up, w_down):
    seq_count = lax.axis_size("seq")
    count, model = f_all.shape
    width = w_gate.shape[1]
    anywhere = pl.BlockSpec(memory_space=pl.ANY)
    dma = pltpu.SemaphoreType.DMA
    return pl.pallas_call(
        functools.partial(ffn_grad_kernel, seq_count),
        out_shape=(
            jax.ShapeDtypeStruct((rows, model), F32),
            jax.ShapeDtypeStruct((count, model), BF16),
            jax.ShapeDtypeStruct((model, width), BF16),
            jax.ShapeDtypeStruct((width, model), BF16),
        ),
        in_specs=[anywhere] * 8,
        out_specs=(vmem(), anywhere, anywhere, anywhere),
        scratch_shapes=[
            pltpu.VMEM((count, model), BF16),
            pltpu.VMEM((count, model), BF16),
            pltpu.VMEM((count, width), BF16),
            pltpu.VMEM((count, width), BF16),
            pltpu.VMEM((count, width), BF16),
            pltpu.VMEM((model, width), BF16),
            pltpu.VMEM((model, width), BF16),
            pltpu.VMEM((width, model), BF16),
            pltpu.VMEM((count - rows, model), BF16),
            pltpu.VMEM((seq_count - 1, rows, model), BF16),
            pltpu.VMEM((2, 256, width), BF16),
            pltpu.VMEM((2, 256, model), BF16),
            dma((8,)),
            dma((seq_count,)),
            dma((seq_count,)),
            dma((3, 2)),
        ],
        compiler_params=pltpu.CompilerParams(
            collective_id=collective_id, has_side_effects=True, vmem_limit_bytes=VMEM_MOST
        ),
        cost_estimate=pl.CostEstimate(
            flops=14 * count * model * width,
            transcendentals=0,
            bytes_accessed=4 * (3 * width * model + 3 * count * model),
        ),
        name="ffn_grad",
    )(f_all, hidden_act, grad_gate, grad_up, g_all, w_gate, w_up, w_down)


def half_turn(value):
    half = HEAD_DIM // 2
    return jnp.concatenate([-value[half:], value[:half]], axis=0)


GATHER_SCOPES = ("all", "all", "ctx", "all", "seq")


def project_kernel(
    halves,
    seq_count,
    chip_count,
    gain_src,
    w_src,
    wo_src,
    g_src,
    x_ref,
    cos_ref,
    sin_ref,
    gains_ref,
    w_ref,
    kv_ref,
    wo_ref,
    g_ref,
    normed_ref,
    rms_ref,
    q_ref,
    gain_a_ref,
    gain_f_ref,
    kv_own,
    w_s,
    gains_s,
    load_sem,
    *sems,
):
    tile = KV_HEADS * HEAD_DIM
    model, own_rows, width = x_ref.shape[1], w_src.shape[0], w_src.shape[1]
    count = width // tile
    peers, begin, relays, waves, settle, end = spread_tools(
        GATHER_SCOPES,
        halves,
        seq_count,
        chip_count,
        (gain_src, w_src, kv_own, wo_src, g_src),
        (gains_ref, w_ref, kv_ref, wo_ref, g_ref),
        sems[:5],
        sems[5:10],
        sems[10],
    )
    meet(peers)
    begin((0, 1))
    x = x_ref[...].astype(F32)
    rms = lax.rsqrt(jnp.mean(x * x, axis=1, keepdims=True) + EPS)
    rms_ref[...] = rms
    relays((0, 1))
    waves((0, 1))
    begin((3, 4))
    settle((0, 1))

    def load(number):
        cols = pl.ds(pl.multiple_of(number * tile, tile), tile)
        return pltpu.make_async_copy(
            w_ref.at[:, :, :, cols], w_s.at[:, :, :, cols], load_sem.at[number]
        )

    load_gains = pltpu.make_async_copy(gains_ref, gains_s, load_sem.at[count])
    load_gains.start()
    for number in range(count):
        load(number).start()
    load_gains.wait()
    for number in range(seq_count * 2 * chip_count):
        at_seq, at_ctx = divmod(number, 2 * chip_count)
        row = gains_s[at_seq, at_ctx, 0:1, :].astype(F32)
        own = slice(number * own_rows, (number + 1) * own_rows)
        gain_a_ref[:, own] = row[:, :own_rows]
        gain_f_ref[:, own] = row[:, own_rows : 2 * own_rows]
    normed_ref[...] = (x_ref[...].astype(F32) * rms_ref[...] * gain_a_ref[...]).astype(BF16)

    def product(number):
        load(number).wait()
        cols = pl.ds(pl.multiple_of(number * tile, tile), tile)
        return dot32(normed_ref[...], w_s[:, :, :, cols].reshape(model, tile), ((1,), (0,)))

    def rotated(value):
        turned = value.T
        pieces = []
        for head in range(tile // HEAD_DIM):
            one = turned[head * HEAD_DIM : (head + 1) * HEAD_DIM]
            pieces.append(one * cos_ref[...] + half_turn(one) * sin_ref[...])
        return jnp.concatenate(pieces, axis=0)

    kv_own[:, :tile] = rotated(product(count - 2)).T.astype(BF16)
    kv_own[:, tile:] = product(count - 1).astype(BF16)
    begin((2,))
    relays((3, 4))

    @pl.loop(0, count - 2)
    def _(number):
        own = pl.ds(pl.multiple_of(number * tile, tile), tile)
        q_ref[own, :] = rotated(product(number)).astype(BF16)

    waves((3, 4))
    waves((2,))
    settle((3, 4, 2))
    end()


def project(collective_id, gain_row, w_qkv, w_out, g_own, x, cosine, sine):
    seq_count, ctx_count = lax.axis_size("seq"), lax.axis_size("ctx")
    chip_count = ctx_count // 2
    rows, model = x.shape
    width = w_qkv.shape[1]
    tile = KV_HEADS * HEAD_DIM
    kv_like = jax.ShapeDtypeStruct((rows, 2 * tile), BF16)
    shapes, halves, sems = spread_sems(
        [gain_row, w_qkv, kv_like, w_out, g_own], GATHER_SCOPES, seq_count, chip_count
    )
    anywhere = pl.BlockSpec(memory_space=pl.ANY)
    return pl.pallas_call(
        functools.partial(project_kernel, halves, seq_count, chip_count),
        out_shape=(
            *shapes,
            jax.ShapeDtypeStruct((rows, model), BF16),
            jax.ShapeDtypeStruct((rows, 1), F32),
            jax.ShapeDtypeStruct((width - 2 * tile, rows), BF16),
            jax.ShapeDtypeStruct((1, model), F32),
            jax.ShapeDtypeStruct((1, model), F32),
        ),
        in_specs=[anywhere] * 4 + [vmem()] * 3,
        out_specs=(anywhere,) * 5 + (vmem(),) * 5,
        scratch_shapes=[
            pltpu.VMEM((rows, 2 * tile), BF16),
            pltpu.VMEM(shapes[1].shape, BF16),
            pltpu.VMEM(shapes[0].shape, BF16),
            pltpu.SemaphoreType.DMA((width // tile + 1,)),
            *sems,
        ],
        compiler_params=pltpu.CompilerParams(
            collective_id=collective_id, has_side_effects=True, vmem_limit_bytes=VMEM_MOST
        ),
        cost_estimate=pl.CostEstimate(
            flops=0, transcendentals=0, bytes_accessed=140 * 3_000_000
        ),
        name="project",
    )(gain_row, w_qkv, w_out, g_own, x, cosine, sine)


def rotated_back(value, cos_ref, sin_ref):
    pieces = []
    for head in range(value.shape[0] // HEAD_DIM):
        one = value[head * HEAD_DIM : (head + 1) * HEAD_DIM]
        pieces.append(one * cos_ref[...] - half_turn(one * sin_ref[...]))
    return jnp.concatenate(pieces, axis=0).T.astype(BF16)


def back_during(inputs, outputs, scratch):
    dq_ref, o_ref, cos_ref, sin_ref, normed_ref, x_ref, rms_ref, gain_ref, grad_ref, w_ref = inputs
    part_out, part_query, part_kv, out_ref, gain_out = outputs
    w_s, g_s, gx_s, ga_s, stage, stage_kv, load_sem, leave_sem = scratch
    tile = KV_HEADS * HEAD_DIM
    q_width = dq_ref.shape[0]
    model = x_ref.shape[1]
    pltpu.make_async_copy(w_ref, w_s, load_sem).start()
    ga_s[...] = grad_ref[...].astype(BF16)
    stream_rows(
        q_width,
        256,
        lambda own: dot32(o_ref[own, :], ga_s[...], ((1,), (0,))),
        stage,
        leave_sem,
        part_out,
    )

    @pl.loop(0, q_width // tile)
    def _(number):
        own = pl.ds(pl.multiple_of(number * tile, tile), tile)
        g_s[:, own] = rotated_back(dq_ref[own, :], cos_ref, sin_ref)

    stream_rows(
        model,
        256,
        lambda own: dot32(normed_ref[:, own], g_s[:, :q_width], ((0,), (0,))),
        stage,
        leave_sem,
        part_query,
    )
    pltpu.make_async_copy(w_ref, w_s, load_sem).wait()

    def grad_x(cols):
        gx_s[:, cols] = dot32(g_s[:, :q_width], w_s[cols, :q_width], ((1,), (1,)))

    tiles(model, 256, grad_x)


def back_after(dkv_ref, inputs, outputs, scratch):
    dq_ref, o_ref, cos_ref, sin_ref, normed_ref, x_ref, rms_ref, gain_ref, grad_ref, w_ref = inputs
    part_out, part_query, part_kv, out_ref, gain_out = outputs
    w_s, g_s, gx_s, ga_s, stage, stage_kv, load_sem, leave_sem = scratch
    tile = KV_HEADS * HEAD_DIM
    q_width = dq_ref.shape[0]
    model = x_ref.shape[1]
    g_s[:, q_width : q_width + tile] = rotated_back(dkv_ref[:, :tile].T, cos_ref, sin_ref)
    g_s[:, q_width + tile :] = dkv_ref[:, tile:].astype(BF16)
    stream_rows(
        model,
        256,
        lambda own: dot32(normed_ref[:, own], g_s[:, q_width:], ((0,), (0,))),
        stage_kv,
        leave_sem,
        part_kv,
    )

    def grad_x(cols):
        gx_s[:, cols] = gx_s[:, cols] + dot32(g_s[:, q_width:], w_s[cols, q_width:], ((1,), (1,)))

    tiles(model, 256, grad_x)
    x = x_ref[...].astype(F32)
    rms = rms_ref[...]
    gain_out[...] = jnp.sum(gx_s[...] * (x * rms), axis=0, keepdims=True)
    scaled = gx_s[...] * gain_ref[...]
    mean = jnp.mean(scaled * x, axis=1, keepdims=True)
    out_ref[...] = grad_ref[...] + (rms * scaled - x * (rms * rms * rms * mean))


def back_work(dq_t, o_t, cosine, sine, normed, x, rms, gain, grad, w_qkv):
    rows, model = x.shape
    width = w_qkv.shape[1]
    q_width = dq_t.shape[0]
    anywhere = pl.BlockSpec(memory_space=pl.ANY)
    return {
        "inputs": [dq_t, o_t, cosine, sine, normed, x, rms, gain, grad, w_qkv],
        "in_specs": [vmem()] * 9 + [anywhere],
        "shapes": [
            jax.ShapeDtypeStruct((q_width, model), BF16),
            jax.ShapeDtypeStruct((model, q_width), BF16),
            jax.ShapeDtypeStruct((model, width - q_width), BF16),
            jax.ShapeDtypeStruct((rows, model), F32),
            jax.ShapeDtypeStruct((1, model), F32),
        ],
        "out_specs": [anywhere, anywhere, anywhere, vmem(), vmem()],
        "scratch": [
            pltpu.VMEM(w_qkv.shape, BF16),
            pltpu.VMEM((rows, width), BF16),
            pltpu.VMEM((rows, model), F32),
            pltpu.VMEM((rows, model), BF16),
            pltpu.VMEM((2, 256, max(model, q_width)), BF16),
            pltpu.VMEM((2, 256, width - q_width), BF16),
            pltpu.SemaphoreType.DMA,
            pltpu.SemaphoreType.DMA((2,)),
        ],
        "during": back_during,
        "after": back_after,
    }


def gather(value, axes, dim=0):
    return lax.all_gather(value, axes, axis=dim, tiled=True)


def scatter_sum(value, axes, dim=0):
    return lax.psum_scatter(value, axes, scatter_dimension=dim, tiled=True)


def norm_back(grad_normed, source, rms_val, gain_val, normed):
    grad_gain = jnp.sum(grad_normed * normed, axis=0)
    scaled = grad_normed * gain_val
    grad_source = rms_val * scaled - source * (rms_val * rms_val * rms_val) * jnp.mean(
        scaled * source, axis=1, keepdims=True
    )
    return (grad_gain, grad_source)


def local(
    hidden_in,
    attn_gain,
    w_query,
    w_key,
    w_value,
    w_out,
    ffn_gain,
    w_gate,
    w_up,
    w_down,
    cotangent,
    doc_lengths,
    selected,
    block_order,
):
    one, rows, model = hidden_in.shape
    seq_count = lax.axis_size("seq")
    ctx_count = lax.axis_size("ctx")
    place = lax.axis_index("ctx").astype(jnp.int32).reshape(1)
    length = rows * ctx_count
    span_len = length // block_order.shape[0]
    q_width = HEADS * HEAD_DIM
    kv_width = KV_HEADS * HEAD_DIM
    own_rows = w_gate.shape[0]
    ff_part = w_gate.shape[1] // seq_count

    def split_columns(weight):
        return weight.reshape(own_rows, seq_count, ff_part).transpose(1, 0, 2)

    own_spans = lax.dynamic_slice_in_dim(block_order, place[0] * (rows // span_len), rows // span_len)
    local_pos = (
        own_spans[:, None] * span_len + jnp.arange(span_len, dtype=jnp.int32)[None, :]
    ).reshape(rows)
    half = HEAD_DIM // 2
    inverse = ROPE_BASE ** (-(jnp.arange(half, dtype=F32) * 2.0 / HEAD_DIM))
    angle = inverse[:, None] * local_pos.astype(F32)[None, :]
    cosine = jnp.concatenate([jnp.cos(angle)] * 2, axis=0)
    sine = jnp.concatenate([jnp.sin(angle)] * 2, axis=0)

    full_down = gather(w_down, "ctx")
    gain_row = jnp.pad(jnp.concatenate([attn_gain, ffn_gain])[None], ((0, 15), (0, 128 - 2 * own_rows)))
    gate_mine, up_mine = swap(0, [split_columns(w_gate), split_columns(w_up)])
    full_gate = gather(gate_mine, "ctx", 1).reshape(model, ff_part)
    full_up = gather(up_mine, "ctx", 1).reshape(model, ff_part)

    grad_y = (
        cotangent.reshape(rows, model).astype(F32) * selected.reshape(rows).astype(F32)[:, None]
    )
    tokens = hidden_in.reshape(rows, model).astype(F32)
    _, w_qkv, kv, full_out, g_all, x_norm, rms_a, q_t, gain_a, gain_f = project(
        1,
        gain_row,
        jnp.concatenate([w_query, w_key, w_value], axis=1),
        w_out,
        grad_y.astype(BF16),
        hidden_in.reshape(rows, model),
        cosine,
        sine,
    )
    w_qkv = w_qkv.reshape(model, q_width + 2 * kv_width)
    kv = kv.reshape(length, 2 * kv_width)
    full_out = full_out.reshape(q_width, model)
    o_t, lse = attend_forward(place, block_order, doc_lengths, q_t, kv)

    middle = tokens + jnp.einsum("ht,hd->td", o_t, full_out, preferred_element_type=F32)
    rms_f = lax.rsqrt(jnp.mean(middle * middle, axis=1, keepdims=True) + EPS)
    normed_f = middle * rms_f
    f_norm = (normed_f * gain_f).astype(BF16)

    f_all, g_slots, gate, grad_hidden = ffn_first(2, f_norm, g_all, full_gate, full_down)
    hidden_act, grad_gate, grad_up, part_gate = ffn_act(f_all, gate, grad_hidden, full_up)
    grad_f_norm, ffn_part, part_up, part_down = ffn_grad(
        3, rows, f_all, hidden_act, grad_gate, grad_up, g_slots, full_gate, full_up, full_down
    )

    def ffn_rows(part):
        return scatter_sum(part.reshape(seq_count, model // seq_count, ff_part), "ctx", 1)

    rows_gate = ffn_rows(part_gate)
    rows_up = ffn_rows(part_up)
    grad_ffn_gain, grad_from_f = norm_back(grad_f_norm, middle, rms_f, gain_f, normed_f)
    grad_middle = grad_y + grad_from_f
    g_attn = grad_middle.astype(BF16)
    do_t = jnp.einsum("td,hd->ht", g_attn, full_out, preferred_element_type=F32).astype(BF16)
    dq_t, dkv = attend_backward(place, block_order, doc_lengths, q_t, kv, o_t, lse, do_t)
    part_down, rows_gate, dkv = lax.optimization_barrier((part_down, rows_gate, dkv))
    grad_w_down = scatter_sum(part_down, "ctx").astype(F32)
    _, ffn_out, part_out, part_query, part_kv, grad_input, grad_attn_gain = fold(
        "fold_kv",
        4,
        [dkv, ffn_part],
        ("ctx", "seq"),
        (1, 2),
        60,
        work=back_work(
            dq_t,
            o_t,
            cosine,
            sine,
            x_norm,
            hidden_in.reshape(rows, model),
            rms_a,
            gain_a,
            grad_middle,
            w_qkv,
        ),
    )
    output = (middle + ffn_out).astype(BF16).reshape(one, rows, model)
    part_gains = jnp.concatenate(
        [grad_attn_gain.reshape(-1, own_rows), grad_ffn_gain.reshape(-1, own_rows)], axis=1
    )
    part_gains = jnp.pad(part_gains[:, None], ((0, 0), (0, 15), (0, 128 - 2 * own_rows)))
    grad_w_out, grad_w_query, grad_w_kv, grad_gains, grad_w_gate, grad_w_up = fold(
        "fold_weights",
        5,
        [part_out, part_query, part_kv, part_gains.reshape(-1, 128).astype(BF16)],
        ("all", "all", "all", "all"),
        (8, 8, 2, 1),
        110,
        [rows_gate, rows_up],
    )
    return (
        output,
        grad_input.reshape(one, rows, model),
        grad_gains[0, :own_rows],
        grad_w_query,
        grad_w_kv[:, :kv_width],
        grad_w_kv[:, kv_width:],
        grad_w_out,
        grad_gains[0, own_rows : 2 * own_rows],
        grad_w_gate,
        grad_w_up,
        grad_w_down,
    )


def solution(mesh):
    return jax.shard_map(
        local,
        mesh=mesh,
        in_specs=(
            P("seq", "ctx", None),
            P(("seq", "ctx")),
            P(("seq", "ctx"), None),
            P(("seq", "ctx"), None),
            P(("seq", "ctx"), None),
            P(("seq", "ctx"), None),
            P(("seq", "ctx")),
            P(("seq", "ctx"), None),
            P(("seq", "ctx"), None),
            P(("seq", "ctx"), None),
            P("seq", "ctx", None),
            P("seq", None),
            P("seq", "ctx"),
            P(),
        ),
        out_specs=(
            P("seq", "ctx", None),
            P("seq", "ctx", None),
            P(("seq", "ctx")),
            P(("seq", "ctx"), None),
            P(("seq", "ctx"), None),
            P(("seq", "ctx"), None),
            P(("seq", "ctx"), None),
            P(("seq", "ctx")),
            P(("seq", "ctx"), None),
            P(("seq", "ctx"), None),
            P(("seq", "ctx"), None),
        ),
        check_vma=False,
    )
```

```python
import functools
import math

import jax
import jax.numpy as jnp
from jax import lax
from jax.experimental import pallas as pl
from jax.experimental.pallas import tpu as pltpu
from jax.sharding import PartitionSpec as P

HEADS = 32
KV_HEADS = 4
HEAD_DIM = 64
GROUP = HEADS // KV_HEADS
SCALE = 1.0 / math.sqrt(HEAD_DIM)
LOG2E = math.log2(math.e)


EPS = 1e-05
ROPE_BASE = 10000.0
NEG = -1e30

F32 = jnp.float32
BF16 = jnp.bfloat16
VMEM_MOST = 56 * 1024 * 1024


def dot32(left, right, dims):
    return lax.dot_general(left, right, (dims, ((), ())), preferred_element_type=F32)


def span_bounds(order_ref, lens_ref, span_len, spans, own_first, own):
    docs = lens_ref.shape[1]
    base = order_ref[own_first + own] * span_len
    pos = lax.broadcasted_iota(jnp.int32, (1, span_len), 1) + base
    start = jnp.zeros((1, span_len), jnp.int32)
    first_start = jnp.int32(0)
    end = jnp.int32(0)
    for number in range(docs):
        end = end + lens_ref[0, number]
        start = jnp.where(pos >= end, end, start)
        first_start = jnp.where(base >= end, end, first_start)
    return base, pos, start, first_start


def allowed_tile(key_base, span_len, pos, start):
    key_pos = lax.broadcasted_iota(jnp.int32, (span_len, span_len), 0) + key_base
    tile = (key_pos <= pos) & (key_pos >= start)
    return jnp.concatenate([tile.astype(F32)] * GROUP, axis=1) > 0.5


def stack_heads(ref, head, own, span_len):
    pieces = []
    for member in range(GROUP):
        row = (head * GROUP + member) * HEAD_DIM
        pieces.append(ref[row : row + HEAD_DIM, own * span_len : (own + 1) * span_len])
    return jnp.concatenate(pieces, axis=1)


def unstack_heads(ref, value, head, own, span_len):
    for member in range(GROUP):
        row = (head * GROUP + member) * HEAD_DIM
        ref[row : row + HEAD_DIM, own * span_len : (own + 1) * span_len] = value[
            :, member * span_len : (member + 1) * span_len
        ].astype(ref.dtype)


def attend_forward_kernel(
    span_len,
    spans,
    place_ref,
    order_ref,
    lens_ref,
    q_ref,
    kv_ref,
    x_ref,
    gain_ref,
    wo_ref,
    o_ref,
    lse_ref,
    middle_ref,
    rms_ref,
    f_ref,
    top_ref,
    sum_ref,
    acc_ref,
    o_s,
    wo_s,
    load_sem,
):
    load = pltpu.make_async_copy(wo_ref, wo_s, load_sem)
    load.start()
    own_count = q_ref.shape[1] // span_len
    own_first = place_ref[0] * own_count
    width = KV_HEADS * HEAD_DIM
    for own in range(own_count):
        base, pos, start, first_start = span_bounds(
            order_ref, lens_ref, span_len, spans, own_first, own
        )
        top_ref[...] = jnp.full(top_ref.shape, NEG, F32)
        sum_ref[...] = jnp.zeros(sum_ref.shape, F32)
        acc_ref[...] = jnp.zeros(acc_ref.shape, F32)
        stacked = [stack_heads(q_ref, head, own, span_len) for head in range(KV_HEADS)]

        @pl.loop(0, spans)
        def _(number):
            key_base = order_ref[number] * span_len

            @pl.when((key_base <= base) & (key_base + span_len > first_start))
            def _():
                allowed = allowed_tile(key_base, span_len, pos, start)
                rows = pl.ds(pl.multiple_of(number * span_len, span_len), span_len)
                for head in range(KV_HEADS):
                    lower = head * HEAD_DIM
                    key = kv_ref[rows, lower : lower + HEAD_DIM]
                    value = kv_ref[rows, width + lower : width + lower + HEAD_DIM]
                    scores = dot32(key, stacked[head], ((1,), (0,))) * (SCALE * LOG2E)
                    scores = jnp.where(allowed, scores, NEG)
                    old = top_ref[head : head + 1, :]
                    new = jnp.maximum(old, jnp.max(scores, axis=0, keepdims=True))
                    decay = jnp.exp2(old - new)
                    expo = jnp.exp2(scores - new)
                    top_ref[head : head + 1, :] = new
                    sum_ref[head : head + 1, :] = sum_ref[head : head + 1, :] * decay + jnp.sum(
                        expo, axis=0, keepdims=True
                    )
                    part = dot32(value, expo.astype(BF16), ((0,), (0,)))
                    acc_ref[head] = acc_ref[head] * decay + part

        for head in range(KV_HEADS):
            total = sum_ref[head : head + 1, :]
            mixed = acc_ref[head] / total
            unstack_heads(o_ref, mixed, head, own, span_len)
            lse_ref[own, head : head + 1, :] = top_ref[head : head + 1, :] + jnp.log2(total)
    o_s[...] = o_ref[...].T
    load.wait()

    def out(cols):
        middle_ref[:, cols] = x_ref[:, cols].astype(F32) + dot32(
            o_s[...], wo_s[:, cols], ((1,), (0,))
        )

    tiles(x_ref.shape[1], 256, out)
    middle = middle_ref[...]
    rms = lax.rsqrt(jnp.mean(middle * middle, axis=1, keepdims=True) + EPS)
    rms_ref[...] = rms
    f_ref[...] = (middle * rms * gain_ref[...]).astype(BF16)


def attend_backward_kernel(
    span_len,
    spans,
    place_ref,
    order_ref,
    lens_ref,
    q_ref,
    kv_ref,
    o_ref,
    lse_ref,
    gf_ref,
    middle_ref,
    rms_ref,
    gain_ref,
    g_ref,
    wo_ref,
    dq_ref,
    dkv_ref,
    grad_ref,
    gain_out,
    dkv_acc,
    dq_acc,
    delta_ref,
    ga_s,
    do_ref,
    wo_s,
    load_sem,
):
    load = pltpu.make_async_copy(wo_ref, wo_s, load_sem)
    load.start()
    rms = rms_ref[...]
    gain_out[...] = jnp.sum(gf_ref[...] * (middle_ref[...] * rms), axis=0, keepdims=True)
    scaled = gf_ref[...] * gain_ref[...]
    mean = jnp.mean(scaled * middle_ref[...], axis=1, keepdims=True)
    grad_ref[...] = g_ref[...].astype(F32) + (
        rms * scaled - middle_ref[...] * (rms * rms * rms * mean)
    )
    ga_s[...] = grad_ref[...].astype(BF16)
    load.wait()

    def grad_mix(own):
        do_ref[own, :] = dot32(wo_s[own, :], ga_s[...], ((1,), (1,))).astype(BF16)

    tiles(do_ref.shape[0], 256, grad_mix)
    own_count = q_ref.shape[1] // span_len
    own_first = place_ref[0] * own_count
    width = KV_HEADS * HEAD_DIM
    dkv_acc[...] = jnp.zeros(dkv_acc.shape, F32)
    for own in range(own_count):
        base, pos, start, first_start = span_bounds(
            order_ref, lens_ref, span_len, spans, own_first, own
        )
        dq_acc[...] = jnp.zeros(dq_acc.shape, F32)
        queries = [stack_heads(q_ref, head, own, span_len) for head in range(KV_HEADS)]
        grads = [stack_heads(do_ref, head, own, span_len) for head in range(KV_HEADS)]
        for head in range(KV_HEADS):
            mixed = stack_heads(o_ref, head, own, span_len)
            delta_ref[head : head + 1, :] = jnp.sum(
                mixed.astype(F32) * grads[head].astype(F32), axis=0, keepdims=True
            )

        @pl.loop(0, spans)
        def _(number):
            key_base = order_ref[number] * span_len

            @pl.when((key_base <= base) & (key_base + span_len > first_start))
            def _():
                allowed = allowed_tile(key_base, span_len, pos, start)
                rows = pl.ds(pl.multiple_of(number * span_len, span_len), span_len)
                for head in range(KV_HEADS):
                    lower = head * HEAD_DIM
                    key = kv_ref[rows, lower : lower + HEAD_DIM]
                    value = kv_ref[rows, width + lower : width + lower + HEAD_DIM]
                    scores = dot32(key, queries[head], ((1,), (0,))) * (SCALE * LOG2E)
                    probs = jnp.where(
                        allowed, jnp.exp2(scores - lse_ref[own, head : head + 1, :]), 0.0
                    )
                    grad_probs = dot32(value, grads[head], ((1,), (0,)))
                    grad_scores = (probs * (grad_probs - delta_ref[head : head + 1, :])).astype(BF16)
                    probs = probs.astype(BF16)
                    dq_acc[head] = dq_acc[head] + dot32(key, grad_scores, ((0,), (0,)))
                    dkv_acc[rows, lower : lower + HEAD_DIM] = (
                        dkv_acc[rows, lower : lower + HEAD_DIM]
                        + dot32(grad_scores, queries[head], ((1,), (1,))) * SCALE
                    )
                    dkv_acc[rows, width + lower : width + lower + HEAD_DIM] = dkv_acc[
                        rows, width + lower : width + lower + HEAD_DIM
                    ] + dot32(probs, grads[head], ((1,), (1,)))

        for head in range(KV_HEADS):
            unstack_heads(dq_ref, dq_acc[head] * SCALE, head, own, span_len)
    dkv_ref[...] = dkv_acc[...].astype(dkv_ref.dtype)


def smem():
    return pl.BlockSpec(memory_space=pltpu.SMEM)


def vmem():
    return pl.BlockSpec(memory_space=pltpu.VMEM)


def attend_forward(place, block_order, doc_lengths, q_t, kv, x, gain, w_out):
    spans = block_order.shape[0]
    span_len = kv.shape[0] // spans
    own_count = q_t.shape[1] // span_len
    lanes = GROUP * span_len
    rows, model = x.shape
    return pl.pallas_call(
        functools.partial(attend_forward_kernel, span_len, spans),
        out_shape=(
            jax.ShapeDtypeStruct(q_t.shape, BF16),
            jax.ShapeDtypeStruct((own_count, KV_HEADS, lanes), F32),
            jax.ShapeDtypeStruct((rows, model), F32),
            jax.ShapeDtypeStruct((rows, 1), F32),
            jax.ShapeDtypeStruct((rows, model), BF16),
        ),
        in_specs=[smem(), smem(), smem()] + [vmem()] * 4 + [pl.BlockSpec(memory_space=pl.ANY)],
        out_specs=(vmem(),) * 5,
        scratch_shapes=[
            pltpu.VMEM((KV_HEADS, lanes), F32),
            pltpu.VMEM((KV_HEADS, lanes), F32),
            pltpu.VMEM((KV_HEADS, HEAD_DIM, lanes), F32),
            pltpu.VMEM(q_t.shape[::-1], BF16),
            pltpu.VMEM(w_out.shape, BF16),
            pltpu.SemaphoreType.DMA,
        ],
        compiler_params=pltpu.CompilerParams(vmem_limit_bytes=VMEM_MOST),
        cost_estimate=pl.CostEstimate(
            flops=2 * HEADS * HEAD_DIM * kv.shape[0] * rows + 2 * w_out.size * rows,
            transcendentals=HEADS * kv.shape[0] * rows // 2,
            bytes_accessed=4 * q_t.size + 2 * kv.size + 2 * w_out.size + 8 * rows * model,
        ),
        name="attend_forward",
    )(place, block_order, doc_lengths, q_t, kv, x, gain, w_out)


def attend_backward(
    place, block_order, doc_lengths, q_t, kv, o_t, lse, grad_f, middle, rms, gain, g_own, w_out
):
    spans = block_order.shape[0]
    span_len = kv.shape[0] // spans
    lanes = GROUP * span_len
    rows, model = middle.shape
    return pl.pallas_call(
        functools.partial(attend_backward_kernel, span_len, spans),
        out_shape=(
            jax.ShapeDtypeStruct(q_t.shape, F32),
            jax.ShapeDtypeStruct(kv.shape, BF16),
            jax.ShapeDtypeStruct((rows, model), F32),
            jax.ShapeDtypeStruct((1, model), F32),
        ),
        in_specs=[smem(), smem(), smem()] + [vmem()] * 9 + [pl.BlockSpec(memory_space=pl.ANY)],
        out_specs=(vmem(),) * 4,
        scratch_shapes=[
            pltpu.VMEM(kv.shape, F32),
            pltpu.VMEM((KV_HEADS, HEAD_DIM, lanes), F32),
            pltpu.VMEM((KV_HEADS, lanes), F32),
            pltpu.VMEM((rows, model), BF16),
            pltpu.VMEM(q_t.shape, BF16),
            pltpu.VMEM(w_out.shape, BF16),
            pltpu.SemaphoreType.DMA,
        ],
        compiler_params=pltpu.CompilerParams(vmem_limit_bytes=VMEM_MOST),
        cost_estimate=pl.CostEstimate(
            flops=5 * HEADS * HEAD_DIM * kv.shape[0] * rows + 2 * w_out.size * rows,
            transcendentals=HEADS * kv.shape[0] * rows // 2,
            bytes_accessed=10 * q_t.size + 4 * kv.size + 2 * w_out.size + 14 * rows * model,
        ),
        name="attend_backward",
    )(place, block_order, doc_lengths, q_t, kv, o_t, lse, grad_f, middle, rms, gain, g_own, w_out)


MESH = pl.DeviceIdType.MESH


def coords():
    ctx = lax.axis_index("ctx")
    return lax.axis_index("seq"), ctx // 2, lax.rem(ctx, 2)


def other(place, step, count):
    return lax.rem(place + step, count)


def meet(devices):
    barrier = pltpu.get_barrier_semaphore()
    for device in devices:
        pl.semaphore_signal(barrier, inc=1, device_id=device, device_id_type=MESH)
    pl.semaphore_wait(barrier, len(devices))


def remote(source, target, send_sem, recv_sem, device):
    return pltpu.make_async_remote_copy(
        src_ref=source,
        dst_ref=target,
        send_sem=send_sem,
        recv_sem=recv_sem,
        device_id=device,
        device_id_type=MESH,
    )


def plane_slots(seq_count):
    seq = lax.axis_index("seq")
    if seq_count == 4:
        beside, above = seq + 1 - 2 * lax.rem(seq, 2), other(seq, 2, 4)
        return [seq, beside, above, 3 - seq], [0, 1, 2, 3]
    return [seq] + [other(seq, step, seq_count) for step in range(1, seq_count)], [0] + [
        seq_count - step for step in range(1, seq_count)
    ]


def spread_tools(scopes, halves, seq_count, chip_count, sources, results, sends, recvs, local_sem):
    _, chip, core = coords()
    ctx = lax.axis_index("ctx")
    ctx_count = 2 * chip_count
    slots, _ = plane_slots(seq_count)
    seq, planes = slots[0], slots[1:]
    sibling = {"ctx": chip * 2 + 1 - core}
    last = chip_count - 1
    sides = [
        (chip < last, {"ctx": lax.rem(chip + 1, chip_count) * 2 + core}),
        (chip > 0, {"ctx": lax.rem(chip + last, chip_count) * 2 + core}),
    ]
    peers = []
    if any(scope != "ctx" for scope in scopes):
        peers += [{"seq": place} for place in planes]
    if any(scope in ("ctx", "all") for scope in scopes):
        peers += [{"ctx": other(chip, step, chip_count) * 2 + core} for step in range(1, chip_count)]
        peers += [sibling]
    locals_ = {}

    def pick(items, *names):
        return [item for item in items if scopes[item] in names]

    started = []

    def part(ref, item, half):
        if half is None:
            return ref
        rows = results[item].shape[-2] // 2
        return ref.at[pl.ds(half * rows, rows)]

    def block(item, at_seq, place, at_core):
        scope = scopes[item]
        at_ctx = place * 2 + at_core
        if scope == "all":
            return results[item].at[at_seq, at_ctx], at_seq * ctx_count + at_ctx
        if scope == "ctx":
            return results[item].at[at_ctx], at_ctx
        return results[item].at[at_seq], at_seq

    def descriptor(item, at_seq, place, half, kind, device, source=None):
        target, number = block(item, at_seq, place, core)
        row = place if scopes[item] in ("ctx", "all") else 0
        return remote(
            part(target if source is None else source, item, half),
            part(target, item, half),
            sends[item].at[row, kind],
            recvs[item].at[2 * number + (half or 0)],
            device,
        )

    def arrival(item, at_seq, place, half, at_core=None):
        target, number = block(item, at_seq, place, core if at_core is None else at_core)
        view = part(target, item, half)
        return remote(
            view, view, sends[item].at[0, 0], recvs[item].at[2 * number + (half or 0)], sibling
        )

    def start(copies, there=None):
        for copy in copies:
            copy.start()
            started.append((there, copy))

    def cut(item):
        return (0, 1) if halves[item] else (None,)

    def plane_copies(item, place, half, source=None):
        if not halves[item]:
            return [
                descriptor(item, seq, place, None, 4 + number, {"seq": to}, source)
                for number, to in enumerate(planes)
            ]
        order = (1, 2) if half == 0 else (2, 1)
        return [
            descriptor(item, seq, place, half, 2 + 2 * half + to + 1, {"seq": slots[to]}, source)
            for to in order
        ]

    kinds_relay = 4 + max(4, seq_count - 1)

    def plane_relay(item, place, there=None):
        if not halves[item]:
            return
        steps = [
            (
                arrival(item, slots[give], place, half),
                descriptor(
                    item, slots[give], place, half, kinds_relay + half, {"seq": slots[3 - give]}
                ),
            )
            for give, half in ((1, 0), (2, 1))
        ]

        def run():
            for got, copy in steps:
                got.wait_recv()
                start([copy], there)

        run() if there is None else pl.when(there)(run)

    def plane_end(item, place, there=None):
        if halves[item]:
            ends = [
                (arrival(item, slots[slot], place, half))
                for slot, half in ((1, 1), (2, 0), (3, 0), (3, 1))
            ]
        else:
            ends = [arrival(item, at_seq, place, None) for at_seq in planes]
        copies = []
        if scopes[item] == "all":
            copies = [
                descriptor(item, at_seq, place, None, kinds_relay + 3 + number, sibling)
                for number, at_seq in enumerate(planes)
            ]

        def run():
            for got in ends:
                got.wait_recv()
            start(copies, there)

        run() if there is None else pl.when(there)(run)

    def pass_on(item, place, there, onward, device):
        steps = []
        for half in cut(item):
            steps.append(
                (
                    arrival(item, seq, place, half),
                    descriptor(item, seq, place, half, half or 0, device),
                    plane_copies(item, place, half) if scopes[item] == "all" else [],
                )
            )
        final = descriptor(item, seq, place, None, kinds_relay + 2, sibling)

        def run():
            for got, copy, copies in steps:
                got.wait_recv()
                pl.when(onward)(copy.start)
                start(copies, there)
            start([final], there)

        pl.when(there)(run)
        for _, copy, _ in steps:
            started.append((there & onward, copy))

    def begin(items):
        for item in items:
            target, _ = block(item, seq, chip, core)
            own = sources[item].at[seq] if scopes[item] == "swap" else sources[item]
            locals_[item] = pltpu.make_async_copy(own, target, local_sem.at[item])
            locals_[item].start()
        for item in pick(items, "ctx", "all"):
            for half in cut(item):
                for side, (there, device) in enumerate(sides):
                    copy = descriptor(
                        item, seq, chip, half, 2 * side + (half or 0), device, sources[item]
                    )
                    pl.when(there)(functools.partial(start, [copy], there))
        for item in pick(items, "swap"):
            start(
                [
                    descriptor(
                        item, seq, chip, None, number, {"seq": place}, sources[item].at[place]
                    )
                    for number, place in enumerate(planes)
                ]
            )
        for item in pick(items, "seq", "all"):
            for half in cut(item):
                start(plane_copies(item, chip, half, sources[item]))
        for item in pick(items, "ctx", "all"):
            start([descriptor(item, seq, chip, None, kinds_relay + 2, sibling, sources[item])])

    def relays(items):
        for item in pick(items, "seq", "all"):
            plane_relay(item, chip)

    def waves(items):
        lines, everywhere = pick(items, "ctx", "all"), pick(items, "all")
        done = []
        for step in range(1, chip_count):
            wave = [
                (lax.rem(chip + chip_count - step, chip_count), chip >= step, *sides[0]),
                (lax.rem(chip + step, chip_count), chip <= last - step, *sides[1]),
            ]
            for place, there, onward, device in wave:
                for item in lines:
                    pass_on(item, place, there, onward, device)
            for item in everywhere:
                for place, there, _, _ in done[-1] if done else []:
                    plane_relay(item, place, there)
            if step == 1:
                for item in pick(items, "seq", "all"):
                    plane_end(item, chip)
            elif step > 2:
                for item in everywhere:
                    for place, there, _, _ in done[-2]:
                        plane_end(item, place, there)
            done.append(wave)
        for item in everywhere:
            for place, there, _, _ in done[-1]:
                plane_relay(item, place, there)
            for wave in done[-2:]:
                for place, there, _, _ in wave:
                    plane_end(item, place, there)

    def settle(items):
        for item in pick(items, "swap"):
            for place in planes:
                arrival(item, place, chip, None).wait_recv()
        for item in pick(items, "ctx", "all"):
            for at_seq in [seq] + (planes if scopes[item] == "all" else []):
                for step in range(chip_count):
                    arrival(item, at_seq, other(chip, step, chip_count), None, 1 - core).wait_recv()
        for item in items:
            locals_[item].wait()

    def end():
        for there, copy in started:
            if there is None:
                copy.wait_send()
            else:
                pl.when(there)(copy.wait_send)

    return peers, begin, relays, waves, settle, end


def spread_sems(arrays, scopes, seq_count, chip_count):
    kinds = 4 + max(4, seq_count - 1) + 3 + seq_count - 1
    sends, recvs, halves, shapes = [], [], [], []
    for array, scope in zip(arrays, scopes):
        lead = {"all": (seq_count, 2 * chip_count), "ctx": (2 * chip_count,)}.get(scope, (seq_count,))
        halves.append(seq_count == 4 and scope in ("all", "seq") and array.shape[0] % 32 == 0)
        shape = array.shape if scope == "swap" else lead + array.shape
        shapes.append(jax.ShapeDtypeStruct(shape, array.dtype))
        rows = chip_count if scope in ("all", "ctx") else 1
        sends.append(pltpu.SemaphoreType.DMA((rows, kinds)))
        recvs.append(pltpu.SemaphoreType.DMA((2 * math.prod(lead),)))
    return shapes, tuple(halves), sends + recvs + [pltpu.SemaphoreType.DMA((len(arrays),))]


def swap_kernel(scopes, halves, seq_count, chip_count, *refs):
    count = len(scopes)
    peers, begin, _, _, settle, end = spread_tools(
        scopes,
        halves,
        seq_count,
        chip_count,
        refs[:count],
        refs[count : 2 * count],
        refs[2 * count : 3 * count],
        refs[3 * count : 4 * count],
        refs[4 * count],
    )
    meet(peers)
    begin(range(count))
    settle(range(count))
    end()


def swap(collective_id, arrays):
    seq_count, chip_count = lax.axis_size("seq"), lax.axis_size("ctx") // 2
    scopes = ("swap",) * len(arrays)
    shapes, halves, sems = spread_sems(arrays, scopes, seq_count, chip_count)
    anywhere = pl.BlockSpec(memory_space=pl.ANY)
    return pl.pallas_call(
        functools.partial(swap_kernel, scopes, halves, seq_count, chip_count),
        out_shape=tuple(shapes),
        in_specs=[anywhere] * len(arrays),
        out_specs=(anywhere,) * len(arrays),
        scratch_shapes=sems,
        compiler_params=pltpu.CompilerParams(collective_id=collective_id, has_side_effects=True),
        cost_estimate=pl.CostEstimate(
            flops=0, transcendentals=0, bytes_accessed=20 * 3_000_000
        ),
        name="swap",
    )(*arrays)


FOLD_SCRATCH = 9
WINDOW = 4


def fold_kernel(kinds, chunk_counts, swap_count, work, seq_count, chip_count, *refs):
    count = len(kinds)
    every = count + swap_count
    sources, swap_sources = refs[:count], refs[count:every]
    extra_in, extra_out = (work[0], work[1]) if work else (0, 0)
    first_out = every + extra_in
    results = refs[first_out : first_out + count]
    swap_results = refs[first_out + count : first_out + every]
    first_rest = first_out + every + extra_out
    rest = refs[first_rest:]
    swap_rest = rest[count * FOLD_SCRATCH : count * FOLD_SCRATCH + 4 * swap_count]
    extra = (
        refs[every:first_out],
        refs[first_out + every : first_rest],
        rest[count * FOLD_SCRATCH + 4 * swap_count :],
    )
    seq, chip, core = coords()
    slots, there = plane_slots(seq_count)
    planes = slots[1:]
    chips = [other(chip, step, chip_count) for step in range(1, chip_count)]
    sibling = {"ctx": chip * 2 + 1 - core}
    peers = []
    if any(kind != "seq" for kind in kinds):
        peers += [{"ctx": place * 2 + core} for place in chips] + [sibling]
    if swap_count or any(kind != "ctx" for kind in kinds):
        peers += [{"seq": place} for place in planes]

    def scratch(item):
        return rest[item * FOLD_SCRATCH : (item + 1) * FOLD_SCRATCH]

    def columns(item, chunk):
        width = sources[item].shape[-1] // chunk_counts[item]
        return slice(chunk * width, (chunk + 1) * width)

    order = []
    for chunk in range(max(chunk_counts, default=0)):
        order += [(item, chunk) for item in range(count) if chunk < chunk_counts[item]]

    loads = []
    for item in range(count):
        mine, sem_s = scratch(item)[0], scratch(item)[7]
        if kinds[item] != "seq":
            load = pltpu.make_async_copy(
                sources[item].at[:, :, core], mine, sem_s.at[4, 0, 0]
            )
            load.start()
            loads.append(load)
    meet(peers)

    waits = []

    def go(source, target, send_sem, recv_sem, device):
        copy = remote(source, target, send_sem, recv_sem, device)
        copy.start()
        waits.append(copy)
        return copy

    firsts = {}
    for item, chunk in order:
        if kinds[item] != "seq":
            _, got1, _, _, _, _, _, sem_s, sem_r = scratch(item)
            cols = columns(item, chunk)
            firsts[item, chunk] = go(
                sources[item].at[:, :, 1 - core, :, cols],
                got1.at[:, :, :, cols],
                sem_s.at[0, chunk, 0],
                sem_r.at[0, chunk, 0],
                sibling,
            )
    swapped = []
    for item in range(swap_count):
        got, sem_s, sem_r, sem_own = swap_rest[4 * item : 4 * item + 4]
        own = pltpu.make_async_copy(swap_sources[item].at[seq], got.at[seq], sem_own)
        own.start()
        swapped.append(own)
        for step, place in enumerate(planes):
            go(swap_sources[item].at[place], got.at[seq], sem_s.at[step], sem_r.at[seq], {"seq": place})
    for load in loads:
        load.wait()

    def block(item, slot, cols):
        if kinds[item] == "seq":
            return sources[item][slot, :, cols].astype(F32)[None]
        mine, got1 = scratch(item)[:2]
        place = slots[slot] if kinds[item] == "all" else 0
        return mine[place, :, :, cols].astype(F32) + got1[place, :, :, cols].astype(F32)

    def turn(item, chunk):
        return (1, 2) if (item + chunk) % 2 == 0 else (2, 1)

    seconds = {}

    def plane_first(item, chunk):
        _, got1, _, got2, keep, _, _, sem_s, sem_r = scratch(item)
        cols = columns(item, chunk)
        if kinds[item] == "all":
            firsts[item, chunk].wait_recv()
        first, _ = turn(item, chunk)
        targets = [(slot, slot) for slot in range(1, seq_count)]
        if seq_count == 4:
            targets = [(3, first), (first, first)]
        row = []
        for number, (slot, to) in enumerate(targets):
            if kinds[item] == "all":
                held = got1.at[slots[slot], :, :, cols]
                held[...] = block(item, slot, cols).astype(BF16)
            else:
                held = sources[item].at[pl.ds(slot, 1), :, cols]
            index = number if seq_count == 4 else there[slot] - 1
            row.append(
                go(
                    held,
                    got2.at[index, :, :, cols],
                    sem_s.at[1, chunk, number],
                    sem_r.at[1, chunk, index],
                    {"seq": slots[to]},
                )
            )
        seconds[item, chunk] = row
        keep[:, :, cols] = block(item, 0, cols)

    def plane_second(item, chunk):
        if seq_count != 4:
            return
        _, got1, spare, got2, keep, _, _, sem_s, sem_r = scratch(item)
        cols = columns(item, chunk)
        _, second = turn(item, chunk)
        across, mine = seconds[item, chunk]
        across.wait_recv()
        if kinds[item] == "all":
            held = got1.at[slots[second], :, :, cols]
        else:
            held = spare.at[:, :, cols]
        held[...] = (block(item, second, cols) + got2[0, :, :, cols].astype(F32)).astype(BF16)
        last = go(
            held,
            got2.at[2, :, :, cols],
            sem_s.at[2, chunk, 0],
            sem_r.at[2, chunk, 0],
            {"seq": slots[second]},
        )
        mine.wait_recv()
        keep[:, :, cols] = keep[:, :, cols] + got2[1, :, :, cols].astype(F32)
        seconds[item, chunk] = [last]

    thirds = {}

    def line(item, chunk):
        _, _, _, got2, keep, pass3, got3, sem_s, sem_r = scratch(item)
        cols = columns(item, chunk)
        if kinds[item] == "ctx":
            firsts[item, chunk].wait_recv()
            keep[:, :, cols] = block(item, 0, cols)
        else:
            for copy in seconds[item, chunk]:
                copy.wait_recv()

        def total(place):
            value = keep[place, :, cols]
            if kinds[item] != "ctx":
                for index in (2,) if seq_count == 4 else range(seq_count - 1):
                    value = value + got2[index, place, :, cols].astype(F32)
            return value

        if kinds[item] == "seq":
            results[item][:, cols] = total(0)
            return
        row = []
        for step, place in enumerate(chips):
            pass3[step, :, cols] = total(place).astype(BF16)
            row.append(
                go(
                    pass3.at[step, :, cols],
                    got3.at[step, :, cols],
                    sem_s.at[3, chunk, step],
                    sem_r.at[3, chunk, step],
                    {"ctx": place * 2 + core},
                )
            )
        results[item][:, cols] = total(chip)
        thirds[item, chunk] = row

    lines = [step for step in order if kinds[step[0]] == "ctx"]
    everywhere = [step for step in order if kinds[step[0]] == "all"]
    flats = [step for step in order if kinds[step[0]] == "seq"]
    for step in lines:
        line(*step)
    for step in everywhere[:WINDOW]:
        plane_first(*step)
    for number, step in enumerate(everywhere):
        plane_second(*step)
        for later in everywhere[number + WINDOW : number + WINDOW + 1]:
            plane_first(*later)
        if number:
            line(*everywhere[number - 1])
    for step in flats:
        plane_first(*step)
    if work:
        work[2](*extra)
    for step in everywhere[-1:]:
        line(*step)
    for step in flats:
        plane_second(*step)
    for step in flats:
        line(*step)
    for item, chunk in lines + everywhere:
        got3 = scratch(item)[6]
        cols = columns(item, chunk)
        for copy in thirds[item, chunk]:
            copy.wait_recv()
        value = results[item][:, cols]
        for step in range(chip_count - 1):
            value = value + got3[step, :, cols].astype(F32)
        results[item][:, cols] = value
    if work:
        work[3](results[0], *extra)
    for item in range(swap_count):
        got, sem_s, sem_r, _ = swap_rest[4 * item : 4 * item + 4]
        swapped[item].wait()
        for place in planes:
            remote(got.at[place], got.at[place], sem_s.at[0], sem_r.at[place], sibling).wait_recv()
        width = got.shape[-1]
        for place in range(seq_count):
            swap_results[item][:, place * width : (place + 1) * width] = got[place].astype(F32)
    for copy in waits:
        copy.wait_send()


def fold(name, collective_id, arrays, kinds, chunk_counts, micros, swaps=(), work=None):
    seq_count, ctx_count = lax.axis_size("seq"), lax.axis_size("ctx")
    chip_count = ctx_count // 2
    inputs, shapes, scratch, in_specs = [], [], [], []
    small = (1, 1, 8, 128)
    dma = pltpu.SemaphoreType.DMA
    for array, kind, chunks in zip(arrays, kinds, chunk_counts):
        parts = 1 if kind == "ctx" else seq_count
        blocks = seq_count if kind == "seq" else parts * ctx_count
        rows, cols = array.shape[0] // blocks, array.shape[1]
        lines = 1 if kind == "seq" else chip_count
        if kind == "seq":
            inputs.append(array.reshape(seq_count, rows, cols))
            in_specs.append(vmem())
            got1, spare = small, (1, rows, cols)
        else:
            inputs.append(array.reshape(parts, chip_count, 2, rows, cols))
            in_specs.append(pl.BlockSpec(memory_space=pl.ANY))
            got1, spare = (parts, chip_count, rows, cols), small[1:]
        shapes.append(jax.ShapeDtypeStruct((rows, cols), F32))
        got2 = small if kind == "ctx" else (seq_count - 1, lines, rows, cols)
        got3 = small[1:] if kind == "seq" else (chip_count - 1, rows, cols)
        most = max(seq_count, chip_count)
        scratch += [
            pltpu.VMEM(got1, BF16),
            pltpu.VMEM(got1, BF16),
            pltpu.VMEM(spare, BF16),
            pltpu.VMEM(got2, BF16),
            pltpu.VMEM((lines, rows, cols), F32),
            pltpu.VMEM(got3, BF16),
            pltpu.VMEM(got3, BF16),
            dma((5, chunks, most)),
            dma((4, chunks, most)),
        ]
    for array in swaps:
        inputs.append(array)
        in_specs.append(pl.BlockSpec(memory_space=pl.ANY))
        shapes.append(jax.ShapeDtypeStruct((array.shape[1], seq_count * array.shape[2]), F32))
        scratch += [
            pltpu.VMEM(array.shape, BF16),
            dma((seq_count - 1,)),
            dma((seq_count,)),
            dma,
        ]
    out_specs = [vmem()] * len(inputs)
    does = None
    if work:
        does = (len(work["inputs"]), len(work["shapes"]), work["during"], work["after"])
        inputs += work["inputs"]
        in_specs += work["in_specs"]
        shapes += work["shapes"]
        out_specs += work["out_specs"]
        scratch += work["scratch"]
    return pl.pallas_call(
        functools.partial(
            fold_kernel, tuple(kinds), tuple(chunk_counts), len(swaps), does, seq_count, chip_count
        ),
        out_shape=tuple(shapes),
        in_specs=in_specs,
        out_specs=tuple(out_specs),
        scratch_shapes=scratch,
        compiler_params=pltpu.CompilerParams(
            collective_id=collective_id, has_side_effects=True, vmem_limit_bytes=VMEM_MOST
        ),
        cost_estimate=pl.CostEstimate(
            flops=0, transcendentals=0, bytes_accessed=int(micros * 3_000_000)
        ),
        name=name,
    )(*inputs)


def tiles(extent, width, visit, first=0):
    whole = extent // width

    @pl.loop(first, whole)
    def _(number):
        visit(pl.ds(pl.multiple_of(number * width, width), width))

    if extent % width:
        visit(pl.ds(whole * width, extent % width))


def stream_rows(extent, width, produce, stage, sem, target):
    whole = extent // width

    def leave(slot, rows, size):
        return pltpu.make_async_copy(
            stage.at[slot, pl.ds(0, size)], target.at[rows], sem.at[slot]
        )

    @pl.loop(0, whole)
    def _(number):
        slot = lax.rem(number, 2)
        rows = pl.ds(pl.multiple_of(number * width, width), width)

        @pl.when(number >= 2)
        def _():
            leave(slot, rows, width).wait()

        stage[slot] = produce(rows).astype(stage.dtype)
        leave(slot, rows, width).start()

    for number in range(max(0, whole - 2), whole):
        leave(number % 2, pl.ds(number * width, width), width).wait()
    if extent % width:
        size = extent % width
        rows = pl.ds(whole * width, size)
        stage[0, :size] = produce(rows).astype(stage.dtype)
        leave(0, rows, size).start()
        leave(0, rows, size).wait()


def ffn_first_kernel(
    seq_count, f_ref, g_ref, wg_ref, wd_ref, f_out, g_out, gate_ref, gh_ref, f_s, g_s, wg, wd, in_sem, f_send, f_recv, out_sem
):
    rows = f_ref.shape[0]
    width = wg.shape[1]
    places, there = plane_slots(seq_count)
    load_f = pltpu.make_async_copy(f_ref, f_s.at[pl.ds(0, rows)], in_sem.at[seq_count])
    load_wd = pltpu.make_async_copy(wd_ref, wd, in_sem.at[seq_count + 1])
    load_wg = pltpu.make_async_copy(wg_ref, wg, in_sem.at[seq_count + 2])
    loads = [load_wd]
    for slot in range(seq_count):
        loads.append(
            pltpu.make_async_copy(
                g_ref.at[places[slot]], g_s.at[pl.ds(slot * rows, rows)], in_sem.at[slot]
            )
        )
    for load in [*loads, load_f, load_wg]:
        load.start()
    meet([{"seq": place} for place in places[1:]])

    started = []

    def f_block(slot, half):
        if half is None:
            return f_s.at[pl.ds(slot * rows, rows)]
        return f_s.at[pl.ds(slot * rows + half * (rows // 2), rows // 2)]

    def f_copy(source, to, slot, half):
        copy = remote(
            source,
            f_block(slot, half),
            f_send.at[len(started)],
            f_recv.at[slot, half or 0],
            {"seq": places[to]},
        )
        copy.start()
        started.append(copy)

    def f_arrive(slot, half):
        block = f_block(slot, half)
        remote(
            block, block, f_send.at[0], f_recv.at[slot, half or 0], {"seq": places[1]}
        ).wait_recv()

    if seq_count == 4:
        for half in (0, 1):
            source = f_ref.at[pl.ds(half * (rows // 2), rows // 2)]
            for to in (1, 2) if half == 0 else (2, 1):
                f_copy(source, to, to, half)
    else:
        for to in range(1, seq_count):
            f_copy(f_ref, to, there[to], None)

    def gate_rows(first, count):
        own = slice(first, first + count)

        def visit(cols):
            gate_ref[own, cols] = dot32(f_s[own, :], wg[:, cols], ((1,), (0,)))

        tiles(width, 256, visit)

    for load in loads:
        load.wait()
    leave_g = pltpu.make_async_copy(g_s, g_out, out_sem.at[1])
    leave_g.start()

    def grad_hidden(cols):
        gh_ref[:, cols] = dot32(g_s[...], wd[cols, :], ((1,), (1,))).astype(gh_ref.dtype)

    tiles(width, 256, grad_hidden)
    for load in (load_f, load_wg):
        load.wait()
    gate_rows(0, rows)
    if seq_count == 4:
        f_arrive(1, 0)
        f_copy(f_block(1, 0), 2, 3, 0)
        f_arrive(2, 1)
        f_copy(f_block(2, 1), 1, 3, 1)
        f_arrive(1, 1)
        f_arrive(2, 0)
        gate_rows(rows, 2 * rows)
        f_arrive(3, 0)
        f_arrive(3, 1)
        leave = pltpu.make_async_copy(f_s, f_out, out_sem.at[0])
        leave.start()
        gate_rows(3 * rows, rows)
    else:
        for slot in range(1, seq_count):
            f_arrive(slot, None)
        leave = pltpu.make_async_copy(f_s, f_out, out_sem.at[0])
        leave.start()
        gate_rows(rows, (seq_count - 1) * rows)
    leave.wait()
    leave_g.wait()
    for copy in started:
        copy.wait_send()


def ffn_act_kernel(
    f_ref, gate_ref, gh_ref, wu_ref, hid, gg, gu, pg_ref, f_s, gate_s, gh_s, wu, stage_f, in_sem, leave_sem
):
    model, width = wu.shape
    loads = [
        pltpu.make_async_copy(source, target, in_sem.at[number])
        for number, (source, target) in enumerate(
            [(f_ref, f_s), (wu_ref, wu), (gate_ref, gate_s), (gh_ref, gh_s)]
        )
    ]
    for load in loads:
        load.start()
    for load in loads[:2]:
        load.wait()

    def act(cols, ready=None):
        up_val = dot32(f_s[...], wu[:, cols], ((1,), (0,)))
        if ready is not None:
            ready()
        gate = gate_s[:, cols]
        grad = gh_s[:, cols].astype(F32)
        sigma = jax.nn.sigmoid(gate)
        activated = gate * sigma
        hid[:, cols] = (activated * up_val).astype(BF16)
        gg[:, cols] = (grad * up_val * (sigma + activated * (1.0 - sigma))).astype(BF16)
        gu[:, cols] = (grad * activated).astype(BF16)

    def ready():
        for load in loads[2:]:
            load.wait()

    act(pl.ds(0, 256), ready)
    tiles(width, 256, act, 1)
    stream_rows(
        model,
        256,
        lambda own: dot32(f_s[:, own], gg[...], ((0,), (0,))),
        stage_f,
        leave_sem,
        pg_ref,
    )


def ffn_grad_kernel(
    seq_count,
    f_ref,
    hid_ref,
    gg_ref,
    gu_ref,
    g_ref,
    wg_ref,
    wu_ref,
    wd_ref,
    gf_ref,
    out_ref,
    pu_ref,
    pd_ref,
    f_s,
    g_s,
    hid,
    gg,
    gu,
    wg,
    wu,
    wd,
    parts,
    got,
    stage_f,
    stage_d,
    in_sem,
    x_send,
    x_recv,
    leave_sem,
):
    rows = gf_ref.shape[0]
    model, width = wg.shape
    places, there = plane_slots(seq_count)
    loads = [
        pltpu.make_async_copy(source, target, in_sem.at[number])
        for number, (source, target) in enumerate(
            [
                (gg_ref, gg),
                (gu_ref, gu),
                (wg_ref, wg),
                (wu_ref, wu),
                (f_ref, f_s),
                (hid_ref, hid),
                (g_ref, g_s),
                (wd_ref, wd),
            ]
        )
    ]
    for load in loads[:4]:
        load.start()
    meet([{"seq": place} for place in places[1:]])
    for load in loads[:4]:
        load.wait()
    for load in loads[4:]:
        load.start()

    def part_copy(slot, cols):
        return remote(
            parts.at[pl.ds((slot - 1) * rows, rows), cols],
            got.at[there[slot] - 1, :, cols],
            x_send.at[slot],
            x_recv.at[there[slot]],
            {"seq": places[slot]},
        )

    def grad_f(cols):
        part = dot32(gg[...], wg[cols, :], ((1,), (1,))) + dot32(gu[...], wu[cols, :], ((1,), (1,)))
        gf_ref[:, cols] = part[:rows]
        parts[:, cols] = part[rows:].astype(BF16)
        for slot in range(1, seq_count):
            part_copy(slot, cols).start()

    tiles(model, 256, grad_f)
    for load in loads[4:]:
        load.wait()
    stream_rows(
        model,
        256,
        lambda own: dot32(f_s[:, own], gu[...], ((0,), (0,))),
        stage_f,
        leave_sem.at[0],
        pu_ref,
    )
    stream_rows(
        width,
        256,
        lambda own: dot32(hid[:, own], g_s[...], ((0,), (0,))),
        stage_d,
        leave_sem.at[2],
        pd_ref,
    )

    def out_copy(cols):
        return pltpu.make_async_copy(f_s.at[:, cols], out_ref.at[:, cols], leave_sem.at[1, 0])

    def out_part(cols):
        f_s[:, cols] = dot32(hid[...], wd[:, cols], ((1,), (0,))).astype(BF16)
        out_copy(cols).start()

    tiles(model, 256, out_part)
    everything = pl.ds(0, model)
    out_copy(everything).wait()
    for slot in range(1, seq_count):
        part_copy(slot, everything).wait_recv()
    total = gf_ref[...]
    for slot in range(seq_count - 1):
        total = total + got[slot].astype(F32)
    gf_ref[...] = total
    for slot in range(1, seq_count):
        part_copy(slot, everything).wait_send()


def ffn_first(collective_id, f_norm, g_all, w_gate, w_down):
    seq_count = lax.axis_size("seq")
    rows, model = f_norm.shape
    width = w_gate.shape[1]
    count = seq_count * rows
    anywhere = pl.BlockSpec(memory_space=pl.ANY)
    dma = pltpu.SemaphoreType.DMA
    return pl.pallas_call(
        functools.partial(ffn_first_kernel, seq_count),
        out_shape=(
            jax.ShapeDtypeStruct((count, model), BF16),
            jax.ShapeDtypeStruct((count, model), BF16),
            jax.ShapeDtypeStruct((count, width), F32),
            jax.ShapeDtypeStruct((count, width), BF16),
        ),
        in_specs=[anywhere] * 4,
        out_specs=(anywhere, anywhere, vmem(), vmem()),
        scratch_shapes=[
            pltpu.VMEM((count, model), BF16),
            pltpu.VMEM((count, model), BF16),
            pltpu.VMEM((model, width), BF16),
            pltpu.VMEM((width, model), BF16),
            dma((seq_count + 3,)),
            dma((max(6, seq_count),)),
            dma((seq_count, 2)),
            dma((2,)),
        ],
        compiler_params=pltpu.CompilerParams(
            collective_id=collective_id, has_side_effects=True, vmem_limit_bytes=VMEM_MOST
        ),
        cost_estimate=pl.CostEstimate(
            flops=8 * count * model * width,
            transcendentals=0,
            bytes_accessed=4 * (2 * width * model + 3 * count * model),
        ),
        name="ffn_first",
    )(f_norm, g_all.reshape(seq_count, rows, model), w_gate, w_down)


def ffn_act(f_all, gate, grad_hidden, w_up):
    count, model = f_all.shape
    width = w_up.shape[1]
    anywhere = pl.BlockSpec(memory_space=pl.ANY)
    dma = pltpu.SemaphoreType.DMA
    return pl.pallas_call(
        ffn_act_kernel,
        out_shape=(
            jax.ShapeDtypeStruct((count, width), BF16),
            jax.ShapeDtypeStruct((count, width), BF16),
            jax.ShapeDtypeStruct((count, width), BF16),
            jax.ShapeDtypeStruct((model, width), BF16),
        ),
        in_specs=[anywhere] * 4,
        out_specs=(vmem(), vmem(), vmem(), anywhere),
        scratch_shapes=[
            pltpu.VMEM((count, model), BF16),
            pltpu.VMEM((count, width), F32),
            pltpu.VMEM((count, width), BF16),
            pltpu.VMEM((model, width), BF16),
            pltpu.VMEM((2, 256, width), BF16),
            dma((4,)),
            dma((2,)),
        ],
        compiler_params=pltpu.CompilerParams(vmem_limit_bytes=VMEM_MOST),
        cost_estimate=pl.CostEstimate(
            flops=4 * count * model * width,
            transcendentals=count * width,
            bytes_accessed=4 * (width * model + 2 * count * model + 3 * count * width),
        ),
        name="ffn_act",
    )(f_all, gate, grad_hidden, w_up)


def ffn_grad(collective_id, rows, f_all, hidden_act, grad_gate, grad_up, g_all, w_gate, w_up, w_down):
    seq_count = lax.axis_size("seq")
    count, model = f_all.shape
    width = w_gate.shape[1]
    anywhere = pl.BlockSpec(memory_space=pl.ANY)
    dma = pltpu.SemaphoreType.DMA
    return pl.pallas_call(
        functools.partial(ffn_grad_kernel, seq_count),
        out_shape=(
            jax.ShapeDtypeStruct((rows, model), F32),
            jax.ShapeDtypeStruct((count, model), BF16),
            jax.ShapeDtypeStruct((model, width), BF16),
            jax.ShapeDtypeStruct((width, model), BF16),
        ),
        in_specs=[anywhere] * 8,
        out_specs=(vmem(), anywhere, anywhere, anywhere),
        scratch_shapes=[
            pltpu.VMEM((count, model), BF16),
            pltpu.VMEM((count, model), BF16),
            pltpu.VMEM((count, width), BF16),
            pltpu.VMEM((count, width), BF16),
            pltpu.VMEM((count, width), BF16),
            pltpu.VMEM((model, width), BF16),
            pltpu.VMEM((model, width), BF16),
            pltpu.VMEM((width, model), BF16),
            pltpu.VMEM((count - rows, model), BF16),
            pltpu.VMEM((seq_count - 1, rows, model), BF16),
            pltpu.VMEM((2, 256, width), BF16),
            pltpu.VMEM((2, 256, model), BF16),
            dma((8,)),
            dma((seq_count,)),
            dma((seq_count,)),
            dma((3, 2)),
        ],
        compiler_params=pltpu.CompilerParams(
            collective_id=collective_id, has_side_effects=True, vmem_limit_bytes=VMEM_MOST
        ),
        cost_estimate=pl.CostEstimate(
            flops=14 * count * model * width,
            transcendentals=0,
            bytes_accessed=4 * (3 * width * model + 3 * count * model),
        ),
        name="ffn_grad",
    )(f_all, hidden_act, grad_gate, grad_up, g_all, w_gate, w_up, w_down)


def half_turn(value):
    half = HEAD_DIM // 2
    return jnp.concatenate([-value[half:], value[:half]], axis=0)


GATHER_SCOPES = ("all", "all", "ctx", "all", "seq")


def project_kernel(
    halves,
    seq_count,
    chip_count,
    gain_src,
    w_src,
    wo_src,
    g_src,
    x_ref,
    cos_ref,
    sin_ref,
    gains_ref,
    w_ref,
    kv_ref,
    wo_ref,
    g_ref,
    normed_ref,
    rms_ref,
    q_ref,
    gain_a_ref,
    gain_f_ref,
    kv_own,
    w_s,
    gains_s,
    load_sem,
    *sems,
):
    tile = KV_HEADS * HEAD_DIM
    model, own_rows, width = x_ref.shape[1], w_src.shape[0], w_src.shape[1]
    count = width // tile
    peers, begin, relays, waves, settle, end = spread_tools(
        GATHER_SCOPES,
        halves,
        seq_count,
        chip_count,
        (gain_src, w_src, kv_own, wo_src, g_src),
        (gains_ref, w_ref, kv_ref, wo_ref, g_ref),
        sems[:5],
        sems[5:10],
        sems[10],
    )
    meet(peers)
    begin((0, 1))
    x = x_ref[...].astype(F32)
    rms = lax.rsqrt(jnp.mean(x * x, axis=1, keepdims=True) + EPS)
    rms_ref[...] = rms
    relays((0, 1))
    waves((0, 1))
    begin((3, 4))
    settle((0, 1))

    def load(number):
        cols = pl.ds(pl.multiple_of(number * tile, tile), tile)
        return pltpu.make_async_copy(
            w_ref.at[:, :, :, cols], w_s.at[:, :, :, cols], load_sem.at[number]
        )

    load_gains = pltpu.make_async_copy(gains_ref, gains_s, load_sem.at[count])
    load_gains.start()
    for number in range(count):
        load(number).start()
    load_gains.wait()
    for number in range(seq_count * 2 * chip_count):
        at_seq, at_ctx = divmod(number, 2 * chip_count)
        row = gains_s[at_seq, at_ctx, 0:1, :].astype(F32)
        own = slice(number * own_rows, (number + 1) * own_rows)
        gain_a_ref[:, own] = row[:, :own_rows]
        gain_f_ref[:, own] = row[:, own_rows : 2 * own_rows]
    normed_ref[...] = (x_ref[...].astype(F32) * rms_ref[...] * gain_a_ref[...]).astype(BF16)

    def product(number):
        load(number).wait()
        cols = pl.ds(pl.multiple_of(number * tile, tile), tile)
        return dot32(normed_ref[...], w_s[:, :, :, cols].reshape(model, tile), ((1,), (0,)))

    def rotated(value):
        turned = value.T
        pieces = []
        for head in range(tile // HEAD_DIM):
            one = turned[head * HEAD_DIM : (head + 1) * HEAD_DIM]
            pieces.append(one * cos_ref[...] + half_turn(one) * sin_ref[...])
        return jnp.concatenate(pieces, axis=0)

    kv_own[:, :tile] = rotated(product(count - 2)).T.astype(BF16)
    kv_own[:, tile:] = product(count - 1).astype(BF16)
    begin((2,))
    relays((3, 4))

    @pl.loop(0, count - 2)
    def _(number):
        own = pl.ds(pl.multiple_of(number * tile, tile), tile)
        q_ref[own, :] = rotated(product(number)).astype(BF16)

    waves((3, 4))
    waves((2,))
    settle((3, 4, 2))
    end()


def project(collective_id, gain_row, w_qkv, w_out, g_own, x, cosine, sine):
    seq_count, ctx_count = lax.axis_size("seq"), lax.axis_size("ctx")
    chip_count = ctx_count // 2
    rows, model = x.shape
    width = w_qkv.shape[1]
    tile = KV_HEADS * HEAD_DIM
    kv_like = jax.ShapeDtypeStruct((rows, 2 * tile), BF16)
    shapes, halves, sems = spread_sems(
        [gain_row, w_qkv, kv_like, w_out, g_own], GATHER_SCOPES, seq_count, chip_count
    )
    anywhere = pl.BlockSpec(memory_space=pl.ANY)
    return pl.pallas_call(
        functools.partial(project_kernel, halves, seq_count, chip_count),
        out_shape=(
            *shapes,
            jax.ShapeDtypeStruct((rows, model), BF16),
            jax.ShapeDtypeStruct((rows, 1), F32),
            jax.ShapeDtypeStruct((width - 2 * tile, rows), BF16),
            jax.ShapeDtypeStruct((1, model), F32),
            jax.ShapeDtypeStruct((1, model), F32),
        ),
        in_specs=[anywhere] * 4 + [vmem()] * 3,
        out_specs=(anywhere,) * 5 + (vmem(),) * 5,
        scratch_shapes=[
            pltpu.VMEM((rows, 2 * tile), BF16),
            pltpu.VMEM(shapes[1].shape, BF16),
            pltpu.VMEM(shapes[0].shape, BF16),
            pltpu.SemaphoreType.DMA((width // tile + 1,)),
            *sems,
        ],
        compiler_params=pltpu.CompilerParams(
            collective_id=collective_id, has_side_effects=True, vmem_limit_bytes=VMEM_MOST
        ),
        cost_estimate=pl.CostEstimate(
            flops=0, transcendentals=0, bytes_accessed=140 * 3_000_000
        ),
        name="project",
    )(gain_row, w_qkv, w_out, g_own, x, cosine, sine)


def rotated_back(value, cos_ref, sin_ref):
    pieces = []
    for head in range(value.shape[0] // HEAD_DIM):
        one = value[head * HEAD_DIM : (head + 1) * HEAD_DIM]
        pieces.append(one * cos_ref[...] - half_turn(one * sin_ref[...]))
    return jnp.concatenate(pieces, axis=0).T.astype(BF16)


def back_during(inputs, outputs, scratch):
    dq_ref, o_ref, cos_ref, sin_ref, normed_ref, x_ref, rms_ref, gain_ref, grad_ref, w_ref = inputs
    part_out, part_query, part_kv, out_ref, gain_out = outputs
    w_s, g_s, gx_s, ga_s, stage, stage_kv, load_sem, leave_sem = scratch
    tile = KV_HEADS * HEAD_DIM
    q_width = dq_ref.shape[0]
    model = x_ref.shape[1]
    pltpu.make_async_copy(w_ref, w_s, load_sem).start()
    ga_s[...] = grad_ref[...].astype(BF16)
    stream_rows(
        q_width,
        256,
        lambda own: dot32(o_ref[own, :], ga_s[...], ((1,), (0,))),
        stage,
        leave_sem,
        part_out,
    )

    @pl.loop(0, q_width // tile)
    def _(number):
        own = pl.ds(pl.multiple_of(number * tile, tile), tile)
        g_s[:, own] = rotated_back(dq_ref[own, :], cos_ref, sin_ref)

    stream_rows(
        model,
        256,
        lambda own: dot32(normed_ref[:, own], g_s[:, :q_width], ((0,), (0,))),
        stage,
        leave_sem,
        part_query,
    )
    pltpu.make_async_copy(w_ref, w_s, load_sem).wait()

    def grad_x(cols):
        gx_s[:, cols] = dot32(g_s[:, :q_width], w_s[cols, :q_width], ((1,), (1,)))

    tiles(model, 256, grad_x)


def back_after(dkv_ref, inputs, outputs, scratch):
    dq_ref, o_ref, cos_ref, sin_ref, normed_ref, x_ref, rms_ref, gain_ref, grad_ref, w_ref = inputs
    part_out, part_query, part_kv, out_ref, gain_out = outputs
    w_s, g_s, gx_s, ga_s, stage, stage_kv, load_sem, leave_sem = scratch
    tile = KV_HEADS * HEAD_DIM
    q_width = dq_ref.shape[0]
    model = x_ref.shape[1]
    g_s[:, q_width : q_width + tile] = rotated_back(dkv_ref[:, :tile].T, cos_ref, sin_ref)
    g_s[:, q_width + tile :] = dkv_ref[:, tile:].astype(BF16)
    stream_rows(
        model,
        256,
        lambda own: dot32(normed_ref[:, own], g_s[:, q_width:], ((0,), (0,))),
        stage_kv,
        leave_sem,
        part_kv,
    )

    def grad_x(cols):
        gx_s[:, cols] = gx_s[:, cols] + dot32(g_s[:, q_width:], w_s[cols, q_width:], ((1,), (1,)))

    tiles(model, 256, grad_x)
    x = x_ref[...].astype(F32)
    rms = rms_ref[...]
    gain_out[...] = jnp.sum(gx_s[...] * (x * rms), axis=0, keepdims=True)
    scaled = gx_s[...] * gain_ref[...]
    mean = jnp.mean(scaled * x, axis=1, keepdims=True)
    out_ref[...] = grad_ref[...] + (rms * scaled - x * (rms * rms * rms * mean))


def back_work(dq_t, o_t, cosine, sine, normed, x, rms, gain, grad, w_qkv):
    rows, model = x.shape
    width = w_qkv.shape[1]
    q_width = dq_t.shape[0]
    anywhere = pl.BlockSpec(memory_space=pl.ANY)
    return {
        "inputs": [dq_t, o_t, cosine, sine, normed, x, rms, gain, grad, w_qkv],
        "in_specs": [vmem()] * 9 + [anywhere],
        "shapes": [
            jax.ShapeDtypeStruct((q_width, model), BF16),
            jax.ShapeDtypeStruct((model, q_width), BF16),
            jax.ShapeDtypeStruct((model, width - q_width), BF16),
            jax.ShapeDtypeStruct((rows, model), F32),
            jax.ShapeDtypeStruct((1, model), F32),
        ],
        "out_specs": [anywhere, anywhere, anywhere, vmem(), vmem()],
        "scratch": [
            pltpu.VMEM(w_qkv.shape, BF16),
            pltpu.VMEM((rows, width), BF16),
            pltpu.VMEM((rows, model), F32),
            pltpu.VMEM((rows, model), BF16),
            pltpu.VMEM((2, 256, max(model, q_width)), BF16),
            pltpu.VMEM((2, 256, width - q_width), BF16),
            pltpu.SemaphoreType.DMA,
            pltpu.SemaphoreType.DMA((2,)),
        ],
        "during": back_during,
        "after": back_after,
    }


def gather(value, axes, dim=0):
    return lax.all_gather(value, axes, axis=dim, tiled=True)


def scatter_sum(value, axes, dim=0):
    return lax.psum_scatter(value, axes, scatter_dimension=dim, tiled=True)


def local(
    hidden_in,
    attn_gain,
    w_query,
    w_key,
    w_value,
    w_out,
    ffn_gain,
    w_gate,
    w_up,
    w_down,
    cotangent,
    doc_lengths,
    selected,
    block_order,
):
    one, rows, model = hidden_in.shape
    seq_count = lax.axis_size("seq")
    ctx_count = lax.axis_size("ctx")
    place = lax.axis_index("ctx").astype(jnp.int32).reshape(1)
    length = rows * ctx_count
    span_len = length // block_order.shape[0]
    q_width = HEADS * HEAD_DIM
    kv_width = KV_HEADS * HEAD_DIM
    own_rows = w_gate.shape[0]
    ff_part = w_gate.shape[1] // seq_count

    def split_columns(weight):
        return weight.reshape(own_rows, seq_count, ff_part).transpose(1, 0, 2)

    own_spans = lax.dynamic_slice_in_dim(block_order, place[0] * (rows // span_len), rows // span_len)
    local_pos = (
        own_spans[:, None] * span_len + jnp.arange(span_len, dtype=jnp.int32)[None, :]
    ).reshape(rows)
    half = HEAD_DIM // 2
    inverse = ROPE_BASE ** (-(jnp.arange(half, dtype=F32) * 2.0 / HEAD_DIM))
    angle = inverse[:, None] * local_pos.astype(F32)[None, :]
    cosine = jnp.concatenate([jnp.cos(angle)] * 2, axis=0)
    sine = jnp.concatenate([jnp.sin(angle)] * 2, axis=0)

    full_down = gather(w_down, "ctx")
    gain_row = jnp.pad(jnp.concatenate([attn_gain, ffn_gain])[None], ((0, 15), (0, 128 - 2 * own_rows)))
    gate_mine, up_mine = swap(0, [split_columns(w_gate), split_columns(w_up)])
    full_gate = gather(gate_mine, "ctx", 1).reshape(model, ff_part)
    full_up = gather(up_mine, "ctx", 1).reshape(model, ff_part)

    g_own = jnp.where(
        selected.reshape(rows)[:, None] != 0, cotangent.reshape(rows, model), jnp.zeros((), BF16)
    )
    _, w_qkv, kv, full_out, g_all, x_norm, rms_a, q_t, gain_a, gain_f = project(
        1,
        gain_row,
        jnp.concatenate([w_query, w_key, w_value], axis=1),
        w_out,
        g_own,
        hidden_in.reshape(rows, model),
        cosine,
        sine,
    )
    w_qkv = w_qkv.reshape(model, q_width + 2 * kv_width)
    kv = kv.reshape(length, 2 * kv_width)
    full_out = full_out.reshape(q_width, model)
    o_t, lse, middle, rms_f, f_norm = attend_forward(
        place, block_order, doc_lengths, q_t, kv, hidden_in.reshape(rows, model), gain_f, full_out
    )
    f_all, g_slots, gate, grad_hidden = ffn_first(2, f_norm, g_all, full_gate, full_down)
    hidden_act, grad_gate, grad_up, part_gate = ffn_act(f_all, gate, grad_hidden, full_up)
    grad_f_norm, ffn_part, part_up, part_down = ffn_grad(
        3, rows, f_all, hidden_act, grad_gate, grad_up, g_slots, full_gate, full_up, full_down
    )

    def ffn_rows(part):
        return scatter_sum(part.reshape(seq_count, model // seq_count, ff_part), "ctx", 1)

    rows_gate = ffn_rows(part_gate)
    rows_up = ffn_rows(part_up)
    dq_t, dkv, grad_middle, grad_ffn_gain = attend_backward(
        place,
        block_order,
        doc_lengths,
        q_t,
        kv,
        o_t,
        lse,
        grad_f_norm,
        middle,
        rms_f,
        gain_f,
        g_own,
        full_out,
    )
    part_down, rows_gate, dkv = lax.optimization_barrier((part_down, rows_gate, dkv))
    grad_w_down = scatter_sum(part_down, "ctx").astype(F32)
    _, ffn_out, grad_w_gate, part_out, part_query, part_kv, grad_input, grad_attn_gain = fold(
        "fold_kv",
        4,
        [dkv, ffn_part],
        ("ctx", "seq"),
        (1, 2),
        60,
        [rows_gate],
        work=back_work(
            dq_t,
            o_t,
            cosine,
            sine,
            x_norm,
            hidden_in.reshape(rows, model),
            rms_a,
            gain_a,
            grad_middle,
            w_qkv,
        ),
    )
    output = (middle + ffn_out).astype(BF16).reshape(one, rows, model)
    part_gains = jnp.concatenate(
        [grad_attn_gain.reshape(-1, own_rows), grad_ffn_gain.reshape(-1, own_rows)], axis=1
    )
    part_gains = jnp.pad(part_gains[:, None], ((0, 0), (0, 15), (0, 128 - 2 * own_rows)))
    grad_w_out, grad_w_query, grad_w_kv, grad_gains, grad_w_up = fold(
        "fold_weights",
        5,
        [part_out, part_query, part_kv, part_gains.reshape(-1, 128).astype(BF16)],
        ("all", "all", "all", "all"),
        (8, 8, 2, 1),
        110,
        [rows_up],
    )
    return (
        output,
        grad_input.reshape(one, rows, model),
        grad_gains[0, :own_rows],
        grad_w_query,
        grad_w_kv[:, :kv_width],
        grad_w_kv[:, kv_width:],
        grad_w_out,
        grad_gains[0, own_rows : 2 * own_rows],
        grad_w_gate,
        grad_w_up,
        grad_w_down,
    )


def solution(mesh):
    return jax.shard_map(
        local,
        mesh=mesh,
        in_specs=(
            P("seq", "ctx", None),
            P(("seq", "ctx")),
            P(("seq", "ctx"), None),
            P(("seq", "ctx"), None),
            P(("seq", "ctx"), None),
            P(("seq", "ctx"), None),
            P(("seq", "ctx")),
            P(("seq", "ctx"), None),
            P(("seq", "ctx"), None),
            P(("seq", "ctx"), None),
            P("seq", "ctx", None),
            P("seq", None),
            P("seq", "ctx"),
            P(),
        ),
        out_specs=(
            P("seq", "ctx", None),
            P("seq", "ctx", None),
            P(("seq", "ctx")),
            P(("seq", "ctx"), None),
            P(("seq", "ctx"), None),
            P(("seq", "ctx"), None),
            P(("seq", "ctx"), None),
            P(("seq", "ctx")),
            P(("seq", "ctx"), None),
            P(("seq", "ctx"), None),
            P(("seq", "ctx"), None),
        ),
        check_vma=False,
    )
```

```python
import functools
import math

import jax
import jax.numpy as jnp
from jax import lax
from jax.experimental import pallas as pl
from jax.experimental.pallas import tpu as pltpu
from jax.sharding import PartitionSpec as P

HEADS = 32
KV_HEADS = 4
HEAD_DIM = 64
GROUP = HEADS // KV_HEADS
SCALE = 1.0 / math.sqrt(HEAD_DIM)
LOG2E = math.log2(math.e)


EPS = 1e-05
ROPE_BASE = 10000.0
NEG = -1e30

F32 = jnp.float32
BF16 = jnp.bfloat16
VMEM_MOST = 56 * 1024 * 1024


def dot32(left, right, dims):
    return lax.dot_general(left, right, (dims, ((), ())), preferred_element_type=F32)


def span_bounds(order_ref, lens_ref, span_len, spans, own_first, own):
    docs = lens_ref.shape[1]
    base = order_ref[own_first + own] * span_len
    pos = lax.broadcasted_iota(jnp.int32, (1, span_len), 1) + base
    start = jnp.zeros((1, span_len), jnp.int32)
    first_start = jnp.int32(0)
    end = jnp.int32(0)
    for number in range(docs):
        end = end + lens_ref[0, number]
        start = jnp.where(pos >= end, end, start)
        first_start = jnp.where(base >= end, end, first_start)
    return base, pos, start, first_start


def allowed_tile(key_base, span_len, pos, start):
    key_pos = lax.broadcasted_iota(jnp.int32, (span_len, span_len), 0) + key_base
    tile = (key_pos <= pos) & (key_pos >= start)
    return jnp.concatenate([tile.astype(F32)] * GROUP, axis=1) > 0.5


def stack_heads(ref, head, own, span_len):
    pieces = []
    for member in range(GROUP):
        row = (head * GROUP + member) * HEAD_DIM
        pieces.append(ref[row : row + HEAD_DIM, own * span_len : (own + 1) * span_len])
    return jnp.concatenate(pieces, axis=1)


def unstack_heads(ref, value, head, own, span_len):
    for member in range(GROUP):
        row = (head * GROUP + member) * HEAD_DIM
        ref[row : row + HEAD_DIM, own * span_len : (own + 1) * span_len] = value[
            :, member * span_len : (member + 1) * span_len
        ].astype(ref.dtype)


def attend_forward_kernel(
    span_len,
    spans,
    place_ref,
    order_ref,
    lens_ref,
    q_ref,
    kv_ref,
    x_ref,
    gain_ref,
    wo_ref,
    o_ref,
    lse_ref,
    middle_ref,
    rms_ref,
    f_ref,
    top_ref,
    sum_ref,
    acc_ref,
    o_s,
    wo_s,
    load_sem,
):
    load = pltpu.make_async_copy(wo_ref, wo_s, load_sem)
    load.start()
    own_count = q_ref.shape[1] // span_len
    own_first = place_ref[0] * own_count
    width = KV_HEADS * HEAD_DIM
    for own in range(own_count):
        base, pos, start, first_start = span_bounds(
            order_ref, lens_ref, span_len, spans, own_first, own
        )
        top_ref[...] = jnp.full(top_ref.shape, NEG, F32)
        sum_ref[...] = jnp.zeros(sum_ref.shape, F32)
        acc_ref[...] = jnp.zeros(acc_ref.shape, F32)
        stacked = [stack_heads(q_ref, head, own, span_len) for head in range(KV_HEADS)]

        @pl.loop(0, spans)
        def _(number):
            key_base = order_ref[number] * span_len

            @pl.when((key_base <= base) & (key_base + span_len > first_start))
            def _():
                allowed = allowed_tile(key_base, span_len, pos, start)
                rows = pl.ds(pl.multiple_of(number * span_len, span_len), span_len)
                for head in range(KV_HEADS):
                    lower = head * HEAD_DIM
                    key = kv_ref[rows, lower : lower + HEAD_DIM]
                    value = kv_ref[rows, width + lower : width + lower + HEAD_DIM]
                    scores = dot32(key, stacked[head], ((1,), (0,))) * (SCALE * LOG2E)
                    scores = jnp.where(allowed, scores, NEG)
                    old = top_ref[head : head + 1, :]
                    new = jnp.maximum(old, jnp.max(scores, axis=0, keepdims=True))
                    decay = jnp.exp2(old - new)
                    expo = jnp.exp2(scores - new)
                    top_ref[head : head + 1, :] = new
                    sum_ref[head : head + 1, :] = sum_ref[head : head + 1, :] * decay + jnp.sum(
                        expo, axis=0, keepdims=True
                    )
                    part = dot32(value, expo.astype(BF16), ((0,), (0,)))
                    acc_ref[head] = acc_ref[head] * decay + part

        for head in range(KV_HEADS):
            total = sum_ref[head : head + 1, :]
            mixed = acc_ref[head] / total
            unstack_heads(o_ref, mixed, head, own, span_len)
            lse_ref[own, head : head + 1, :] = top_ref[head : head + 1, :] + jnp.log2(total)
    o_s[...] = o_ref[...].T
    load.wait()

    def out(cols):
        middle_ref[:, cols] = x_ref[:, cols].astype(F32) + dot32(
            o_s[...], wo_s[:, cols], ((1,), (0,))
        )

    tiles(x_ref.shape[1], 256, out)
    middle = middle_ref[...]
    rms = lax.rsqrt(jnp.mean(middle * middle, axis=1, keepdims=True) + EPS)
    rms_ref[...] = rms
    f_ref[...] = (middle * rms * gain_ref[...]).astype(BF16)


def attend_backward_kernel(
    span_len,
    spans,
    place_ref,
    order_ref,
    lens_ref,
    q_ref,
    kv_ref,
    o_ref,
    lse_ref,
    gf_ref,
    middle_ref,
    rms_ref,
    gain_ref,
    g_ref,
    wo_ref,
    dq_ref,
    dkv_ref,
    grad_ref,
    gain_out,
    dkv_acc,
    dq_acc,
    delta_ref,
    ga_s,
    do_ref,
    wo_s,
    load_sem,
):
    load = pltpu.make_async_copy(wo_ref, wo_s, load_sem)
    load.start()
    rms = rms_ref[...]
    gain_out[...] = jnp.sum(gf_ref[...] * (middle_ref[...] * rms), axis=0, keepdims=True)
    scaled = gf_ref[...] * gain_ref[...]
    mean = jnp.mean(scaled * middle_ref[...], axis=1, keepdims=True)
    grad_ref[...] = g_ref[...].astype(F32) + (
        rms * scaled - middle_ref[...] * (rms * rms * rms * mean)
    )
    ga_s[...] = grad_ref[...].astype(BF16)
    load.wait()

    def grad_mix(own):
        do_ref[own, :] = dot32(wo_s[own, :], ga_s[...], ((1,), (1,))).astype(BF16)

    tiles(do_ref.shape[0], 256, grad_mix)
    own_count = q_ref.shape[1] // span_len
    own_first = place_ref[0] * own_count
    width = KV_HEADS * HEAD_DIM
    dkv_acc[...] = jnp.zeros(dkv_acc.shape, F32)
    for own in range(own_count):
        base, pos, start, first_start = span_bounds(
            order_ref, lens_ref, span_len, spans, own_first, own
        )
        dq_acc[...] = jnp.zeros(dq_acc.shape, F32)
        queries = [stack_heads(q_ref, head, own, span_len) for head in range(KV_HEADS)]
        grads = [stack_heads(do_ref, head, own, span_len) for head in range(KV_HEADS)]
        for head in range(KV_HEADS):
            mixed = stack_heads(o_ref, head, own, span_len)
            delta_ref[head : head + 1, :] = jnp.sum(
                mixed.astype(F32) * grads[head].astype(F32), axis=0, keepdims=True
            )

        @pl.loop(0, spans)
        def _(number):
            key_base = order_ref[number] * span_len

            @pl.when((key_base <= base) & (key_base + span_len > first_start))
            def _():
                allowed = allowed_tile(key_base, span_len, pos, start)
                rows = pl.ds(pl.multiple_of(number * span_len, span_len), span_len)
                for head in range(KV_HEADS):
                    lower = head * HEAD_DIM
                    key = kv_ref[rows, lower : lower + HEAD_DIM]
                    value = kv_ref[rows, width + lower : width + lower + HEAD_DIM]
                    scores = dot32(key, queries[head], ((1,), (0,))) * (SCALE * LOG2E)
                    probs = jnp.where(
                        allowed, jnp.exp2(scores - lse_ref[own, head : head + 1, :]), 0.0
                    )
                    grad_probs = dot32(value, grads[head], ((1,), (0,)))
                    grad_scores = (probs * (grad_probs - delta_ref[head : head + 1, :])).astype(BF16)
                    probs = probs.astype(BF16)
                    dq_acc[head] = dq_acc[head] + dot32(key, grad_scores, ((0,), (0,)))
                    dkv_acc[rows, lower : lower + HEAD_DIM] = (
                        dkv_acc[rows, lower : lower + HEAD_DIM]
                        + dot32(grad_scores, queries[head], ((1,), (1,))) * SCALE
                    )
                    dkv_acc[rows, width + lower : width + lower + HEAD_DIM] = dkv_acc[
                        rows, width + lower : width + lower + HEAD_DIM
                    ] + dot32(probs, grads[head], ((1,), (1,)))

        for head in range(KV_HEADS):
            unstack_heads(dq_ref, dq_acc[head] * SCALE, head, own, span_len)
    dkv_ref[...] = dkv_acc[...].astype(dkv_ref.dtype)


def smem():
    return pl.BlockSpec(memory_space=pltpu.SMEM)


def vmem():
    return pl.BlockSpec(memory_space=pltpu.VMEM)


def attend_forward(place, block_order, doc_lengths, q_t, kv, x, gain, w_out):
    spans = block_order.shape[0]
    span_len = kv.shape[0] // spans
    own_count = q_t.shape[1] // span_len
    lanes = GROUP * span_len
    rows, model = x.shape
    return pl.pallas_call(
        functools.partial(attend_forward_kernel, span_len, spans),
        out_shape=(
            jax.ShapeDtypeStruct(q_t.shape, BF16),
            jax.ShapeDtypeStruct((own_count, KV_HEADS, lanes), F32),
            jax.ShapeDtypeStruct((rows, model), F32),
            jax.ShapeDtypeStruct((rows, 1), F32),
            jax.ShapeDtypeStruct((rows, model), BF16),
        ),
        in_specs=[smem(), smem(), smem()] + [vmem()] * 4 + [pl.BlockSpec(memory_space=pl.ANY)],
        out_specs=(vmem(),) * 5,
        scratch_shapes=[
            pltpu.VMEM((KV_HEADS, lanes), F32),
            pltpu.VMEM((KV_HEADS, lanes), F32),
            pltpu.VMEM((KV_HEADS, HEAD_DIM, lanes), F32),
            pltpu.VMEM(q_t.shape[::-1], BF16),
            pltpu.VMEM(w_out.shape, BF16),
            pltpu.SemaphoreType.DMA,
        ],
        compiler_params=pltpu.CompilerParams(vmem_limit_bytes=VMEM_MOST),
        cost_estimate=pl.CostEstimate(
            flops=2 * HEADS * HEAD_DIM * kv.shape[0] * rows + 2 * w_out.size * rows,
            transcendentals=HEADS * kv.shape[0] * rows // 2,
            bytes_accessed=4 * q_t.size + 2 * kv.size + 2 * w_out.size + 8 * rows * model,
        ),
        name="attend_forward",
    )(place, block_order, doc_lengths, q_t, kv, x, gain, w_out)


def attend_backward(
    place, block_order, doc_lengths, q_t, kv, o_t, lse, grad_f, middle, rms, gain, g_own, w_out
):
    spans = block_order.shape[0]
    span_len = kv.shape[0] // spans
    lanes = GROUP * span_len
    rows, model = middle.shape
    return pl.pallas_call(
        functools.partial(attend_backward_kernel, span_len, spans),
        out_shape=(
            jax.ShapeDtypeStruct(q_t.shape, F32),
            jax.ShapeDtypeStruct(kv.shape, BF16),
            jax.ShapeDtypeStruct((rows, model), F32),
            jax.ShapeDtypeStruct((1, model), F32),
        ),
        in_specs=[smem(), smem(), smem()] + [vmem()] * 9 + [pl.BlockSpec(memory_space=pl.ANY)],
        out_specs=(vmem(),) * 4,
        scratch_shapes=[
            pltpu.VMEM(kv.shape, F32),
            pltpu.VMEM((KV_HEADS, HEAD_DIM, lanes), F32),
            pltpu.VMEM((KV_HEADS, lanes), F32),
            pltpu.VMEM((rows, model), BF16),
            pltpu.VMEM(q_t.shape, BF16),
            pltpu.VMEM(w_out.shape, BF16),
            pltpu.SemaphoreType.DMA,
        ],
        compiler_params=pltpu.CompilerParams(vmem_limit_bytes=VMEM_MOST),
        cost_estimate=pl.CostEstimate(
            flops=5 * HEADS * HEAD_DIM * kv.shape[0] * rows + 2 * w_out.size * rows,
            transcendentals=HEADS * kv.shape[0] * rows // 2,
            bytes_accessed=10 * q_t.size + 4 * kv.size + 2 * w_out.size + 14 * rows * model,
        ),
        name="attend_backward",
    )(place, block_order, doc_lengths, q_t, kv, o_t, lse, grad_f, middle, rms, gain, g_own, w_out)


MESH = pl.DeviceIdType.MESH


def coords():
    ctx = lax.axis_index("ctx")
    return lax.axis_index("seq"), ctx // 2, lax.rem(ctx, 2)


def other(place, step, count):
    return lax.rem(place + step, count)


def meet(devices):
    barrier = pltpu.get_barrier_semaphore()
    for device in devices:
        pl.semaphore_signal(barrier, inc=1, device_id=device, device_id_type=MESH)
    pl.semaphore_wait(barrier, len(devices))


def remote(source, target, send_sem, recv_sem, device):
    return pltpu.make_async_remote_copy(
        src_ref=source,
        dst_ref=target,
        send_sem=send_sem,
        recv_sem=recv_sem,
        device_id=device,
        device_id_type=MESH,
    )


def plane_slots(seq_count):
    seq = lax.axis_index("seq")
    if seq_count == 4:
        beside, above = seq + 1 - 2 * lax.rem(seq, 2), other(seq, 2, 4)
        return [seq, beside, above, 3 - seq], [0, 1, 2, 3]
    return [seq] + [other(seq, step, seq_count) for step in range(1, seq_count)], [0] + [
        seq_count - step for step in range(1, seq_count)
    ]


def spread_tools(scopes, halves, seq_count, chip_count, sources, results, sends, recvs, local_sem):
    _, chip, core = coords()
    ctx = lax.axis_index("ctx")
    ctx_count = 2 * chip_count
    slots, _ = plane_slots(seq_count)
    seq, planes = slots[0], slots[1:]
    sibling = {"ctx": chip * 2 + 1 - core}
    last = chip_count - 1
    sides = [
        (chip < last, {"ctx": lax.rem(chip + 1, chip_count) * 2 + core}),
        (chip > 0, {"ctx": lax.rem(chip + last, chip_count) * 2 + core}),
    ]
    peers = []
    if any(scope != "ctx" for scope in scopes):
        peers += [{"seq": place} for place in planes]
    if any(scope in ("ctx", "all") for scope in scopes):
        peers += [{"ctx": other(chip, step, chip_count) * 2 + core} for step in range(1, chip_count)]
        peers += [sibling]
    locals_ = {}

    def pick(items, *names):
        return [item for item in items if scopes[item] in names]

    started = []

    def part(ref, item, half):
        if half is None:
            return ref
        rows = results[item].shape[-2] // 2
        return ref.at[pl.ds(half * rows, rows)]

    def block(item, at_seq, place, at_core):
        scope = scopes[item]
        at_ctx = place * 2 + at_core
        if scope == "all":
            return results[item].at[at_seq, at_ctx], at_seq * ctx_count + at_ctx
        if scope == "ctx":
            return results[item].at[at_ctx], at_ctx
        return results[item].at[at_seq], at_seq

    def descriptor(item, at_seq, place, half, kind, device, source=None):
        target, number = block(item, at_seq, place, core)
        row = place if scopes[item] in ("ctx", "all") else 0
        return remote(
            part(target if source is None else source, item, half),
            part(target, item, half),
            sends[item].at[row, kind],
            recvs[item].at[2 * number + (half or 0)],
            device,
        )

    def arrival(item, at_seq, place, half, at_core=None):
        target, number = block(item, at_seq, place, core if at_core is None else at_core)
        view = part(target, item, half)
        return remote(
            view, view, sends[item].at[0, 0], recvs[item].at[2 * number + (half or 0)], sibling
        )

    def start(copies, there=None):
        for copy in copies:
            copy.start()
            started.append((there, copy))

    def cut(item):
        return (0, 1) if halves[item] else (None,)

    def plane_copies(item, place, half, source=None):
        if not halves[item]:
            return [
                descriptor(item, seq, place, None, 4 + number, {"seq": to}, source)
                for number, to in enumerate(planes)
            ]
        order = (1, 2) if half == 0 else (2, 1)
        return [
            descriptor(item, seq, place, half, 2 + 2 * half + to + 1, {"seq": slots[to]}, source)
            for to in order
        ]

    kinds_relay = 4 + max(4, seq_count - 1)

    def plane_relay(item, place, there=None):
        if not halves[item]:
            return
        steps = [
            (
                arrival(item, slots[give], place, half),
                descriptor(
                    item, slots[give], place, half, kinds_relay + half, {"seq": slots[3 - give]}
                ),
            )
            for give, half in ((1, 0), (2, 1))
        ]

        def run():
            for got, copy in steps:
                got.wait_recv()
                start([copy], there)

        run() if there is None else pl.when(there)(run)

    def plane_end(item, place, there=None):
        if halves[item]:
            ends = [
                (arrival(item, slots[slot], place, half))
                for slot, half in ((1, 1), (2, 0), (3, 0), (3, 1))
            ]
        else:
            ends = [arrival(item, at_seq, place, None) for at_seq in planes]
        copies = []
        if scopes[item] == "all":
            copies = [
                descriptor(item, at_seq, place, None, kinds_relay + 3 + number, sibling)
                for number, at_seq in enumerate(planes)
            ]

        def run():
            for got in ends:
                got.wait_recv()
            start(copies, there)

        run() if there is None else pl.when(there)(run)

    def pass_on(item, place, there, onward, device):
        steps = []
        for half in cut(item):
            steps.append(
                (
                    arrival(item, seq, place, half),
                    descriptor(item, seq, place, half, half or 0, device),
                    plane_copies(item, place, half) if scopes[item] == "all" else [],
                )
            )
        final = descriptor(item, seq, place, None, kinds_relay + 2, sibling)

        def run():
            for got, copy, copies in steps:
                got.wait_recv()
                pl.when(onward)(copy.start)
                start(copies, there)
            start([final], there)

        pl.when(there)(run)
        for _, copy, _ in steps:
            started.append((there & onward, copy))

    def begin(items):
        for item in items:
            target, _ = block(item, seq, chip, core)
            own = sources[item].at[seq] if scopes[item] == "swap" else sources[item]
            locals_[item] = pltpu.make_async_copy(own, target, local_sem.at[item])
            locals_[item].start()
        for item in pick(items, "ctx", "all"):
            for half in cut(item):
                for side, (there, device) in enumerate(sides):
                    copy = descriptor(
                        item, seq, chip, half, 2 * side + (half or 0), device, sources[item]
                    )
                    pl.when(there)(functools.partial(start, [copy], there))
        for item in pick(items, "swap"):
            start(
                [
                    descriptor(
                        item, seq, chip, None, number, {"seq": place}, sources[item].at[place]
                    )
                    for number, place in enumerate(planes)
                ]
            )
        for item in pick(items, "seq", "all"):
            for half in cut(item):
                start(plane_copies(item, chip, half, sources[item]))
        for item in pick(items, "ctx", "all"):
            start([descriptor(item, seq, chip, None, kinds_relay + 2, sibling, sources[item])])

    def relays(items):
        for item in pick(items, "seq", "all"):
            plane_relay(item, chip)

    def waves(items):
        lines, everywhere = pick(items, "ctx", "all"), pick(items, "all")
        done = []
        for step in range(1, chip_count):
            wave = [
                (lax.rem(chip + chip_count - step, chip_count), chip >= step, *sides[0]),
                (lax.rem(chip + step, chip_count), chip <= last - step, *sides[1]),
            ]
            for place, there, onward, device in wave:
                for item in lines:
                    pass_on(item, place, there, onward, device)
            for item in everywhere:
                for place, there, _, _ in done[-1] if done else []:
                    plane_relay(item, place, there)
            if step == 1:
                for item in pick(items, "seq", "all"):
                    plane_end(item, chip)
            elif step > 2:
                for item in everywhere:
                    for place, there, _, _ in done[-2]:
                        plane_end(item, place, there)
            done.append(wave)
        for item in everywhere:
            for place, there, _, _ in done[-1]:
                plane_relay(item, place, there)
            for wave in done[-2:]:
                for place, there, _, _ in wave:
                    plane_end(item, place, there)

    def settle(items):
        for item in pick(items, "swap"):
            for place in planes:
                arrival(item, place, chip, None).wait_recv()
        for item in pick(items, "ctx", "all"):
            for at_seq in [seq] + (planes if scopes[item] == "all" else []):
                for step in range(chip_count):
                    arrival(item, at_seq, other(chip, step, chip_count), None, 1 - core).wait_recv()
        for item in items:
            locals_[item].wait()

    def end():
        for there, copy in started:
            if there is None:
                copy.wait_send()
            else:
                pl.when(there)(copy.wait_send)

    return peers, begin, relays, waves, settle, end


def spread_sems(arrays, scopes, seq_count, chip_count):
    kinds = 4 + max(4, seq_count - 1) + 3 + seq_count - 1
    sends, recvs, halves, shapes = [], [], [], []
    for array, scope in zip(arrays, scopes):
        lead = {"all": (seq_count, 2 * chip_count), "ctx": (2 * chip_count,)}.get(scope, (seq_count,))
        halves.append(seq_count == 4 and scope in ("all", "seq") and array.shape[0] % 32 == 0)
        shape = array.shape if scope == "swap" else lead + array.shape
        shapes.append(jax.ShapeDtypeStruct(shape, array.dtype))
        rows = chip_count if scope in ("all", "ctx") else 1
        sends.append(pltpu.SemaphoreType.DMA((rows, kinds)))
        recvs.append(pltpu.SemaphoreType.DMA((2 * math.prod(lead),)))
    return shapes, tuple(halves), sends + recvs + [pltpu.SemaphoreType.DMA((len(arrays),))]


def swap_kernel(scopes, halves, seq_count, chip_count, *refs):
    count = len(scopes)
    peers, begin, _, _, settle, end = spread_tools(
        scopes,
        halves,
        seq_count,
        chip_count,
        refs[:count],
        refs[count : 2 * count],
        refs[2 * count : 3 * count],
        refs[3 * count : 4 * count],
        refs[4 * count],
    )
    meet(peers)
    begin(range(count))
    settle(range(count))
    end()


def swap(collective_id, arrays):
    seq_count, chip_count = lax.axis_size("seq"), lax.axis_size("ctx") // 2
    scopes = ("swap",) * len(arrays)
    shapes, halves, sems = spread_sems(arrays, scopes, seq_count, chip_count)
    anywhere = pl.BlockSpec(memory_space=pl.ANY)
    return pl.pallas_call(
        functools.partial(swap_kernel, scopes, halves, seq_count, chip_count),
        out_shape=tuple(shapes),
        in_specs=[anywhere] * len(arrays),
        out_specs=(anywhere,) * len(arrays),
        scratch_shapes=sems,
        compiler_params=pltpu.CompilerParams(collective_id=collective_id, has_side_effects=True),
        cost_estimate=pl.CostEstimate(
            flops=0, transcendentals=0, bytes_accessed=20 * 3_000_000
        ),
        name="swap",
    )(*arrays)


FOLD_SCRATCH = 9
WINDOW = 4


def fold_kernel(kinds, chunk_counts, swap_count, work, seq_count, chip_count, *refs):
    count = len(kinds)
    every = count + swap_count
    sources, swap_sources = refs[:count], refs[count:every]
    extra_in, extra_out = (work[0], work[1]) if work else (0, 0)
    first_out = every + extra_in
    results = refs[first_out : first_out + count]
    swap_results = refs[first_out + count : first_out + every]
    first_rest = first_out + every + extra_out
    rest = refs[first_rest:]
    swap_rest = rest[count * FOLD_SCRATCH : count * FOLD_SCRATCH + 4 * swap_count]
    extra = (
        refs[every:first_out],
        refs[first_out + every : first_rest],
        rest[count * FOLD_SCRATCH + 4 * swap_count :],
    )
    seq, chip, core = coords()
    slots, there = plane_slots(seq_count)
    planes = slots[1:]
    chips = [other(chip, step, chip_count) for step in range(1, chip_count)]
    sibling = {"ctx": chip * 2 + 1 - core}
    peers = []
    if any(kind != "seq" for kind in kinds):
        peers += [{"ctx": place * 2 + core} for place in chips] + [sibling]
    if swap_count or any(kind != "ctx" for kind in kinds):
        peers += [{"seq": place} for place in planes]

    def scratch(item):
        return rest[item * FOLD_SCRATCH : (item + 1) * FOLD_SCRATCH]

    def columns(item, chunk):
        width = sources[item].shape[-1] // chunk_counts[item]
        return slice(chunk * width, (chunk + 1) * width)

    order = []
    for chunk in range(max(chunk_counts, default=0)):
        order += [(item, chunk) for item in range(count) if chunk < chunk_counts[item]]

    loads = []
    for item in range(count):
        mine, sem_s = scratch(item)[0], scratch(item)[7]
        if kinds[item] != "seq":
            load = pltpu.make_async_copy(
                sources[item].at[:, :, core], mine, sem_s.at[4, 0, 0]
            )
            load.start()
            loads.append(load)
    meet(peers)

    waits = []

    def go(source, target, send_sem, recv_sem, device):
        copy = remote(source, target, send_sem, recv_sem, device)
        copy.start()
        waits.append(copy)
        return copy

    firsts = {}
    for item, chunk in order:
        if kinds[item] != "seq":
            _, got1, _, _, _, _, _, sem_s, sem_r = scratch(item)
            cols = columns(item, chunk)
            firsts[item, chunk] = go(
                sources[item].at[:, :, 1 - core, :, cols],
                got1.at[:, :, :, cols],
                sem_s.at[0, chunk, 0],
                sem_r.at[0, chunk, 0],
                sibling,
            )
    swapped = []
    for item in range(swap_count):
        got, sem_s, sem_r, sem_own = swap_rest[4 * item : 4 * item + 4]
        own = pltpu.make_async_copy(swap_sources[item].at[seq], got.at[seq], sem_own)
        own.start()
        swapped.append(own)
        for step, place in enumerate(planes):
            go(swap_sources[item].at[place], got.at[seq], sem_s.at[step], sem_r.at[seq], {"seq": place})
    for load in loads:
        load.wait()

    def block(item, slot, cols):
        if kinds[item] == "seq":
            return sources[item][slot, :, cols].astype(F32)[None]
        mine, got1 = scratch(item)[:2]
        place = slots[slot] if kinds[item] == "all" else 0
        return mine[place, :, :, cols].astype(F32) + got1[place, :, :, cols].astype(F32)

    def turn(item, chunk):
        return (1, 2) if (item + chunk) % 2 == 0 else (2, 1)

    seconds = {}

    def plane_first(item, chunk):
        _, got1, _, got2, keep, _, _, sem_s, sem_r = scratch(item)
        cols = columns(item, chunk)
        if kinds[item] == "all":
            firsts[item, chunk].wait_recv()
        first, _ = turn(item, chunk)
        targets = [(slot, slot) for slot in range(1, seq_count)]
        if seq_count == 4:
            targets = [(3, first), (first, first)]
        row = []
        for number, (slot, to) in enumerate(targets):
            if kinds[item] == "all":
                held = got1.at[slots[slot], :, :, cols]
                held[...] = block(item, slot, cols).astype(BF16)
            else:
                held = sources[item].at[pl.ds(slot, 1), :, cols]
            index = number if seq_count == 4 else there[slot] - 1
            row.append(
                go(
                    held,
                    got2.at[index, :, :, cols],
                    sem_s.at[1, chunk, number],
                    sem_r.at[1, chunk, index],
                    {"seq": slots[to]},
                )
            )
        seconds[item, chunk] = row
        keep[:, :, cols] = block(item, 0, cols)

    def plane_second(item, chunk):
        if seq_count != 4:
            return
        _, got1, spare, got2, keep, _, _, sem_s, sem_r = scratch(item)
        cols = columns(item, chunk)
        _, second = turn(item, chunk)
        across, mine = seconds[item, chunk]
        across.wait_recv()
        if kinds[item] == "all":
            held = got1.at[slots[second], :, :, cols]
        else:
            held = spare.at[:, :, cols]
        held[...] = (block(item, second, cols) + got2[0, :, :, cols].astype(F32)).astype(BF16)
        last = go(
            held,
            got2.at[2, :, :, cols],
            sem_s.at[2, chunk, 0],
            sem_r.at[2, chunk, 0],
            {"seq": slots[second]},
        )
        mine.wait_recv()
        keep[:, :, cols] = keep[:, :, cols] + got2[1, :, :, cols].astype(F32)
        seconds[item, chunk] = [last]

    thirds = {}

    def line(item, chunk):
        _, _, _, got2, keep, pass3, got3, sem_s, sem_r = scratch(item)
        cols = columns(item, chunk)
        if kinds[item] == "ctx":
            firsts[item, chunk].wait_recv()
            keep[:, :, cols] = block(item, 0, cols)
        else:
            for copy in seconds[item, chunk]:
                copy.wait_recv()

        def total(place):
            value = keep[place, :, cols]
            if kinds[item] != "ctx":
                for index in (2,) if seq_count == 4 else range(seq_count - 1):
                    value = value + got2[index, place, :, cols].astype(F32)
            return value

        if kinds[item] == "seq":
            results[item][:, cols] = total(0)
            return
        row = []
        for step, place in enumerate(chips):
            pass3[step, :, cols] = total(place).astype(BF16)
            row.append(
                go(
                    pass3.at[step, :, cols],
                    got3.at[step, :, cols],
                    sem_s.at[3, chunk, step],
                    sem_r.at[3, chunk, step],
                    {"ctx": place * 2 + core},
                )
            )
        results[item][:, cols] = total(chip)
        thirds[item, chunk] = row

    lines = [step for step in order if kinds[step[0]] == "ctx"]
    everywhere = [step for step in order if kinds[step[0]] == "all"]
    flats = [step for step in order if kinds[step[0]] == "seq"]
    for step in lines:
        line(*step)
    for step in everywhere[:WINDOW]:
        plane_first(*step)
    for number, step in enumerate(everywhere):
        plane_second(*step)
        for later in everywhere[number + WINDOW : number + WINDOW + 1]:
            plane_first(*later)
        if number:
            line(*everywhere[number - 1])
    for step in flats:
        plane_first(*step)
    if work:
        work[2](*extra)
    for step in everywhere[-1:]:
        line(*step)
    for step in flats:
        plane_second(*step)
    for step in flats:
        line(*step)
    for item, chunk in lines + everywhere:
        got3 = scratch(item)[6]
        cols = columns(item, chunk)
        for copy in thirds[item, chunk]:
            copy.wait_recv()
        value = results[item][:, cols]
        for step in range(chip_count - 1):
            value = value + got3[step, :, cols].astype(F32)
        results[item][:, cols] = value
    if work:
        work[3](results[0], *extra)
    for item in range(swap_count):
        got, sem_s, sem_r, _ = swap_rest[4 * item : 4 * item + 4]
        swapped[item].wait()
        for place in planes:
            remote(got.at[place], got.at[place], sem_s.at[0], sem_r.at[place], sibling).wait_recv()
        width = got.shape[-1]
        for place in range(seq_count):
            swap_results[item][:, place * width : (place + 1) * width] = got[place].astype(F32)
    for copy in waits:
        copy.wait_send()


def fold(name, collective_id, arrays, kinds, chunk_counts, micros, swaps=(), work=None):
    seq_count, ctx_count = lax.axis_size("seq"), lax.axis_size("ctx")
    chip_count = ctx_count // 2
    inputs, shapes, scratch, in_specs = [], [], [], []
    small = (1, 1, 8, 128)
    dma = pltpu.SemaphoreType.DMA
    for array, kind, chunks in zip(arrays, kinds, chunk_counts):
        parts = 1 if kind == "ctx" else seq_count
        blocks = seq_count if kind == "seq" else parts * ctx_count
        rows, cols = array.shape[0] // blocks, array.shape[1]
        lines = 1 if kind == "seq" else chip_count
        if kind == "seq":
            inputs.append(array.reshape(seq_count, rows, cols))
            in_specs.append(vmem())
            got1, spare = small, (1, rows, cols)
        else:
            inputs.append(array.reshape(parts, chip_count, 2, rows, cols))
            in_specs.append(pl.BlockSpec(memory_space=pl.ANY))
            got1, spare = (parts, chip_count, rows, cols), small[1:]
        shapes.append(jax.ShapeDtypeStruct((rows, cols), F32))
        got2 = small if kind == "ctx" else (seq_count - 1, lines, rows, cols)
        got3 = small[1:] if kind == "seq" else (chip_count - 1, rows, cols)
        most = max(seq_count, chip_count)
        scratch += [
            pltpu.VMEM(got1, BF16),
            pltpu.VMEM(got1, BF16),
            pltpu.VMEM(spare, BF16),
            pltpu.VMEM(got2, BF16),
            pltpu.VMEM((lines, rows, cols), F32),
            pltpu.VMEM(got3, BF16),
            pltpu.VMEM(got3, BF16),
            dma((5, chunks, most)),
            dma((4, chunks, most)),
        ]
    for array in swaps:
        inputs.append(array)
        in_specs.append(pl.BlockSpec(memory_space=pl.ANY))
        shapes.append(jax.ShapeDtypeStruct((array.shape[1], seq_count * array.shape[2]), F32))
        scratch += [
            pltpu.VMEM(array.shape, BF16),
            dma((seq_count - 1,)),
            dma((seq_count,)),
            dma,
        ]
    out_specs = [vmem()] * len(inputs)
    does = None
    if work:
        does = (len(work["inputs"]), len(work["shapes"]), work["during"], work["after"])
        inputs += work["inputs"]
        in_specs += work["in_specs"]
        shapes += work["shapes"]
        out_specs += work["out_specs"]
        scratch += work["scratch"]
    return pl.pallas_call(
        functools.partial(
            fold_kernel, tuple(kinds), tuple(chunk_counts), len(swaps), does, seq_count, chip_count
        ),
        out_shape=tuple(shapes),
        in_specs=in_specs,
        out_specs=tuple(out_specs),
        scratch_shapes=scratch,
        compiler_params=pltpu.CompilerParams(
            collective_id=collective_id, has_side_effects=True, vmem_limit_bytes=VMEM_MOST
        ),
        cost_estimate=pl.CostEstimate(
            flops=0, transcendentals=0, bytes_accessed=int(micros * 3_000_000)
        ),
        name=name,
    )(*inputs)


def tiles(extent, width, visit, first=0):
    whole = extent // width

    @pl.loop(first, whole)
    def _(number):
        visit(pl.ds(pl.multiple_of(number * width, width), width))

    if extent % width:
        visit(pl.ds(whole * width, extent % width))


def stream_rows(extent, width, produce, stage, sem, target):
    whole = extent // width

    def leave(slot, rows, size):
        return pltpu.make_async_copy(
            stage.at[slot, pl.ds(0, size)], target.at[rows], sem.at[slot]
        )

    @pl.loop(0, whole)
    def _(number):
        slot = lax.rem(number, 2)
        rows = pl.ds(pl.multiple_of(number * width, width), width)

        @pl.when(number >= 2)
        def _():
            leave(slot, rows, width).wait()

        stage[slot] = produce(rows).astype(stage.dtype)
        leave(slot, rows, width).start()

    for number in range(max(0, whole - 2), whole):
        leave(number % 2, pl.ds(number * width, width), width).wait()
    if extent % width:
        size = extent % width
        rows = pl.ds(whole * width, size)
        stage[0, :size] = produce(rows).astype(stage.dtype)
        leave(0, rows, size).start()
        leave(0, rows, size).wait()


def ffn_first_kernel(
    seq_count, f_ref, g_ref, wg_ref, wd_ref, f_out, g_out, gate_ref, gh_ref, f_s, g_s, wg, wd, in_sem, f_send, f_recv, out_sem
):
    rows = f_ref.shape[0]
    width = wg.shape[1]
    places, there = plane_slots(seq_count)
    load_f = pltpu.make_async_copy(f_ref, f_s.at[pl.ds(0, rows)], in_sem.at[seq_count])
    load_wd = pltpu.make_async_copy(wd_ref, wd, in_sem.at[seq_count + 1])
    load_wg = pltpu.make_async_copy(wg_ref, wg, in_sem.at[seq_count + 2])
    loads = [load_wd]
    for slot in range(seq_count):
        loads.append(
            pltpu.make_async_copy(
                g_ref.at[places[slot]], g_s.at[pl.ds(slot * rows, rows)], in_sem.at[slot]
            )
        )
    for load in [*loads, load_f, load_wg]:
        load.start()
    meet([{"seq": place} for place in places[1:]])

    started = []

    def f_block(slot, half):
        if half is None:
            return f_s.at[pl.ds(slot * rows, rows)]
        return f_s.at[pl.ds(slot * rows + half * (rows // 2), rows // 2)]

    def f_copy(source, to, slot, half):
        copy = remote(
            source,
            f_block(slot, half),
            f_send.at[len(started)],
            f_recv.at[slot, half or 0],
            {"seq": places[to]},
        )
        copy.start()
        started.append(copy)

    def f_arrive(slot, half):
        block = f_block(slot, half)
        remote(
            block, block, f_send.at[0], f_recv.at[slot, half or 0], {"seq": places[1]}
        ).wait_recv()

    if seq_count == 4:
        for half in (0, 1):
            source = f_ref.at[pl.ds(half * (rows // 2), rows // 2)]
            for to in (1, 2) if half == 0 else (2, 1):
                f_copy(source, to, to, half)
    else:
        for to in range(1, seq_count):
            f_copy(f_ref, to, there[to], None)

    def gate_rows(first, count):
        own = slice(first, first + count)

        def visit(cols):
            gate_ref[own, cols] = dot32(f_s[own, :], wg[:, cols], ((1,), (0,)))

        tiles(width, 256, visit)

    for load in loads:
        load.wait()
    leave_g = pltpu.make_async_copy(g_s, g_out, out_sem.at[1])
    leave_g.start()

    def grad_hidden(cols):
        gh_ref[:, cols] = dot32(g_s[...], wd[cols, :], ((1,), (1,))).astype(gh_ref.dtype)

    tiles(width, 256, grad_hidden)
    for load in (load_f, load_wg):
        load.wait()
    gate_rows(0, rows)
    if seq_count == 4:
        f_arrive(1, 0)
        f_copy(f_block(1, 0), 2, 3, 0)
        f_arrive(2, 1)
        f_copy(f_block(2, 1), 1, 3, 1)
        f_arrive(1, 1)
        f_arrive(2, 0)
        gate_rows(rows, 2 * rows)
        f_arrive(3, 0)
        f_arrive(3, 1)
        leave = pltpu.make_async_copy(f_s, f_out, out_sem.at[0])
        leave.start()
        gate_rows(3 * rows, rows)
    else:
        for slot in range(1, seq_count):
            f_arrive(slot, None)
        leave = pltpu.make_async_copy(f_s, f_out, out_sem.at[0])
        leave.start()
        gate_rows(rows, (seq_count - 1) * rows)
    leave.wait()
    leave_g.wait()
    for copy in started:
        copy.wait_send()


def ffn_act_kernel(
    f_ref, gate_ref, gh_ref, wu_ref, hid, gg, gu, pg_ref, f_s, gate_s, gh_s, wu, stage_f, in_sem, leave_sem
):
    model, width = wu.shape
    loads = [
        pltpu.make_async_copy(source, target, in_sem.at[number])
        for number, (source, target) in enumerate(
            [(f_ref, f_s), (wu_ref, wu), (gate_ref, gate_s), (gh_ref, gh_s)]
        )
    ]
    for load in loads:
        load.start()
    for load in loads[:2]:
        load.wait()

    def act(cols, ready=None):
        up_val = dot32(f_s[...], wu[:, cols], ((1,), (0,)))
        if ready is not None:
            ready()
        gate = gate_s[:, cols]
        grad = gh_s[:, cols].astype(F32)
        sigma = jax.nn.sigmoid(gate)
        activated = gate * sigma
        hid[:, cols] = (activated * up_val).astype(BF16)
        gg[:, cols] = (grad * up_val * (sigma + activated * (1.0 - sigma))).astype(BF16)
        gu[:, cols] = (grad * activated).astype(BF16)

    def ready():
        for load in loads[2:]:
            load.wait()

    act(pl.ds(0, 256), ready)
    tiles(width, 256, act, 1)
    stream_rows(
        model,
        256,
        lambda own: dot32(f_s[:, own], gg[...], ((0,), (0,))),
        stage_f,
        leave_sem,
        pg_ref,
    )


def ffn_grad_kernel(
    seq_count,
    f_ref,
    hid_ref,
    gg_ref,
    gu_ref,
    g_ref,
    wg_ref,
    wu_ref,
    wd_ref,
    gf_ref,
    out_ref,
    pu_ref,
    pd_ref,
    f_s,
    g_s,
    hid,
    gg,
    gu,
    wg,
    wu,
    wd,
    parts,
    got,
    stage_f,
    stage_d,
    in_sem,
    x_send,
    x_recv,
    leave_sem,
):
    rows = gf_ref.shape[0]
    model, width = wg.shape
    places, there = plane_slots(seq_count)
    loads = [
        pltpu.make_async_copy(source, target, in_sem.at[number])
        for number, (source, target) in enumerate(
            [
                (gg_ref, gg),
                (gu_ref, gu),
                (wg_ref, wg),
                (wu_ref, wu),
                (f_ref, f_s),
                (hid_ref, hid),
                (g_ref, g_s),
                (wd_ref, wd),
            ]
        )
    ]
    for load in loads[:4]:
        load.start()
    meet([{"seq": place} for place in places[1:]])
    for load in loads[:4]:
        load.wait()
    for load in loads[4:]:
        load.start()

    def part_copy(slot, cols):
        return remote(
            parts.at[pl.ds((slot - 1) * rows, rows), cols],
            got.at[there[slot] - 1, :, cols],
            x_send.at[slot],
            x_recv.at[there[slot]],
            {"seq": places[slot]},
        )

    def grad_f(cols):
        part = dot32(gg[...], wg[cols, :], ((1,), (1,))) + dot32(gu[...], wu[cols, :], ((1,), (1,)))
        gf_ref[:, cols] = part[:rows]
        parts[:, cols] = part[rows:].astype(BF16)
        for slot in range(1, seq_count):
            part_copy(slot, cols).start()

    tiles(model, 256, grad_f)
    for load in loads[4:]:
        load.wait()
    stream_rows(
        model,
        256,
        lambda own: dot32(f_s[:, own], gu[...], ((0,), (0,))),
        stage_f,
        leave_sem.at[0],
        pu_ref,
    )
    stream_rows(
        width,
        256,
        lambda own: dot32(hid[:, own], g_s[...], ((0,), (0,))),
        stage_d,
        leave_sem.at[2],
        pd_ref,
    )

    def out_copy(cols):
        return pltpu.make_async_copy(f_s.at[:, cols], out_ref.at[:, cols], leave_sem.at[1, 0])

    def out_part(cols):
        f_s[:, cols] = dot32(hid[...], wd[:, cols], ((1,), (0,))).astype(BF16)
        out_copy(cols).start()

    tiles(model, 256, out_part)
    everything = pl.ds(0, model)
    out_copy(everything).wait()
    for slot in range(1, seq_count):
        part_copy(slot, everything).wait_recv()
    total = gf_ref[...]
    for slot in range(seq_count - 1):
        total = total + got[slot].astype(F32)
    gf_ref[...] = total
    for slot in range(1, seq_count):
        part_copy(slot, everything).wait_send()


def ffn_first(collective_id, f_norm, g_all, w_gate, w_down):
    seq_count = lax.axis_size("seq")
    rows, model = f_norm.shape
    width = w_gate.shape[1]
    count = seq_count * rows
    anywhere = pl.BlockSpec(memory_space=pl.ANY)
    dma = pltpu.SemaphoreType.DMA
    return pl.pallas_call(
        functools.partial(ffn_first_kernel, seq_count),
        out_shape=(
            jax.ShapeDtypeStruct((count, model), BF16),
            jax.ShapeDtypeStruct((count, model), BF16),
            jax.ShapeDtypeStruct((count, width), F32),
            jax.ShapeDtypeStruct((count, width), BF16),
        ),
        in_specs=[anywhere] * 4,
        out_specs=(anywhere, anywhere, vmem(), vmem()),
        scratch_shapes=[
            pltpu.VMEM((count, model), BF16),
            pltpu.VMEM((count, model), BF16),
            pltpu.VMEM((model, width), BF16),
            pltpu.VMEM((width, model), BF16),
            dma((seq_count + 3,)),
            dma((max(6, seq_count),)),
            dma((seq_count, 2)),
            dma((2,)),
        ],
        compiler_params=pltpu.CompilerParams(
            collective_id=collective_id, has_side_effects=True, vmem_limit_bytes=VMEM_MOST
        ),
        cost_estimate=pl.CostEstimate(
            flops=8 * count * model * width,
            transcendentals=0,
            bytes_accessed=4 * (2 * width * model + 3 * count * model),
        ),
        name="ffn_first",
    )(f_norm, g_all.reshape(seq_count, rows, model), w_gate, w_down)


def ffn_act(f_all, gate, grad_hidden, w_up):
    count, model = f_all.shape
    width = w_up.shape[1]
    anywhere = pl.BlockSpec(memory_space=pl.ANY)
    dma = pltpu.SemaphoreType.DMA
    return pl.pallas_call(
        ffn_act_kernel,
        out_shape=(
            jax.ShapeDtypeStruct((count, width), BF16),
            jax.ShapeDtypeStruct((count, width), BF16),
            jax.ShapeDtypeStruct((count, width), BF16),
            jax.ShapeDtypeStruct((model, width), BF16),
        ),
        in_specs=[anywhere] * 4,
        out_specs=(vmem(), vmem(), vmem(), anywhere),
        scratch_shapes=[
            pltpu.VMEM((count, model), BF16),
            pltpu.VMEM((count, width), F32),
            pltpu.VMEM((count, width), BF16),
            pltpu.VMEM((model, width), BF16),
            pltpu.VMEM((2, 256, width), BF16),
            dma((4,)),
            dma((2,)),
        ],
        compiler_params=pltpu.CompilerParams(vmem_limit_bytes=VMEM_MOST),
        cost_estimate=pl.CostEstimate(
            flops=4 * count * model * width,
            transcendentals=count * width,
            bytes_accessed=4 * (width * model + 2 * count * model + 3 * count * width),
        ),
        name="ffn_act",
    )(f_all, gate, grad_hidden, w_up)


def ffn_grad(collective_id, rows, f_all, hidden_act, grad_gate, grad_up, g_all, w_gate, w_up, w_down):
    seq_count = lax.axis_size("seq")
    count, model = f_all.shape
    width = w_gate.shape[1]
    anywhere = pl.BlockSpec(memory_space=pl.ANY)
    dma = pltpu.SemaphoreType.DMA
    return pl.pallas_call(
        functools.partial(ffn_grad_kernel, seq_count),
        out_shape=(
            jax.ShapeDtypeStruct((rows, model), F32),
            jax.ShapeDtypeStruct((count, model), BF16),
            jax.ShapeDtypeStruct((model, width), BF16),
            jax.ShapeDtypeStruct((width, model), BF16),
        ),
        in_specs=[anywhere] * 8,
        out_specs=(vmem(), anywhere, anywhere, anywhere),
        scratch_shapes=[
            pltpu.VMEM((count, model), BF16),
            pltpu.VMEM((count, model), BF16),
            pltpu.VMEM((count, width), BF16),
            pltpu.VMEM((count, width), BF16),
            pltpu.VMEM((count, width), BF16),
            pltpu.VMEM((model, width), BF16),
            pltpu.VMEM((model, width), BF16),
            pltpu.VMEM((width, model), BF16),
            pltpu.VMEM((count - rows, model), BF16),
            pltpu.VMEM((seq_count - 1, rows, model), BF16),
            pltpu.VMEM((2, 256, width), BF16),
            pltpu.VMEM((2, 256, model), BF16),
            dma((8,)),
            dma((seq_count,)),
            dma((seq_count,)),
            dma((3, 2)),
        ],
        compiler_params=pltpu.CompilerParams(
            collective_id=collective_id, has_side_effects=True, vmem_limit_bytes=VMEM_MOST
        ),
        cost_estimate=pl.CostEstimate(
            flops=14 * count * model * width,
            transcendentals=0,
            bytes_accessed=4 * (3 * width * model + 3 * count * model),
        ),
        name="ffn_grad",
    )(f_all, hidden_act, grad_gate, grad_up, g_all, w_gate, w_up, w_down)


def half_turn(value):
    half = HEAD_DIM // 2
    return jnp.concatenate([-value[half:], value[:half]], axis=0)


GATHER_SCOPES = ("all", "all", "ctx", "all", "seq")


def project_kernel(
    halves,
    seq_count,
    chip_count,
    gain_src,
    w_src,
    wo_src,
    g_src,
    x_ref,
    cos_ref,
    sin_ref,
    gains_ref,
    w_ref,
    kv_ref,
    wo_ref,
    g_ref,
    normed_ref,
    rms_ref,
    q_ref,
    gain_a_ref,
    gain_f_ref,
    kv_own,
    w_s,
    gains_s,
    load_sem,
    *sems,
):
    tile = KV_HEADS * HEAD_DIM
    model, own_rows, width = x_ref.shape[1], w_src.shape[0], w_src.shape[1]
    count = width // tile
    peers, begin, relays, waves, settle, end = spread_tools(
        GATHER_SCOPES,
        halves,
        seq_count,
        chip_count,
        (gain_src, w_src, kv_own, wo_src, g_src),
        (gains_ref, w_ref, kv_ref, wo_ref, g_ref),
        sems[:5],
        sems[5:10],
        sems[10],
    )
    meet(peers)
    begin((0, 1))
    x = x_ref[...].astype(F32)
    rms = lax.rsqrt(jnp.mean(x * x, axis=1, keepdims=True) + EPS)
    rms_ref[...] = rms
    relays((0, 1))
    waves((0, 1))
    begin((3, 4))
    settle((0, 1))

    def load(number):
        cols = pl.ds(pl.multiple_of(number * tile, tile), tile)
        return pltpu.make_async_copy(
            w_ref.at[:, :, :, cols], w_s.at[:, :, :, cols], load_sem.at[number]
        )

    load_gains = pltpu.make_async_copy(gains_ref, gains_s, load_sem.at[count])
    load_gains.start()
    for number in range(count):
        load(number).start()
    load_gains.wait()
    for number in range(seq_count * 2 * chip_count):
        at_seq, at_ctx = divmod(number, 2 * chip_count)
        row = gains_s[at_seq, at_ctx, 0:1, :].astype(F32)
        own = slice(number * own_rows, (number + 1) * own_rows)
        gain_a_ref[:, own] = row[:, :own_rows]
        gain_f_ref[:, own] = row[:, own_rows : 2 * own_rows]
    normed_ref[...] = (x_ref[...].astype(F32) * rms_ref[...] * gain_a_ref[...]).astype(BF16)

    def product(number):
        load(number).wait()
        cols = pl.ds(pl.multiple_of(number * tile, tile), tile)
        return dot32(normed_ref[...], w_s[:, :, :, cols].reshape(model, tile), ((1,), (0,)))

    def rotated(value):
        turned = value.T
        pieces = []
        for head in range(tile // HEAD_DIM):
            one = turned[head * HEAD_DIM : (head + 1) * HEAD_DIM]
            pieces.append(one * cos_ref[...] + half_turn(one) * sin_ref[...])
        return jnp.concatenate(pieces, axis=0)

    kv_own[:, :tile] = rotated(product(count - 2)).T.astype(BF16)
    kv_own[:, tile:] = product(count - 1).astype(BF16)
    begin((2,))
    relays((3, 4))

    @pl.loop(0, count - 2)
    def _(number):
        own = pl.ds(pl.multiple_of(number * tile, tile), tile)
        q_ref[own, :] = rotated(product(number)).astype(BF16)

    waves((3, 4, 2))
    settle((3, 4, 2))
    end()


def project(collective_id, gain_row, w_qkv, w_out, g_own, x, cosine, sine):
    seq_count, ctx_count = lax.axis_size("seq"), lax.axis_size("ctx")
    chip_count = ctx_count // 2
    rows, model = x.shape
    width = w_qkv.shape[1]
    tile = KV_HEADS * HEAD_DIM
    kv_like = jax.ShapeDtypeStruct((rows, 2 * tile), BF16)
    shapes, halves, sems = spread_sems(
        [gain_row, w_qkv, kv_like, w_out, g_own], GATHER_SCOPES, seq_count, chip_count
    )
    anywhere = pl.BlockSpec(memory_space=pl.ANY)
    return pl.pallas_call(
        functools.partial(project_kernel, halves, seq_count, chip_count),
        out_shape=(
            *shapes,
            jax.ShapeDtypeStruct((rows, model), BF16),
            jax.ShapeDtypeStruct((rows, 1), F32),
            jax.ShapeDtypeStruct((width - 2 * tile, rows), BF16),
            jax.ShapeDtypeStruct((1, model), F32),
            jax.ShapeDtypeStruct((1, model), F32),
        ),
        in_specs=[anywhere] * 4 + [vmem()] * 3,
        out_specs=(anywhere,) * 5 + (vmem(),) * 5,
        scratch_shapes=[
            pltpu.VMEM((rows, 2 * tile), BF16),
            pltpu.VMEM(shapes[1].shape, BF16),
            pltpu.VMEM(shapes[0].shape, BF16),
            pltpu.SemaphoreType.DMA((width // tile + 1,)),
            *sems,
        ],
        compiler_params=pltpu.CompilerParams(
            collective_id=collective_id, has_side_effects=True, vmem_limit_bytes=VMEM_MOST
        ),
        cost_estimate=pl.CostEstimate(
            flops=0, transcendentals=0, bytes_accessed=140 * 3_000_000
        ),
        name="project",
    )(gain_row, w_qkv, w_out, g_own, x, cosine, sine)


def rotated_back(value, cos_ref, sin_ref):
    pieces = []
    for head in range(value.shape[0] // HEAD_DIM):
        one = value[head * HEAD_DIM : (head + 1) * HEAD_DIM]
        pieces.append(one * cos_ref[...] - half_turn(one * sin_ref[...]))
    return jnp.concatenate(pieces, axis=0).T.astype(BF16)


def back_during(inputs, outputs, scratch):
    dq_ref, o_ref, cos_ref, sin_ref, normed_ref, x_ref, rms_ref, gain_ref, grad_ref, w_ref = inputs
    part_out, part_query, part_kv, out_ref, gain_out = outputs
    w_s, g_s, gx_s, ga_s, stage, stage_kv, load_sem, leave_sem = scratch
    tile = KV_HEADS * HEAD_DIM
    q_width = dq_ref.shape[0]
    model = x_ref.shape[1]
    pltpu.make_async_copy(w_ref, w_s, load_sem).start()
    ga_s[...] = grad_ref[...].astype(BF16)
    stream_rows(
        q_width,
        256,
        lambda own: dot32(o_ref[own, :], ga_s[...], ((1,), (0,))),
        stage,
        leave_sem,
        part_out,
    )

    @pl.loop(0, q_width // tile)
    def _(number):
        own = pl.ds(pl.multiple_of(number * tile, tile), tile)
        g_s[:, own] = rotated_back(dq_ref[own, :], cos_ref, sin_ref)

    stream_rows(
        model,
        256,
        lambda own: dot32(normed_ref[:, own], g_s[:, :q_width], ((0,), (0,))),
        stage,
        leave_sem,
        part_query,
    )
    pltpu.make_async_copy(w_ref, w_s, load_sem).wait()

    def grad_x(cols):
        gx_s[:, cols] = dot32(g_s[:, :q_width], w_s[cols, :q_width], ((1,), (1,)))

    tiles(model, 256, grad_x)


def back_after(dkv_ref, inputs, outputs, scratch):
    dq_ref, o_ref, cos_ref, sin_ref, normed_ref, x_ref, rms_ref, gain_ref, grad_ref, w_ref = inputs
    part_out, part_query, part_kv, out_ref, gain_out = outputs
    w_s, g_s, gx_s, ga_s, stage, stage_kv, load_sem, leave_sem = scratch
    tile = KV_HEADS * HEAD_DIM
    q_width = dq_ref.shape[0]
    model = x_ref.shape[1]
    g_s[:, q_width : q_width + tile] = rotated_back(dkv_ref[:, :tile].T, cos_ref, sin_ref)
    g_s[:, q_width + tile :] = dkv_ref[:, tile:].astype(BF16)
    stream_rows(
        model,
        256,
        lambda own: dot32(normed_ref[:, own], g_s[:, q_width:], ((0,), (0,))),
        stage_kv,
        leave_sem,
        part_kv,
    )

    def grad_x(cols):
        gx_s[:, cols] = gx_s[:, cols] + dot32(g_s[:, q_width:], w_s[cols, q_width:], ((1,), (1,)))

    tiles(model, 256, grad_x)
    x = x_ref[...].astype(F32)
    rms = rms_ref[...]
    gain_out[...] = jnp.sum(gx_s[...] * (x * rms), axis=0, keepdims=True)
    scaled = gx_s[...] * gain_ref[...]
    mean = jnp.mean(scaled * x, axis=1, keepdims=True)
    out_ref[...] = grad_ref[...] + (rms * scaled - x * (rms * rms * rms * mean))


def back_work(dq_t, o_t, cosine, sine, normed, x, rms, gain, grad, w_qkv):
    rows, model = x.shape
    width = w_qkv.shape[1]
    q_width = dq_t.shape[0]
    anywhere = pl.BlockSpec(memory_space=pl.ANY)
    return {
        "inputs": [dq_t, o_t, cosine, sine, normed, x, rms, gain, grad, w_qkv],
        "in_specs": [vmem()] * 9 + [anywhere],
        "shapes": [
            jax.ShapeDtypeStruct((q_width, model), BF16),
            jax.ShapeDtypeStruct((model, q_width), BF16),
            jax.ShapeDtypeStruct((model, width - q_width), BF16),
            jax.ShapeDtypeStruct((rows, model), F32),
            jax.ShapeDtypeStruct((1, model), F32),
        ],
        "out_specs": [anywhere, anywhere, anywhere, vmem(), vmem()],
        "scratch": [
            pltpu.VMEM(w_qkv.shape, BF16),
            pltpu.VMEM((rows, width), BF16),
            pltpu.VMEM((rows, model), F32),
            pltpu.VMEM((rows, model), BF16),
            pltpu.VMEM((2, 256, max(model, q_width)), BF16),
            pltpu.VMEM((2, 256, width - q_width), BF16),
            pltpu.SemaphoreType.DMA,
            pltpu.SemaphoreType.DMA((2,)),
        ],
        "during": back_during,
        "after": back_after,
    }


def gather(value, axes, dim=0):
    return lax.all_gather(value, axes, axis=dim, tiled=True)


def scatter_sum(value, axes, dim=0):
    return lax.psum_scatter(value, axes, scatter_dimension=dim, tiled=True)


def local(
    hidden_in,
    attn_gain,
    w_query,
    w_key,
    w_value,
    w_out,
    ffn_gain,
    w_gate,
    w_up,
    w_down,
    cotangent,
    doc_lengths,
    selected,
    block_order,
):
    one, rows, model = hidden_in.shape
    seq_count = lax.axis_size("seq")
    ctx_count = lax.axis_size("ctx")
    place = lax.axis_index("ctx").astype(jnp.int32).reshape(1)
    length = rows * ctx_count
    span_len = length // block_order.shape[0]
    q_width = HEADS * HEAD_DIM
    kv_width = KV_HEADS * HEAD_DIM
    own_rows = w_gate.shape[0]
    ff_part = w_gate.shape[1] // seq_count

    def split_columns(weight):
        return weight.reshape(own_rows, seq_count, ff_part).transpose(1, 0, 2)

    own_spans = lax.dynamic_slice_in_dim(block_order, place[0] * (rows // span_len), rows // span_len)
    local_pos = (
        own_spans[:, None] * span_len + jnp.arange(span_len, dtype=jnp.int32)[None, :]
    ).reshape(rows)
    half = HEAD_DIM // 2
    inverse = ROPE_BASE ** (-(jnp.arange(half, dtype=F32) * 2.0 / HEAD_DIM))
    angle = inverse[:, None] * local_pos.astype(F32)[None, :]
    cosine = jnp.concatenate([jnp.cos(angle)] * 2, axis=0)
    sine = jnp.concatenate([jnp.sin(angle)] * 2, axis=0)

    full_down = gather(w_down, "ctx")
    gain_row = jnp.pad(jnp.concatenate([attn_gain, ffn_gain])[None], ((0, 15), (0, 128 - 2 * own_rows)))
    gate_mine, up_mine = swap(0, [split_columns(w_gate), split_columns(w_up)])
    full_gate = gather(gate_mine, "ctx", 1).reshape(model, ff_part)
    full_up = gather(up_mine, "ctx", 1).reshape(model, ff_part)

    g_own = jnp.where(
        selected.reshape(rows)[:, None] != 0, cotangent.reshape(rows, model), jnp.zeros((), BF16)
    )
    _, w_qkv, kv, full_out, g_all, x_norm, rms_a, q_t, gain_a, gain_f = project(
        1,
        gain_row,
        jnp.concatenate([w_query, w_key, w_value], axis=1),
        w_out,
        g_own,
        hidden_in.reshape(rows, model),
        cosine,
        sine,
    )
    w_qkv = w_qkv.reshape(model, q_width + 2 * kv_width)
    kv = kv.reshape(length, 2 * kv_width)
    full_out = full_out.reshape(q_width, model)
    o_t, lse, middle, rms_f, f_norm = attend_forward(
        place, block_order, doc_lengths, q_t, kv, hidden_in.reshape(rows, model), gain_f, full_out
    )
    f_all, g_slots, gate, grad_hidden = ffn_first(2, f_norm, g_all, full_gate, full_down)
    hidden_act, grad_gate, grad_up, part_gate = ffn_act(f_all, gate, grad_hidden, full_up)
    grad_f_norm, ffn_part, part_up, part_down = ffn_grad(
        3, rows, f_all, hidden_act, grad_gate, grad_up, g_slots, full_gate, full_up, full_down
    )

    def ffn_rows(part):
        return scatter_sum(part.reshape(seq_count, model // seq_count, ff_part), "ctx", 1)

    rows_gate = ffn_rows(part_gate)
    rows_up = ffn_rows(part_up)
    dq_t, dkv, grad_middle, grad_ffn_gain = attend_backward(
        place,
        block_order,
        doc_lengths,
        q_t,
        kv,
        o_t,
        lse,
        grad_f_norm,
        middle,
        rms_f,
        gain_f,
        g_own,
        full_out,
    )
    part_down, rows_gate, dkv = lax.optimization_barrier((part_down, rows_gate, dkv))
    grad_w_down = scatter_sum(part_down, "ctx").astype(F32)
    _, ffn_out, grad_w_gate, part_out, part_query, part_kv, grad_input, grad_attn_gain = fold(
        "fold_kv",
        4,
        [dkv, ffn_part],
        ("ctx", "seq"),
        (1, 2),
        60,
        [rows_gate],
        work=back_work(
            dq_t,
            o_t,
            cosine,
            sine,
            x_norm,
            hidden_in.reshape(rows, model),
            rms_a,
            gain_a,
            grad_middle,
            w_qkv,
        ),
    )
    output = (middle + ffn_out).astype(BF16).reshape(one, rows, model)
    part_gains = jnp.concatenate(
        [grad_attn_gain.reshape(-1, own_rows), grad_ffn_gain.reshape(-1, own_rows)], axis=1
    )
    part_gains = jnp.pad(part_gains[:, None], ((0, 0), (0, 15), (0, 128 - 2 * own_rows)))
    grad_w_out, grad_w_query, grad_w_kv, grad_gains, grad_w_up = fold(
        "fold_weights",
        5,
        [part_out, part_query, part_kv, part_gains.reshape(-1, 128).astype(BF16)],
        ("all", "all", "all", "all"),
        (8, 8, 2, 1),
        110,
        [rows_up],
    )
    return (
        output,
        grad_input.reshape(one, rows, model),
        grad_gains[0, :own_rows],
        grad_w_query,
        grad_w_kv[:, :kv_width],
        grad_w_kv[:, kv_width:],
        grad_w_out,
        grad_gains[0, own_rows : 2 * own_rows],
        grad_w_gate,
        grad_w_up,
        grad_w_down,
    )


def solution(mesh):
    return jax.shard_map(
        local,
        mesh=mesh,
        in_specs=(
            P("seq", "ctx", None),
            P(("seq", "ctx")),
            P(("seq", "ctx"), None),
            P(("seq", "ctx"), None),
            P(("seq", "ctx"), None),
            P(("seq", "ctx"), None),
            P(("seq", "ctx")),
            P(("seq", "ctx"), None),
            P(("seq", "ctx"), None),
            P(("seq", "ctx"), None),
            P("seq", "ctx", None),
            P("seq", None),
            P("seq", "ctx"),
            P(),
        ),
        out_specs=(
            P("seq", "ctx", None),
            P("seq", "ctx", None),
            P(("seq", "ctx")),
            P(("seq", "ctx"), None),
            P(("seq", "ctx"), None),
            P(("seq", "ctx"), None),
            P(("seq", "ctx"), None),
            P(("seq", "ctx")),
            P(("seq", "ctx"), None),
            P(("seq", "ctx"), None),
            P(("seq", "ctx"), None),
        ),
        check_vma=False,
    )
```

```python
import functools
import math

import jax
import jax.numpy as jnp
from jax import lax
from jax.experimental import pallas as pl
from jax.experimental.pallas import tpu as pltpu
from jax.sharding import PartitionSpec as P

HEADS = 32
KV_HEADS = 4
HEAD_DIM = 64
GROUP = HEADS // KV_HEADS
SCALE = 1.0 / math.sqrt(HEAD_DIM)
LOG2E = math.log2(math.e)


EPS = 1e-05
ROPE_BASE = 10000.0
NEG = -1e30

F32 = jnp.float32
BF16 = jnp.bfloat16
VMEM_MOST = 56 * 1024 * 1024


def dot32(left, right, dims):
    return lax.dot_general(left, right, (dims, ((), ())), preferred_element_type=F32)


def span_bounds(order_ref, lens_ref, span_len, spans, own_first, own):
    docs = lens_ref.shape[1]
    base = order_ref[own_first + own] * span_len
    pos = lax.broadcasted_iota(jnp.int32, (1, span_len), 1) + base
    start = jnp.zeros((1, span_len), jnp.int32)
    first_start = jnp.int32(0)
    end = jnp.int32(0)
    for number in range(docs):
        end = end + lens_ref[0, number]
        start = jnp.where(pos >= end, end, start)
        first_start = jnp.where(base >= end, end, first_start)
    return base, pos, start, first_start


def allowed_tile(key_base, span_len, pos, start):
    key_pos = lax.broadcasted_iota(jnp.int32, (span_len, span_len), 0) + key_base
    tile = (key_pos <= pos) & (key_pos >= start)
    return jnp.concatenate([tile.astype(F32)] * GROUP, axis=1) > 0.5


def stack_heads(ref, head, own, span_len):
    pieces = []
    for member in range(GROUP):
        row = (head * GROUP + member) * HEAD_DIM
        pieces.append(ref[row : row + HEAD_DIM, own * span_len : (own + 1) * span_len])
    return jnp.concatenate(pieces, axis=1)


def unstack_heads(ref, value, head, own, span_len):
    for member in range(GROUP):
        row = (head * GROUP + member) * HEAD_DIM
        ref[row : row + HEAD_DIM, own * span_len : (own + 1) * span_len] = value[
            :, member * span_len : (member + 1) * span_len
        ].astype(ref.dtype)


def attend_forward_kernel(
    span_len,
    spans,
    place_ref,
    order_ref,
    lens_ref,
    q_ref,
    kv_ref,
    x_ref,
    gain_ref,
    wo_ref,
    o_ref,
    lse_ref,
    middle_ref,
    rms_ref,
    f_ref,
    top_ref,
    sum_ref,
    acc_ref,
    o_s,
    wo_s,
    load_sem,
):
    load = pltpu.make_async_copy(wo_ref, wo_s, load_sem)
    load.start()
    own_count = q_ref.shape[1] // span_len
    own_first = place_ref[0] * own_count
    width = KV_HEADS * HEAD_DIM
    for own in range(own_count):
        base, pos, start, first_start = span_bounds(
            order_ref, lens_ref, span_len, spans, own_first, own
        )
        top_ref[...] = jnp.full(top_ref.shape, NEG, F32)
        sum_ref[...] = jnp.zeros(sum_ref.shape, F32)
        acc_ref[...] = jnp.zeros(acc_ref.shape, F32)
        stacked = [stack_heads(q_ref, head, own, span_len) for head in range(KV_HEADS)]

        @pl.loop(0, spans)
        def _(number):
            key_base = order_ref[number] * span_len

            @pl.when((key_base <= base) & (key_base + span_len > first_start))
            def _():
                allowed = allowed_tile(key_base, span_len, pos, start)
                rows = pl.ds(pl.multiple_of(number * span_len, span_len), span_len)
                for head in range(KV_HEADS):
                    lower = head * HEAD_DIM
                    key = kv_ref[rows, lower : lower + HEAD_DIM]
                    value = kv_ref[rows, width + lower : width + lower + HEAD_DIM]
                    scores = dot32(key, stacked[head], ((1,), (0,))) * (SCALE * LOG2E)
                    scores = jnp.where(allowed, scores, NEG)
                    old = top_ref[head : head + 1, :]
                    new = jnp.maximum(old, jnp.max(scores, axis=0, keepdims=True))
                    decay = jnp.exp2(old - new)
                    expo = jnp.exp2(scores - new)
                    top_ref[head : head + 1, :] = new
                    sum_ref[head : head + 1, :] = sum_ref[head : head + 1, :] * decay + jnp.sum(
                        expo, axis=0, keepdims=True
                    )
                    part = dot32(value, expo.astype(BF16), ((0,), (0,)))
                    acc_ref[head] = acc_ref[head] * decay + part

        for head in range(KV_HEADS):
            total = sum_ref[head : head + 1, :]
            mixed = acc_ref[head] / total
            unstack_heads(o_ref, mixed, head, own, span_len)
            lse_ref[own, head : head + 1, :] = top_ref[head : head + 1, :] + jnp.log2(total)
    o_s[...] = o_ref[...].T
    load.wait()

    def out(cols):
        middle_ref[:, cols] = x_ref[:, cols].astype(F32) + dot32(
            o_s[...], wo_s[:, cols], ((1,), (0,))
        )

    tiles(x_ref.shape[1], 256, out)
    middle = middle_ref[...]
    rms = lax.rsqrt(jnp.mean(middle * middle, axis=1, keepdims=True) + EPS)
    rms_ref[...] = rms
    f_ref[...] = (middle * rms * gain_ref[...]).astype(BF16)


def attend_backward_kernel(
    span_len,
    spans,
    place_ref,
    order_ref,
    lens_ref,
    q_ref,
    kv_ref,
    o_ref,
    lse_ref,
    gf_ref,
    middle_ref,
    rms_ref,
    gain_ref,
    g_ref,
    wo_ref,
    dq_ref,
    dkv_ref,
    grad_ref,
    gain_out,
    dkv_acc,
    dq_acc,
    delta_ref,
    ga_s,
    do_ref,
    wo_s,
    load_sem,
):
    load = pltpu.make_async_copy(wo_ref, wo_s, load_sem)
    load.start()
    rms = rms_ref[...]
    gain_out[...] = jnp.sum(gf_ref[...] * (middle_ref[...] * rms), axis=0, keepdims=True)
    scaled = gf_ref[...] * gain_ref[...]
    mean = jnp.mean(scaled * middle_ref[...], axis=1, keepdims=True)
    grad_ref[...] = g_ref[...].astype(F32) + (
        rms * scaled - middle_ref[...] * (rms * rms * rms * mean)
    )
    ga_s[...] = grad_ref[...].astype(BF16)
    load.wait()

    def grad_mix(own):
        do_ref[own, :] = dot32(wo_s[own, :], ga_s[...], ((1,), (1,))).astype(BF16)

    tiles(do_ref.shape[0], 256, grad_mix)
    own_count = q_ref.shape[1] // span_len
    own_first = place_ref[0] * own_count
    width = KV_HEADS * HEAD_DIM
    dkv_acc[...] = jnp.zeros(dkv_acc.shape, F32)
    for own in range(own_count):
        base, pos, start, first_start = span_bounds(
            order_ref, lens_ref, span_len, spans, own_first, own
        )
        dq_acc[...] = jnp.zeros(dq_acc.shape, F32)
        queries = [stack_heads(q_ref, head, own, span_len) for head in range(KV_HEADS)]
        grads = [stack_heads(do_ref, head, own, span_len) for head in range(KV_HEADS)]
        for head in range(KV_HEADS):
            mixed = stack_heads(o_ref, head, own, span_len)
            delta_ref[head : head + 1, :] = jnp.sum(
                mixed.astype(F32) * grads[head].astype(F32), axis=0, keepdims=True
            )

        @pl.loop(0, spans)
        def _(number):
            key_base = order_ref[number] * span_len

            @pl.when((key_base <= base) & (key_base + span_len > first_start))
            def _():
                allowed = allowed_tile(key_base, span_len, pos, start)
                rows = pl.ds(pl.multiple_of(number * span_len, span_len), span_len)
                for head in range(KV_HEADS):
                    lower = head * HEAD_DIM
                    key = kv_ref[rows, lower : lower + HEAD_DIM]
                    value = kv_ref[rows, width + lower : width + lower + HEAD_DIM]
                    scores = dot32(key, queries[head], ((1,), (0,))) * (SCALE * LOG2E)
                    probs = jnp.where(
                        allowed, jnp.exp2(scores - lse_ref[own, head : head + 1, :]), 0.0
                    )
                    grad_probs = dot32(value, grads[head], ((1,), (0,)))
                    grad_scores = (probs * (grad_probs - delta_ref[head : head + 1, :])).astype(BF16)
                    probs = probs.astype(BF16)
                    dq_acc[head] = dq_acc[head] + dot32(key, grad_scores, ((0,), (0,)))
                    dkv_acc[rows, lower : lower + HEAD_DIM] = (
                        dkv_acc[rows, lower : lower + HEAD_DIM]
                        + dot32(grad_scores, queries[head], ((1,), (1,))) * SCALE
                    )
                    dkv_acc[rows, width + lower : width + lower + HEAD_DIM] = dkv_acc[
                        rows, width + lower : width + lower + HEAD_DIM
                    ] + dot32(probs, grads[head], ((1,), (1,)))

        for head in range(KV_HEADS):
            unstack_heads(dq_ref, dq_acc[head] * SCALE, head, own, span_len)
    dkv_ref[...] = dkv_acc[...].astype(dkv_ref.dtype)


def smem():
    return pl.BlockSpec(memory_space=pltpu.SMEM)


def vmem():
    return pl.BlockSpec(memory_space=pltpu.VMEM)


def attend_forward(place, block_order, doc_lengths, q_t, kv, x, gain, w_out):
    spans = block_order.shape[0]
    span_len = kv.shape[0] // spans
    own_count = q_t.shape[1] // span_len
    lanes = GROUP * span_len
    rows, model = x.shape
    return pl.pallas_call(
        functools.partial(attend_forward_kernel, span_len, spans),
        out_shape=(
            jax.ShapeDtypeStruct(q_t.shape, BF16),
            jax.ShapeDtypeStruct((own_count, KV_HEADS, lanes), F32),
            jax.ShapeDtypeStruct((rows, model), F32),
            jax.ShapeDtypeStruct((rows, 1), F32),
            jax.ShapeDtypeStruct((rows, model), BF16),
        ),
        in_specs=[smem(), smem(), smem()] + [vmem()] * 4 + [pl.BlockSpec(memory_space=pl.ANY)],
        out_specs=(vmem(),) * 5,
        scratch_shapes=[
            pltpu.VMEM((KV_HEADS, lanes), F32),
            pltpu.VMEM((KV_HEADS, lanes), F32),
            pltpu.VMEM((KV_HEADS, HEAD_DIM, lanes), F32),
            pltpu.VMEM(q_t.shape[::-1], BF16),
            pltpu.VMEM(w_out.shape, BF16),
            pltpu.SemaphoreType.DMA,
        ],
        compiler_params=pltpu.CompilerParams(vmem_limit_bytes=VMEM_MOST),
        cost_estimate=pl.CostEstimate(
            flops=2 * HEADS * HEAD_DIM * kv.shape[0] * rows + 2 * w_out.size * rows,
            transcendentals=HEADS * kv.shape[0] * rows // 2,
            bytes_accessed=4 * q_t.size + 2 * kv.size + 2 * w_out.size + 8 * rows * model,
        ),
        name="attend_forward",
    )(place, block_order, doc_lengths, q_t, kv, x, gain, w_out)


def attend_backward(
    place, block_order, doc_lengths, q_t, kv, o_t, lse, grad_f, middle, rms, gain, g_own, w_out
):
    spans = block_order.shape[0]
    span_len = kv.shape[0] // spans
    lanes = GROUP * span_len
    rows, model = middle.shape
    return pl.pallas_call(
        functools.partial(attend_backward_kernel, span_len, spans),
        out_shape=(
            jax.ShapeDtypeStruct(q_t.shape, F32),
            jax.ShapeDtypeStruct(kv.shape, BF16),
            jax.ShapeDtypeStruct((rows, model), F32),
            jax.ShapeDtypeStruct((1, model), F32),
        ),
        in_specs=[smem(), smem(), smem()] + [vmem()] * 9 + [pl.BlockSpec(memory_space=pl.ANY)],
        out_specs=(vmem(),) * 4,
        scratch_shapes=[
            pltpu.VMEM(kv.shape, F32),
            pltpu.VMEM((KV_HEADS, HEAD_DIM, lanes), F32),
            pltpu.VMEM((KV_HEADS, lanes), F32),
            pltpu.VMEM((rows, model), BF16),
            pltpu.VMEM(q_t.shape, BF16),
            pltpu.VMEM(w_out.shape, BF16),
            pltpu.SemaphoreType.DMA,
        ],
        compiler_params=pltpu.CompilerParams(vmem_limit_bytes=VMEM_MOST),
        cost_estimate=pl.CostEstimate(
            flops=5 * HEADS * HEAD_DIM * kv.shape[0] * rows + 2 * w_out.size * rows,
            transcendentals=HEADS * kv.shape[0] * rows // 2,
            bytes_accessed=10 * q_t.size + 4 * kv.size + 2 * w_out.size + 14 * rows * model,
        ),
        name="attend_backward",
    )(place, block_order, doc_lengths, q_t, kv, o_t, lse, grad_f, middle, rms, gain, g_own, w_out)


MESH = pl.DeviceIdType.MESH


def coords():
    ctx = lax.axis_index("ctx")
    return lax.axis_index("seq"), ctx // 2, lax.rem(ctx, 2)


def other(place, step, count):
    return lax.rem(place + step, count)


def meet(devices):
    barrier = pltpu.get_barrier_semaphore()
    for device in devices:
        pl.semaphore_signal(barrier, inc=1, device_id=device, device_id_type=MESH)
    pl.semaphore_wait(barrier, len(devices))


def remote(source, target, send_sem, recv_sem, device):
    return pltpu.make_async_remote_copy(
        src_ref=source,
        dst_ref=target,
        send_sem=send_sem,
        recv_sem=recv_sem,
        device_id=device,
        device_id_type=MESH,
    )


def plane_slots(seq_count):
    seq = lax.axis_index("seq")
    if seq_count == 4:
        beside, above = seq + 1 - 2 * lax.rem(seq, 2), other(seq, 2, 4)
        return [seq, beside, above, 3 - seq], [0, 1, 2, 3]
    return [seq] + [other(seq, step, seq_count) for step in range(1, seq_count)], [0] + [
        seq_count - step for step in range(1, seq_count)
    ]


def spread_tools(scopes, halves, seq_count, chip_count, sources, results, sends, recvs, local_sem):
    _, chip, core = coords()
    ctx = lax.axis_index("ctx")
    ctx_count = 2 * chip_count
    slots, _ = plane_slots(seq_count)
    seq, planes = slots[0], slots[1:]
    sibling = {"ctx": chip * 2 + 1 - core}
    last = chip_count - 1
    sides = [
        (chip < last, {"ctx": lax.rem(chip + 1, chip_count) * 2 + core}),
        (chip > 0, {"ctx": lax.rem(chip + last, chip_count) * 2 + core}),
    ]
    peers = []
    if any(scope != "ctx" for scope in scopes):
        peers += [{"seq": place} for place in planes]
    if any(scope in ("ctx", "all") for scope in scopes):
        peers += [{"ctx": other(chip, step, chip_count) * 2 + core} for step in range(1, chip_count)]
        peers += [sibling]
    locals_ = {}

    def pick(items, *names):
        return [item for item in items if scopes[item] in names]

    started = []

    def part(ref, item, half):
        if half is None:
            return ref
        rows = results[item].shape[-2] // 2
        return ref.at[pl.ds(half * rows, rows)]

    def block(item, at_seq, place, at_core):
        scope = scopes[item]
        at_ctx = place * 2 + at_core
        if scope == "all":
            return results[item].at[at_seq, at_ctx], at_seq * ctx_count + at_ctx
        if scope == "ctx":
            return results[item].at[at_ctx], at_ctx
        return results[item].at[at_seq], at_seq

    def descriptor(item, at_seq, place, half, kind, device, source=None):
        target, number = block(item, at_seq, place, core)
        row = place if scopes[item] in ("ctx", "all") else 0
        return remote(
            part(target if source is None else source, item, half),
            part(target, item, half),
            sends[item].at[row, kind],
            recvs[item].at[2 * number + (half or 0)],
            device,
        )

    def arrival(item, at_seq, place, half, at_core=None):
        target, number = block(item, at_seq, place, core if at_core is None else at_core)
        view = part(target, item, half)
        return remote(
            view, view, sends[item].at[0, 0], recvs[item].at[2 * number + (half or 0)], sibling
        )

    def start(copies, there=None):
        for copy in copies:
            copy.start()
            started.append((there, copy))

    def cut(item):
        return (0, 1) if halves[item] else (None,)

    def plane_copies(item, place, half, source=None):
        if not halves[item]:
            return [
                descriptor(item, seq, place, None, 4 + number, {"seq": to}, source)
                for number, to in enumerate(planes)
            ]
        order = (1, 2) if half == 0 else (2, 1)
        return [
            descriptor(item, seq, place, half, 2 + 2 * half + to + 1, {"seq": slots[to]}, source)
            for to in order
        ]

    kinds_relay = 4 + max(4, seq_count - 1)

    def plane_relay(item, place, there=None):
        if not halves[item]:
            return
        steps = [
            (
                arrival(item, slots[give], place, half),
                descriptor(
                    item, slots[give], place, half, kinds_relay + half, {"seq": slots[3 - give]}
                ),
            )
            for give, half in ((1, 0), (2, 1))
        ]

        def run():
            for got, copy in steps:
                got.wait_recv()
                start([copy], there)

        run() if there is None else pl.when(there)(run)

    def plane_end(item, place, there=None):
        if halves[item]:
            ends = [
                (arrival(item, slots[slot], place, half))
                for slot, half in ((1, 1), (2, 0), (3, 0), (3, 1))
            ]
        else:
            ends = [arrival(item, at_seq, place, None) for at_seq in planes]
        copies = []
        if scopes[item] == "all":
            copies = [
                descriptor(item, at_seq, place, None, kinds_relay + 3 + number, sibling)
                for number, at_seq in enumerate(planes)
            ]

        def run():
            for got in ends:
                got.wait_recv()
            start(copies, there)

        run() if there is None else pl.when(there)(run)

    def pass_on(item, place, there, onward, device):
        steps = []
        for half in cut(item):
            steps.append(
                (
                    arrival(item, seq, place, half),
                    descriptor(item, seq, place, half, half or 0, device),
                    plane_copies(item, place, half) if scopes[item] == "all" else [],
                )
            )
        final = descriptor(item, seq, place, None, kinds_relay + 2, sibling)

        def run():
            for got, copy, copies in steps:
                got.wait_recv()
                pl.when(onward)(copy.start)
                start(copies, there)
            start([final], there)

        pl.when(there)(run)
        for _, copy, _ in steps:
            started.append((there & onward, copy))

    def piece(item, place):
        if len(sources[item].shape) == 3:
            return sources[item].at[place]
        width = results[item].shape[-1]
        return sources[item].at[:, pl.ds(pl.multiple_of(place * width, 128), width)]

    def begin(items):
        for item in items:
            target, _ = block(item, seq, chip, core)
            own = piece(item, seq) if scopes[item] == "swap" else sources[item]
            locals_[item] = pltpu.make_async_copy(own, target, local_sem.at[item])
            locals_[item].start()
        for item in pick(items, "ctx", "all"):
            for half in cut(item):
                for side, (there, device) in enumerate(sides):
                    copy = descriptor(
                        item, seq, chip, half, 2 * side + (half or 0), device, sources[item]
                    )
                    pl.when(there)(functools.partial(start, [copy], there))
        for item in pick(items, "swap"):
            start(
                [
                    descriptor(
                        item, seq, chip, None, number, {"seq": place}, piece(item, place)
                    )
                    for number, place in enumerate(planes)
                ]
            )
        for item in pick(items, "seq", "all"):
            for half in cut(item):
                start(plane_copies(item, chip, half, sources[item]))
        for item in pick(items, "ctx", "all"):
            start([descriptor(item, seq, chip, None, kinds_relay + 2, sibling, sources[item])])

    def relays(items):
        for item in pick(items, "seq", "all"):
            plane_relay(item, chip)

    def waves(items):
        lines, everywhere = pick(items, "ctx", "all"), pick(items, "all")
        done = []
        for step in range(1, chip_count):
            wave = [
                (lax.rem(chip + chip_count - step, chip_count), chip >= step, *sides[0]),
                (lax.rem(chip + step, chip_count), chip <= last - step, *sides[1]),
            ]
            for place, there, onward, device in wave:
                for item in lines:
                    pass_on(item, place, there, onward, device)
            for item in everywhere:
                for place, there, _, _ in done[-1] if done else []:
                    plane_relay(item, place, there)
            if step == 1:
                for item in pick(items, "seq", "all"):
                    plane_end(item, chip)
            elif step > 2:
                for item in everywhere:
                    for place, there, _, _ in done[-2]:
                        plane_end(item, place, there)
            done.append(wave)
        for item in everywhere:
            for place, there, _, _ in done[-1]:
                plane_relay(item, place, there)
            for wave in done[-2:]:
                for place, there, _, _ in wave:
                    plane_end(item, place, there)

    def settle(items):
        for item in pick(items, "swap"):
            for place in planes:
                arrival(item, place, chip, None).wait_recv()
        for item in pick(items, "ctx", "all"):
            for at_seq in [seq] + (planes if scopes[item] == "all" else []):
                for step in range(chip_count):
                    arrival(item, at_seq, other(chip, step, chip_count), None, 1 - core).wait_recv()
        for item in items:
            locals_[item].wait()

    def end():
        for there, copy in started:
            if there is None:
                copy.wait_send()
            else:
                pl.when(there)(copy.wait_send)

    return peers, begin, relays, waves, settle, end


def spread_sems(arrays, scopes, seq_count, chip_count):
    kinds = 4 + max(4, seq_count - 1) + 3 + seq_count - 1
    sends, recvs, halves, shapes = [], [], [], []
    for array, scope in zip(arrays, scopes):
        lead = {"all": (seq_count, 2 * chip_count), "ctx": (2 * chip_count,)}.get(scope, (seq_count,))
        halves.append(seq_count == 4 and scope in ("all", "seq") and array.shape[0] % 32 == 0)
        shape = array.shape if scope == "swap" else lead + array.shape
        if scope == "swap" and array.ndim == 2:
            shape = (seq_count, array.shape[0], array.shape[1] // seq_count)
        shapes.append(jax.ShapeDtypeStruct(shape, array.dtype))
        rows = chip_count if scope in ("all", "ctx") else 1
        sends.append(pltpu.SemaphoreType.DMA((rows, kinds)))
        recvs.append(pltpu.SemaphoreType.DMA((2 * math.prod(lead),)))
    return shapes, tuple(halves), sends + recvs + [pltpu.SemaphoreType.DMA((len(arrays),))]


def swap_kernel(scopes, halves, seq_count, chip_count, *refs):
    count = len(scopes)
    peers, begin, _, _, settle, end = spread_tools(
        scopes,
        halves,
        seq_count,
        chip_count,
        refs[:count],
        refs[count : 2 * count],
        refs[2 * count : 3 * count],
        refs[3 * count : 4 * count],
        refs[4 * count],
    )
    meet(peers)
    begin(range(count))
    settle(range(count))
    end()


def swap(collective_id, arrays):
    seq_count, chip_count = lax.axis_size("seq"), lax.axis_size("ctx") // 2
    scopes = ("swap",) * len(arrays)
    shapes, halves, sems = spread_sems(arrays, scopes, seq_count, chip_count)
    anywhere = pl.BlockSpec(memory_space=pl.ANY)
    return pl.pallas_call(
        functools.partial(swap_kernel, scopes, halves, seq_count, chip_count),
        out_shape=tuple(shapes),
        in_specs=[anywhere] * len(arrays),
        out_specs=(anywhere,) * len(arrays),
        scratch_shapes=sems,
        compiler_params=pltpu.CompilerParams(collective_id=collective_id, has_side_effects=True),
        cost_estimate=pl.CostEstimate(
            flops=0, transcendentals=0, bytes_accessed=20 * 3_000_000
        ),
        name="swap",
    )(*arrays)


FOLD_SCRATCH = 9
WINDOW = 4


def fold_kernel(kinds, chunk_counts, swap_count, work, seq_count, chip_count, *refs):
    count = len(kinds)
    every = count + swap_count
    sources, swap_sources = refs[:count], refs[count:every]
    extra_in, extra_out = (work[0], work[1]) if work else (0, 0)
    first_out = every + extra_in
    results = refs[first_out : first_out + count]
    swap_results = refs[first_out + count : first_out + every]
    first_rest = first_out + every + extra_out
    rest = refs[first_rest:]
    swap_rest = rest[count * FOLD_SCRATCH : count * FOLD_SCRATCH + 4 * swap_count]
    extra = (
        refs[every:first_out],
        refs[first_out + every : first_rest],
        rest[count * FOLD_SCRATCH + 4 * swap_count :],
    )
    seq, chip, core = coords()
    slots, there = plane_slots(seq_count)
    planes = slots[1:]
    chips = [other(chip, step, chip_count) for step in range(1, chip_count)]
    sibling = {"ctx": chip * 2 + 1 - core}
    peers = []
    if any(kind != "seq" for kind in kinds):
        peers += [{"ctx": place * 2 + core} for place in chips] + [sibling]
    if swap_count or any(kind != "ctx" for kind in kinds):
        peers += [{"seq": place} for place in planes]

    def scratch(item):
        return rest[item * FOLD_SCRATCH : (item + 1) * FOLD_SCRATCH]

    def columns(item, chunk):
        width = sources[item].shape[-1] // chunk_counts[item]
        return slice(chunk * width, (chunk + 1) * width)

    order = []
    for chunk in range(max(chunk_counts, default=0)):
        order += [(item, chunk) for item in range(count) if chunk < chunk_counts[item]]

    loads = []
    for item in range(count):
        mine, sem_s = scratch(item)[0], scratch(item)[7]
        if kinds[item] != "seq":
            load = pltpu.make_async_copy(
                sources[item].at[:, :, core], mine, sem_s.at[4, 0, 0]
            )
            load.start()
            loads.append(load)
    meet(peers)

    waits = []

    def go(source, target, send_sem, recv_sem, device):
        copy = remote(source, target, send_sem, recv_sem, device)
        copy.start()
        waits.append(copy)
        return copy

    firsts = {}
    for item, chunk in order:
        if kinds[item] != "seq":
            _, got1, _, _, _, _, _, sem_s, sem_r = scratch(item)
            cols = columns(item, chunk)
            firsts[item, chunk] = go(
                sources[item].at[:, :, 1 - core, :, cols],
                got1.at[:, :, :, cols],
                sem_s.at[0, chunk, 0],
                sem_r.at[0, chunk, 0],
                sibling,
            )
    swapped = []
    for item in range(swap_count):
        got, sem_s, sem_r, sem_own = swap_rest[4 * item : 4 * item + 4]
        own = pltpu.make_async_copy(swap_sources[item].at[seq], got.at[seq], sem_own)
        own.start()
        swapped.append(own)
        for step, place in enumerate(planes):
            go(swap_sources[item].at[place], got.at[seq], sem_s.at[step], sem_r.at[seq], {"seq": place})
    for load in loads:
        load.wait()

    def block(item, slot, cols):
        if kinds[item] == "seq":
            return sources[item][slot, :, cols].astype(F32)[None]
        mine, got1 = scratch(item)[:2]
        place = slots[slot] if kinds[item] == "all" else 0
        return mine[place, :, :, cols].astype(F32) + got1[place, :, :, cols].astype(F32)

    def turn(item, chunk):
        return (1, 2) if (item + chunk) % 2 == 0 else (2, 1)

    seconds = {}

    def plane_first(item, chunk):
        _, got1, _, got2, keep, _, _, sem_s, sem_r = scratch(item)
        cols = columns(item, chunk)
        if kinds[item] == "all":
            firsts[item, chunk].wait_recv()
        first, _ = turn(item, chunk)
        targets = [(slot, slot) for slot in range(1, seq_count)]
        if seq_count == 4:
            targets = [(3, first), (first, first)]
        row = []
        for number, (slot, to) in enumerate(targets):
            if kinds[item] == "all":
                held = got1.at[slots[slot], :, :, cols]
                held[...] = block(item, slot, cols).astype(BF16)
            else:
                held = sources[item].at[pl.ds(slot, 1), :, cols]
            index = number if seq_count == 4 else there[slot] - 1
            row.append(
                go(
                    held,
                    got2.at[index, :, :, cols],
                    sem_s.at[1, chunk, number],
                    sem_r.at[1, chunk, index],
                    {"seq": slots[to]},
                )
            )
        seconds[item, chunk] = row
        keep[:, :, cols] = block(item, 0, cols)

    def plane_second(item, chunk):
        if seq_count != 4:
            return
        _, got1, spare, got2, keep, _, _, sem_s, sem_r = scratch(item)
        cols = columns(item, chunk)
        _, second = turn(item, chunk)
        across, mine = seconds[item, chunk]
        across.wait_recv()
        if kinds[item] == "all":
            held = got1.at[slots[second], :, :, cols]
        else:
            held = spare.at[:, :, cols]
        held[...] = (block(item, second, cols) + got2[0, :, :, cols].astype(F32)).astype(BF16)
        last = go(
            held,
            got2.at[2, :, :, cols],
            sem_s.at[2, chunk, 0],
            sem_r.at[2, chunk, 0],
            {"seq": slots[second]},
        )
        mine.wait_recv()
        keep[:, :, cols] = keep[:, :, cols] + got2[1, :, :, cols].astype(F32)
        seconds[item, chunk] = [last]

    thirds = {}

    def line(item, chunk):
        _, _, _, got2, keep, pass3, got3, sem_s, sem_r = scratch(item)
        cols = columns(item, chunk)
        if kinds[item] == "ctx":
            firsts[item, chunk].wait_recv()
            keep[:, :, cols] = block(item, 0, cols)
        else:
            for copy in seconds[item, chunk]:
                copy.wait_recv()

        def total(place):
            value = keep[place, :, cols]
            if kinds[item] != "ctx":
                for index in (2,) if seq_count == 4 else range(seq_count - 1):
                    value = value + got2[index, place, :, cols].astype(F32)
            return value

        if kinds[item] == "seq":
            results[item][:, cols] = total(0)
            return
        row = []
        for step, place in enumerate(chips):
            pass3[step, :, cols] = total(place).astype(BF16)
            row.append(
                go(
                    pass3.at[step, :, cols],
                    got3.at[step, :, cols],
                    sem_s.at[3, chunk, step],
                    sem_r.at[3, chunk, step],
                    {"ctx": place * 2 + core},
                )
            )
        results[item][:, cols] = total(chip)
        thirds[item, chunk] = row

    lines = [step for step in order if kinds[step[0]] == "ctx"]
    everywhere = [step for step in order if kinds[step[0]] == "all"]
    flats = [step for step in order if kinds[step[0]] == "seq"]
    for step in lines:
        line(*step)
    for step in everywhere[:WINDOW]:
        plane_first(*step)
    for number, step in enumerate(everywhere):
        plane_second(*step)
        for later in everywhere[number + WINDOW : number + WINDOW + 1]:
            plane_first(*later)
        if number:
            line(*everywhere[number - 1])
    for step in flats:
        plane_first(*step)
    if work:
        work[2](*extra)
    for step in everywhere[-1:]:
        line(*step)
    for step in flats:
        plane_second(*step)
    for step in flats:
        line(*step)
    for item, chunk in lines + everywhere:
        got3 = scratch(item)[6]
        cols = columns(item, chunk)
        for copy in thirds[item, chunk]:
            copy.wait_recv()
        value = results[item][:, cols]
        for step in range(chip_count - 1):
            value = value + got3[step, :, cols].astype(F32)
        results[item][:, cols] = value
    if work:
        work[3](results[0], *extra)
    for item in range(swap_count):
        got, sem_s, sem_r, _ = swap_rest[4 * item : 4 * item + 4]
        swapped[item].wait()
        for place in planes:
            remote(got.at[place], got.at[place], sem_s.at[0], sem_r.at[place], sibling).wait_recv()
        width = got.shape[-1]
        for place in range(seq_count):
            swap_results[item][:, place * width : (place + 1) * width] = got[place].astype(F32)
    for copy in waits:
        copy.wait_send()


def fold(name, collective_id, arrays, kinds, chunk_counts, micros, swaps=(), work=None):
    seq_count, ctx_count = lax.axis_size("seq"), lax.axis_size("ctx")
    chip_count = ctx_count // 2
    inputs, shapes, scratch, in_specs = [], [], [], []
    small = (1, 1, 8, 128)
    dma = pltpu.SemaphoreType.DMA
    for array, kind, chunks in zip(arrays, kinds, chunk_counts):
        parts = 1 if kind == "ctx" else seq_count
        blocks = seq_count if kind == "seq" else parts * ctx_count
        rows, cols = array.shape[0] // blocks, array.shape[1]
        lines = 1 if kind == "seq" else chip_count
        if kind == "seq":
            inputs.append(array.reshape(seq_count, rows, cols))
            in_specs.append(vmem())
            got1, spare = small, (1, rows, cols)
        else:
            inputs.append(array.reshape(parts, chip_count, 2, rows, cols))
            in_specs.append(pl.BlockSpec(memory_space=pl.ANY))
            got1, spare = (parts, chip_count, rows, cols), small[1:]
        shapes.append(jax.ShapeDtypeStruct((rows, cols), F32))
        got2 = small if kind == "ctx" else (seq_count - 1, lines, rows, cols)
        got3 = small[1:] if kind == "seq" else (chip_count - 1, rows, cols)
        most = max(seq_count, chip_count)
        scratch += [
            pltpu.VMEM(got1, BF16),
            pltpu.VMEM(got1, BF16),
            pltpu.VMEM(spare, BF16),
            pltpu.VMEM(got2, BF16),
            pltpu.VMEM((lines, rows, cols), F32),
            pltpu.VMEM(got3, BF16),
            pltpu.VMEM(got3, BF16),
            dma((5, chunks, most)),
            dma((4, chunks, most)),
        ]
    for array in swaps:
        inputs.append(array)
        in_specs.append(pl.BlockSpec(memory_space=pl.ANY))
        shapes.append(jax.ShapeDtypeStruct((array.shape[1], seq_count * array.shape[2]), F32))
        scratch += [
            pltpu.VMEM(array.shape, BF16),
            dma((seq_count - 1,)),
            dma((seq_count,)),
            dma,
        ]
    out_specs = [vmem()] * len(inputs)
    does = None
    if work:
        does = (len(work["inputs"]), len(work["shapes"]), work["during"], work["after"])
        inputs += work["inputs"]
        in_specs += work["in_specs"]
        shapes += work["shapes"]
        out_specs += work["out_specs"]
        scratch += work["scratch"]
    return pl.pallas_call(
        functools.partial(
            fold_kernel, tuple(kinds), tuple(chunk_counts), len(swaps), does, seq_count, chip_count
        ),
        out_shape=tuple(shapes),
        in_specs=in_specs,
        out_specs=tuple(out_specs),
        scratch_shapes=scratch,
        compiler_params=pltpu.CompilerParams(
            collective_id=collective_id, has_side_effects=True, vmem_limit_bytes=VMEM_MOST
        ),
        cost_estimate=pl.CostEstimate(
            flops=0, transcendentals=0, bytes_accessed=int(micros * 3_000_000)
        ),
        name=name,
    )(*inputs)


def tiles(extent, width, visit, first=0):
    whole = extent // width

    @pl.loop(first, whole)
    def _(number):
        visit(pl.ds(pl.multiple_of(number * width, width), width))

    if extent % width:
        visit(pl.ds(whole * width, extent % width))


def stream_rows(extent, width, produce, stage, sem, target):
    whole = extent // width

    def leave(slot, rows, size):
        return pltpu.make_async_copy(
            stage.at[slot, pl.ds(0, size)], target.at[rows], sem.at[slot]
        )

    @pl.loop(0, whole)
    def _(number):
        slot = lax.rem(number, 2)
        rows = pl.ds(pl.multiple_of(number * width, width), width)

        @pl.when(number >= 2)
        def _():
            leave(slot, rows, width).wait()

        stage[slot] = produce(rows).astype(stage.dtype)
        leave(slot, rows, width).start()

    for number in range(max(0, whole - 2), whole):
        leave(number % 2, pl.ds(number * width, width), width).wait()
    if extent % width:
        size = extent % width
        rows = pl.ds(whole * width, size)
        stage[0, :size] = produce(rows).astype(stage.dtype)
        leave(0, rows, size).start()
        leave(0, rows, size).wait()


def ffn_first_kernel(
    seq_count, f_ref, g_ref, wg_ref, wd_ref, f_out, g_out, gate_ref, gh_ref, f_s, g_s, wg, wd, in_sem, f_send, f_recv, out_sem
):
    rows = f_ref.shape[0]
    width = wg.shape[1]
    places, there = plane_slots(seq_count)
    load_f = pltpu.make_async_copy(f_ref, f_s.at[pl.ds(0, rows)], in_sem.at[seq_count])
    load_wd = pltpu.make_async_copy(wd_ref, wd, in_sem.at[seq_count + 1])
    load_wg = pltpu.make_async_copy(wg_ref, wg, in_sem.at[seq_count + 2])
    loads = [load_wd]
    for slot in range(seq_count):
        loads.append(
            pltpu.make_async_copy(
                g_ref.at[places[slot]], g_s.at[pl.ds(slot * rows, rows)], in_sem.at[slot]
            )
        )
    for load in [*loads, load_f, load_wg]:
        load.start()
    meet([{"seq": place} for place in places[1:]])

    started = []

    def f_block(slot, half):
        if half is None:
            return f_s.at[pl.ds(slot * rows, rows)]
        return f_s.at[pl.ds(slot * rows + half * (rows // 2), rows // 2)]

    def f_copy(source, to, slot, half):
        copy = remote(
            source,
            f_block(slot, half),
            f_send.at[len(started)],
            f_recv.at[slot, half or 0],
            {"seq": places[to]},
        )
        copy.start()
        started.append(copy)

    def f_arrive(slot, half):
        block = f_block(slot, half)
        remote(
            block, block, f_send.at[0], f_recv.at[slot, half or 0], {"seq": places[1]}
        ).wait_recv()

    if seq_count == 4:
        for half in (0, 1):
            source = f_ref.at[pl.ds(half * (rows // 2), rows // 2)]
            for to in (1, 2) if half == 0 else (2, 1):
                f_copy(source, to, to, half)
    else:
        for to in range(1, seq_count):
            f_copy(f_ref, to, there[to], None)

    def gate_rows(first, count):
        own = slice(first, first + count)

        def visit(cols):
            gate_ref[own, cols] = dot32(f_s[own, :], wg[:, cols], ((1,), (0,)))

        tiles(width, 256, visit)

    for load in loads:
        load.wait()
    leave_g = pltpu.make_async_copy(g_s, g_out, out_sem.at[1])
    leave_g.start()

    def grad_hidden(cols):
        gh_ref[:, cols] = dot32(g_s[...], wd[cols, :], ((1,), (1,))).astype(gh_ref.dtype)

    tiles(width, 256, grad_hidden)
    for load in (load_f, load_wg):
        load.wait()
    gate_rows(0, rows)
    if seq_count == 4:
        f_arrive(1, 0)
        f_copy(f_block(1, 0), 2, 3, 0)
        f_arrive(2, 1)
        f_copy(f_block(2, 1), 1, 3, 1)
        f_arrive(1, 1)
        f_arrive(2, 0)
        gate_rows(rows, 2 * rows)
        f_arrive(3, 0)
        f_arrive(3, 1)
        leave = pltpu.make_async_copy(f_s, f_out, out_sem.at[0])
        leave.start()
        gate_rows(3 * rows, rows)
    else:
        for slot in range(1, seq_count):
            f_arrive(slot, None)
        leave = pltpu.make_async_copy(f_s, f_out, out_sem.at[0])
        leave.start()
        gate_rows(rows, (seq_count - 1) * rows)
    leave.wait()
    leave_g.wait()
    for copy in started:
        copy.wait_send()


def ffn_act_kernel(
    f_ref, gate_ref, gh_ref, wu_ref, hid, gg, gu, pg_ref, f_s, gate_s, gh_s, wu, stage_f, in_sem, leave_sem
):
    model, width = wu.shape
    loads = [
        pltpu.make_async_copy(source, target, in_sem.at[number])
        for number, (source, target) in enumerate(
            [(f_ref, f_s), (wu_ref, wu), (gate_ref, gate_s), (gh_ref, gh_s)]
        )
    ]
    for load in loads:
        load.start()
    for load in loads[:2]:
        load.wait()

    def act(cols, ready=None):
        up_val = dot32(f_s[...], wu[:, cols], ((1,), (0,)))
        if ready is not None:
            ready()
        gate = gate_s[:, cols]
        grad = gh_s[:, cols].astype(F32)
        sigma = jax.nn.sigmoid(gate)
        activated = gate * sigma
        hid[:, cols] = (activated * up_val).astype(BF16)
        gg[:, cols] = (grad * up_val * (sigma + activated * (1.0 - sigma))).astype(BF16)
        gu[:, cols] = (grad * activated).astype(BF16)

    def ready():
        for load in loads[2:]:
            load.wait()

    act(pl.ds(0, 256), ready)
    tiles(width, 256, act, 1)
    stream_rows(
        model,
        256,
        lambda own: dot32(f_s[:, own], gg[...], ((0,), (0,))),
        stage_f,
        leave_sem,
        pg_ref,
    )


def ffn_grad_kernel(
    seq_count,
    f_ref,
    hid_ref,
    gg_ref,
    gu_ref,
    g_ref,
    wg_ref,
    wu_ref,
    wd_ref,
    gf_ref,
    out_ref,
    pu_ref,
    pd_ref,
    f_s,
    g_s,
    hid,
    gg,
    gu,
    wg,
    wu,
    wd,
    parts,
    got,
    stage_f,
    stage_d,
    in_sem,
    x_send,
    x_recv,
    leave_sem,
):
    rows = gf_ref.shape[0]
    model, width = wg.shape
    places, there = plane_slots(seq_count)
    loads = [
        pltpu.make_async_copy(source, target, in_sem.at[number])
        for number, (source, target) in enumerate(
            [
                (gg_ref, gg),
                (gu_ref, gu),
                (wg_ref, wg),
                (wu_ref, wu),
                (f_ref, f_s),
                (hid_ref, hid),
                (g_ref, g_s),
                (wd_ref, wd),
            ]
        )
    ]
    for load in loads[:4]:
        load.start()
    meet([{"seq": place} for place in places[1:]])
    for load in loads[:4]:
        load.wait()
    for load in loads[4:]:
        load.start()

    def part_copy(slot, cols):
        return remote(
            parts.at[pl.ds((slot - 1) * rows, rows), cols],
            got.at[there[slot] - 1, :, cols],
            x_send.at[slot],
            x_recv.at[there[slot]],
            {"seq": places[slot]},
        )

    def grad_f(cols):
        part = dot32(gg[...], wg[cols, :], ((1,), (1,))) + dot32(gu[...], wu[cols, :], ((1,), (1,)))
        gf_ref[:, cols] = part[:rows]
        parts[:, cols] = part[rows:].astype(BF16)
        for slot in range(1, seq_count):
            part_copy(slot, cols).start()

    tiles(model, 256, grad_f)
    for load in loads[4:]:
        load.wait()
    stream_rows(
        model,
        256,
        lambda own: dot32(f_s[:, own], gu[...], ((0,), (0,))),
        stage_f,
        leave_sem.at[0],
        pu_ref,
    )
    stream_rows(
        width,
        256,
        lambda own: dot32(hid[:, own], g_s[...], ((0,), (0,))),
        stage_d,
        leave_sem.at[2],
        pd_ref,
    )

    def out_copy(cols):
        return pltpu.make_async_copy(f_s.at[:, cols], out_ref.at[:, cols], leave_sem.at[1, 0])

    def out_part(cols):
        f_s[:, cols] = dot32(hid[...], wd[:, cols], ((1,), (0,))).astype(BF16)
        out_copy(cols).start()

    tiles(model, 256, out_part)
    everything = pl.ds(0, model)
    out_copy(everything).wait()
    for slot in range(1, seq_count):
        part_copy(slot, everything).wait_recv()
    total = gf_ref[...]
    for slot in range(seq_count - 1):
        total = total + got[slot].astype(F32)
    gf_ref[...] = total
    for slot in range(1, seq_count):
        part_copy(slot, everything).wait_send()


def ffn_first(collective_id, f_norm, g_all, w_gate, w_down):
    seq_count = lax.axis_size("seq")
    rows, model = f_norm.shape
    width = w_gate.shape[1]
    count = seq_count * rows
    anywhere = pl.BlockSpec(memory_space=pl.ANY)
    dma = pltpu.SemaphoreType.DMA
    return pl.pallas_call(
        functools.partial(ffn_first_kernel, seq_count),
        out_shape=(
            jax.ShapeDtypeStruct((count, model), BF16),
            jax.ShapeDtypeStruct((count, model), BF16),
            jax.ShapeDtypeStruct((count, width), F32),
            jax.ShapeDtypeStruct((count, width), BF16),
        ),
        in_specs=[anywhere] * 4,
        out_specs=(anywhere, anywhere, vmem(), vmem()),
        scratch_shapes=[
            pltpu.VMEM((count, model), BF16),
            pltpu.VMEM((count, model), BF16),
            pltpu.VMEM((model, width), BF16),
            pltpu.VMEM((width, model), BF16),
            dma((seq_count + 3,)),
            dma((max(6, seq_count),)),
            dma((seq_count, 2)),
            dma((2,)),
        ],
        compiler_params=pltpu.CompilerParams(
            collective_id=collective_id, has_side_effects=True, vmem_limit_bytes=VMEM_MOST
        ),
        cost_estimate=pl.CostEstimate(
            flops=8 * count * model * width,
            transcendentals=0,
            bytes_accessed=4 * (2 * width * model + 3 * count * model),
        ),
        name="ffn_first",
    )(f_norm, g_all.reshape(seq_count, rows, model), w_gate, w_down)


def ffn_act(f_all, gate, grad_hidden, w_up):
    count, model = f_all.shape
    width = w_up.shape[1]
    anywhere = pl.BlockSpec(memory_space=pl.ANY)
    dma = pltpu.SemaphoreType.DMA
    return pl.pallas_call(
        ffn_act_kernel,
        out_shape=(
            jax.ShapeDtypeStruct((count, width), BF16),
            jax.ShapeDtypeStruct((count, width), BF16),
            jax.ShapeDtypeStruct((count, width), BF16),
            jax.ShapeDtypeStruct((model, width), BF16),
        ),
        in_specs=[anywhere] * 4,
        out_specs=(vmem(), vmem(), vmem(), anywhere),
        scratch_shapes=[
            pltpu.VMEM((count, model), BF16),
            pltpu.VMEM((count, width), F32),
            pltpu.VMEM((count, width), BF16),
            pltpu.VMEM((model, width), BF16),
            pltpu.VMEM((2, 256, width), BF16),
            dma((4,)),
            dma((2,)),
        ],
        compiler_params=pltpu.CompilerParams(vmem_limit_bytes=VMEM_MOST),
        cost_estimate=pl.CostEstimate(
            flops=4 * count * model * width,
            transcendentals=count * width,
            bytes_accessed=4 * (width * model + 2 * count * model + 3 * count * width),
        ),
        name="ffn_act",
    )(f_all, gate, grad_hidden, w_up)


def ffn_grad(collective_id, rows, f_all, hidden_act, grad_gate, grad_up, g_all, w_gate, w_up, w_down):
    seq_count = lax.axis_size("seq")
    count, model = f_all.shape
    width = w_gate.shape[1]
    anywhere = pl.BlockSpec(memory_space=pl.ANY)
    dma = pltpu.SemaphoreType.DMA
    return pl.pallas_call(
        functools.partial(ffn_grad_kernel, seq_count),
        out_shape=(
            jax.ShapeDtypeStruct((rows, model), F32),
            jax.ShapeDtypeStruct((count, model), BF16),
            jax.ShapeDtypeStruct((model, width), BF16),
            jax.ShapeDtypeStruct((width, model), BF16),
        ),
        in_specs=[anywhere] * 8,
        out_specs=(vmem(), anywhere, anywhere, anywhere),
        scratch_shapes=[
            pltpu.VMEM((count, model), BF16),
            pltpu.VMEM((count, model), BF16),
            pltpu.VMEM((count, width), BF16),
            pltpu.VMEM((count, width), BF16),
            pltpu.VMEM((count, width), BF16),
            pltpu.VMEM((model, width), BF16),
            pltpu.VMEM((model, width), BF16),
            pltpu.VMEM((width, model), BF16),
            pltpu.VMEM((count - rows, model), BF16),
            pltpu.VMEM((seq_count - 1, rows, model), BF16),
            pltpu.VMEM((2, 256, width), BF16),
            pltpu.VMEM((2, 256, model), BF16),
            dma((8,)),
            dma((seq_count,)),
            dma((seq_count,)),
            dma((3, 2)),
        ],
        compiler_params=pltpu.CompilerParams(
            collective_id=collective_id, has_side_effects=True, vmem_limit_bytes=VMEM_MOST
        ),
        cost_estimate=pl.CostEstimate(
            flops=14 * count * model * width,
            transcendentals=0,
            bytes_accessed=4 * (3 * width * model + 3 * count * model),
        ),
        name="ffn_grad",
    )(f_all, hidden_act, grad_gate, grad_up, g_all, w_gate, w_up, w_down)


def half_turn(value):
    half = HEAD_DIM // 2
    return jnp.concatenate([-value[half:], value[:half]], axis=0)


GATHER_SCOPES = ("all", "all", "ctx", "all", "seq")


def project_kernel(
    halves,
    seq_count,
    chip_count,
    gain_src,
    w_src,
    wo_src,
    g_src,
    x_ref,
    cos_ref,
    sin_ref,
    gains_ref,
    w_ref,
    kv_ref,
    wo_ref,
    g_ref,
    normed_ref,
    rms_ref,
    q_ref,
    gain_a_ref,
    gain_f_ref,
    kv_own,
    w_s,
    gains_s,
    load_sem,
    *sems,
):
    tile = KV_HEADS * HEAD_DIM
    model, own_rows, width = x_ref.shape[1], w_src.shape[0], w_src.shape[1]
    count = width // tile
    peers, begin, relays, waves, settle, end = spread_tools(
        GATHER_SCOPES,
        halves,
        seq_count,
        chip_count,
        (gain_src, w_src, kv_own, wo_src, g_src),
        (gains_ref, w_ref, kv_ref, wo_ref, g_ref),
        sems[:5],
        sems[5:10],
        sems[10],
    )
    meet(peers)
    begin((0, 1))
    x = x_ref[...].astype(F32)
    rms = lax.rsqrt(jnp.mean(x * x, axis=1, keepdims=True) + EPS)
    rms_ref[...] = rms
    relays((0, 1))
    waves((0, 1))
    begin((3,))
    settle((0, 1))

    def load(number):
        cols = pl.ds(pl.multiple_of(number * tile, tile), tile)
        return pltpu.make_async_copy(
            w_ref.at[:, :, :, cols], w_s.at[:, :, :, cols], load_sem.at[number]
        )

    load_gains = pltpu.make_async_copy(gains_ref, gains_s, load_sem.at[count])
    load_gains.start()
    for number in range(count):
        load(number).start()
    load_gains.wait()
    for number in range(seq_count * 2 * chip_count):
        at_seq, at_ctx = divmod(number, 2 * chip_count)
        row = gains_s[at_seq, at_ctx, 0:1, :].astype(F32)
        own = slice(number * own_rows, (number + 1) * own_rows)
        gain_a_ref[:, own] = row[:, :own_rows]
        gain_f_ref[:, own] = row[:, own_rows : 2 * own_rows]
    normed_ref[...] = (x_ref[...].astype(F32) * rms_ref[...] * gain_a_ref[...]).astype(BF16)

    def product(number):
        load(number).wait()
        cols = pl.ds(pl.multiple_of(number * tile, tile), tile)
        return dot32(normed_ref[...], w_s[:, :, :, cols].reshape(model, tile), ((1,), (0,)))

    def rotated(value):
        turned = value.T
        pieces = []
        for head in range(tile // HEAD_DIM):
            one = turned[head * HEAD_DIM : (head + 1) * HEAD_DIM]
            pieces.append(one * cos_ref[...] + half_turn(one) * sin_ref[...])
        return jnp.concatenate(pieces, axis=0)

    kv_own[:, :tile] = rotated(product(count - 2)).T.astype(BF16)
    kv_own[:, tile:] = product(count - 1).astype(BF16)
    begin((2,))
    begin((4,))
    relays((3, 4))

    @pl.loop(0, count - 2)
    def _(number):
        own = pl.ds(pl.multiple_of(number * tile, tile), tile)
        q_ref[own, :] = rotated(product(number)).astype(BF16)

    waves((3, 4, 2))
    settle((3, 4, 2))
    end()


def project(collective_id, gain_row, w_qkv, w_out, g_own, x, cosine, sine):
    seq_count, ctx_count = lax.axis_size("seq"), lax.axis_size("ctx")
    chip_count = ctx_count // 2
    rows, model = x.shape
    width = w_qkv.shape[1]
    tile = KV_HEADS * HEAD_DIM
    kv_like = jax.ShapeDtypeStruct((rows, 2 * tile), BF16)
    shapes, halves, sems = spread_sems(
        [gain_row, w_qkv, kv_like, w_out, g_own], GATHER_SCOPES, seq_count, chip_count
    )
    anywhere = pl.BlockSpec(memory_space=pl.ANY)
    return pl.pallas_call(
        functools.partial(project_kernel, halves, seq_count, chip_count),
        out_shape=(
            *shapes,
            jax.ShapeDtypeStruct((rows, model), BF16),
            jax.ShapeDtypeStruct((rows, 1), F32),
            jax.ShapeDtypeStruct((width - 2 * tile, rows), BF16),
            jax.ShapeDtypeStruct((1, model), F32),
            jax.ShapeDtypeStruct((1, model), F32),
        ),
        in_specs=[anywhere] * 4 + [vmem()] * 3,
        out_specs=(anywhere,) * 5 + (vmem(),) * 5,
        scratch_shapes=[
            pltpu.VMEM((rows, 2 * tile), BF16),
            pltpu.VMEM(shapes[1].shape, BF16),
            pltpu.VMEM(shapes[0].shape, BF16),
            pltpu.SemaphoreType.DMA((width // tile + 1,)),
            *sems,
        ],
        compiler_params=pltpu.CompilerParams(
            collective_id=collective_id, has_side_effects=True, vmem_limit_bytes=VMEM_MOST
        ),
        cost_estimate=pl.CostEstimate(
            flops=0, transcendentals=0, bytes_accessed=140 * 3_000_000
        ),
        name="project",
    )(gain_row, w_qkv, w_out, g_own, x, cosine, sine)


def rotated_back(value, cos_ref, sin_ref):
    pieces = []
    for head in range(value.shape[0] // HEAD_DIM):
        one = value[head * HEAD_DIM : (head + 1) * HEAD_DIM]
        pieces.append(one * cos_ref[...] - half_turn(one * sin_ref[...]))
    return jnp.concatenate(pieces, axis=0).T.astype(BF16)


def back_during(inputs, outputs, scratch):
    dq_ref, o_ref, cos_ref, sin_ref, normed_ref, x_ref, rms_ref, gain_ref, grad_ref, w_ref = inputs
    part_out, part_query, part_kv, out_ref, gain_out = outputs
    w_s, g_s, gx_s, ga_s, stage, stage_kv, load_sem, leave_sem = scratch
    tile = KV_HEADS * HEAD_DIM
    q_width = dq_ref.shape[0]
    model = x_ref.shape[1]
    pltpu.make_async_copy(w_ref, w_s, load_sem).start()
    ga_s[...] = grad_ref[...].astype(BF16)
    stream_rows(
        q_width,
        256,
        lambda own: dot32(o_ref[own, :], ga_s[...], ((1,), (0,))),
        stage,
        leave_sem,
        part_out,
    )

    @pl.loop(0, q_width // tile)
    def _(number):
        own = pl.ds(pl.multiple_of(number * tile, tile), tile)
        g_s[:, own] = rotated_back(dq_ref[own, :], cos_ref, sin_ref)

    stream_rows(
        model,
        256,
        lambda own: dot32(normed_ref[:, own], g_s[:, :q_width], ((0,), (0,))),
        stage,
        leave_sem,
        part_query,
    )
    pltpu.make_async_copy(w_ref, w_s, load_sem).wait()

    def grad_x(cols):
        gx_s[:, cols] = dot32(g_s[:, :q_width], w_s[cols, :q_width], ((1,), (1,)))

    tiles(model, 256, grad_x)


def back_after(dkv_ref, inputs, outputs, scratch):
    dq_ref, o_ref, cos_ref, sin_ref, normed_ref, x_ref, rms_ref, gain_ref, grad_ref, w_ref = inputs
    part_out, part_query, part_kv, out_ref, gain_out = outputs
    w_s, g_s, gx_s, ga_s, stage, stage_kv, load_sem, leave_sem = scratch
    tile = KV_HEADS * HEAD_DIM
    q_width = dq_ref.shape[0]
    model = x_ref.shape[1]
    g_s[:, q_width : q_width + tile] = rotated_back(dkv_ref[:, :tile].T, cos_ref, sin_ref)
    g_s[:, q_width + tile :] = dkv_ref[:, tile:].astype(BF16)
    stream_rows(
        model,
        256,
        lambda own: dot32(normed_ref[:, own], g_s[:, q_width:], ((0,), (0,))),
        stage_kv,
        leave_sem,
        part_kv,
    )

    def grad_x(cols):
        gx_s[:, cols] = gx_s[:, cols] + dot32(g_s[:, q_width:], w_s[cols, q_width:], ((1,), (1,)))

    tiles(model, 256, grad_x)
    x = x_ref[...].astype(F32)
    rms = rms_ref[...]
    gain_out[...] = jnp.sum(gx_s[...] * (x * rms), axis=0, keepdims=True)
    scaled = gx_s[...] * gain_ref[...]
    mean = jnp.mean(scaled * x, axis=1, keepdims=True)
    out_ref[...] = grad_ref[...] + (rms * scaled - x * (rms * rms * rms * mean))


def back_work(dq_t, o_t, cosine, sine, normed, x, rms, gain, grad, w_qkv):
    rows, model = x.shape
    width = w_qkv.shape[1]
    q_width = dq_t.shape[0]
    anywhere = pl.BlockSpec(memory_space=pl.ANY)
    return {
        "inputs": [dq_t, o_t, cosine, sine, normed, x, rms, gain, grad, w_qkv],
        "in_specs": [vmem()] * 9 + [anywhere],
        "shapes": [
            jax.ShapeDtypeStruct((q_width, model), BF16),
            jax.ShapeDtypeStruct((model, q_width), BF16),
            jax.ShapeDtypeStruct((model, width - q_width), BF16),
            jax.ShapeDtypeStruct((rows, model), F32),
            jax.ShapeDtypeStruct((1, model), F32),
        ],
        "out_specs": [anywhere, anywhere, anywhere, vmem(), vmem()],
        "scratch": [
            pltpu.VMEM(w_qkv.shape, BF16),
            pltpu.VMEM((rows, width), BF16),
            pltpu.VMEM((rows, model), F32),
            pltpu.VMEM((rows, model), BF16),
            pltpu.VMEM((2, 256, max(model, q_width)), BF16),
            pltpu.VMEM((2, 256, width - q_width), BF16),
            pltpu.SemaphoreType.DMA,
            pltpu.SemaphoreType.DMA((2,)),
        ],
        "during": back_during,
        "after": back_after,
    }


def gather(value, axes, dim=0):
    return lax.all_gather(value, axes, axis=dim, tiled=True)


def scatter_sum(value, axes, dim=0):
    return lax.psum_scatter(value, axes, scatter_dimension=dim, tiled=True)


def local(
    hidden_in,
    attn_gain,
    w_query,
    w_key,
    w_value,
    w_out,
    ffn_gain,
    w_gate,
    w_up,
    w_down,
    cotangent,
    doc_lengths,
    selected,
    block_order,
):
    one, rows, model = hidden_in.shape
    seq_count = lax.axis_size("seq")
    ctx_count = lax.axis_size("ctx")
    place = lax.axis_index("ctx").astype(jnp.int32).reshape(1)
    length = rows * ctx_count
    span_len = length // block_order.shape[0]
    q_width = HEADS * HEAD_DIM
    kv_width = KV_HEADS * HEAD_DIM
    own_rows = w_gate.shape[0]
    ff_part = w_gate.shape[1] // seq_count

    def split_columns(weight):
        if ff_part % 128 == 0:
            return weight
        return weight.reshape(own_rows, seq_count, ff_part).transpose(1, 0, 2)

    own_spans = lax.dynamic_slice_in_dim(block_order, place[0] * (rows // span_len), rows // span_len)
    local_pos = (
        own_spans[:, None] * span_len + jnp.arange(span_len, dtype=jnp.int32)[None, :]
    ).reshape(rows)
    half = HEAD_DIM // 2
    inverse = ROPE_BASE ** (-(jnp.arange(half, dtype=F32) * 2.0 / HEAD_DIM))
    angle = inverse[:, None] * local_pos.astype(F32)[None, :]
    cosine = jnp.concatenate([jnp.cos(angle)] * 2, axis=0)
    sine = jnp.concatenate([jnp.sin(angle)] * 2, axis=0)

    full_down = gather(w_down, "ctx")
    gain_row = jnp.pad(jnp.concatenate([attn_gain, ffn_gain])[None], ((0, 15), (0, 128 - 2 * own_rows)))
    gate_mine, up_mine = swap(0, [split_columns(w_gate), split_columns(w_up)])
    full_gate = gather(gate_mine, "ctx", 1).reshape(model, ff_part)
    full_up = gather(up_mine, "ctx", 1).reshape(model, ff_part)

    g_own = jnp.where(
        selected.reshape(rows)[:, None] != 0, cotangent.reshape(rows, model), jnp.zeros((), BF16)
    )
    _, w_qkv, kv, full_out, g_all, x_norm, rms_a, q_t, gain_a, gain_f = project(
        1,
        gain_row,
        jnp.concatenate([w_query, w_key, w_value], axis=1),
        w_out,
        g_own,
        hidden_in.reshape(rows, model),
        cosine,
        sine,
    )
    w_qkv = w_qkv.reshape(model, q_width + 2 * kv_width)
    kv = kv.reshape(length, 2 * kv_width)
    full_out = full_out.reshape(q_width, model)
    o_t, lse, middle, rms_f, f_norm = attend_forward(
        place, block_order, doc_lengths, q_t, kv, hidden_in.reshape(rows, model), gain_f, full_out
    )
    f_all, g_slots, gate, grad_hidden = ffn_first(2, f_norm, g_all, full_gate, full_down)
    hidden_act, grad_gate, grad_up, part_gate = ffn_act(f_all, gate, grad_hidden, full_up)
    grad_f_norm, ffn_part, part_up, part_down = ffn_grad(
        3, rows, f_all, hidden_act, grad_gate, grad_up, g_slots, full_gate, full_up, full_down
    )

    def ffn_rows(part):
        return scatter_sum(part.reshape(seq_count, model // seq_count, ff_part), "ctx", 1)

    rows_gate = ffn_rows(part_gate)
    rows_up = ffn_rows(part_up)
    dq_t, dkv, grad_middle, grad_ffn_gain = attend_backward(
        place,
        block_order,
        doc_lengths,
        q_t,
        kv,
        o_t,
        lse,
        grad_f_norm,
        middle,
        rms_f,
        gain_f,
        g_own,
        full_out,
    )
    part_down, rows_gate, dkv = lax.optimization_barrier((part_down, rows_gate, dkv))
    grad_w_down = scatter_sum(part_down, "ctx").astype(F32)
    _, ffn_out, grad_w_gate, part_out, part_query, part_kv, grad_input, grad_attn_gain = fold(
        "fold_kv",
        4,
        [dkv, ffn_part],
        ("ctx", "seq"),
        (1, 2),
        60,
        [rows_gate],
        work=back_work(
            dq_t,
            o_t,
            cosine,
            sine,
            x_norm,
            hidden_in.reshape(rows, model),
            rms_a,
            gain_a,
            grad_middle,
            w_qkv,
        ),
    )
    output = (middle + ffn_out).astype(BF16).reshape(one, rows, model)
    part_gains = jnp.concatenate(
        [grad_attn_gain.reshape(-1, own_rows), grad_ffn_gain.reshape(-1, own_rows)], axis=1
    )
    part_gains = jnp.pad(part_gains[:, None], ((0, 0), (0, 15), (0, 128 - 2 * own_rows)))
    grad_w_out, grad_w_query, grad_w_kv, grad_gains, grad_w_up = fold(
        "fold_weights",
        5,
        [part_out, part_query, part_kv, part_gains.reshape(-1, 128).astype(BF16)],
        ("all", "all", "all", "all"),
        (8, 8, 2, 1),
        110,
        [rows_up],
    )
    return (
        output,
        grad_input.reshape(one, rows, model),
        grad_gains[0, :own_rows],
        grad_w_query,
        grad_w_kv[:, :kv_width],
        grad_w_kv[:, kv_width:],
        grad_w_out,
        grad_gains[0, own_rows : 2 * own_rows],
        grad_w_gate,
        grad_w_up,
        grad_w_down,
    )


def solution(mesh):
    return jax.shard_map(
        local,
        mesh=mesh,
        in_specs=(
            P("seq", "ctx", None),
            P(("seq", "ctx")),
            P(("seq", "ctx"), None),
            P(("seq", "ctx"), None),
            P(("seq", "ctx"), None),
            P(("seq", "ctx"), None),
            P(("seq", "ctx")),
            P(("seq", "ctx"), None),
            P(("seq", "ctx"), None),
            P(("seq", "ctx"), None),
            P("seq", "ctx", None),
            P("seq", None),
            P("seq", "ctx"),
            P(),
        ),
        out_specs=(
            P("seq", "ctx", None),
            P("seq", "ctx", None),
            P(("seq", "ctx")),
            P(("seq", "ctx"), None),
            P(("seq", "ctx"), None),
            P(("seq", "ctx"), None),
            P(("seq", "ctx"), None),
            P(("seq", "ctx")),
            P(("seq", "ctx"), None),
            P(("seq", "ctx"), None),
            P(("seq", "ctx"), None),
        ),
        check_vma=False,
    )
```
